32 devices in a mesh: grp: 4 (over z), blk: 8 (over y, x, core).
Axes of the slice: x: 2, y: 2, z: 4, core: 2. Of those that a mesh axis runs over, the one named last changes fastest.
Arguments:
- tokens: bfloat16 [8192, 2048], P(('grp', 'blk')), may hold values from -9 to 9
- block_group: int32 [64], replicated, may hold values from 0 to 3, as said below
- block_slot: int32 [64], replicated, may hold values from 0 to 15, as said below
- attn_gain: bfloat16 [2048], P(('grp', 'blk')), may hold values from 0.5 to 1.5
- w_query: bfloat16 [2048, 2048], P(('grp', 'blk')), may hold values from -0.5 to 0.5
- w_key: bfloat16 [2048, 512], P(('grp', 'blk')), may hold values from -0.5 to 0.5
- w_value: bfloat16 [2048, 512], P(('grp', 'blk')), may hold values from -0.125 to 0.125
- w_out: bfloat16 [2048, 2048], P(('grp', 'blk')), may hold values from -2 to 2
- mlp_gain: bfloat16 [2048], P(('grp', 'blk')), may hold values from 0.5 to 1.5
- w_gate: bfloat16 [2048, 8192], P(None, ('grp', 'blk')), may hold values from -0.125 to 0.125
- w_up: bfloat16 [2048, 8192], P(None, ('grp', 'blk')), may hold values from -0.125 to 0.125
- w_down: bfloat16 [8192, 2048], P(('grp', 'blk')), may hold values from -0.5 to 0.5
- cotangent: bfloat16 [8192, 2048], P(('grp', 'blk')), may hold values from -6 to 6
Outputs:
- output: bfloat16 [8192, 2048], P(('grp', 'blk'))
- tokens_grad: bfloat16 [8192, 2048], P(('grp', 'blk'))
- attn_gain_grad: float32 [2048], P(('grp', 'blk'))
- w_query_grad: float32 [2048, 2048], P(('grp', 'blk'))
- w_key_grad: float32 [2048, 512], P(('grp', 'blk'))
- w_value_grad: float32 [2048, 512], P(('grp', 'blk'))
- w_out_grad: float32 [2048, 2048], P(('grp', 'blk'))
- mlp_gain_grad: float32 [2048], P(('grp', 'blk'))
- w_gate_grad: float32 [2048, 8192], P(None, ('grp', 'blk'))
- w_up_grad: float32 [2048, 8192], P(None, ('grp', 'blk'))
- w_down_grad: float32 [8192, 2048], P(('grp', 'blk'))
- rms_stats: float32 [3], replicated
The draws below stay inside these ranges and needn't reach their ends.
Inputs may be any that keep to these rules, and one draw needn't show every extreme that they name: `block_group`: each group has 16 blocks, one of each slot, and all of them lie in one aligned run of 16 blocks. `block_slot`: slots below 8 are the prompt's parts in order, the others its continuations.
All inputs are finite; a program needn't handle non-finite values.
Results may differ from the reference program's by a relative error of at most 0.019.
Values may be sent and summed in bfloat16 or wider, within the bound.
A program may use at most 448 MiB of HBM per device.

```python
import jax
import jax.numpy as jnp
from jax import lax

D = 2048
HEADS = 32
KV_HEADS = 8
HEAD_DIM = 64
FF = 8192
BLOCK = 128
PROMPT_BLOCKS = 8
GROUP_BLOCKS = 16
NBLK = 64
ROW_BLOCKS = 16
GROUPS = 4
TOKENS = 8192


def draw_tokens(key, part):
    row_index = jnp.arange(TOKENS, dtype=jnp.float32)
    rise_factor = jnp.exp(jnp.log(3.0) * (row_index / (TOKENS - 1) - 0.5))
    base_draw = jax.random.truncated_normal(key, -4.0, 4.0, (TOKENS, D), jnp.float32)
    return (base_draw * rise_factor[:, None]).astype(jnp.bfloat16)


def block_tables(key):
    row_count = NBLK // ROW_BLOCKS
    row_keys = jax.random.split(jax.random.fold_in(key, 11), row_count)

    def permute(row_key):
        return jax.random.permutation(row_key, ROW_BLOCKS)
    row_perms = jax.vmap(permute)(row_keys).astype(jnp.int32)
    row_ids = jnp.arange(row_count, dtype=jnp.int32)[:, None]
    groups = row_ids * (ROW_BLOCKS // GROUP_BLOCKS) + row_perms // GROUP_BLOCKS
    slot_ids = row_perms % GROUP_BLOCKS
    return (groups.reshape(NBLK).astype(jnp.int32), slot_ids.reshape(NBLK).astype(jnp.int32))


def draw_block_group(key, part):
    return block_tables(key)[0]


def draw_block_slot(key, part):
    return block_tables(key)[1]


def levels(key, shape, pieces, least, largest):
    level, own = 1.0, jax.random.fold_in(key, 6)
    for dim, shards_of in pieces:
        steps = jnp.exp(jax.random.uniform(jax.random.fold_in(own, dim), (shards_of,), jnp.float32, least / len(pieces), largest / len(pieces)))
        level = level * jnp.repeat(steps, shape[dim] // shards_of).reshape([-1 if axis == dim else 1 for axis in range(len(shape))])
    return level


def bell_draw(own_key, shape, spread, limit, pieces=(), kind=jnp.bfloat16):
    array = spread * jax.random.normal(own_key, shape, jnp.float32)
    if pieces:
        array = array * levels(own_key, shape, pieces, -0.22, 0.18)
    return jnp.clip(array, -limit, limit).astype(kind)


def setup_inputs(seed: int = 0) -> dict:
    splits = jax.random.split(jax.random.key(seed), 14)
    return {
        "tokens": draw_tokens(jax.random.fold_in(splits[13], 71), 0),
        "block_group": draw_block_group(jax.random.fold_in(splits[13], 71), 0),
        "block_slot": draw_block_slot(jax.random.fold_in(splits[13], 71), 0),
        "attn_gain": jnp.clip(1.0 + 0.1 * jax.random.normal(splits[3], (D,), jnp.float32), 0.5, 1.5).astype(jnp.bfloat16),
        "w_query": bell_draw(splits[4], (D, D), (D // 16) ** -0.5, 0.5, ((0, 32),)),
        "w_key": bell_draw(splits[5], (D, KV_HEADS * HEAD_DIM), (D // 16) ** -0.5, 0.5, ((0, 32),)),
        "w_value": bell_draw(splits[6], (D, KV_HEADS * HEAD_DIM), D ** -0.5, 0.125, ((0, 32),)),
        "w_out": bell_draw(splits[7], (D, D), (max(D // 256, 1)) ** -0.5, 2.0, ((0, 32),)),
        "mlp_gain": jnp.clip(1.0 + 0.1 * jax.random.normal(splits[8], (D,), jnp.float32), 0.5, 1.5).astype(jnp.bfloat16),
        "w_gate": bell_draw(splits[9], (D, FF), D ** -0.5, 0.125, ((1, 32),)),
        "w_up": bell_draw(splits[10], (D, FF), D ** -0.5, 0.125, ((1, 32),)),
        "w_down": bell_draw(splits[11], (FF, D), (FF // 64) ** -0.5, 0.5, ((0, 32),)),
        "cotangent": bell_draw(splits[12], (TOKENS, D), 1.0, 6.0, ((0, 32),)),
    }


ATTN_MULT = 0.015625
RESID_MULT = 0.22
EPSILON = 1e-05
MASKED = -1e+30
HIGH = lax.Precision.HIGHEST

@jax.custom_vjp
def low(v):
    return lax.optimization_barrier(v.astype(jnp.bfloat16)).astype(jnp.float32)

@jax.custom_vjp
def low_back(v):
    return v

def low_keep(v):
    return (low(v), None)

def low_pass(kept, grad):
    return (grad,)

def back_keep(v):
    return (v, None)

def back_low(kept, grad):
    return (low(grad),)
low.defvjp(low_keep, low_pass)
low_back.defvjp(back_keep, back_low)

def rms_norm(values, gain):
    factor = lax.rsqrt(lax.optimization_barrier(jnp.mean(values * values, axis=-1, keepdims=True)) + EPSILON)
    return values * factor * gain

def matmul(left, right):
    return jnp.dot(left, right, precision=HIGH, preferred_element_type=jnp.float32)

def attend(query_heads, key_heads, value_heads, visible):
    raw_scores = jnp.einsum('ikgd,jkd->kgij', query_heads, key_heads, precision=HIGH)
    scores = low_back(ATTN_MULT * raw_scores)
    scores = jnp.where(visible, scores, MASKED)
    row_peak = lax.optimization_barrier(jnp.max(scores, axis=-1, keepdims=True))
    shifted = jnp.exp(scores - row_peak)
    soft_probs = shifted / lax.optimization_barrier(jnp.sum(shifted, axis=-1, keepdims=True))
    mixed_rows = jnp.einsum('kgij,jkd->ikgd', low(soft_probs), value_heads, precision=HIGH)
    return mixed_rows.reshape(mixed_rows.shape[0], D)

def block_forward(layer_in, gain_one, w_query, w_key, w_value, w_out, gain_two, w_gate, w_up, w_down, block_order, inverse, visible):
    seq_len = GROUP_BLOCKS * BLOCK
    per_group = HEADS // KV_HEADS
    normed_one = low(rms_norm(layer_in, gain_one))
    queries = low_back(low(matmul(normed_one, w_query)))
    key_rows = low_back(low(matmul(normed_one, w_key)))
    value_rows = low_back(low(matmul(normed_one, w_value)))
    query_groups = queries.reshape(NBLK, BLOCK, D)[block_order].reshape(GROUPS, seq_len, KV_HEADS, per_group, HEAD_DIM)
    key_groups = key_rows.reshape(NBLK, BLOCK, KV_HEADS * HEAD_DIM)[block_order].reshape(GROUPS, seq_len, KV_HEADS, HEAD_DIM)
    value_groups = value_rows.reshape(NBLK, BLOCK, KV_HEADS * HEAD_DIM)[block_order].reshape(GROUPS, seq_len, KV_HEADS, HEAD_DIM)

    def one_group(operands):
        return attend(operands[0], operands[1], operands[2], visible)
    mixed_rows = lax.map(jax.checkpoint(one_group), (query_groups, key_groups, value_groups))
    attended = mixed_rows.reshape(NBLK, BLOCK, D)[inverse].reshape(TOKENS, D)
    attended = low_back(low(attended))
    branch_attn = low_back(matmul(attended, w_out))
    residual = layer_in + RESID_MULT * branch_attn
    normed_two = low(rms_norm(residual, gain_two))
    gate_act = low_back(matmul(normed_two, w_gate))
    up_act = low_back(matmul(normed_two, w_up))
    hidden = low(jax.nn.silu(gate_act) * up_act)
    branch_mlp = low_back(matmul(hidden, w_down))
    layer_out = residual + RESID_MULT * branch_mlp
    return (layer_out, branch_attn, branch_mlp)

def reference(tokens, block_group, block_slot, attn_gain, w_query, w_key, w_value, w_out, mlp_gain, w_gate, w_up, w_down, cotangent):
    block_order = jnp.argsort(block_group * GROUP_BLOCKS + block_slot).astype(jnp.int32)
    inverse = jnp.argsort(block_order).astype(jnp.int32)
    seq_len = GROUP_BLOCKS * BLOCK
    prompt_len = PROMPT_BLOCKS * BLOCK
    places = jnp.arange(seq_len, dtype=jnp.int32)
    slot_of = places // BLOCK
    position = jnp.where(slot_of < PROMPT_BLOCKS, places, prompt_len + places % BLOCK)
    visible = (position[None, :] <= position[:, None]) & ((slot_of[None, :] < PROMPT_BLOCKS) | (slot_of[None, :] == slot_of[:, None]))
    primals = tuple((argument.astype(jnp.float32) for argument in (tokens, attn_gain, w_query, w_key, w_value, w_out, mlp_gain, w_gate, w_up, w_down)))

    def forward(*inputs):
        return block_forward(*inputs, block_order, inverse, visible)
    outputs, pullback = jax.vjp(forward, *primals)
    layer_out, branch_attn, branch_mlp = outputs
    gradients = pullback((cotangent.astype(jnp.float32), jnp.zeros_like(branch_attn), jnp.zeros_like(branch_mlp)))
    scaled_attn = RESID_MULT * branch_attn
    scaled_mlp = RESID_MULT * branch_mlp
    rms_stats = jnp.stack([jnp.sqrt(jnp.mean(layer_out * layer_out)), jnp.sqrt(jnp.mean(scaled_attn * scaled_attn)), jnp.sqrt(jnp.mean(scaled_mlp * scaled_mlp))])
    return (layer_out.astype(jnp.bfloat16), gradients[0].astype(jnp.bfloat16), gradients[1], gradients[2], gradients[3], gradients[4], gradients[5], gradients[6], gradients[7], gradients[8], gradients[9], rms_stats)
```

```python
import jax
import jax.numpy as jnp
from jax import lax
from jax.sharding import Mesh
from jax.sharding import PartitionSpec as P

D = 2048
HEADS = 32
KV_HEADS = 8
HEAD_DIM = 64
BLOCK = 128
PROMPT_BLOCKS = 8
GROUP_BLOCKS = 16
PER_GROUP = HEADS // KV_HEADS

ATTN_MULT = 0.015625
RESID_MULT = 0.22
EPSILON = 1e-05
MASKED = -1e30

PLANE = ("chip", "core")
EVERY = ("grp", "chip", "core")
BF16 = jnp.bfloat16
F32 = jnp.float32


def matmul(left, right):
    return jnp.dot(left, right, preferred_element_type=F32)


def over_rows(left, right):
    return lax.dot_general(left, right, (((0,), (0,)), ((), ())), preferred_element_type=F32)


def over_cols(left, right):
    return lax.dot_general(left, right, (((1,), (1,)), ((), ())), preferred_element_type=F32)


def gather(values, axes, axis=0):
    return lax.all_gather(values, axes, axis=axis, tiled=True)


def scatter(values, axes, axis=0):
    return lax.psum_scatter(values, axes, scatter_dimension=axis, tiled=True)


def norm_parts(values):
    factor = lax.rsqrt(jnp.mean(values * values, axis=-1, keepdims=True) + EPSILON)
    return factor


def norm_back(values, factor, gain, grad):
    scaled = gain * grad
    inner = jnp.mean(values * scaled, axis=-1, keepdims=True)
    return factor * scaled - values * (factor * factor * factor * inner), jnp.sum(
        grad * values * factor, axis=0
    )


def on_device(
    tokens,
    block_group,
    block_slot,
    attn_gain,
    w_query,
    w_key,
    w_value,
    w_out,
    mlp_gain,
    w_gate,
    w_up,
    w_down,
    cotangent,
):
    tok_axes, weight_axes = TOK_AXES, WEIGHT_AXES
    grps = lax.axis_size("grp")
    devs = lax.axis_size(PLANE)
    rows = tokens.shape[0]
    w_rows = w_query.shape[0]
    q_heads = HEADS // devs
    kv_heads = max(1, KV_HEADS // devs)
    kv_copies = max(1, devs // KV_HEADS)
    q_cols, kv_cols = q_heads * HEAD_DIM, kv_heads * HEAD_DIM
    row_blocks = rows // BLOCK * devs
    row_groups = row_blocks // GROUP_BLOCKS

    row_first = lax.axis_index("grp") * row_blocks
    keys = lax.dynamic_slice_in_dim(block_group, row_first, row_blocks) * GROUP_BLOCKS
    keys = keys + lax.dynamic_slice_in_dim(block_slot, row_first, row_blocks)
    rank = jnp.sum((keys[None, :] < keys[:, None]).astype(jnp.int32), axis=1)
    ids = jnp.arange(row_blocks, dtype=jnp.int32)
    order = jnp.sum(jnp.where(rank[None, :] == ids[:, None], ids[None, :], 0), axis=1)

    def kv_split(w):
        w = w.reshape(w_rows, devs // kv_copies, kv_cols)
        return jnp.repeat(w, kv_copies, axis=1) if kv_copies > 1 else w

    gains = jnp.stack([attn_gain, mlp_gain], axis=1)
    gains = jnp.broadcast_to(
        jnp.pad(gains, ((0, 0), (0, 126)))[:, None, :], (w_rows, devs, 128)
    )
    packed = jnp.concatenate(
        [w_query.reshape(w_rows, devs, q_cols), kv_split(w_key), kv_split(w_value), gains], axis=2
    )
    packed = lax.all_to_all(packed, PLANE, split_axis=1, concat_axis=0, tiled=True)
    packed = gather(packed.reshape(devs * w_rows, q_cols + 2 * kv_cols + 128), "grp")
    w_qkv = packed[:, : q_cols + 2 * kv_cols]
    gain_one = packed[:, q_cols + 2 * kv_cols].astype(F32)
    gain_two = packed[:, q_cols + 2 * kv_cols + 1].astype(F32)

    all_tokens = gather(tokens, PLANE)
    layer_all = all_tokens.astype(F32)
    normed_one = (layer_all * norm_parts(layer_all) * gain_one).astype(BF16)
    qkv = matmul(normed_one, w_qkv).astype(BF16)
    qkv = qkv.reshape(row_blocks, BLOCK, q_cols + 2 * kv_cols)[order]
    qkv = qkv.reshape(row_groups, GROUP_BLOCKS * BLOCK, q_cols + 2 * kv_cols)
    seq = GROUP_BLOCKS * BLOCK
    per_kv = q_heads // kv_heads
    q = qkv[:, :, :q_cols].reshape(row_groups, seq, kv_heads, per_kv, HEAD_DIM)
    k = qkv[:, :, q_cols : q_cols + kv_cols].reshape(row_groups, seq, kv_heads, HEAD_DIM)
    v = qkv[:, :, q_cols + kv_cols :].reshape(row_groups, seq, kv_heads, HEAD_DIM)
    prompt = PROMPT_BLOCKS * BLOCK
    row_id = jnp.arange(seq)
    q_b = q.reshape(row_groups, GROUP_BLOCKS, BLOCK, kv_heads, per_kv, HEAD_DIM)
    k_b = k.reshape(row_groups, GROUP_BLOCKS, BLOCK, kv_heads, HEAD_DIM)
    v_b = v.reshape(row_groups, GROUP_BLOCKS, BLOCK, kv_heads, HEAD_DIM)
    k_p, v_p = k[:, :prompt], v[:, :prompt]
    starts = jnp.minimum(jnp.arange(GROUP_BLOCKS), PROMPT_BLOCKS) * BLOCK
    see_p = jnp.arange(prompt)[None, :] < starts[:, None]
    see_o = jnp.arange(BLOCK)[None, :] <= jnp.arange(BLOCK)[:, None]

    def all_scores():
        far = jnp.einsum("gbikpd,gjkd->gbkpij", q_b, k_p, preferred_element_type=F32)
        far = jnp.where(see_p[None, :, None, None, None, :], far * ATTN_MULT, MASKED)
        own = jnp.einsum("gbikpd,gbjkd->gbkpij", q_b, k_b, preferred_element_type=F32)
        own = jnp.where(see_o[None, None, None, None, :, :], own * ATTN_MULT, MASKED)
        return far, own

    far, own = all_scores()
    peak = jnp.maximum(far.max(-1, keepdims=True), own.max(-1, keepdims=True))
    far, own = jnp.exp(far - peak), jnp.exp(own - peak)
    total = far.sum(-1, keepdims=True) + own.sum(-1, keepdims=True)
    far_p, own_p = far / total, own / total
    attended = jnp.einsum(
        "gbkpij,gjkd->gbikpd", far_p.astype(BF16), v_p, preferred_element_type=F32
    ) + jnp.einsum("gbkpij,gbjkd->gbikpd", own_p.astype(BF16), v_b, preferred_element_type=F32)
    attended = attended.astype(BF16).reshape(row_blocks, BLOCK, q_cols)[rank]
    attended = lax.all_to_all(
        attended.reshape(row_blocks * BLOCK, q_cols), PLANE, split_axis=0, concat_axis=1, tiled=True
    )

    out_full = gather(w_out, EVERY)
    layer_in = tokens.astype(F32)
    branch_attn = matmul(attended, out_full)
    residual = layer_in + RESID_MULT * branch_attn
    factor_two = norm_parts(residual)
    normed_two = gather((residual * factor_two * gain_two).astype(BF16), tok_axes)
    upstream = cotangent.astype(F32)
    d_branch_mlp = gather((RESID_MULT * upstream).astype(BF16), tok_axes)

    gate_w = gather(w_gate, weight_axes, axis=1)
    up_w = gather(w_up, weight_axes, axis=1)
    down_w = gather(w_down, weight_axes)
    gate_act = matmul(normed_two, gate_w)
    up_act = matmul(normed_two, up_w)
    sig = jax.nn.sigmoid(gate_act)
    silu = gate_act * sig
    hidden = (silu * up_act).astype(BF16)
    branch_mlp = scatter(matmul(hidden, down_w).astype(BF16), tok_axes).astype(F32)
    layer_out = residual + RESID_MULT * branch_mlp

    grad_down = scatter(over_rows(hidden, d_branch_mlp).astype(BF16), weight_axes).astype(F32)
    d_hidden = over_cols(d_branch_mlp, down_w)
    d_gate = (d_hidden * up_act * (sig * (1.0 + gate_act * (1.0 - sig)))).astype(BF16)
    d_up = (d_hidden * silu).astype(BF16)
    grad_gate = scatter(over_rows(normed_two, d_gate).astype(BF16), weight_axes, axis=1).astype(F32)
    grad_up = scatter(over_rows(normed_two, d_up).astype(BF16), weight_axes, axis=1).astype(F32)
    d_normed_two = over_cols(d_gate, gate_w) + over_cols(d_up, up_w)
    d_normed_two = scatter(d_normed_two.astype(BF16), tok_axes).astype(F32)

    d_residual_norm, d_gain_two = norm_back(residual, factor_two, gain_two, d_normed_two)
    d_residual = upstream + d_residual_norm
    d_branch_attn = (RESID_MULT * d_residual).astype(BF16)
    grad_out = scatter(over_rows(attended, d_branch_attn).astype(BF16), EVERY).astype(F32)
    d_attended = over_cols(d_branch_attn, out_full).astype(BF16)
    d_attended = lax.all_to_all(d_attended, PLANE, split_axis=1, concat_axis=0, tiled=True)
    d_b = d_attended.reshape(row_blocks, BLOCK, q_cols)[order]
    d_b = d_b.reshape(row_groups, GROUP_BLOCKS, BLOCK, kv_heads, per_kv, HEAD_DIM)

    far_s = jnp.einsum("gbikpd,gjkd->gbkpij", d_b, v_p, preferred_element_type=F32)
    own_s = jnp.einsum("gbikpd,gbjkd->gbkpij", d_b, v_b, preferred_element_type=F32)
    mean_s = (far_p * far_s).sum(-1, keepdims=True) + (own_p * own_s).sum(-1, keepdims=True)
    far_d = (far_p * (far_s - mean_s)).astype(BF16)
    own_d = (own_p * (own_s - mean_s)).astype(BF16)
    far_p, own_p = far_p.astype(BF16), own_p.astype(BF16)
    d_q = ATTN_MULT * (
        jnp.einsum("gbkpij,gjkd->gbikpd", far_d, k_p, preferred_element_type=F32)
        + jnp.einsum("gbkpij,gbjkd->gbikpd", own_d, k_b, preferred_element_type=F32)
    )
    d_k = jnp.einsum("gbkpij,gbikpd->gbjkd", own_d, q_b, preferred_element_type=F32)
    d_v = jnp.einsum("gbkpij,gbikpd->gbjkd", own_p, d_b, preferred_element_type=F32)
    d_kp = jnp.einsum("gbkpij,gbikpd->gjkd", far_d, q_b, preferred_element_type=F32)
    d_vp = jnp.einsum("gbkpij,gbikpd->gjkd", far_p, d_b, preferred_element_type=F32)
    d_k = ATTN_MULT * jnp.concatenate([d_k.reshape(row_groups, seq, kv_cols)[:, :prompt] + d_kp.reshape(row_groups, prompt, kv_cols), d_k.reshape(row_groups, seq, kv_cols)[:, prompt:]], axis=1)
    d_v = jnp.concatenate([d_v.reshape(row_groups, seq, kv_cols)[:, :prompt] + d_vp.reshape(row_groups, prompt, kv_cols), d_v.reshape(row_groups, seq, kv_cols)[:, prompt:]], axis=1)
    d_qkv = jnp.concatenate([d_q.reshape(row_groups, seq, q_cols), d_k, d_v], axis=2).astype(BF16)
    d_qkv = d_qkv.reshape(row_blocks, BLOCK, q_cols + 2 * kv_cols)[rank]
    d_qkv = d_qkv.reshape(row_blocks * BLOCK, q_cols + 2 * kv_cols)

    d_normed_one = scatter(over_cols(d_qkv, w_qkv).astype(BF16), PLANE).astype(F32)
    d_input_norm, d_gain_one = norm_back(layer_in, norm_parts(layer_in), gain_one, d_normed_one)
    tokens_grad = (d_residual + d_input_norm).astype(BF16)

    grad_qkv = over_rows(normed_one, d_qkv)
    d_gains = jnp.pad(jnp.stack([d_gain_one, d_gain_two], axis=1), ((0, 0), (0, 126)))
    sent = scatter(jnp.concatenate([grad_qkv, d_gains], axis=1).astype(BF16), "grp")
    sent = sent.reshape(devs, w_rows, q_cols + 2 * kv_cols + 128)
    sent = lax.all_to_all(sent, PLANE, split_axis=0, concat_axis=0, tiled=True).astype(F32)

    def kv_join(g):
        g = g.reshape(devs // kv_copies, kv_copies, w_rows, kv_cols)
        g = jnp.sum(g, axis=1) if kv_copies > 1 else g[:, 0]
        return jnp.swapaxes(g, 0, 1).reshape(w_rows, KV_HEADS * HEAD_DIM)

    grad_query = jnp.swapaxes(sent[:, :, :q_cols], 0, 1).reshape(w_rows, D)
    grad_key = kv_join(sent[:, :, q_cols : q_cols + kv_cols])
    grad_value = kv_join(sent[:, :, q_cols + kv_cols : q_cols + 2 * kv_cols])
    gains_sum = jnp.sum(sent[:, :, q_cols + 2 * kv_cols :], axis=0)

    scaled_attn = RESID_MULT * branch_attn
    scaled_mlp = RESID_MULT * branch_mlp
    squares = jnp.stack(
        [
            jnp.sum(layer_out * layer_out),
            jnp.sum(scaled_attn * scaled_attn),
            jnp.sum(scaled_mlp * scaled_mlp),
        ]
    )
    totals = lax.psum(squares, EVERY)
    rms_stats = jnp.sqrt(totals / (rows * grps * devs * D))
    return (
        layer_out.astype(BF16),
        tokens_grad,
        gains_sum[:, 0],
        grad_query,
        grad_key,
        grad_value,
        grad_out,
        gains_sum[:, 1],
        grad_gate,
        grad_up,
        grad_down,
        rms_stats,
    )


TOK_AXES, WEIGHT_AXES = PLANE, ("grp",)


def solution(mesh):
    shape = (mesh.shape["grp"], mesh.shape["blk"] // 2, 2)
    mesh = Mesh(mesh.devices.reshape(shape), EVERY)
    row, col, vec = P(EVERY, None), P(None, EVERY), P(EVERY)
    return jax.shard_map(
        on_device,
        mesh=mesh,
        in_specs=(row, P(), P(), vec, row, row, row, row, vec, col, col, row, row),
        out_specs=(row, row, vec, row, row, row, row, vec, col, col, row, P()),
        check_vma=False,
    )
```

```python
import functools

import jax
import jax.numpy as jnp
from jax import lax
from jax.experimental import pallas as pl
from jax.experimental.pallas import tpu as pltpu
from jax.sharding import Mesh
from jax.sharding import PartitionSpec as P

D = 2048
HEADS = 32
KV_HEADS = 8
HEAD_DIM = 64
BLOCK = 128
PROMPT_BLOCKS = 8
GROUP_BLOCKS = 16
PER_GROUP = HEADS // KV_HEADS

ATTN_MULT = 0.015625
RESID_MULT = 0.22
EPSILON = 1e-05
MASKED = -1e30

PLANE = ("chip", "core")
EVERY = ("grp", "chip", "core")
BF16 = jnp.bfloat16
F32 = jnp.float32


MESH = pl.DeviceIdType.MESH
ANY = pl.BlockSpec(memory_space=pl.ANY)
VMEM = pl.BlockSpec(memory_space=pltpu.VMEM)


def place():
    return lax.axis_index("chip"), lax.axis_index("core")


def flip(chip, step, chips):
    return jnp.bitwise_xor(chip, step) if chips == 4 else lax.rem(chip + step, chips)


def unflip(chip, step, chips):
    return jnp.bitwise_xor(chip, step) if chips == 4 else lax.rem(chip + chips - step, chips)


def greet(peers):
    barrier = pltpu.get_barrier_semaphore()
    for chip, core in peers:
        pl.semaphore_signal(
            barrier, inc=1, device_id={"chip": chip, "core": core}, device_id_type=MESH
        )
    pl.semaphore_wait(barrier, len(peers))


def remote(src, dst, send, recv, chip, core):
    return pltpu.make_async_remote_copy(
        src_ref=src,
        dst_ref=dst,
        send_sem=send,
        recv_sem=recv,
        device_id={"chip": chip, "core": core},
        device_id_type=MESH,
    )


class Gather:
    def __init__(self, chips, inner, x_ref, o_ref, send, recv, local):
        self.chips, self.inner, self.x, self.o = chips, inner, x_ref, o_ref
        self.send, self.recv, self.local = send, recv, local
        self.chip, self.core = place()
        self.half = x_ref.shape[0] // 2
        self.started = []

    def greet(self):
        steps = (1, 2) if self.chips == 4 else range(1, self.chips)
        peers = [(flip(self.chip, s, self.chips), self.core) for s in steps]
        greet(peers + [(self.chip, 1 - self.core)])

    def piece(self, slot, h):
        at = pl.ds(h * self.half, self.half)
        return self.o.at[at, slot] if self.inner else self.o.at[slot, at]

    def own(self, h):
        return self.x.at[pl.ds(h * self.half, self.half)]

    def slot(self, chip, core):
        return chip * 2 + core

    def push(self, src, slot, h, chip, core):
        i = len(self.started)
        copy = remote(src, self.piece(slot, h), self.send.at[i], self.recv.at[slot, h], chip, core)
        copy.start()
        self.started.append(copy)

    def wait_for(self, slot, h):
        remote(
            self.own(h), self.piece(slot, h), self.send.at[0], self.recv.at[slot, h],
            self.chip, 1 - self.core,
        ).wait_recv()

    def start(self):
        me = self.slot(self.chip, self.core)
        if self.chips == 4:
            for h, s in ((0, 1), (1, 2), (1, 1), (0, 2)):
                self.push(self.own(h), me, h, flip(self.chip, s, 4), self.core)
        else:
            for s in range(1, self.chips):
                for h in range(2):
                    self.push(self.own(h), me, h, flip(self.chip, s, self.chips), self.core)
        for h in range(2):
            self.push(self.own(h), me, h, self.chip, 1 - self.core)
        whole = self.o.at[:, me] if self.inner else self.o.at[me]
        self.mine = pltpu.make_async_copy(self.x, whole, self.local)
        self.mine.start()

    def relay(self):
        if self.chips == 4:
            plan = ((1, 0, 2), (2, 1, 1), (1, 1, 0), (2, 0, 0), (3, 0, 0), (3, 1, 0))
        else:
            plan = tuple((s, h, 0) for s in range(1, self.chips) for h in range(2))
        for s, h, onward in plan:
            slot = self.slot(unflip(self.chip, s, self.chips), self.core)
            self.wait_for(slot, h)
            if onward:
                self.push(self.piece(slot, h), slot, h, flip(self.chip, onward, 4), self.core)
            self.push(self.piece(slot, h), slot, h, self.chip, 1 - self.core)

    def finish(self):
        for s in range(self.chips):
            slot = self.slot(unflip(self.chip, s, self.chips), 1 - self.core)
            for h in range(2):
                self.wait_for(slot, h)
        for copy in self.started:
            copy.wait_send()
        self.mine.wait()


def gather_sems(chips):
    return [
        pltpu.SemaphoreType.DMA((4 * chips + 4,)),
        pltpu.SemaphoreType.DMA((2 * chips, 2)),
        pltpu.SemaphoreType.DMA,
    ]


def gather_kernel(chips, inner, x_ref, o_ref, *sems):
    run = Gather(chips, inner, x_ref, o_ref, *sems)
    run.greet()
    run.start()
    run.relay()
    run.finish()


def plane_gather(x, chips, call_id, inner=False):
    devs = 2 * chips
    shape = (x.shape[0], devs) + x.shape[1:] if inner else (devs,) + x.shape
    return pl.pallas_call(
        functools.partial(gather_kernel, chips, inner),
        out_shape=jax.ShapeDtypeStruct(shape, x.dtype),
        in_specs=[ANY],
        out_specs=ANY,
        scratch_shapes=gather_sems(chips),
        compiler_params=pltpu.CompilerParams(collective_id=call_id, has_side_effects=True),
    )(x)


def reduce_kernel(chips, inner, p_ref, o_ref, total, mine, twin, moved, corner, landed, lsem, tsend, trecv, msend, mrecv, csend, crecv):
    chip, core = place()
    sib = 1 - core
    half = (p_ref.shape[0] if inner else p_ref.shape[1]) // 2
    block = (lambda slot: p_ref.at[:, slot]) if inner else (lambda slot: p_ref.at[slot])
    steps = (1, 2) if chips == 4 else tuple(range(1, chips))
    peers = [(flip(chip, s, chips), core) for s in steps]
    greet(peers + [(chip, sib)])
    order = (3, 1, 2, 0) if chips == 4 else tuple(range(1, chips)) + (0,)
    loads, twins = {}, {}
    for s in order:
        to = flip(chip, s, chips) * 2
        twins[s] = remote(block(to + sib), twin.at[s], tsend.at[s], trecv.at[s], chip, sib)
        twins[s].start()
        loads[s] = pltpu.make_async_copy(block(to + core), mine.at[s], lsem.at[s])
        loads[s].start()

    def part(s, h):
        at = pl.ds(h * half, half)
        return mine[s, at].astype(F32) + twin[s, at].astype(F32)

    def ready(s):
        loads[s].wait()
        twins[s].wait_recv()

    sent = []
    if chips == 4:
        corners = []
        ready(3)
        for h, s in ((0, 1), (1, 2)):
            moved[3, pl.ds(h * half, half)] = part(3, h).astype(BF16)
            copy = remote(moved.at[3, pl.ds(h * half, half)], corner.at[h], csend.at[h], crecv.at[h], flip(chip, s, 4), core)
            copy.start()
            corners.append(copy)

        def send(s, h):
            at = pl.ds(h * half, half)
            copy = remote(moved.at[s, at], landed.at[s - 1, at], msend.at[s - 1, h], mrecv.at[s - 1, h], flip(chip, s, 4), core)
            copy.start()
            sent.append(copy)

        for s, h in ((1, 0), (2, 1)):
            ready(s)
            moved[s, pl.ds(h * half, half)] = part(s, h).astype(BF16)
            send(s, h)
        for s, h in ((2, 0), (1, 1)):
            corners[h].wait_recv()
            moved[s, pl.ds(h * half, half)] = (part(s, h) + corner[h].astype(F32)).astype(BF16)
            send(s, h)
        for copy in corners:
            copy.wait_send()
    else:
        for s in steps:
            ready(s)
            for h in range(2):
                at = pl.ds(h * half, half)
                moved[s, at] = part(s, h).astype(BF16)
                copy = remote(moved.at[s, at], landed.at[s - 1, at], msend.at[s - 1, h], mrecv.at[s - 1, h], flip(chip, s, chips), core)
                copy.start()
                sent.append(copy)
    ready(0)
    for h in range(2):
        total[pl.ds(h * half, half)] = part(0, h)
    for copy in sent:
        copy.wait()
    for s in steps[:-1]:
        total[...] += landed[s - 1].astype(F32)
    o_ref[...] = (total[...] + landed[steps[-1] - 1].astype(F32)).astype(o_ref.dtype)
    for s in order:
        twins[s].wait_send()


def plane_reduce(p, chips, call_id, dtype=F32, inner=False):
    block = (p.shape[0],) + p.shape[2:] if inner else p.shape[1:]
    steps = 2 if chips == 4 else chips - 1
    return pl.pallas_call(
        functools.partial(reduce_kernel, chips, inner),
        out_shape=jax.ShapeDtypeStruct(block, dtype),
        in_specs=[ANY],
        out_specs=VMEM,
        scratch_shapes=[
            pltpu.VMEM(block, F32),
            pltpu.VMEM((chips,) + block, BF16),
            pltpu.VMEM((chips,) + block, BF16),
            pltpu.VMEM((chips,) + block, BF16),
            pltpu.VMEM((2, block[0] // 2) + block[1:], BF16),
            pltpu.VMEM((steps,) + block, BF16),
            pltpu.SemaphoreType.DMA((chips,)),
            pltpu.SemaphoreType.DMA((chips,)),
            pltpu.SemaphoreType.DMA((chips,)),
            pltpu.SemaphoreType.DMA((steps, 2)),
            pltpu.SemaphoreType.DMA((steps, 2)),
            pltpu.SemaphoreType.DMA((2,)),
            pltpu.SemaphoreType.DMA((2,)),
        ],
        compiler_params=pltpu.CompilerParams(
            collective_id=call_id, has_side_effects=True, vmem_limit_bytes=56 << 20
        ),
    )(p)


def exchange_kernel(chips, cut, paste, x_ref, o_ref, send, recv, local):
    chip, core = place()
    me = chip * 2 + core
    peers = [(flip(chip, s, chips), c) for s in range(1, chips) for c in (core, 1 - core)]
    peers = peers + [(chip, 1 - core)]
    greet(peers)
    far = [p for p in ([3, 1, 2] if chips == 4 else range(1, chips))]
    order = [(flip(chip, s, chips), c) for s in far for c in (core, 1 - core)] + [(chip, 1 - core)]
    copies = []
    for i, (to, c) in enumerate(order):
        copy = remote(cut(x_ref, to * 2 + c), paste(o_ref, me), send.at[i], recv.at[me], to, c)
        copy.start()
        copies.append(copy)
    mine = pltpu.make_async_copy(cut(x_ref, me), paste(o_ref, me), local)
    mine.start()
    for s in far:
        for c in (core, 1 - core):
            slot = unflip(chip, s, chips) * 2 + c
            remote(cut(x_ref, me), paste(o_ref, slot), send.at[0], recv.at[slot], chip, 1 - core).wait_recv()
    slot = chip * 2 + 1 - core
    remote(cut(x_ref, me), paste(o_ref, slot), send.at[0], recv.at[slot], chip, 1 - core).wait_recv()
    for copy in copies:
        copy.wait_send()
    mine.wait()


def plane_exchange(x, shape, cut, paste, chips, call_id):
    return pl.pallas_call(
        functools.partial(exchange_kernel, chips, cut, paste),
        out_shape=jax.ShapeDtypeStruct(shape, x.dtype),
        in_specs=[ANY],
        out_specs=ANY,
        scratch_shapes=[
            pltpu.SemaphoreType.DMA((2 * chips,)),
            pltpu.SemaphoreType.DMA((2 * chips,)),
            pltpu.SemaphoreType.DMA,
        ],
        compiler_params=pltpu.CompilerParams(collective_id=call_id, has_side_effects=True),
    )(x)


def by_slot(ref, dev):
    return ref.at[dev]


def by_rows(rows):
    return lambda ref, dev: ref.at[pl.ds(pl.multiple_of(dev * rows, rows), rows)]


def by_cols(cols):
    return lambda ref, dev: ref.at[:, pl.ds(pl.multiple_of(dev * cols, cols), cols)]


def matmul(left, right):
    return jnp.dot(left, right, preferred_element_type=F32)


def over_rows(left, right):
    return lax.dot_general(left, right, (((0,), (0,)), ((), ())), preferred_element_type=F32)


def over_cols(left, right):
    return lax.dot_general(left, right, (((1,), (1,)), ((), ())), preferred_element_type=F32)


def gather(values, axes, axis=0):
    return lax.all_gather(values, axes, axis=axis, tiled=True)


def scatter(values, axes, axis=0):
    return lax.psum_scatter(values, axes, scatter_dimension=axis, tiled=True)


def norm_parts(values):
    factor = lax.rsqrt(jnp.mean(values * values, axis=-1, keepdims=True) + EPSILON)
    return factor


def norm_back(values, factor, gain, grad):
    scaled = gain * grad
    inner = jnp.mean(values * scaled, axis=-1, keepdims=True)
    return factor * scaled - values * (factor * factor * factor * inner), jnp.sum(
        grad * values * factor, axis=0
    )


def on_device(
    tokens,
    block_group,
    block_slot,
    attn_gain,
    w_query,
    w_key,
    w_value,
    w_out,
    mlp_gain,
    w_gate,
    w_up,
    w_down,
    cotangent,
):
    grps = lax.axis_size("grp")
    devs = lax.axis_size(PLANE)
    chips = devs // 2
    rows = tokens.shape[0]
    w_rows = w_query.shape[0]
    q_heads = HEADS // devs
    kv_heads = max(1, KV_HEADS // devs)
    kv_copies = max(1, devs // KV_HEADS)
    q_cols, kv_cols = q_heads * HEAD_DIM, kv_heads * HEAD_DIM
    row_blocks = rows // BLOCK * devs
    row_groups = row_blocks // GROUP_BLOCKS

    row_first = lax.axis_index("grp") * row_blocks
    keys = lax.dynamic_slice_in_dim(block_group, row_first, row_blocks) * GROUP_BLOCKS
    keys = keys + lax.dynamic_slice_in_dim(block_slot, row_first, row_blocks)
    rank = jnp.sum((keys[None, :] < keys[:, None]).astype(jnp.int32), axis=1)
    ids = jnp.arange(row_blocks, dtype=jnp.int32)
    order = jnp.sum(jnp.where(rank[None, :] == ids[:, None], ids[None, :], 0), axis=1)

    def kv_split(w):
        w = w.reshape(w_rows, devs // kv_copies, kv_cols)
        return jnp.repeat(w, kv_copies, axis=1) if kv_copies > 1 else w

    gains = jnp.stack([attn_gain, mlp_gain], axis=1)
    gains = jnp.broadcast_to(
        jnp.pad(gains, ((0, 0), (0, 126)))[:, None, :], (w_rows, devs, 128)
    )
    packed = jnp.concatenate(
        [w_query.reshape(w_rows, devs, q_cols), kv_split(w_key), kv_split(w_value), gains], axis=2
    )
    packed = jnp.swapaxes(packed, 0, 1)
    packed = plane_exchange(packed, packed.shape, by_slot, by_slot, chips, 1)
    packed, w_out = lax.optimization_barrier((packed, w_out))
    packed = gather(packed.reshape(devs * w_rows, q_cols + 2 * kv_cols + 128), "grp")
    w_qkv = packed[:, : q_cols + 2 * kv_cols]
    gain_one = packed[:, q_cols + 2 * kv_cols].astype(F32)
    gain_two = packed[:, q_cols + 2 * kv_cols + 1].astype(F32)

    all_tokens = plane_gather(tokens, chips, 2).reshape(devs * rows, D)
    layer_all = all_tokens.astype(F32)
    normed_one = (layer_all * norm_parts(layer_all) * gain_one).astype(BF16)
    qkv = matmul(normed_one, w_qkv).astype(BF16)
    qkv = qkv.reshape(row_blocks, BLOCK, q_cols + 2 * kv_cols)[order]
    qkv = qkv.reshape(row_groups, GROUP_BLOCKS * BLOCK, q_cols + 2 * kv_cols)
    seq = GROUP_BLOCKS * BLOCK
    per_kv = q_heads // kv_heads
    q = qkv[:, :, :q_cols].reshape(row_groups, seq, kv_heads, per_kv, HEAD_DIM)
    k = qkv[:, :, q_cols : q_cols + kv_cols].reshape(row_groups, seq, kv_heads, HEAD_DIM)
    v = qkv[:, :, q_cols + kv_cols :].reshape(row_groups, seq, kv_heads, HEAD_DIM)
    prompt = PROMPT_BLOCKS * BLOCK
    row_id = jnp.arange(seq)
    q_b = q.reshape(row_groups, GROUP_BLOCKS, BLOCK, kv_heads, per_kv, HEAD_DIM)
    k_b = k.reshape(row_groups, GROUP_BLOCKS, BLOCK, kv_heads, HEAD_DIM)
    v_b = v.reshape(row_groups, GROUP_BLOCKS, BLOCK, kv_heads, HEAD_DIM)
    k_p, v_p = k[:, :prompt], v[:, :prompt]
    starts = jnp.minimum(jnp.arange(GROUP_BLOCKS), PROMPT_BLOCKS) * BLOCK
    see_p = jnp.arange(prompt)[None, :] < starts[:, None]
    see_o = jnp.arange(BLOCK)[None, :] <= jnp.arange(BLOCK)[:, None]

    def all_scores():
        far = jnp.einsum("gbikpd,gjkd->gbkpij", q_b, k_p, preferred_element_type=F32)
        far = jnp.where(see_p[None, :, None, None, None, :], far * ATTN_MULT, MASKED)
        own = jnp.einsum("gbikpd,gbjkd->gbkpij", q_b, k_b, preferred_element_type=F32)
        own = jnp.where(see_o[None, None, None, None, :, :], own * ATTN_MULT, MASKED)
        return far, own

    far, own = all_scores()
    peak = jnp.maximum(far.max(-1, keepdims=True), own.max(-1, keepdims=True))
    far, own = jnp.exp(far - peak), jnp.exp(own - peak)
    total = far.sum(-1, keepdims=True) + own.sum(-1, keepdims=True)
    far_p, own_p = far / total, own / total
    attended = jnp.einsum(
        "gbkpij,gjkd->gbikpd", far_p.astype(BF16), v_p, preferred_element_type=F32
    ) + jnp.einsum("gbkpij,gbjkd->gbikpd", own_p.astype(BF16), v_b, preferred_element_type=F32)
    attended = attended.astype(BF16).reshape(row_blocks, BLOCK, q_cols)[rank]
    attended = plane_exchange(
        attended.reshape(row_blocks * BLOCK, q_cols), (rows, D), by_rows(rows), by_cols(q_cols), chips, 3
    )

    out_full = gather(w_out[None], "grp")
    out_full = plane_gather(out_full, chips, 4, inner=True).reshape(D, D)
    layer_in = tokens.astype(F32)
    branch_attn = matmul(attended, out_full)
    residual = layer_in + RESID_MULT * branch_attn
    factor_two = norm_parts(residual)
    normed_two = (residual * factor_two * gain_two).astype(BF16)
    normed_two = plane_gather(normed_two, chips, 2).reshape(devs * rows, D)
    upstream = cotangent.astype(F32)
    d_branch_mlp = plane_gather((RESID_MULT * upstream).astype(BF16), chips, 2)
    d_branch_mlp = d_branch_mlp.reshape(devs * rows, D)

    gate_w = gather(w_gate, "grp", axis=1)
    up_w = gather(w_up, "grp", axis=1)
    down_w = gather(w_down, "grp")
    gate_act = matmul(normed_two, gate_w)
    up_act = matmul(normed_two, up_w)
    sig = jax.nn.sigmoid(gate_act)
    silu = gate_act * sig
    hidden = (silu * up_act).astype(BF16)
    part_down = over_rows(hidden, d_branch_mlp).astype(BF16)
    d_hidden = over_cols(d_branch_mlp, down_w)
    d_gate = (d_hidden * up_act * (sig * (1.0 + gate_act * (1.0 - sig)))).astype(BF16)
    d_up = (d_hidden * silu).astype(BF16)
    part_gate = over_rows(normed_two, d_gate).astype(BF16)
    part_up = over_rows(normed_two, d_up).astype(BF16)
    d_gate, d_up, part_down, part_gate, part_up = lax.optimization_barrier(
        (d_gate, d_up, part_down, part_gate, part_up)
    )
    grad_down = scatter(part_down, "grp")
    grad_gate = scatter(part_gate, "grp", axis=1)
    grad_up = scatter(part_up, "grp", axis=1)
    d_normed_two = over_cols(d_gate, gate_w) + over_cols(d_up, up_w)
    d_normed_two = plane_reduce(d_normed_two.astype(BF16).reshape(devs, rows, D), chips, 5)

    d_residual_norm, d_gain_two = norm_back(residual, factor_two, gain_two, d_normed_two)
    d_residual = upstream + d_residual_norm
    d_branch_attn = (RESID_MULT * d_residual).astype(BF16)
    grad_out = over_rows(attended, d_branch_attn).astype(BF16).reshape(grps, devs, w_rows, D)
    grad_out = plane_reduce(grad_out, chips, 6, dtype=BF16, inner=True)
    grad_out, grad_down = lax.optimization_barrier((grad_out, grad_down))
    grad_out = scatter(grad_out, "grp").reshape(w_rows, D).astype(F32)
    d_attended = over_cols(d_branch_attn, out_full).astype(BF16)
    d_attended = plane_exchange(
        d_attended, (devs * rows, q_cols), by_cols(q_cols), by_rows(rows), chips, 7
    )
    d_b = d_attended.reshape(row_blocks, BLOCK, q_cols)[order]
    d_b = d_b.reshape(row_groups, GROUP_BLOCKS, BLOCK, kv_heads, per_kv, HEAD_DIM)

    far_s = jnp.einsum("gbikpd,gjkd->gbkpij", d_b, v_p, preferred_element_type=F32)
    own_s = jnp.einsum("gbikpd,gbjkd->gbkpij", d_b, v_b, preferred_element_type=F32)
    mean_s = (far_p * far_s).sum(-1, keepdims=True) + (own_p * own_s).sum(-1, keepdims=True)
    far_d = (far_p * (far_s - mean_s)).astype(BF16)
    own_d = (own_p * (own_s - mean_s)).astype(BF16)
    far_p, own_p = far_p.astype(BF16), own_p.astype(BF16)
    d_q = ATTN_MULT * (
        jnp.einsum("gbkpij,gjkd->gbikpd", far_d, k_p, preferred_element_type=F32)
        + jnp.einsum("gbkpij,gbjkd->gbikpd", own_d, k_b, preferred_element_type=F32)
    )
    d_k = jnp.einsum("gbkpij,gbikpd->gbjkd", own_d, q_b, preferred_element_type=F32)
    d_v = jnp.einsum("gbkpij,gbikpd->gbjkd", own_p, d_b, preferred_element_type=F32)
    d_kp = jnp.einsum("gbkpij,gbikpd->gjkd", far_d, q_b, preferred_element_type=F32)
    d_vp = jnp.einsum("gbkpij,gbikpd->gjkd", far_p, d_b, preferred_element_type=F32)
    d_k = ATTN_MULT * jnp.concatenate([d_k.reshape(row_groups, seq, kv_cols)[:, :prompt] + d_kp.reshape(row_groups, prompt, kv_cols), d_k.reshape(row_groups, seq, kv_cols)[:, prompt:]], axis=1)
    d_v = jnp.concatenate([d_v.reshape(row_groups, seq, kv_cols)[:, :prompt] + d_vp.reshape(row_groups, prompt, kv_cols), d_v.reshape(row_groups, seq, kv_cols)[:, prompt:]], axis=1)
    d_qkv = jnp.concatenate([d_q.reshape(row_groups, seq, q_cols), d_k, d_v], axis=2).astype(BF16)
    d_qkv = d_qkv.reshape(row_blocks, BLOCK, q_cols + 2 * kv_cols)[rank]
    d_qkv = d_qkv.reshape(row_blocks * BLOCK, q_cols + 2 * kv_cols)

    d_normed_one = over_cols(d_qkv, w_qkv).astype(BF16).reshape(devs, rows, D)
    d_normed_one = plane_reduce(d_normed_one, chips, 5)
    d_input_norm, d_gain_one = norm_back(layer_in, norm_parts(layer_in), gain_one, d_normed_one)
    tokens_grad = (d_residual + d_input_norm).astype(BF16)

    grad_qkv = over_rows(normed_one, d_qkv)
    d_gains = jnp.pad(jnp.stack([d_gain_one, d_gain_two], axis=1), ((0, 0), (0, 126)))
    sent = jnp.concatenate([grad_qkv, d_gains], axis=1).astype(BF16)
    sent, grad_gate, grad_up = lax.optimization_barrier((sent, grad_gate, grad_up))
    sent = scatter(sent, "grp")
    sent = sent.reshape(devs, w_rows, q_cols + 2 * kv_cols + 128)
    sent = plane_exchange(sent, sent.shape, by_slot, by_slot, chips, 1).astype(F32)

    def kv_join(g):
        g = g.reshape(devs // kv_copies, kv_copies, w_rows, kv_cols)
        g = jnp.sum(g, axis=1) if kv_copies > 1 else g[:, 0]
        return jnp.swapaxes(g, 0, 1).reshape(w_rows, KV_HEADS * HEAD_DIM)

    grad_query = jnp.swapaxes(sent[:, :, :q_cols], 0, 1).reshape(w_rows, D)
    grad_key = kv_join(sent[:, :, q_cols : q_cols + kv_cols])
    grad_value = kv_join(sent[:, :, q_cols + kv_cols : q_cols + 2 * kv_cols])
    gains_sum = jnp.sum(sent[:, :, q_cols + 2 * kv_cols :], axis=0)

    branch_mlp = matmul(hidden, down_w).astype(BF16).reshape(devs, rows, D)
    branch_mlp, d_qkv = lax.optimization_barrier((branch_mlp, d_qkv))
    branch_mlp = plane_reduce(branch_mlp, chips, 5)
    layer_out = residual + RESID_MULT * branch_mlp
    scaled_attn = RESID_MULT * branch_attn
    scaled_mlp = RESID_MULT * branch_mlp
    squares = jnp.stack(
        [
            jnp.sum(layer_out * layer_out),
            jnp.sum(scaled_attn * scaled_attn),
            jnp.sum(scaled_mlp * scaled_mlp),
        ]
    )
    totals = lax.psum(squares, EVERY)
    rms_stats = jnp.sqrt(totals / (rows * grps * devs * D))
    return (
        layer_out.astype(BF16),
        tokens_grad,
        gains_sum[:, 0],
        grad_query,
        grad_key,
        grad_value,
        grad_out,
        gains_sum[:, 1],
        grad_gate.astype(F32),
        grad_up.astype(F32),
        grad_down.astype(F32),
        rms_stats,
    )


def solution(mesh):
    shape = (mesh.shape["grp"], mesh.shape["blk"] // 2, 2)
    mesh = Mesh(mesh.devices.reshape(shape), EVERY)
    row, col, vec = P(EVERY, None), P(None, EVERY), P(EVERY)
    return jax.shard_map(
        on_device,
        mesh=mesh,
        in_specs=(row, P(), P(), vec, row, row, row, row, vec, col, col, row, row),
        out_specs=(row, row, vec, row, row, row, row, vec, col, col, row, P()),
        check_vma=False,
    )
```

```python
import functools

import jax
import jax.numpy as jnp
from jax import lax
from jax.experimental import pallas as pl
from jax.experimental.pallas import tpu as pltpu
from jax.sharding import Mesh
from jax.sharding import PartitionSpec as P

D = 2048
HEADS = 32
KV_HEADS = 8
HEAD_DIM = 64
BLOCK = 128
PROMPT_BLOCKS = 8
GROUP_BLOCKS = 16
PER_GROUP = HEADS // KV_HEADS

ATTN_MULT = 0.015625
RESID_MULT = 0.22
EPSILON = 1e-05
MASKED = -1e30

PLANE = ("chip", "core")
EVERY = ("grp", "chip", "core")
BF16 = jnp.bfloat16
F32 = jnp.float32


MESH = pl.DeviceIdType.MESH
BRIEF = pl.CostEstimate(flops=1000, bytes_accessed=1000, transcendentals=0)
ANY = pl.BlockSpec(memory_space=pl.ANY)
VMEM = pl.BlockSpec(memory_space=pltpu.VMEM)


def place():
    return lax.axis_index("chip"), lax.axis_index("core")


def flip(chip, step, chips):
    return jnp.bitwise_xor(chip, step) if chips == 4 else lax.rem(chip + step, chips)


def unflip(chip, step, chips):
    return jnp.bitwise_xor(chip, step) if chips == 4 else lax.rem(chip + chips - step, chips)


def greet(peers):
    barrier = pltpu.get_barrier_semaphore()
    for chip, core in peers:
        pl.semaphore_signal(
            barrier, inc=1, device_id={"chip": chip, "core": core}, device_id_type=MESH
        )
    pl.semaphore_wait(barrier, len(peers))


def remote(src, dst, send, recv, chip, core):
    return pltpu.make_async_remote_copy(
        src_ref=src,
        dst_ref=dst,
        send_sem=send,
        recv_sem=recv,
        device_id={"chip": chip, "core": core},
        device_id_type=MESH,
    )


class Gather:
    def __init__(self, chips, inner, x_ref, o_ref, send, recv, local):
        self.chips, self.inner, self.x, self.o = chips, inner, x_ref, o_ref
        self.send, self.recv, self.local = send, recv, local
        self.chip, self.core = place()
        self.half = x_ref.shape[0] // 2
        self.started = []

    def greet(self):
        steps = (1, 2) if self.chips == 4 else range(1, self.chips)
        peers = [(flip(self.chip, s, self.chips), self.core) for s in steps]
        greet(peers + [(self.chip, 1 - self.core)])

    def piece(self, slot, h):
        at = pl.ds(h * self.half, self.half)
        return self.o.at[at, slot] if self.inner else self.o.at[slot, at]

    def own(self, h):
        return self.x.at[pl.ds(h * self.half, self.half)]

    def slot(self, chip, core):
        return chip * 2 + core

    def push(self, src, slot, h, chip, core):
        i = len(self.started)
        copy = remote(src, self.piece(slot, h), self.send.at[i], self.recv.at[slot, h], chip, core)
        copy.start()
        self.started.append(copy)

    def wait_for(self, slot, h):
        remote(
            self.own(h), self.piece(slot, h), self.send.at[0], self.recv.at[slot, h],
            self.chip, 1 - self.core,
        ).wait_recv()

    def start(self):
        me = self.slot(self.chip, self.core)
        if self.chips == 4:
            for h, s in ((0, 1), (1, 2), (1, 1), (0, 2)):
                self.push(self.own(h), me, h, flip(self.chip, s, 4), self.core)
        else:
            for s in range(1, self.chips):
                for h in range(2):
                    self.push(self.own(h), me, h, flip(self.chip, s, self.chips), self.core)
        for h in range(2):
            self.push(self.own(h), me, h, self.chip, 1 - self.core)
        whole = self.o.at[:, me] if self.inner else self.o.at[me]
        self.mine = pltpu.make_async_copy(self.x, whole, self.local)
        self.mine.start()

    def relay(self):
        if self.chips == 4:
            plan = ((1, 0, 2), (2, 1, 1), (1, 1, 0), (2, 0, 0), (3, 0, 0), (3, 1, 0))
        else:
            plan = tuple((s, h, 0) for s in range(1, self.chips) for h in range(2))
        for s, h, onward in plan:
            slot = self.slot(unflip(self.chip, s, self.chips), self.core)
            self.wait_for(slot, h)
            if onward:
                self.push(self.piece(slot, h), slot, h, flip(self.chip, onward, 4), self.core)
            self.push(self.piece(slot, h), slot, h, self.chip, 1 - self.core)

    def finish(self):
        for s in range(self.chips):
            slot = self.slot(unflip(self.chip, s, self.chips), 1 - self.core)
            for h in range(2):
                self.wait_for(slot, h)
        for copy in self.started:
            copy.wait_send()
        self.mine.wait()


def gather_sems(chips):
    return [
        pltpu.SemaphoreType.DMA((4 * chips + 4,)),
        pltpu.SemaphoreType.DMA((2 * chips, 2)),
        pltpu.SemaphoreType.DMA,
    ]


def gather_kernel(chips, inner, x_ref, o_ref, *sems):
    run = Gather(chips, inner, x_ref, o_ref, *sems)
    run.greet()
    run.start()
    run.relay()
    run.finish()


def plane_gather(x, chips, call_id, inner=False):
    devs = 2 * chips
    shape = (x.shape[0], devs) + x.shape[1:] if inner else (devs,) + x.shape
    return pl.pallas_call(
        functools.partial(gather_kernel, chips, inner),
        out_shape=jax.ShapeDtypeStruct(shape, x.dtype),
        in_specs=[ANY],
        out_specs=ANY,
        scratch_shapes=gather_sems(chips),
        cost_estimate=BRIEF,
        compiler_params=pltpu.CompilerParams(collective_id=call_id, has_side_effects=True),
    )(x)


def reduce_kernel(chips, inner, p_ref, o_ref, total, mine, twin, moved, corner, landed, lsem, tsend, trecv, msend, mrecv, csend, crecv):
    chip, core = place()
    sib = 1 - core
    half = (p_ref.shape[0] if inner else p_ref.shape[1]) // 2
    block = (lambda slot: p_ref.at[:, slot]) if inner else (lambda slot: p_ref.at[slot])
    steps = (1, 2) if chips == 4 else tuple(range(1, chips))
    peers = [(flip(chip, s, chips), core) for s in steps]
    greet(peers + [(chip, sib)])
    order = (3, 1, 2, 0) if chips == 4 else tuple(range(1, chips)) + (0,)
    loads, twins = {}, {}
    for s in order:
        to = flip(chip, s, chips) * 2
        twins[s] = remote(block(to + sib), twin.at[s], tsend.at[s], trecv.at[s], chip, sib)
        twins[s].start()
        loads[s] = pltpu.make_async_copy(block(to + core), mine.at[s], lsem.at[s])
        loads[s].start()

    def part(s, h):
        at = pl.ds(h * half, half)
        return mine[s, at].astype(F32) + twin[s, at].astype(F32)

    def ready(s):
        loads[s].wait()
        twins[s].wait_recv()

    sent = []
    if chips == 4:
        corners = []
        ready(3)
        for h, s in ((0, 1), (1, 2)):
            moved[3, pl.ds(h * half, half)] = part(3, h).astype(BF16)
            copy = remote(moved.at[3, pl.ds(h * half, half)], corner.at[h], csend.at[h], crecv.at[h], flip(chip, s, 4), core)
            copy.start()
            corners.append(copy)

        def send(s, h):
            at = pl.ds(h * half, half)
            copy = remote(moved.at[s, at], landed.at[s - 1, at], msend.at[s - 1, h], mrecv.at[s - 1, h], flip(chip, s, 4), core)
            copy.start()
            sent.append(copy)

        for s, h in ((1, 0), (2, 1)):
            ready(s)
            moved[s, pl.ds(h * half, half)] = part(s, h).astype(BF16)
            send(s, h)
        for s, h in ((2, 0), (1, 1)):
            corners[h].wait_recv()
            moved[s, pl.ds(h * half, half)] = (part(s, h) + corner[h].astype(F32)).astype(BF16)
            send(s, h)
        for copy in corners:
            copy.wait_send()
    else:
        for s in steps:
            ready(s)
            for h in range(2):
                at = pl.ds(h * half, half)
                moved[s, at] = part(s, h).astype(BF16)
                copy = remote(moved.at[s, at], landed.at[s - 1, at], msend.at[s - 1, h], mrecv.at[s - 1, h], flip(chip, s, chips), core)
                copy.start()
                sent.append(copy)
    ready(0)
    for h in range(2):
        total[pl.ds(h * half, half)] = part(0, h)
    for copy in sent:
        copy.wait()
    for s in steps[:-1]:
        total[...] += landed[s - 1].astype(F32)
    o_ref[...] = (total[...] + landed[steps[-1] - 1].astype(F32)).astype(o_ref.dtype)
    for s in order:
        twins[s].wait_send()


def plane_reduce(p, chips, call_id, dtype=F32, inner=False):
    block = (p.shape[0],) + p.shape[2:] if inner else p.shape[1:]
    steps = 2 if chips == 4 else chips - 1
    return pl.pallas_call(
        functools.partial(reduce_kernel, chips, inner),
        out_shape=jax.ShapeDtypeStruct(block, dtype),
        in_specs=[ANY],
        out_specs=VMEM,
        scratch_shapes=[
            pltpu.VMEM(block, F32),
            pltpu.VMEM((chips,) + block, BF16),
            pltpu.VMEM((chips,) + block, BF16),
            pltpu.VMEM((chips,) + block, BF16),
            pltpu.VMEM((2, block[0] // 2) + block[1:], BF16),
            pltpu.VMEM((steps,) + block, BF16),
            pltpu.SemaphoreType.DMA((chips,)),
            pltpu.SemaphoreType.DMA((chips,)),
            pltpu.SemaphoreType.DMA((chips,)),
            pltpu.SemaphoreType.DMA((steps, 2)),
            pltpu.SemaphoreType.DMA((steps, 2)),
            pltpu.SemaphoreType.DMA((2,)),
            pltpu.SemaphoreType.DMA((2,)),
        ],
        cost_estimate=BRIEF,
        compiler_params=pltpu.CompilerParams(
            collective_id=call_id, has_side_effects=True, vmem_limit_bytes=56 << 20
        ),
    )(p)


def exchange_kernel(chips, cut, paste, x_ref, o_ref, send, recv, local):
    chip, core = place()
    me = chip * 2 + core
    peers = [(flip(chip, s, chips), c) for s in range(1, chips) for c in (core, 1 - core)]
    peers = peers + [(chip, 1 - core)]
    greet(peers)
    far = [p for p in ([3, 1, 2] if chips == 4 else range(1, chips))]
    order = [(flip(chip, s, chips), c) for s in far for c in (core, 1 - core)] + [(chip, 1 - core)]
    copies = []
    for i, (to, c) in enumerate(order):
        copy = remote(cut(x_ref, to * 2 + c), paste(o_ref, me), send.at[i], recv.at[me], to, c)
        copy.start()
        copies.append(copy)
    mine = pltpu.make_async_copy(cut(x_ref, me), paste(o_ref, me), local)
    mine.start()
    for s in far:
        for c in (core, 1 - core):
            slot = unflip(chip, s, chips) * 2 + c
            remote(cut(x_ref, me), paste(o_ref, slot), send.at[0], recv.at[slot], chip, 1 - core).wait_recv()
    slot = chip * 2 + 1 - core
    remote(cut(x_ref, me), paste(o_ref, slot), send.at[0], recv.at[slot], chip, 1 - core).wait_recv()
    for copy in copies:
        copy.wait_send()
    mine.wait()


def plane_exchange(x, shape, cut, paste, chips, call_id):
    return pl.pallas_call(
        functools.partial(exchange_kernel, chips, cut, paste),
        out_shape=jax.ShapeDtypeStruct(shape, x.dtype),
        in_specs=[ANY],
        out_specs=ANY,
        scratch_shapes=[
            pltpu.SemaphoreType.DMA((2 * chips,)),
            pltpu.SemaphoreType.DMA((2 * chips,)),
            pltpu.SemaphoreType.DMA,
        ],
        cost_estimate=BRIEF,
        compiler_params=pltpu.CompilerParams(collective_id=call_id, has_side_effects=True),
    )(x)


def by_slot(ref, dev):
    return ref.at[dev]


def by_rows(rows):
    return lambda ref, dev: ref.at[pl.ds(pl.multiple_of(dev * rows, rows), rows)]


def by_cols(cols):
    return lambda ref, dev: ref.at[:, pl.ds(pl.multiple_of(dev * cols, cols), cols)]


def matmul(left, right):
    return jnp.dot(left, right, preferred_element_type=F32)


def over_rows(left, right):
    return lax.dot_general(left, right, (((0,), (0,)), ((), ())), preferred_element_type=F32)


def over_cols(left, right):
    return lax.dot_general(left, right, (((1,), (1,)), ((), ())), preferred_element_type=F32)


def gather(values, axes, axis=0):
    return lax.all_gather(values, axes, axis=axis, tiled=True)


def scatter(values, axes, axis=0):
    return lax.psum_scatter(values, axes, scatter_dimension=axis, tiled=True)


def dot_nt(left, right):
    return lax.dot_general(left, right, (((1,), (1,)), ((), ())), preferred_element_type=F32)


def head_stack(values, heads):
    col_head = lax.broadcasted_iota(jnp.int32, values.shape, 1) // HEAD_DIM
    return jnp.concatenate(
        [jnp.where(col_head == h, values, jnp.zeros_like(values)) for h in range(heads)], axis=0
    )


def head_pick(stacked, heads):
    rows = stacked.shape[0] // heads
    col_head = lax.broadcasted_iota(jnp.int32, (rows, stacked.shape[1]), 1) // HEAD_DIM
    total = jnp.zeros((rows, stacked.shape[1]), F32)
    for h in range(heads):
        total = jnp.where(col_head == h, stacked[h * rows : (h + 1) * rows], total)
    return total


def head_fold(values, heads):
    total = values[:, :HEAD_DIM]
    for h in range(1, heads):
        total = total + values[:, h * HEAD_DIM : (h + 1) * HEAD_DIM]
    return total


def repeat_heads(values, heads):
    return jnp.concatenate([values] * heads, axis=1)


def own_rows(order_ref, slot):
    return pl.ds(pl.multiple_of(order_ref[slot] * BLOCK, BLOCK), BLOCK)


def load_prompt(heads, order_ref, qkv_ref, k_ref, v_ref, first):
    q_cols = heads * HEAD_DIM
    for s in range(PROMPT_BLOCKS):
        pair = qkv_ref[own_rows(order_ref, first + s), q_cols:]
        at = pl.ds(s * BLOCK, BLOCK)
        k_ref[at] = repeat_heads(pair[:, :HEAD_DIM], heads)
        v_ref[at] = repeat_heads(pair[:, HEAD_DIM:], heads)


def soft_parts(heads, slot, q_stack, k_far, k_own):
    far = dot_nt(k_far, q_stack)
    own = dot_nt(k_own, q_stack)
    limit = jnp.minimum(slot, PROMPT_BLOCKS) * BLOCK
    far = jnp.where(lax.broadcasted_iota(jnp.int32, far.shape, 0) < limit, far, MASKED)
    key = lax.broadcasted_iota(jnp.int32, own.shape, 0)
    row = lax.broadcasted_iota(jnp.int32, own.shape, 1) % BLOCK
    own = jnp.where(key <= row, own, MASKED)
    peak = jnp.maximum(jnp.max(far, axis=0, keepdims=True), jnp.max(own, axis=0, keepdims=True))
    far, own = jnp.exp(far - peak), jnp.exp(own - peak)
    scale = 1.0 / (jnp.sum(far, axis=0, keepdims=True) + jnp.sum(own, axis=0, keepdims=True))
    return far * scale, own * scale


def scaled_stack(q, heads):
    return head_stack((q.astype(F32) * ATTN_MULT).astype(BF16), heads)


def attend_kernel(heads, order_ref, qkv_ref, o_ref, k_ref, v_ref, vt_ref):
    first, slot = pl.program_id(0) * GROUP_BLOCKS, pl.program_id(1)
    q_cols = heads * HEAD_DIM

    @pl.when(slot == 0)
    def _():
        load_prompt(heads, order_ref, qkv_ref, k_ref, v_ref, first)
        vt_ref[...] = v_ref[...].astype(F32).T.astype(BF16)

    rows = own_rows(order_ref, first + slot)
    mine = qkv_ref[rows, :]
    k_own = repeat_heads(mine[:, q_cols : q_cols + HEAD_DIM], heads)
    v_own = repeat_heads(mine[:, q_cols + HEAD_DIM :], heads)
    far, own = soft_parts(heads, slot, scaled_stack(mine[:, :q_cols], heads), k_ref[...], k_own)
    mixed = matmul(vt_ref[...], far.astype(BF16))
    mixed += matmul(v_own.astype(F32).T.astype(BF16), own.astype(BF16))
    o_ref[rows, :] = head_pick(mixed.T, heads).astype(BF16)


def attend_back_kernel(
    heads, order_ref, qkv_ref, d_ref, o_ref, k_ref, v_ref, kt_ref, dk_ref, dv_ref
):
    first, slot = pl.program_id(0) * GROUP_BLOCKS, pl.program_id(1)
    q_cols = heads * HEAD_DIM

    @pl.when(slot == 0)
    def _():
        load_prompt(heads, order_ref, qkv_ref, k_ref, v_ref, first)
        kt_ref[...] = k_ref[...].astype(F32).T.astype(BF16)
        dk_ref[...] = jnp.zeros_like(dk_ref)
        dv_ref[...] = jnp.zeros_like(dv_ref)

    rows = own_rows(order_ref, first + slot)
    mine = qkv_ref[rows, :]
    k_own = repeat_heads(mine[:, q_cols : q_cols + HEAD_DIM], heads)
    v_own = repeat_heads(mine[:, q_cols + HEAD_DIM :], heads)
    q_stack = scaled_stack(mine[:, :q_cols], heads)
    d_stack = head_stack(d_ref[rows, :], heads)
    far, own = soft_parts(heads, slot, q_stack, k_ref[...], k_own)
    d_far, d_own = dot_nt(v_ref[...], d_stack), dot_nt(v_own, d_stack)
    mean = jnp.sum(far * d_far, axis=0, keepdims=True) + jnp.sum(own * d_own, axis=0, keepdims=True)
    d_far = (far * (d_far - mean)).astype(BF16)
    d_own = (own * (d_own - mean)).astype(BF16)
    dv_ref[...] += matmul(far.astype(BF16), d_stack)
    dk_ref[...] += matmul(d_far, q_stack)
    dv_own = matmul(own.astype(BF16), d_stack)
    dk_own = matmul(d_own, q_stack)
    d_q = matmul(kt_ref[...], d_far) + matmul(k_own.astype(F32).T.astype(BF16), d_own)
    o_ref[rows, :q_cols] = (head_pick(d_q.T, heads) * ATTN_MULT).astype(BF16)

    def fold(d_k, d_v):
        return jnp.concatenate([head_fold(d_k, heads), head_fold(d_v, heads)], axis=1).astype(BF16)

    @pl.when(slot < PROMPT_BLOCKS)
    def _():
        at = pl.ds(pl.multiple_of(slot * BLOCK, BLOCK), BLOCK)
        dk_ref[at] += dk_own
        dv_ref[at] += dv_own

    @pl.when(slot >= PROMPT_BLOCKS)
    def _():
        o_ref[rows, q_cols:] = fold(dk_own, dv_own)

    @pl.when(slot == GROUP_BLOCKS - 1)
    def _():
        for s in range(PROMPT_BLOCKS):
            at = pl.ds(s * BLOCK, BLOCK)
            o_ref[own_rows(order_ref, first + s), q_cols:] = fold(dk_ref[at], dv_ref[at])


def whole(shape):
    return pl.BlockSpec(shape, lambda g, s, order: (0,) * len(shape))


def attend(qkv, order, heads):
    tokens, cols = qkv.shape
    prompt, q_cols = PROMPT_BLOCKS * BLOCK, heads * HEAD_DIM
    return pl.pallas_call(
        functools.partial(attend_kernel, heads),
        out_shape=jax.ShapeDtypeStruct((tokens, q_cols), BF16),
        grid_spec=pltpu.PrefetchScalarGridSpec(
            num_scalar_prefetch=1,
            grid=(tokens // (GROUP_BLOCKS * BLOCK), GROUP_BLOCKS),
            in_specs=[whole((tokens, cols))],
            out_specs=whole((tokens, q_cols)),
            scratch_shapes=[
                pltpu.VMEM((prompt, q_cols), BF16),
                pltpu.VMEM((prompt, q_cols), BF16),
                pltpu.VMEM((q_cols, prompt), BF16),
            ],
        ),
        cost_estimate=BRIEF,
        compiler_params=pltpu.CompilerParams(vmem_limit_bytes=40 << 20),
    )(order, qkv)


def attend_back(qkv, d_attended, order, heads):
    tokens, cols = qkv.shape
    prompt, q_cols = PROMPT_BLOCKS * BLOCK, heads * HEAD_DIM
    return pl.pallas_call(
        functools.partial(attend_back_kernel, heads),
        out_shape=jax.ShapeDtypeStruct((tokens, cols), BF16),
        grid_spec=pltpu.PrefetchScalarGridSpec(
            num_scalar_prefetch=1,
            grid=(tokens // (GROUP_BLOCKS * BLOCK), GROUP_BLOCKS),
            in_specs=[whole((tokens, cols)), whole((tokens, q_cols))],
            out_specs=whole((tokens, cols)),
            scratch_shapes=[
                pltpu.VMEM((prompt, q_cols), BF16),
                pltpu.VMEM((prompt, q_cols), BF16),
                pltpu.VMEM((q_cols, prompt), BF16),
                pltpu.VMEM((prompt, q_cols), F32),
                pltpu.VMEM((prompt, q_cols), F32),
            ],
        ),
        cost_estimate=BRIEF,
        compiler_params=pltpu.CompilerParams(vmem_limit_bytes=40 << 20),
    )(order, qkv, d_attended)


def total_kernel(grps, chips, x_ref, o_ref, over_z, over_plane, send, recv, psend, precv):
    grp = lax.axis_index("grp")
    chip, core = place()
    me = chip * 2 + core
    far = [lax.rem(grp + s, grps) for s in range(1, grps)]
    near = [(flip(chip, s, chips), c) for s in range(1, chips) for c in (core, 1 - core)]
    near = near + [(chip, 1 - core)]
    barrier = pltpu.get_barrier_semaphore()
    for g in far:
        pl.semaphore_signal(barrier, inc=1, device_id={"grp": g}, device_id_type=MESH)
    for to, c in near:
        pl.semaphore_signal(
            barrier, inc=1, device_id={"chip": to, "core": c}, device_id_type=MESH
        )
    pl.semaphore_wait(barrier, len(far) + len(near))
    copies = []
    for i, g in enumerate(far):
        copy = pltpu.make_async_remote_copy(
            src_ref=x_ref,
            dst_ref=over_z.at[grp],
            send_sem=send.at[i],
            recv_sem=recv.at[grp],
            device_id={"grp": g},
            device_id_type=MESH,
        )
        copy.start()
        copies.append(copy)
    over_z[grp] = x_ref[...]
    for g in far:
        pltpu.make_async_remote_copy(
            src_ref=x_ref,
            dst_ref=over_z.at[g],
            send_sem=send.at[0],
            recv_sem=recv.at[g],
            device_id={"grp": g},
            device_id_type=MESH,
        ).wait_recv()
    over_plane[me] = jnp.sum(over_z[...], axis=0)
    for i, (to, c) in enumerate(near):
        copy = remote(over_plane.at[me], over_plane.at[me], psend.at[i], precv.at[me], to, c)
        copy.start()
        copies.append(copy)
    for to, c in near:
        slot = to * 2 + c
        remote(over_plane.at[me], over_plane.at[slot], psend.at[0], precv.at[slot], to, c).wait_recv()
    for copy in copies:
        copy.wait_send()
    o_ref[...] = jnp.sum(over_plane[...], axis=0)


def total(x, grps, chips, call_id):
    devs = 2 * chips
    return pl.pallas_call(
        functools.partial(total_kernel, grps, chips),
        out_shape=jax.ShapeDtypeStruct(x.shape, F32),
        in_specs=[VMEM],
        out_specs=VMEM,
        scratch_shapes=[
            pltpu.VMEM((grps,) + x.shape, F32),
            pltpu.VMEM((devs,) + x.shape, F32),
            pltpu.SemaphoreType.DMA((grps,)),
            pltpu.SemaphoreType.DMA((grps,)),
            pltpu.SemaphoreType.DMA((devs,)),
            pltpu.SemaphoreType.DMA((devs,)),
        ],
        cost_estimate=BRIEF,
        compiler_params=pltpu.CompilerParams(collective_id=call_id, has_side_effects=True),
    )(x)


def norm_parts(values):
    factor = lax.rsqrt(jnp.mean(values * values, axis=-1, keepdims=True) + EPSILON)
    return factor


def norm_back(values, factor, gain, grad):
    scaled = gain * grad
    inner = jnp.mean(values * scaled, axis=-1, keepdims=True)
    return factor * scaled - values * (factor * factor * factor * inner), jnp.sum(
        grad * values * factor, axis=0
    )


def on_device(
    tokens,
    block_group,
    block_slot,
    attn_gain,
    w_query,
    w_key,
    w_value,
    w_out,
    mlp_gain,
    w_gate,
    w_up,
    w_down,
    cotangent,
):
    grps = lax.axis_size("grp")
    devs = lax.axis_size(PLANE)
    chips = devs // 2
    rows = tokens.shape[0]
    w_rows = w_query.shape[0]
    q_heads = HEADS // devs
    kv_heads = 1
    assert devs % KV_HEADS == 0
    kv_copies = max(1, devs // KV_HEADS)
    q_cols, kv_cols = q_heads * HEAD_DIM, kv_heads * HEAD_DIM
    row_blocks = rows // BLOCK * devs
    row_groups = row_blocks // GROUP_BLOCKS

    row_first = lax.axis_index("grp") * row_blocks
    keys = lax.dynamic_slice_in_dim(block_group, row_first, row_blocks) * GROUP_BLOCKS
    keys = keys + lax.dynamic_slice_in_dim(block_slot, row_first, row_blocks)
    rank = jnp.sum((keys[None, :] < keys[:, None]).astype(jnp.int32), axis=1)
    ids = jnp.arange(row_blocks, dtype=jnp.int32)
    order = jnp.sum(jnp.where(rank[None, :] == ids[:, None], ids[None, :], 0), axis=1)

    def kv_split(w):
        w = w.reshape(w_rows, devs // kv_copies, kv_cols)
        return jnp.repeat(w, kv_copies, axis=1) if kv_copies > 1 else w

    gains = jnp.stack([attn_gain, mlp_gain], axis=1)
    cols = D // 4
    room = cols - q_cols - 2 * kv_cols
    gains = jnp.pad(gains, ((0, 0), (0, room - 2)))
    gains = jnp.broadcast_to(gains[:, None, :], (w_rows, devs, room))
    packed = jnp.concatenate(
        [w_query.reshape(w_rows, devs, q_cols), kv_split(w_key), kv_split(w_value), gains], axis=2
    )
    packed = jnp.swapaxes(packed, 0, 1)
    packed = plane_exchange(packed, packed.shape, by_slot, by_slot, chips, 1)
    packed = jnp.concatenate([packed.reshape(devs * w_rows, cols), w_out.reshape(-1, cols)])
    packed = gather(packed[None], "grp")
    out_full = packed[:, devs * w_rows :].reshape(grps, w_rows, D)
    packed = packed[:, : devs * w_rows].reshape(D, cols)
    w_qkv = packed[:, : q_cols + 2 * kv_cols]
    gain_one = packed[:, q_cols + 2 * kv_cols].astype(F32)
    gain_two = packed[:, q_cols + 2 * kv_cols + 1].astype(F32)

    all_tokens = plane_gather(tokens, chips, 2).reshape(devs * rows, D)
    layer_all = all_tokens.astype(F32)
    normed_one = (layer_all * norm_parts(layer_all) * gain_one).astype(BF16)
    qkv = matmul(normed_one, w_qkv).astype(BF16)
    attended = attend(qkv, order, q_heads)
    attended = plane_exchange(
        attended, (rows, D), by_rows(rows), by_cols(q_cols), chips, 3
    )

    out_full = plane_gather(out_full, chips, 4, inner=True).reshape(D, D)
    layer_in = tokens.astype(F32)
    branch_attn = matmul(attended, out_full)
    residual = layer_in + RESID_MULT * branch_attn
    factor_two = norm_parts(residual)
    normed_two = (residual * factor_two * gain_two).astype(BF16)
    normed_two = plane_gather(normed_two, chips, 2).reshape(devs * rows, D)
    upstream = cotangent.astype(F32)
    d_branch_mlp = (RESID_MULT * upstream).astype(BF16)
    d_branch_mlp, normed_two = lax.optimization_barrier((d_branch_mlp, normed_two))
    d_branch_mlp = plane_gather(d_branch_mlp, chips, 2)
    d_branch_mlp = d_branch_mlp.reshape(devs * rows, D)

    gate_w = gather(w_gate, "grp", axis=1)
    up_w = gather(w_up, "grp", axis=1)
    down_w = gather(w_down, "grp")
    gate_act = matmul(normed_two, gate_w)
    up_act = matmul(normed_two, up_w)
    sig = jax.nn.sigmoid(gate_act)
    silu = gate_act * sig
    hidden = (silu * up_act).astype(BF16)
    part_down = over_rows(hidden, d_branch_mlp).astype(BF16)
    d_hidden = over_cols(d_branch_mlp, down_w)
    d_gate = (d_hidden * up_act * (sig * (1.0 + gate_act * (1.0 - sig)))).astype(BF16)
    d_up = (d_hidden * silu).astype(BF16)
    part_gate = over_rows(normed_two, d_gate).astype(BF16)
    part_up = over_rows(normed_two, d_up).astype(BF16)
    d_gate, d_up, part_down, part_gate, part_up = lax.optimization_barrier(
        (d_gate, d_up, part_down, part_gate, part_up)
    )
    grad_down = scatter(part_down, "grp")
    grad_gate = scatter(part_gate, "grp", axis=1)
    grad_up = scatter(part_up, "grp", axis=1)
    d_normed_two = over_cols(d_gate, gate_w) + over_cols(d_up, up_w)
    d_normed_two = plane_reduce(d_normed_two.astype(BF16).reshape(devs, rows, D), chips, 5)

    d_residual_norm, d_gain_two = norm_back(residual, factor_two, gain_two, d_normed_two)
    d_residual = upstream + d_residual_norm
    d_branch_attn = (RESID_MULT * d_residual).astype(BF16)
    grad_out = over_rows(attended, d_branch_attn).astype(BF16).reshape(grps, devs, w_rows, D)
    grad_out = plane_reduce(grad_out, chips, 6, dtype=BF16, inner=True)
    grad_out, grad_down = lax.optimization_barrier((grad_out, grad_down))
    grad_out = scatter(grad_out, "grp").reshape(w_rows, D).astype(F32)
    d_attended = over_cols(d_branch_attn, out_full).astype(BF16)
    d_attended = plane_exchange(
        d_attended, (devs * rows, q_cols), by_cols(q_cols), by_rows(rows), chips, 7
    )
    d_qkv = attend_back(qkv, d_attended, order, q_heads)
    sent = over_rows(normed_one, d_qkv).astype(BF16)
    sent, d_qkv = lax.optimization_barrier((sent, d_qkv))
    sent, grad_gate, grad_up = lax.optimization_barrier((sent, grad_gate, grad_up))
    sent = scatter(sent, "grp")

    d_normed_one = over_cols(d_qkv, w_qkv).astype(BF16).reshape(devs, rows, D)
    d_normed_one = plane_reduce(d_normed_one, chips, 5)
    d_input_norm, d_gain_one = norm_back(layer_in, norm_parts(layer_in), gain_one, d_normed_one)
    tokens_grad = (d_residual + d_input_norm).astype(BF16)

    sent = sent.reshape(devs, w_rows, q_cols + 2 * kv_cols)
    sent = plane_exchange(sent, sent.shape, by_slot, by_slot, chips, 9).astype(F32)

    def kv_join(g):
        g = g.reshape(devs // kv_copies, kv_copies, w_rows, kv_cols)
        g = jnp.sum(g, axis=1) if kv_copies > 1 else g[:, 0]
        return jnp.swapaxes(g, 0, 1).reshape(w_rows, KV_HEADS * HEAD_DIM)

    grad_query = jnp.swapaxes(sent[:, :, :q_cols], 0, 1).reshape(w_rows, D)
    grad_key = kv_join(sent[:, :, q_cols : q_cols + kv_cols])
    grad_value = kv_join(sent[:, :, q_cols + kv_cols : q_cols + 2 * kv_cols])

    branch_mlp = matmul(hidden, down_w).astype(BF16).reshape(devs, rows, D)
    branch_mlp, d_normed_one = lax.optimization_barrier((branch_mlp, d_normed_one))
    branch_mlp = plane_reduce(branch_mlp, chips, 5)
    layer_out = residual + RESID_MULT * branch_mlp
    scaled_attn = RESID_MULT * branch_attn
    scaled_mlp = RESID_MULT * branch_mlp
    squares = jnp.stack(
        [
            jnp.sum(layer_out * layer_out),
            jnp.sum(scaled_attn * scaled_attn),
            jnp.sum(scaled_mlp * scaled_mlp),
        ]
    )
    totals = jnp.stack([d_gain_one, d_gain_two, jnp.pad(squares, (0, D - 3))])
    totals = total(jnp.pad(totals, ((0, 5), (0, 0))), grps, chips, 8)
    rms_stats = jnp.sqrt(totals[2, :3] / (rows * grps * devs * D))
    gain_first = (lax.axis_index("grp") * devs + lax.axis_index(PLANE)) * w_rows
    gain_grads = lax.dynamic_slice(totals, (0, gain_first), (2, w_rows))
    return (
        layer_out.astype(BF16),
        tokens_grad,
        gain_grads[0],
        grad_query,
        grad_key,
        grad_value,
        grad_out,
        gain_grads[1],
        grad_gate.astype(F32),
        grad_up.astype(F32),
        grad_down.astype(F32),
        rms_stats,
    )


def solution(mesh):
    shape = (mesh.shape["grp"], mesh.shape["blk"] // 2, 2)
    mesh = Mesh(mesh.devices.reshape(shape), EVERY)
    row, col, vec = P(EVERY, None), P(None, EVERY), P(EVERY)
    return jax.shard_map(
        on_device,
        mesh=mesh,
        in_specs=(row, P(), P(), vec, row, row, row, row, vec, col, col, row, row),
        out_specs=(row, row, vec, row, row, row, row, vec, col, col, row, P()),
        check_vma=False,
    )
```

```python
import functools

import jax
import jax.numpy as jnp
from jax import lax
from jax.experimental import pallas as pl
from jax.experimental.pallas import tpu as pltpu
from jax.sharding import Mesh
from jax.sharding import PartitionSpec as P

D = 2048
HEADS = 32
KV_HEADS = 8
HEAD_DIM = 64
BLOCK = 128
PROMPT_BLOCKS = 8
GROUP_BLOCKS = 16
PER_GROUP = HEADS // KV_HEADS

ATTN_MULT = 0.015625
RESID_MULT = 0.22
EPSILON = 1e-05
MASKED = -1e30

PLANE = ("chip", "core")
EVERY = ("grp", "chip", "core")
BF16 = jnp.bfloat16
F32 = jnp.float32


MESH = pl.DeviceIdType.MESH
BRIEF = pl.CostEstimate(flops=1000, bytes_accessed=1000, transcendentals=0)
ANY = pl.BlockSpec(memory_space=pl.ANY)
VMEM = pl.BlockSpec(memory_space=pltpu.VMEM)


def place():
    return lax.axis_index("chip"), lax.axis_index("core")


def flip(chip, step, chips):
    return jnp.bitwise_xor(chip, step) if chips == 4 else lax.rem(chip + step, chips)


def unflip(chip, step, chips):
    return jnp.bitwise_xor(chip, step) if chips == 4 else lax.rem(chip + chips - step, chips)


def greet(peers):
    barrier = pltpu.get_barrier_semaphore()
    for chip, core in peers:
        pl.semaphore_signal(
            barrier, inc=1, device_id={"chip": chip, "core": core}, device_id_type=MESH
        )
    pl.semaphore_wait(barrier, len(peers))


def remote(src, dst, send, recv, chip, core):
    return pltpu.make_async_remote_copy(
        src_ref=src,
        dst_ref=dst,
        send_sem=send,
        recv_sem=recv,
        device_id={"chip": chip, "core": core},
        device_id_type=MESH,
    )


class Gather:
    def __init__(self, chips, inner, x_ref, o_ref, send, recv, local):
        self.chips, self.inner, self.x, self.o = chips, inner, x_ref, o_ref
        self.send, self.recv, self.local = send, recv, local
        self.chip, self.core = place()
        self.half = x_ref.shape[0] // 2
        self.started = []

    def greet(self):
        steps = (1, 2) if self.chips == 4 else range(1, self.chips)
        peers = [(flip(self.chip, s, self.chips), self.core) for s in steps]
        greet(peers + [(self.chip, 1 - self.core)])

    def piece(self, slot, h):
        at = pl.ds(h * self.half, self.half)
        return self.o.at[at, slot] if self.inner else self.o.at[slot, at]

    def own(self, h):
        return self.x.at[pl.ds(h * self.half, self.half)]

    def slot(self, chip, core):
        return chip * 2 + core

    def push(self, src, slot, h, chip, core):
        i = len(self.started)
        copy = remote(src, self.piece(slot, h), self.send.at[i], self.recv.at[slot, h], chip, core)
        copy.start()
        self.started.append(copy)

    def wait_for(self, slot, h):
        remote(
            self.own(h), self.piece(slot, h), self.send.at[0], self.recv.at[slot, h],
            self.chip, 1 - self.core,
        ).wait_recv()

    def start(self):
        me = self.slot(self.chip, self.core)
        if self.chips == 4:
            for h, s in ((0, 1), (1, 2), (1, 1), (0, 2)):
                self.push(self.own(h), me, h, flip(self.chip, s, 4), self.core)
        else:
            for s in range(1, self.chips):
                for h in range(2):
                    self.push(self.own(h), me, h, flip(self.chip, s, self.chips), self.core)
        for h in range(2):
            self.push(self.own(h), me, h, self.chip, 1 - self.core)
        whole = self.o.at[:, me] if self.inner else self.o.at[me]
        self.mine = pltpu.make_async_copy(self.x, whole, self.local)
        self.mine.start()

    def relay(self):
        if self.chips == 4:
            plan = ((1, 0, 2), (2, 1, 1), (1, 1, 0), (2, 0, 0), (3, 0, 0), (3, 1, 0))
        else:
            plan = tuple((s, h, 0) for s in range(1, self.chips) for h in range(2))
        for s, h, onward in plan:
            slot = self.slot(unflip(self.chip, s, self.chips), self.core)
            self.wait_for(slot, h)
            if onward:
                self.push(self.piece(slot, h), slot, h, flip(self.chip, onward, 4), self.core)
            self.push(self.piece(slot, h), slot, h, self.chip, 1 - self.core)

    def finish(self):
        for s in range(self.chips):
            slot = self.slot(unflip(self.chip, s, self.chips), 1 - self.core)
            for h in range(2):
                self.wait_for(slot, h)
        for copy in self.started:
            copy.wait_send()
        self.mine.wait()


def gather_sems(chips):
    return [
        pltpu.SemaphoreType.DMA((4 * chips + 4,)),
        pltpu.SemaphoreType.DMA((2 * chips, 2)),
        pltpu.SemaphoreType.DMA,
    ]


def gather_kernel(chips, inner, x_ref, o_ref, *sems):
    run = Gather(chips, inner, x_ref, o_ref, *sems)
    run.greet()
    run.start()
    run.relay()
    run.finish()


def plane_gather(x, chips, call_id, inner=False):
    devs = 2 * chips
    shape = (x.shape[0], devs) + x.shape[1:] if inner else (devs,) + x.shape
    return pl.pallas_call(
        functools.partial(gather_kernel, chips, inner),
        out_shape=jax.ShapeDtypeStruct(shape, x.dtype),
        in_specs=[ANY],
        out_specs=ANY,
        scratch_shapes=gather_sems(chips),
        cost_estimate=BRIEF,
        compiler_params=pltpu.CompilerParams(collective_id=call_id, has_side_effects=True),
    )(x)


def reduce_kernel(chips, inner, p_ref, o_ref, total, mine, twin, moved, corner, landed, lsem, tsend, trecv, msend, mrecv, csend, crecv):
    chip, core = place()
    sib = 1 - core
    half = (p_ref.shape[0] if inner else p_ref.shape[1]) // 2
    block = (lambda slot: p_ref.at[:, slot]) if inner else (lambda slot: p_ref.at[slot])
    steps = (1, 2) if chips == 4 else tuple(range(1, chips))
    peers = [(flip(chip, s, chips), core) for s in steps]
    greet(peers + [(chip, sib)])
    order = (3, 1, 2, 0) if chips == 4 else tuple(range(1, chips)) + (0,)
    loads, twins = {}, {}
    for s in order:
        to = flip(chip, s, chips) * 2
        twins[s] = remote(block(to + sib), twin.at[s], tsend.at[s], trecv.at[s], chip, sib)
        twins[s].start()
        loads[s] = pltpu.make_async_copy(block(to + core), mine.at[s], lsem.at[s])
        loads[s].start()

    def part(s, h):
        at = pl.ds(h * half, half)
        return mine[s, at].astype(F32) + twin[s, at].astype(F32)

    def ready(s):
        loads[s].wait()
        twins[s].wait_recv()

    sent = []
    if chips == 4:
        corners = []
        ready(3)
        for h, s in ((0, 1), (1, 2)):
            moved[3, pl.ds(h * half, half)] = part(3, h).astype(BF16)
            copy = remote(moved.at[3, pl.ds(h * half, half)], corner.at[h], csend.at[h], crecv.at[h], flip(chip, s, 4), core)
            copy.start()
            corners.append(copy)

        def send(s, h):
            at = pl.ds(h * half, half)
            copy = remote(moved.at[s, at], landed.at[s - 1, at], msend.at[s - 1, h], mrecv.at[s - 1, h], flip(chip, s, 4), core)
            copy.start()
            sent.append(copy)

        for s, h in ((1, 0), (2, 1)):
            ready(s)
            moved[s, pl.ds(h * half, half)] = part(s, h).astype(BF16)
            send(s, h)
        for s, h in ((2, 0), (1, 1)):
            corners[h].wait_recv()
            moved[s, pl.ds(h * half, half)] = (part(s, h) + corner[h].astype(F32)).astype(BF16)
            send(s, h)
        for copy in corners:
            copy.wait_send()
    else:
        for s in steps:
            ready(s)
            for h in range(2):
                at = pl.ds(h * half, half)
                moved[s, at] = part(s, h).astype(BF16)
                copy = remote(moved.at[s, at], landed.at[s - 1, at], msend.at[s - 1, h], mrecv.at[s - 1, h], flip(chip, s, chips), core)
                copy.start()
                sent.append(copy)
    ready(0)
    for h in range(2):
        total[pl.ds(h * half, half)] = part(0, h)
    for copy in sent:
        copy.wait()
    for s in steps[:-1]:
        total[...] += landed[s - 1].astype(F32)
    o_ref[...] = (total[...] + landed[steps[-1] - 1].astype(F32)).astype(o_ref.dtype)
    for s in order:
        twins[s].wait_send()


def plane_reduce(p, chips, call_id, dtype=F32, inner=False):
    block = (p.shape[0],) + p.shape[2:] if inner else p.shape[1:]
    steps = 2 if chips == 4 else chips - 1
    return pl.pallas_call(
        functools.partial(reduce_kernel, chips, inner),
        out_shape=jax.ShapeDtypeStruct(block, dtype),
        in_specs=[ANY],
        out_specs=VMEM,
        scratch_shapes=[
            pltpu.VMEM(block, F32),
            pltpu.VMEM((chips,) + block, BF16),
            pltpu.VMEM((chips,) + block, BF16),
            pltpu.VMEM((chips,) + block, BF16),
            pltpu.VMEM((2, block[0] // 2) + block[1:], BF16),
            pltpu.VMEM((steps,) + block, BF16),
            pltpu.SemaphoreType.DMA((chips,)),
            pltpu.SemaphoreType.DMA((chips,)),
            pltpu.SemaphoreType.DMA((chips,)),
            pltpu.SemaphoreType.DMA((steps, 2)),
            pltpu.SemaphoreType.DMA((steps, 2)),
            pltpu.SemaphoreType.DMA((2,)),
            pltpu.SemaphoreType.DMA((2,)),
        ],
        cost_estimate=BRIEF,
        compiler_params=pltpu.CompilerParams(
            collective_id=call_id, has_side_effects=True, vmem_limit_bytes=56 << 20
        ),
    )(p)


class Drift:
    def __init__(self, pairs, axis):
        self.axis = axis
        self.chip, self.core = place()
        away = lax.dynamic_index_in_dim(pairs, 1 - self.core, axis + 1, keepdims=False)
        self.mine = lax.dynamic_index_in_dim(pairs, self.core, axis + 1, keepdims=False)
        self.twin = lax.ppermute(away, "core", [(0, 1), (1, 0)])

    def part(self, step):
        at = jnp.bitwise_xor(self.chip, step)
        mine = lax.dynamic_index_in_dim(self.mine, at, self.axis, keepdims=False)
        twin = lax.dynamic_index_in_dim(self.twin, at, self.axis, keepdims=False)
        return mine.astype(F32) + twin.astype(F32)

    def parts(self):
        return tuple(self.part(step).astype(BF16) for step in (1, 2, 3))

    @staticmethod
    def send(parts):
        return tuple(
            lax.ppermute(part, "chip", [(c, c ^ step) for c in range(4)])
            for step, part in zip((3, 1, 2), (parts[2], parts[0], parts[1]))
        )

    def finish(self, came):
        total = self.part(0)
        for part in came:
            total = total + part.astype(F32)
        return total


def exchange_kernel(chips, cut, paste, x_ref, o_ref, send, recv, local):
    chip, core = place()
    me = chip * 2 + core
    peers = [(flip(chip, s, chips), c) for s in range(1, chips) for c in (core, 1 - core)]
    peers = peers + [(chip, 1 - core)]
    greet(peers)
    far = [p for p in ([3, 1, 2] if chips == 4 else range(1, chips))]
    order = [(flip(chip, s, chips), c) for s in far for c in (core, 1 - core)] + [(chip, 1 - core)]
    copies = []
    for i, (to, c) in enumerate(order):
        copy = remote(cut(x_ref, to * 2 + c), paste(o_ref, me), send.at[i], recv.at[me], to, c)
        copy.start()
        copies.append(copy)
    mine = pltpu.make_async_copy(cut(x_ref, me), paste(o_ref, me), local)
    mine.start()
    for s in far:
        for c in (core, 1 - core):
            slot = unflip(chip, s, chips) * 2 + c
            remote(cut(x_ref, me), paste(o_ref, slot), send.at[0], recv.at[slot], chip, 1 - core).wait_recv()
    slot = chip * 2 + 1 - core
    remote(cut(x_ref, me), paste(o_ref, slot), send.at[0], recv.at[slot], chip, 1 - core).wait_recv()
    for copy in copies:
        copy.wait_send()
    mine.wait()


def plane_exchange(x, shape, cut, paste, chips, call_id):
    return pl.pallas_call(
        functools.partial(exchange_kernel, chips, cut, paste),
        out_shape=jax.ShapeDtypeStruct(shape, x.dtype),
        in_specs=[ANY],
        out_specs=ANY,
        scratch_shapes=[
            pltpu.SemaphoreType.DMA((2 * chips,)),
            pltpu.SemaphoreType.DMA((2 * chips,)),
            pltpu.SemaphoreType.DMA,
        ],
        cost_estimate=BRIEF,
        compiler_params=pltpu.CompilerParams(collective_id=call_id, has_side_effects=True),
    )(x)


def by_slot(ref, dev):
    return ref.at[dev]


def by_rows(rows):
    return lambda ref, dev: ref.at[pl.ds(pl.multiple_of(dev * rows, rows), rows)]


def by_cols(cols):
    return lambda ref, dev: ref.at[:, pl.ds(pl.multiple_of(dev * cols, cols), cols)]


def matmul(left, right):
    return jnp.dot(left, right, preferred_element_type=F32)


def over_rows(left, right):
    return lax.dot_general(left, right, (((0,), (0,)), ((), ())), preferred_element_type=F32)


def over_cols(left, right):
    return lax.dot_general(left, right, (((1,), (1,)), ((), ())), preferred_element_type=F32)


def gather(values, axes, axis=0):
    return lax.all_gather(values, axes, axis=axis, tiled=True)


def scatter(values, axes, axis=0):
    return lax.psum_scatter(values, axes, scatter_dimension=axis, tiled=True)


def dot_nt(left, right):
    return lax.dot_general(left, right, (((1,), (1,)), ((), ())), preferred_element_type=F32)


def head_stack(values, heads):
    col_head = lax.broadcasted_iota(jnp.int32, values.shape, 1) // HEAD_DIM
    return jnp.concatenate(
        [jnp.where(col_head == h, values, jnp.zeros_like(values)) for h in range(heads)], axis=0
    )


def head_pick(stacked, heads):
    rows = stacked.shape[0] // heads
    col_head = lax.broadcasted_iota(jnp.int32, (rows, stacked.shape[1]), 1) // HEAD_DIM
    total = jnp.zeros((rows, stacked.shape[1]), F32)
    for h in range(heads):
        total = jnp.where(col_head == h, stacked[h * rows : (h + 1) * rows], total)
    return total


def head_fold(values, heads):
    total = values[:, :HEAD_DIM]
    for h in range(1, heads):
        total = total + values[:, h * HEAD_DIM : (h + 1) * HEAD_DIM]
    return total


def repeat_heads(values, heads):
    return jnp.concatenate([values] * heads, axis=1)


def own_rows(order_ref, slot):
    return pl.ds(pl.multiple_of(order_ref[slot] * BLOCK, BLOCK), BLOCK)


def load_prompt(heads, order_ref, qkv_ref, k_ref, v_ref, first):
    q_cols = heads * HEAD_DIM
    for s in range(PROMPT_BLOCKS):
        pair = qkv_ref[own_rows(order_ref, first + s), q_cols:]
        at = pl.ds(s * BLOCK, BLOCK)
        k_ref[at] = repeat_heads(pair[:, :HEAD_DIM], heads)
        v_ref[at] = repeat_heads(pair[:, HEAD_DIM:], heads)


def soft_parts(heads, slot, q_stack, k_far, k_own):
    far = dot_nt(k_far, q_stack)
    own = dot_nt(k_own, q_stack)
    limit = jnp.minimum(slot, PROMPT_BLOCKS) * BLOCK
    far = jnp.where(lax.broadcasted_iota(jnp.int32, far.shape, 0) < limit, far, MASKED)
    key = lax.broadcasted_iota(jnp.int32, own.shape, 0)
    row = lax.broadcasted_iota(jnp.int32, own.shape, 1) % BLOCK
    own = jnp.where(key <= row, own, MASKED)
    peak = jnp.maximum(jnp.max(far, axis=0, keepdims=True), jnp.max(own, axis=0, keepdims=True))
    far, own = jnp.exp(far - peak), jnp.exp(own - peak)
    scale = 1.0 / (jnp.sum(far, axis=0, keepdims=True) + jnp.sum(own, axis=0, keepdims=True))
    return far * scale, own * scale


def scaled_stack(q, heads):
    return head_stack((q.astype(F32) * ATTN_MULT).astype(BF16), heads)


def attend_kernel(heads, order_ref, qkv_ref, o_ref, k_ref, v_ref, vt_ref):
    first, slot = pl.program_id(0) * GROUP_BLOCKS, pl.program_id(1)
    q_cols = heads * HEAD_DIM

    @pl.when(slot == 0)
    def _():
        load_prompt(heads, order_ref, qkv_ref, k_ref, v_ref, first)
        vt_ref[...] = v_ref[...].astype(F32).T.astype(BF16)

    rows = own_rows(order_ref, first + slot)
    mine = qkv_ref[rows, :]
    k_own = repeat_heads(mine[:, q_cols : q_cols + HEAD_DIM], heads)
    v_own = repeat_heads(mine[:, q_cols + HEAD_DIM :], heads)
    far, own = soft_parts(heads, slot, scaled_stack(mine[:, :q_cols], heads), k_ref[...], k_own)
    mixed = matmul(vt_ref[...], far.astype(BF16))
    mixed += matmul(v_own.astype(F32).T.astype(BF16), own.astype(BF16))
    o_ref[rows, :] = head_pick(mixed.T, heads).astype(BF16)


def attend_back_kernel(
    heads, order_ref, qkv_ref, d_ref, o_ref, k_ref, v_ref, kt_ref, dk_ref, dv_ref
):
    first, slot = pl.program_id(0) * GROUP_BLOCKS, pl.program_id(1)
    q_cols = heads * HEAD_DIM

    @pl.when(slot == 0)
    def _():
        load_prompt(heads, order_ref, qkv_ref, k_ref, v_ref, first)
        kt_ref[...] = k_ref[...].astype(F32).T.astype(BF16)
        dk_ref[...] = jnp.zeros_like(dk_ref)
        dv_ref[...] = jnp.zeros_like(dv_ref)

    rows = own_rows(order_ref, first + slot)
    mine = qkv_ref[rows, :]
    k_own = repeat_heads(mine[:, q_cols : q_cols + HEAD_DIM], heads)
    v_own = repeat_heads(mine[:, q_cols + HEAD_DIM :], heads)
    q_stack = scaled_stack(mine[:, :q_cols], heads)
    d_stack = head_stack(d_ref[rows, :], heads)
    far, own = soft_parts(heads, slot, q_stack, k_ref[...], k_own)
    d_far, d_own = dot_nt(v_ref[...], d_stack), dot_nt(v_own, d_stack)
    mean = jnp.sum(far * d_far, axis=0, keepdims=True) + jnp.sum(own * d_own, axis=0, keepdims=True)
    d_far = (far * (d_far - mean)).astype(BF16)
    d_own = (own * (d_own - mean)).astype(BF16)
    dv_ref[...] += matmul(far.astype(BF16), d_stack)
    dk_ref[...] += matmul(d_far, q_stack)
    dv_own = matmul(own.astype(BF16), d_stack)
    dk_own = matmul(d_own, q_stack)
    d_q = matmul(kt_ref[...], d_far) + matmul(k_own.astype(F32).T.astype(BF16), d_own)
    o_ref[rows, :q_cols] = (head_pick(d_q.T, heads) * ATTN_MULT).astype(BF16)

    def fold(d_k, d_v):
        return jnp.concatenate([head_fold(d_k, heads), head_fold(d_v, heads)], axis=1).astype(BF16)

    @pl.when(slot < PROMPT_BLOCKS)
    def _():
        at = pl.ds(pl.multiple_of(slot * BLOCK, BLOCK), BLOCK)
        dk_ref[at] += dk_own
        dv_ref[at] += dv_own

    @pl.when(slot >= PROMPT_BLOCKS)
    def _():
        o_ref[rows, q_cols:] = fold(dk_own, dv_own)

    @pl.when(slot == GROUP_BLOCKS - 1)
    def _():
        for s in range(PROMPT_BLOCKS):
            at = pl.ds(s * BLOCK, BLOCK)
            o_ref[own_rows(order_ref, first + s), q_cols:] = fold(dk_ref[at], dv_ref[at])


def whole(shape):
    return pl.BlockSpec(shape, lambda g, s, order: (0,) * len(shape))


def attend(qkv, order, heads):
    tokens, cols = qkv.shape
    prompt, q_cols = PROMPT_BLOCKS * BLOCK, heads * HEAD_DIM
    return pl.pallas_call(
        functools.partial(attend_kernel, heads),
        out_shape=jax.ShapeDtypeStruct((tokens, q_cols), BF16),
        grid_spec=pltpu.PrefetchScalarGridSpec(
            num_scalar_prefetch=1,
            grid=(tokens // (GROUP_BLOCKS * BLOCK), GROUP_BLOCKS),
            in_specs=[whole((tokens, cols))],
            out_specs=whole((tokens, q_cols)),
            scratch_shapes=[
                pltpu.VMEM((prompt, q_cols), BF16),
                pltpu.VMEM((prompt, q_cols), BF16),
                pltpu.VMEM((q_cols, prompt), BF16),
            ],
        ),
        cost_estimate=BRIEF,
        compiler_params=pltpu.CompilerParams(vmem_limit_bytes=40 << 20),
    )(order, qkv)


def attend_back(qkv, d_attended, order, heads):
    tokens, cols = qkv.shape
    prompt, q_cols = PROMPT_BLOCKS * BLOCK, heads * HEAD_DIM
    return pl.pallas_call(
        functools.partial(attend_back_kernel, heads),
        out_shape=jax.ShapeDtypeStruct((tokens, cols), BF16),
        grid_spec=pltpu.PrefetchScalarGridSpec(
            num_scalar_prefetch=1,
            grid=(tokens // (GROUP_BLOCKS * BLOCK), GROUP_BLOCKS),
            in_specs=[whole((tokens, cols)), whole((tokens, q_cols))],
            out_specs=whole((tokens, cols)),
            scratch_shapes=[
                pltpu.VMEM((prompt, q_cols), BF16),
                pltpu.VMEM((prompt, q_cols), BF16),
                pltpu.VMEM((q_cols, prompt), BF16),
                pltpu.VMEM((prompt, q_cols), F32),
                pltpu.VMEM((prompt, q_cols), F32),
            ],
        ),
        cost_estimate=BRIEF,
        compiler_params=pltpu.CompilerParams(vmem_limit_bytes=40 << 20),
    )(order, qkv, d_attended)


def total_kernel(grps, chips, x_ref, o_ref, over_z, over_plane, send, recv, psend, precv):
    grp = lax.axis_index("grp")
    chip, core = place()
    me = chip * 2 + core
    far = [lax.rem(grp + s, grps) for s in range(1, grps)]
    near = [(flip(chip, s, chips), c) for s in range(1, chips) for c in (core, 1 - core)]
    near = near + [(chip, 1 - core)]
    barrier = pltpu.get_barrier_semaphore()
    for g in far:
        pl.semaphore_signal(barrier, inc=1, device_id={"grp": g}, device_id_type=MESH)
    for to, c in near:
        pl.semaphore_signal(
            barrier, inc=1, device_id={"chip": to, "core": c}, device_id_type=MESH
        )
    pl.semaphore_wait(barrier, len(far) + len(near))
    copies = []
    for i, g in enumerate(far):
        copy = pltpu.make_async_remote_copy(
            src_ref=x_ref,
            dst_ref=over_z.at[grp],
            send_sem=send.at[i],
            recv_sem=recv.at[grp],
            device_id={"grp": g},
            device_id_type=MESH,
        )
        copy.start()
        copies.append(copy)
    over_z[grp] = x_ref[...]
    for g in far:
        pltpu.make_async_remote_copy(
            src_ref=x_ref,
            dst_ref=over_z.at[g],
            send_sem=send.at[0],
            recv_sem=recv.at[g],
            device_id={"grp": g},
            device_id_type=MESH,
        ).wait_recv()
    over_plane[me] = jnp.sum(over_z[...], axis=0)
    for i, (to, c) in enumerate(near):
        copy = remote(over_plane.at[me], over_plane.at[me], psend.at[i], precv.at[me], to, c)
        copy.start()
        copies.append(copy)
    for to, c in near:
        slot = to * 2 + c
        remote(over_plane.at[me], over_plane.at[slot], psend.at[0], precv.at[slot], to, c).wait_recv()
    for copy in copies:
        copy.wait_send()
    o_ref[...] = jnp.sum(over_plane[...], axis=0)


def total(x, grps, chips, call_id):
    devs = 2 * chips
    return pl.pallas_call(
        functools.partial(total_kernel, grps, chips),
        out_shape=jax.ShapeDtypeStruct(x.shape, F32),
        in_specs=[VMEM],
        out_specs=VMEM,
        scratch_shapes=[
            pltpu.VMEM((grps,) + x.shape, F32),
            pltpu.VMEM((devs,) + x.shape, F32),
            pltpu.SemaphoreType.DMA((grps,)),
            pltpu.SemaphoreType.DMA((grps,)),
            pltpu.SemaphoreType.DMA((devs,)),
            pltpu.SemaphoreType.DMA((devs,)),
        ],
        cost_estimate=BRIEF,
        compiler_params=pltpu.CompilerParams(collective_id=call_id, has_side_effects=True),
    )(x)


def params(axes, mib=56):
    return pltpu.CompilerParams(
        dimension_semantics=("arbitrary",) * axes, vmem_limit_bytes=mib << 20
    )


def tile_rows(count, limit):
    while count % limit:
        limit //= 2
    return limit


def widen_kernel(n_ref, w_ref, h_ref, ht_ref, s_ref, t_ref, nt_ref):
    values = n_ref[...]
    gate, up = matmul(values, w_ref[0, 0]), matmul(values, w_ref[0, 1])
    sig = 1.0 / (1.0 + jnp.exp(-gate))
    silu = gate * sig
    hidden = (silu * up).astype(BF16)
    h_ref[0] = hidden
    ht_ref[0] = hidden.T
    s_ref[0] = silu.astype(BF16)
    t_ref[0] = (up * (sig * (1.0 + gate * (1.0 - sig)))).astype(BF16)

    @pl.when(pl.program_id(1) == 0)
    def _():
        nt_ref[...] = values.T


def widen(normed, weights):
    tokens, depth = normed.shape
    shards, _, _, width = weights.shape
    rows = tile_rows(tokens, 1024)
    tall = jax.ShapeDtypeStruct((shards, tokens, width), BF16)
    tall_spec = pl.BlockSpec((1, rows, width), lambda r, s: (s, r, 0))
    return pl.pallas_call(
        widen_kernel,
        out_shape=(
            tall,
            jax.ShapeDtypeStruct((shards, width, tokens), BF16),
            tall,
            tall,
            jax.ShapeDtypeStruct((depth, tokens), BF16),
        ),
        grid=(tokens // rows, shards),
        in_specs=[
            pl.BlockSpec((rows, depth), lambda r, s: (r, 0)),
            pl.BlockSpec((1, 2, depth, width), lambda r, s: (s, 0, 0, 0)),
        ],
        out_specs=(
            tall_spec,
            pl.BlockSpec((1, width, rows), lambda r, s: (s, 0, r)),
            tall_spec,
            tall_spec,
            pl.BlockSpec((depth, rows), lambda r, s: (0, r)),
        ),
        cost_estimate=BRIEF,
        compiler_params=params(2),
    )(normed, weights)


def down_part_kernel(ht_ref, d_ref, o_ref):
    o_ref[0] = matmul(ht_ref[0], d_ref[...]).astype(BF16)


def down_part(hidden_t, upstream):
    shards, width, tokens = hidden_t.shape
    depth = upstream.shape[1]
    cols = tile_rows(depth, 1024)
    return pl.pallas_call(
        down_part_kernel,
        out_shape=jax.ShapeDtypeStruct((shards, width, depth), BF16),
        grid=(depth // cols, shards),
        in_specs=[
            pl.BlockSpec((1, width, tokens), lambda c, s: (s, 0, 0)),
            pl.BlockSpec((tokens, cols), lambda c, s: (0, c)),
        ],
        out_specs=pl.BlockSpec((1, width, cols), lambda c, s: (s, 0, c)),
        cost_estimate=BRIEF,
        compiler_params=params(2),
    )(hidden_t, upstream)


def mix_kernel(h_ref, w_ref, m_ref):
    mixed = None
    for i in range(w_ref.shape[0]):
        part = matmul(h_ref[i], w_ref[i])
        mixed = part if mixed is None else mixed + part
    m_ref[...] = mixed.astype(BF16)


def narrow_specs(hidden, weights):
    shards, tokens, width = hidden.shape
    depth = weights.shape[2]
    rows = tile_rows(tokens, 512)
    return (
        tokens // rows,
        pl.BlockSpec((shards, rows, width), lambda r: (0, r, 0)),
        pl.BlockSpec((rows, depth), lambda r: (r, 0)),
        pl.BlockSpec(weights.shape, lambda r: (0, 0, 0), pipeline_mode=pl.Buffered(1)),
    )


def mix(hidden, weights):
    steps, tall_spec, flat_spec, weight_spec = narrow_specs(hidden, weights)
    return pl.pallas_call(
        mix_kernel,
        out_shape=jax.ShapeDtypeStruct((hidden.shape[1], weights.shape[2]), BF16),
        grid=(steps,),
        in_specs=[tall_spec, weight_spec],
        out_specs=flat_spec,
        cost_estimate=BRIEF,
        compiler_params=params(1),
    )(hidden, weights)


def narrow_back_kernel(s_ref, t_ref, d_ref, w_ref, dg_ref, du_ref):
    upstream = d_ref[...]
    for i in range(w_ref.shape[0]):
        d_hidden = dot_nt(upstream, w_ref[i])
        dg_ref[i] = (d_hidden * t_ref[i].astype(F32)).astype(BF16)
        du_ref[i] = (d_hidden * s_ref[i].astype(F32)).astype(BF16)


def narrow_back(silu, slope, upstream, weights):
    steps, tall_spec, flat_spec, weight_spec = narrow_specs(silu, weights)
    tall = jax.ShapeDtypeStruct(silu.shape, BF16)
    return pl.pallas_call(
        narrow_back_kernel,
        out_shape=(tall, tall),
        grid=(steps,),
        in_specs=[tall_spec, tall_spec, flat_spec, weight_spec],
        out_specs=(tall_spec, tall_spec),
        cost_estimate=BRIEF,
        compiler_params=params(1),
    )(silu, slope, upstream, weights)


def widen_part_kernel(nt_ref, dg_ref, du_ref, o_ref):
    values = nt_ref[...]
    o_ref[0, 0] = matmul(values, dg_ref[0]).astype(BF16)
    o_ref[0, 1] = matmul(values, du_ref[0]).astype(BF16)


def widen_part(normed_t, d_gate, d_up):
    depth, tokens = normed_t.shape
    shards, _, width = d_gate.shape
    rows = tile_rows(depth, 1024)
    tall_spec = pl.BlockSpec((1, tokens, width), lambda r, s: (s, 0, 0))
    return pl.pallas_call(
        widen_part_kernel,
        out_shape=jax.ShapeDtypeStruct((shards, 2, depth, width), BF16),
        grid=(depth // rows, shards),
        in_specs=[pl.BlockSpec((rows, tokens), lambda r, s: (r, 0)), tall_spec, tall_spec],
        out_specs=pl.BlockSpec((1, 2, rows, width), lambda r, s: (s, 0, r, 0)),
        cost_estimate=BRIEF,
        compiler_params=params(2),
    )(normed_t, d_gate, d_up)


def widen_back_kernel(dg_ref, du_ref, w_ref, o_ref):
    total = None
    for i in range(w_ref.shape[0]):
        part = dot_nt(dg_ref[i], w_ref[i, 0]) + dot_nt(du_ref[i], w_ref[i, 1])
        total = part if total is None else total + part
    o_ref[...] = total.astype(BF16)


def widen_back(d_gate, d_up, weights):
    shards, tokens, width = d_gate.shape
    depth = weights.shape[2]
    rows = tile_rows(tokens, 512)
    tall_spec = pl.BlockSpec((shards, rows, width), lambda r: (0, r, 0))
    return pl.pallas_call(
        widen_back_kernel,
        out_shape=jax.ShapeDtypeStruct((tokens, depth), BF16),
        grid=(tokens // rows,),
        in_specs=[
            tall_spec,
            tall_spec,
            pl.BlockSpec(weights.shape, lambda r: (0, 0, 0, 0), pipeline_mode=pl.Buffered(1)),
        ],
        out_specs=pl.BlockSpec((rows, depth), lambda r: (r, 0)),
        cost_estimate=BRIEF,
        compiler_params=params(1),
    )(d_gate, d_up, weights)


def norm_parts(values):
    factor = lax.rsqrt(jnp.mean(values * values, axis=-1, keepdims=True) + EPSILON)
    return factor


def norm_back(values, factor, gain, grad):
    scaled = gain * grad
    inner = jnp.mean(values * scaled, axis=-1, keepdims=True)
    return factor * scaled - values * (factor * factor * factor * inner), jnp.sum(
        grad * values * factor, axis=0
    )


def on_device(
    tokens,
    block_group,
    block_slot,
    attn_gain,
    w_query,
    w_key,
    w_value,
    w_out,
    mlp_gain,
    w_gate,
    w_up,
    w_down,
    cotangent,
):
    grps = lax.axis_size("grp")
    devs = lax.axis_size(PLANE)
    chips = devs // 2
    rows = tokens.shape[0]
    w_rows = w_query.shape[0]
    q_heads = HEADS // devs
    kv_heads = 1
    assert devs % KV_HEADS == 0
    kv_copies = max(1, devs // KV_HEADS)
    q_cols, kv_cols = q_heads * HEAD_DIM, kv_heads * HEAD_DIM
    row_blocks = rows // BLOCK * devs
    row_groups = row_blocks // GROUP_BLOCKS

    row_first = lax.axis_index("grp") * row_blocks
    keys = lax.dynamic_slice_in_dim(block_group, row_first, row_blocks) * GROUP_BLOCKS
    keys = keys + lax.dynamic_slice_in_dim(block_slot, row_first, row_blocks)
    rank = jnp.sum((keys[None, :] < keys[:, None]).astype(jnp.int32), axis=1)
    ids = jnp.arange(row_blocks, dtype=jnp.int32)
    order = jnp.sum(jnp.where(rank[None, :] == ids[:, None], ids[None, :], 0), axis=1)

    def kv_split(w):
        w = w.reshape(w_rows, devs // kv_copies, kv_cols)
        return jnp.repeat(w, kv_copies, axis=1) if kv_copies > 1 else w

    gains = jnp.stack([attn_gain, mlp_gain], axis=1)
    cols = D // 4
    room = cols - q_cols - 2 * kv_cols
    gains = jnp.pad(gains, ((0, 0), (0, room - 2)))
    gains = jnp.broadcast_to(gains[:, None, :], (w_rows, devs, room))
    packed = jnp.concatenate(
        [w_query.reshape(w_rows, devs, q_cols), kv_split(w_key), kv_split(w_value), gains], axis=2
    )
    packed = jnp.swapaxes(packed, 0, 1)
    packed = plane_exchange(packed, packed.shape, by_slot, by_slot, chips, 1)
    packed = jnp.concatenate([packed.reshape(devs * w_rows, cols), w_out.reshape(-1, cols)])
    packed = gather(packed[None], "grp")
    out_full = packed[:, devs * w_rows :].reshape(grps, w_rows, D)
    packed = packed[:, : devs * w_rows].reshape(D, cols)
    w_qkv = packed[:, : q_cols + 2 * kv_cols]
    gain_one = packed[:, q_cols + 2 * kv_cols].astype(F32)
    gain_two = packed[:, q_cols + 2 * kv_cols + 1].astype(F32)

    all_tokens = plane_gather(tokens, chips, 2).reshape(devs * rows, D)
    layer_all = all_tokens.astype(F32)
    normed_one = (layer_all * norm_parts(layer_all) * gain_one).astype(BF16)
    qkv = matmul(normed_one, w_qkv).astype(BF16)
    attended = attend(qkv, order, q_heads)
    attended = plane_exchange(
        attended, (rows, D), by_rows(rows), by_cols(q_cols), chips, 3
    )

    out_full = plane_gather(out_full, chips, 4, inner=True).reshape(D, D)
    layer_in = tokens.astype(F32)
    branch_attn = matmul(attended, out_full)
    residual = layer_in + RESID_MULT * branch_attn
    factor_two = norm_parts(residual)
    normed_two = (residual * factor_two * gain_two).astype(BF16)
    normed_two = plane_gather(normed_two, chips, 2).reshape(devs * rows, D)
    upstream = cotangent.astype(F32)
    d_branch_mlp = (RESID_MULT * upstream).astype(BF16)
    d_branch_mlp, normed_two = lax.optimization_barrier((d_branch_mlp, normed_two))
    d_branch_mlp = plane_gather(d_branch_mlp, chips, 2)
    d_branch_mlp = d_branch_mlp.reshape(devs * rows, D)

    wide_w = gather(jnp.stack([w_gate, w_up])[None], "grp")
    down_w = gather(w_down[None], "grp")
    normed_two, d_branch_mlp = lax.optimization_barrier((normed_two, d_branch_mlp))
    hidden, hidden_t, silu, slope, normed_t = widen(normed_two, wide_w)
    part_down = down_part(hidden_t, d_branch_mlp)
    part_down, hidden, silu = lax.optimization_barrier((part_down, hidden, silu))
    grad_down = scatter(part_down, "grp")
    branch_mlp = mix(hidden, down_w)
    drift_mlp = None
    if chips == 4:
        drift_mlp = Drift(branch_mlp.reshape(4, 2, rows, D), 0)
    branch_mlp, silu = lax.optimization_barrier((branch_mlp, silu))
    d_gate, d_up = narrow_back(silu, slope, d_branch_mlp, down_w)
    if chips == 4:
        sent_mlp, d_gate, d_up = lax.optimization_barrier((drift_mlp.parts(), d_gate, d_up))
        sent_mlp = Drift.send(sent_mlp)
    part_wide = widen_part(normed_t, d_gate, d_up)
    part_wide, d_gate, d_up = lax.optimization_barrier((part_wide, d_gate, d_up))
    grad_wide = scatter(part_wide, "grp")
    d_normed_two = widen_back(d_gate, d_up, wide_w)
    if chips == 4:
        sent_mlp, d_normed_two = lax.optimization_barrier((sent_mlp, d_normed_two))
        branch_mlp = drift_mlp.finish(sent_mlp)
    d_normed_two = plane_reduce(d_normed_two.reshape(devs, rows, D), chips, 5)
    if chips != 4:
        branch_mlp = plane_reduce(branch_mlp.reshape(devs, rows, D), chips, 5)
    layer_out = residual + RESID_MULT * branch_mlp

    d_residual_norm, d_gain_two = norm_back(residual, factor_two, gain_two, d_normed_two)
    d_residual = upstream + d_residual_norm
    d_branch_attn = (RESID_MULT * d_residual).astype(BF16)
    grad_out = over_rows(attended, d_branch_attn).astype(BF16)
    grad_out, d_branch_attn = lax.optimization_barrier((grad_out, d_branch_attn))
    if chips == 4:
        drift_out = Drift(grad_out.reshape(grps, 4, 2, w_rows, D), 1)
    d_attended = over_cols(d_branch_attn, out_full).astype(BF16)
    d_attended = plane_exchange(
        d_attended, (devs * rows, q_cols), by_cols(q_cols), by_rows(rows), chips, 7
    )
    if chips == 4:
        sent_out, d_attended = lax.optimization_barrier((drift_out.parts(), d_attended))
        sent_out = Drift.send(sent_out)
    d_attended, grad_down = lax.optimization_barrier((d_attended, grad_down))
    d_qkv = attend_back(qkv, d_attended, order, q_heads)
    if chips == 4:
        sent_out, d_qkv = lax.optimization_barrier((sent_out, d_qkv))
        grad_out = drift_out.finish(sent_out).astype(BF16)
    else:
        grad_out = plane_reduce(
            grad_out.reshape(grps, devs, w_rows, D), chips, 6, dtype=BF16, inner=True
        )
    grad_out = scatter(grad_out, "grp").reshape(w_rows, D).astype(F32)
    sent = over_rows(normed_one, d_qkv).astype(BF16)
    sent, d_qkv = lax.optimization_barrier((sent, d_qkv))
    sent, grad_wide = lax.optimization_barrier((sent, grad_wide))
    sent = scatter(sent, "grp")

    d_normed_one = over_cols(d_qkv, w_qkv).astype(BF16).reshape(devs, rows, D)
    d_normed_one = plane_reduce(d_normed_one, chips, 5)
    d_input_norm, d_gain_one = norm_back(layer_in, norm_parts(layer_in), gain_one, d_normed_one)
    tokens_grad = (d_residual + d_input_norm).astype(BF16)

    sent = sent.reshape(devs, w_rows, q_cols + 2 * kv_cols)
    sent = plane_exchange(sent, sent.shape, by_slot, by_slot, chips, 9).astype(F32)

    def kv_join(g):
        g = g.reshape(devs // kv_copies, kv_copies, w_rows, kv_cols)
        g = jnp.sum(g, axis=1) if kv_copies > 1 else g[:, 0]
        return jnp.swapaxes(g, 0, 1).reshape(w_rows, KV_HEADS * HEAD_DIM)

    grad_query = jnp.swapaxes(sent[:, :, :q_cols], 0, 1).reshape(w_rows, D)
    grad_key = kv_join(sent[:, :, q_cols : q_cols + kv_cols])
    grad_value = kv_join(sent[:, :, q_cols + kv_cols : q_cols + 2 * kv_cols])

    scaled_attn = RESID_MULT * branch_attn
    scaled_mlp = RESID_MULT * branch_mlp
    squares = jnp.stack(
        [
            jnp.sum(layer_out * layer_out),
            jnp.sum(scaled_attn * scaled_attn),
            jnp.sum(scaled_mlp * scaled_mlp),
        ]
    )
    totals = jnp.stack([d_gain_one, d_gain_two, jnp.pad(squares, (0, D - 3))])
    totals = total(jnp.pad(totals, ((0, 5), (0, 0))), grps, chips, 8)
    rms_stats = jnp.sqrt(totals[2, :3] / (rows * grps * devs * D))
    gain_first = (lax.axis_index("grp") * devs + lax.axis_index(PLANE)) * w_rows
    gain_grads = lax.dynamic_slice(totals, (0, gain_first), (2, w_rows))
    return (
        layer_out.astype(BF16),
        tokens_grad,
        gain_grads[0],
        grad_query,
        grad_key,
        grad_value,
        grad_out,
        gain_grads[1],
        grad_wide[0, 0].astype(F32),
        grad_wide[0, 1].astype(F32),
        grad_down[0].astype(F32),
        rms_stats,
    )


def solution(mesh):
    shape = (mesh.shape["grp"], mesh.shape["blk"] // 2, 2)
    mesh = Mesh(mesh.devices.reshape(shape), EVERY)
    row, col, vec = P(EVERY, None), P(None, EVERY), P(EVERY)
    return jax.shard_map(
        on_device,
        mesh=mesh,
        in_specs=(row, P(), P(), vec, row, row, row, row, vec, col, col, row, row),
        out_specs=(row, row, vec, row, row, row, row, vec, col, col, row, P()),
        check_vma=False,
    )
```

```python
import functools

import jax
import jax.numpy as jnp
from jax import lax
from jax.experimental import pallas as pl
from jax.experimental.pallas import tpu as pltpu
from jax.sharding import Mesh
from jax.sharding import PartitionSpec as P

D = 2048
HEADS = 32
KV_HEADS = 8
HEAD_DIM = 64
BLOCK = 128
PROMPT_BLOCKS = 8
GROUP_BLOCKS = 16
PER_GROUP = HEADS // KV_HEADS

ATTN_MULT = 0.015625
RESID_MULT = 0.22
EPSILON = 1e-05
MASKED = -1e30

PLANE = ("chip", "core")
EVERY = ("grp", "chip", "core")
BF16 = jnp.bfloat16
F32 = jnp.float32


MESH = pl.DeviceIdType.MESH
BRIEF = pl.CostEstimate(flops=1000, bytes_accessed=1000, transcendentals=0)
ANY = pl.BlockSpec(memory_space=pl.ANY)
VMEM = pl.BlockSpec(memory_space=pltpu.VMEM)


def place():
    return lax.axis_index("chip"), lax.axis_index("core")


def flip(chip, step, chips):
    return jnp.bitwise_xor(chip, step) if chips == 4 else lax.rem(chip + step, chips)


def unflip(chip, step, chips):
    return jnp.bitwise_xor(chip, step) if chips == 4 else lax.rem(chip + chips - step, chips)


def greet(peers):
    barrier = pltpu.get_barrier_semaphore()
    for chip, core in peers:
        pl.semaphore_signal(
            barrier, inc=1, device_id={"chip": chip, "core": core}, device_id_type=MESH
        )
    pl.semaphore_wait(barrier, len(peers))


def remote(src, dst, send, recv, chip, core):
    return pltpu.make_async_remote_copy(
        src_ref=src,
        dst_ref=dst,
        send_sem=send,
        recv_sem=recv,
        device_id={"chip": chip, "core": core},
        device_id_type=MESH,
    )


class Gather:
    def __init__(self, chips, inner, x_ref, o_ref, send, recv, local):
        self.chips, self.inner, self.x, self.o = chips, inner, x_ref, o_ref
        self.send, self.recv, self.local = send, recv, local
        self.chip, self.core = place()
        self.half = x_ref.shape[0] // 2
        self.started = []

    def greet(self):
        steps = (1, 2) if self.chips == 4 else range(1, self.chips)
        peers = [(flip(self.chip, s, self.chips), self.core) for s in steps]
        greet(peers + [(self.chip, 1 - self.core)])

    def piece(self, slot, h):
        at = pl.ds(h * self.half, self.half)
        return self.o.at[at, slot] if self.inner else self.o.at[slot, at]

    def own(self, h):
        return self.x.at[pl.ds(h * self.half, self.half)]

    def slot(self, chip, core):
        return chip * 2 + core

    def push(self, src, slot, h, chip, core):
        i = len(self.started)
        copy = remote(src, self.piece(slot, h), self.send.at[i], self.recv.at[slot, h], chip, core)
        copy.start()
        self.started.append(copy)

    def wait_for(self, slot, h):
        remote(
            self.own(h), self.piece(slot, h), self.send.at[0], self.recv.at[slot, h],
            self.chip, 1 - self.core,
        ).wait_recv()

    def start(self):
        me = self.slot(self.chip, self.core)
        if self.chips == 4:
            for h, s in ((0, 1), (1, 2), (1, 1), (0, 2)):
                self.push(self.own(h), me, h, flip(self.chip, s, 4), self.core)
        else:
            for s in range(1, self.chips):
                for h in range(2):
                    self.push(self.own(h), me, h, flip(self.chip, s, self.chips), self.core)
        for h in range(2):
            self.push(self.own(h), me, h, self.chip, 1 - self.core)
        whole = self.o.at[:, me] if self.inner else self.o.at[me]
        self.mine = pltpu.make_async_copy(self.x, whole, self.local)
        self.mine.start()

    def relay(self):
        if self.chips == 4:
            plan = ((1, 0, 2), (2, 1, 1), (1, 1, 0), (2, 0, 0), (3, 0, 0), (3, 1, 0))
        else:
            plan = tuple((s, h, 0) for s in range(1, self.chips) for h in range(2))
        for s, h, onward in plan:
            slot = self.slot(unflip(self.chip, s, self.chips), self.core)
            self.wait_for(slot, h)
            if onward:
                self.push(self.piece(slot, h), slot, h, flip(self.chip, onward, 4), self.core)
            self.push(self.piece(slot, h), slot, h, self.chip, 1 - self.core)

    def finish(self):
        for s in range(self.chips):
            slot = self.slot(unflip(self.chip, s, self.chips), 1 - self.core)
            for h in range(2):
                self.wait_for(slot, h)
        for copy in self.started:
            copy.wait_send()
        self.mine.wait()


def gather_sems(chips):
    return [
        pltpu.SemaphoreType.DMA((4 * chips + 4,)),
        pltpu.SemaphoreType.DMA((2 * chips, 2)),
        pltpu.SemaphoreType.DMA,
    ]


def gather_kernel(chips, inner, x_ref, o_ref, *sems):
    run = Gather(chips, inner, x_ref, o_ref, *sems)
    run.greet()
    run.start()
    run.relay()
    run.finish()


def plane_gather(x, chips, call_id, inner=False):
    devs = 2 * chips
    shape = (x.shape[0], devs) + x.shape[1:] if inner else (devs,) + x.shape
    return pl.pallas_call(
        functools.partial(gather_kernel, chips, inner),
        out_shape=jax.ShapeDtypeStruct(shape, x.dtype),
        in_specs=[ANY],
        out_specs=ANY,
        scratch_shapes=gather_sems(chips),
        cost_estimate=BRIEF,
        compiler_params=pltpu.CompilerParams(collective_id=call_id, has_side_effects=True),
    )(x)


def reduce_kernel(chips, inner, p_ref, o_ref, total, mine, twin, moved, corner, landed, lsem, tsend, trecv, msend, mrecv, csend, crecv):
    chip, core = place()
    sib = 1 - core
    half = (p_ref.shape[0] if inner else p_ref.shape[1]) // 2
    block = (lambda slot: p_ref.at[:, slot]) if inner else (lambda slot: p_ref.at[slot])
    steps = (1, 2) if chips == 4 else tuple(range(1, chips))
    peers = [(flip(chip, s, chips), core) for s in steps]
    greet(peers + [(chip, sib)])
    order = (3, 1, 2, 0) if chips == 4 else tuple(range(1, chips)) + (0,)
    loads, twins = {}, {}
    for s in order:
        to = flip(chip, s, chips) * 2
        twins[s] = remote(block(to + sib), twin.at[s], tsend.at[s], trecv.at[s], chip, sib)
        twins[s].start()
        loads[s] = pltpu.make_async_copy(block(to + core), mine.at[s], lsem.at[s])
        loads[s].start()

    def part(s, h):
        at = pl.ds(h * half, half)
        return mine[s, at].astype(F32) + twin[s, at].astype(F32)

    def ready(s):
        loads[s].wait()
        twins[s].wait_recv()

    sent = []
    if chips == 4:
        corners = []
        ready(3)
        for h, s in ((0, 1), (1, 2)):
            moved[3, pl.ds(h * half, half)] = part(3, h).astype(BF16)
            copy = remote(moved.at[3, pl.ds(h * half, half)], corner.at[h], csend.at[h], crecv.at[h], flip(chip, s, 4), core)
            copy.start()
            corners.append(copy)

        def send(s, h):
            at = pl.ds(h * half, half)
            copy = remote(moved.at[s, at], landed.at[s - 1, at], msend.at[s - 1, h], mrecv.at[s - 1, h], flip(chip, s, 4), core)
            copy.start()
            sent.append(copy)

        for s, h in ((1, 0), (2, 1)):
            ready(s)
            moved[s, pl.ds(h * half, half)] = part(s, h).astype(BF16)
            send(s, h)
        for s, h in ((2, 0), (1, 1)):
            corners[h].wait_recv()
            moved[s, pl.ds(h * half, half)] = (part(s, h) + corner[h].astype(F32)).astype(BF16)
            send(s, h)
        for copy in corners:
            copy.wait_send()
    else:
        for s in steps:
            ready(s)
            for h in range(2):
                at = pl.ds(h * half, half)
                moved[s, at] = part(s, h).astype(BF16)
                copy = remote(moved.at[s, at], landed.at[s - 1, at], msend.at[s - 1, h], mrecv.at[s - 1, h], flip(chip, s, chips), core)
                copy.start()
                sent.append(copy)
    ready(0)
    for h in range(2):
        total[pl.ds(h * half, half)] = part(0, h)
    for copy in sent:
        copy.wait()
    for s in steps[:-1]:
        total[...] += landed[s - 1].astype(F32)
    o_ref[...] = (total[...] + landed[steps[-1] - 1].astype(F32)).astype(o_ref.dtype)
    for s in order:
        twins[s].wait_send()


def plane_reduce(p, chips, call_id, dtype=F32, inner=False):
    block = (p.shape[0],) + p.shape[2:] if inner else p.shape[1:]
    steps = 2 if chips == 4 else chips - 1
    return pl.pallas_call(
        functools.partial(reduce_kernel, chips, inner),
        out_shape=jax.ShapeDtypeStruct(block, dtype),
        in_specs=[ANY],
        out_specs=VMEM,
        scratch_shapes=[
            pltpu.VMEM(block, F32),
            pltpu.VMEM((chips,) + block, BF16),
            pltpu.VMEM((chips,) + block, BF16),
            pltpu.VMEM((chips,) + block, BF16),
            pltpu.VMEM((2, block[0] // 2) + block[1:], BF16),
            pltpu.VMEM((steps,) + block, BF16),
            pltpu.SemaphoreType.DMA((chips,)),
            pltpu.SemaphoreType.DMA((chips,)),
            pltpu.SemaphoreType.DMA((chips,)),
            pltpu.SemaphoreType.DMA((steps, 2)),
            pltpu.SemaphoreType.DMA((steps, 2)),
            pltpu.SemaphoreType.DMA((2,)),
            pltpu.SemaphoreType.DMA((2,)),
        ],
        cost_estimate=BRIEF,
        compiler_params=pltpu.CompilerParams(
            collective_id=call_id, has_side_effects=True, vmem_limit_bytes=56 << 20
        ),
    )(p)


def swap_chips(values, step):
    return lax.ppermute(values, "chip", [(c, c ^ step) for c in range(4)])


class Drift:
    def __init__(self, pairs, axis):
        self.axis = axis
        self.chip, self.core = place()
        away = lax.dynamic_index_in_dim(pairs, 1 - self.core, axis + 1, keepdims=False)
        self.mine = lax.dynamic_index_in_dim(pairs, self.core, axis + 1, keepdims=False)
        self.twin = lax.ppermute(away, "core", [(0, 1), (1, 0)])

    def part(self, step):
        at = jnp.bitwise_xor(self.chip, step)
        mine = lax.dynamic_index_in_dim(self.mine, at, self.axis, keepdims=False)
        twin = lax.dynamic_index_in_dim(self.twin, at, self.axis, keepdims=False)
        return mine.astype(F32) + twin.astype(F32)

    def parts(self):
        return tuple(self.part(step).astype(BF16) for step in (1, 2, 3))

    @staticmethod
    def send(parts):
        return tuple(
            swap_chips(part, step)
            for step, part in zip((3, 1, 2), (parts[2], parts[0], parts[1]))
        )

    def finish(self, came):
        total = self.part(0)
        for part in came:
            total = total + part.astype(F32)
        return total


def exchange_kernel(chips, cut, paste, x_ref, o_ref, send, recv, local):
    chip, core = place()
    me = chip * 2 + core
    peers = [(flip(chip, s, chips), c) for s in range(1, chips) for c in (core, 1 - core)]
    peers = peers + [(chip, 1 - core)]
    greet(peers)
    far = [p for p in ([3, 1, 2] if chips == 4 else range(1, chips))]
    order = [(flip(chip, s, chips), c) for s in far for c in (core, 1 - core)] + [(chip, 1 - core)]
    copies = []
    for i, (to, c) in enumerate(order):
        copy = remote(cut(x_ref, to * 2 + c), paste(o_ref, me), send.at[i], recv.at[me], to, c)
        copy.start()
        copies.append(copy)
    mine = pltpu.make_async_copy(cut(x_ref, me), paste(o_ref, me), local)
    mine.start()
    for s in far:
        for c in (core, 1 - core):
            slot = unflip(chip, s, chips) * 2 + c
            remote(cut(x_ref, me), paste(o_ref, slot), send.at[0], recv.at[slot], chip, 1 - core).wait_recv()
    slot = chip * 2 + 1 - core
    remote(cut(x_ref, me), paste(o_ref, slot), send.at[0], recv.at[slot], chip, 1 - core).wait_recv()
    for copy in copies:
        copy.wait_send()
    mine.wait()


def plane_exchange(x, shape, cut, paste, chips, call_id):
    return pl.pallas_call(
        functools.partial(exchange_kernel, chips, cut, paste),
        out_shape=jax.ShapeDtypeStruct(shape, x.dtype),
        in_specs=[ANY],
        out_specs=ANY,
        scratch_shapes=[
            pltpu.SemaphoreType.DMA((2 * chips,)),
            pltpu.SemaphoreType.DMA((2 * chips,)),
            pltpu.SemaphoreType.DMA,
        ],
        cost_estimate=BRIEF,
        compiler_params=pltpu.CompilerParams(collective_id=call_id, has_side_effects=True),
    )(x)


def by_slot(ref, dev):
    return ref.at[dev]


def by_rows(rows):
    return lambda ref, dev: ref.at[pl.ds(pl.multiple_of(dev * rows, rows), rows)]


def by_cols(cols):
    return lambda ref, dev: ref.at[:, pl.ds(pl.multiple_of(dev * cols, cols), cols)]


def matmul(left, right):
    return jnp.dot(left, right, preferred_element_type=F32)


def over_rows(left, right):
    return lax.dot_general(left, right, (((0,), (0,)), ((), ())), preferred_element_type=F32)


def over_cols(left, right):
    return lax.dot_general(left, right, (((1,), (1,)), ((), ())), preferred_element_type=F32)


def gather(values, axes, axis=0):
    return lax.all_gather(values, axes, axis=axis, tiled=True)


def scatter(values, axes, axis=0):
    return lax.psum_scatter(values, axes, scatter_dimension=axis, tiled=True)


def dot_nt(left, right):
    return lax.dot_general(left, right, (((1,), (1,)), ((), ())), preferred_element_type=F32)


def head_stack(values, heads):
    col_head = lax.broadcasted_iota(jnp.int32, values.shape, 1) // HEAD_DIM
    return jnp.concatenate(
        [jnp.where(col_head == h, values, jnp.zeros_like(values)) for h in range(heads)], axis=0
    )


def head_pick(stacked, heads):
    rows = stacked.shape[0] // heads
    col_head = lax.broadcasted_iota(jnp.int32, (rows, stacked.shape[1]), 1) // HEAD_DIM
    total = jnp.zeros((rows, stacked.shape[1]), F32)
    for h in range(heads):
        total = jnp.where(col_head == h, stacked[h * rows : (h + 1) * rows], total)
    return total


def head_fold(values, heads):
    total = values[:, :HEAD_DIM]
    for h in range(1, heads):
        total = total + values[:, h * HEAD_DIM : (h + 1) * HEAD_DIM]
    return total


def repeat_heads(values, heads):
    return jnp.concatenate([values] * heads, axis=1)


def own_rows(order_ref, slot):
    return pl.ds(pl.multiple_of(order_ref[slot] * BLOCK, BLOCK), BLOCK)


def load_prompt(heads, order_ref, qkv_ref, k_ref, v_ref, first):
    q_cols = heads * HEAD_DIM
    for s in range(PROMPT_BLOCKS):
        pair = qkv_ref[own_rows(order_ref, first + s), q_cols:]
        at = pl.ds(s * BLOCK, BLOCK)
        k_ref[at] = repeat_heads(pair[:, :HEAD_DIM], heads)
        v_ref[at] = repeat_heads(pair[:, HEAD_DIM:], heads)


def soft_parts(heads, slot, q_stack, k_far, k_own):
    far = dot_nt(k_far, q_stack)
    own = dot_nt(k_own, q_stack)
    limit = jnp.minimum(slot, PROMPT_BLOCKS) * BLOCK
    far = jnp.where(lax.broadcasted_iota(jnp.int32, far.shape, 0) < limit, far, MASKED)
    key = lax.broadcasted_iota(jnp.int32, own.shape, 0)
    row = lax.broadcasted_iota(jnp.int32, own.shape, 1) % BLOCK
    own = jnp.where(key <= row, own, MASKED)
    peak = jnp.maximum(jnp.max(far, axis=0, keepdims=True), jnp.max(own, axis=0, keepdims=True))
    far, own = jnp.exp(far - peak), jnp.exp(own - peak)
    scale = 1.0 / (jnp.sum(far, axis=0, keepdims=True) + jnp.sum(own, axis=0, keepdims=True))
    return far * scale, own * scale


def scaled_stack(q, heads):
    return head_stack((q.astype(F32) * ATTN_MULT).astype(BF16), heads)


def attend_kernel(heads, order_ref, qkv_ref, o_ref, k_ref, v_ref, vt_ref):
    first, slot = pl.program_id(0) * GROUP_BLOCKS, pl.program_id(1)
    q_cols = heads * HEAD_DIM

    @pl.when(slot == 0)
    def _():
        load_prompt(heads, order_ref, qkv_ref, k_ref, v_ref, first)
        vt_ref[...] = v_ref[...].astype(F32).T.astype(BF16)

    rows = own_rows(order_ref, first + slot)
    mine = qkv_ref[rows, :]
    k_own = repeat_heads(mine[:, q_cols : q_cols + HEAD_DIM], heads)
    v_own = repeat_heads(mine[:, q_cols + HEAD_DIM :], heads)
    far, own = soft_parts(heads, slot, scaled_stack(mine[:, :q_cols], heads), k_ref[...], k_own)
    mixed = matmul(vt_ref[...], far.astype(BF16))
    mixed += matmul(v_own.astype(F32).T.astype(BF16), own.astype(BF16))
    o_ref[rows, :] = head_pick(mixed.T, heads).astype(BF16)


def attend_back_kernel(
    heads, order_ref, qkv_ref, d_ref, o_ref, k_ref, v_ref, kt_ref, dk_ref, dv_ref
):
    first, slot = pl.program_id(0) * GROUP_BLOCKS, pl.program_id(1)
    q_cols = heads * HEAD_DIM

    @pl.when(slot == 0)
    def _():
        load_prompt(heads, order_ref, qkv_ref, k_ref, v_ref, first)
        kt_ref[...] = k_ref[...].astype(F32).T.astype(BF16)
        dk_ref[...] = jnp.zeros_like(dk_ref)
        dv_ref[...] = jnp.zeros_like(dv_ref)

    rows = own_rows(order_ref, first + slot)
    mine = qkv_ref[rows, :]
    k_own = repeat_heads(mine[:, q_cols : q_cols + HEAD_DIM], heads)
    v_own = repeat_heads(mine[:, q_cols + HEAD_DIM :], heads)
    q_stack = scaled_stack(mine[:, :q_cols], heads)
    d_stack = head_stack(d_ref[rows, :], heads)
    far, own = soft_parts(heads, slot, q_stack, k_ref[...], k_own)
    d_far, d_own = dot_nt(v_ref[...], d_stack), dot_nt(v_own, d_stack)
    mean = jnp.sum(far * d_far, axis=0, keepdims=True) + jnp.sum(own * d_own, axis=0, keepdims=True)
    d_far = (far * (d_far - mean)).astype(BF16)
    d_own = (own * (d_own - mean)).astype(BF16)
    dv_ref[...] += matmul(far.astype(BF16), d_stack)
    dk_ref[...] += matmul(d_far, q_stack)
    dv_own = matmul(own.astype(BF16), d_stack)
    dk_own = matmul(d_own, q_stack)
    d_q = matmul(kt_ref[...], d_far) + matmul(k_own.astype(F32).T.astype(BF16), d_own)
    o_ref[rows, :q_cols] = (head_pick(d_q.T, heads) * ATTN_MULT).astype(BF16)

    def fold(d_k, d_v):
        return jnp.concatenate([head_fold(d_k, heads), head_fold(d_v, heads)], axis=1).astype(BF16)

    @pl.when(slot < PROMPT_BLOCKS)
    def _():
        at = pl.ds(pl.multiple_of(slot * BLOCK, BLOCK), BLOCK)
        dk_ref[at] += dk_own
        dv_ref[at] += dv_own

    @pl.when(slot >= PROMPT_BLOCKS)
    def _():
        o_ref[rows, q_cols:] = fold(dk_own, dv_own)

    @pl.when(slot == GROUP_BLOCKS - 1)
    def _():
        for s in range(PROMPT_BLOCKS):
            at = pl.ds(s * BLOCK, BLOCK)
            o_ref[own_rows(order_ref, first + s), q_cols:] = fold(dk_ref[at], dv_ref[at])


def whole(shape):
    return pl.BlockSpec(shape, lambda g, s, order: (0,) * len(shape))


def attend(qkv, order, heads):
    tokens, cols = qkv.shape
    prompt, q_cols = PROMPT_BLOCKS * BLOCK, heads * HEAD_DIM
    return pl.pallas_call(
        functools.partial(attend_kernel, heads),
        out_shape=jax.ShapeDtypeStruct((tokens, q_cols), BF16),
        grid_spec=pltpu.PrefetchScalarGridSpec(
            num_scalar_prefetch=1,
            grid=(tokens // (GROUP_BLOCKS * BLOCK), GROUP_BLOCKS),
            in_specs=[whole((tokens, cols))],
            out_specs=whole((tokens, q_cols)),
            scratch_shapes=[
                pltpu.VMEM((prompt, q_cols), BF16),
                pltpu.VMEM((prompt, q_cols), BF16),
                pltpu.VMEM((q_cols, prompt), BF16),
            ],
        ),
        cost_estimate=BRIEF,
        compiler_params=pltpu.CompilerParams(vmem_limit_bytes=40 << 20),
    )(order, qkv)


def attend_back(qkv, d_attended, order, heads):
    tokens, cols = qkv.shape
    prompt, q_cols = PROMPT_BLOCKS * BLOCK, heads * HEAD_DIM
    return pl.pallas_call(
        functools.partial(attend_back_kernel, heads),
        out_shape=jax.ShapeDtypeStruct((tokens, cols), BF16),
        grid_spec=pltpu.PrefetchScalarGridSpec(
            num_scalar_prefetch=1,
            grid=(tokens // (GROUP_BLOCKS * BLOCK), GROUP_BLOCKS),
            in_specs=[whole((tokens, cols)), whole((tokens, q_cols))],
            out_specs=whole((tokens, cols)),
            scratch_shapes=[
                pltpu.VMEM((prompt, q_cols), BF16),
                pltpu.VMEM((prompt, q_cols), BF16),
                pltpu.VMEM((q_cols, prompt), BF16),
                pltpu.VMEM((prompt, q_cols), F32),
                pltpu.VMEM((prompt, q_cols), F32),
            ],
        ),
        cost_estimate=BRIEF,
        compiler_params=pltpu.CompilerParams(vmem_limit_bytes=40 << 20),
    )(order, qkv, d_attended)


def total_kernel(grps, chips, x_ref, o_ref, over_z, over_plane, send, recv, psend, precv):
    grp = lax.axis_index("grp")
    chip, core = place()
    me = chip * 2 + core
    far = [lax.rem(grp + s, grps) for s in range(1, grps)]
    near = [(flip(chip, s, chips), c) for s in range(1, chips) for c in (core, 1 - core)]
    near = near + [(chip, 1 - core)]
    barrier = pltpu.get_barrier_semaphore()
    for g in far:
        pl.semaphore_signal(barrier, inc=1, device_id={"grp": g}, device_id_type=MESH)
    for to, c in near:
        pl.semaphore_signal(
            barrier, inc=1, device_id={"chip": to, "core": c}, device_id_type=MESH
        )
    pl.semaphore_wait(barrier, len(far) + len(near))
    copies = []
    for i, g in enumerate(far):
        copy = pltpu.make_async_remote_copy(
            src_ref=x_ref,
            dst_ref=over_z.at[grp],
            send_sem=send.at[i],
            recv_sem=recv.at[grp],
            device_id={"grp": g},
            device_id_type=MESH,
        )
        copy.start()
        copies.append(copy)
    over_z[grp] = x_ref[...]
    for g in far:
        pltpu.make_async_remote_copy(
            src_ref=x_ref,
            dst_ref=over_z.at[g],
            send_sem=send.at[0],
            recv_sem=recv.at[g],
            device_id={"grp": g},
            device_id_type=MESH,
        ).wait_recv()
    over_plane[me] = jnp.sum(over_z[...], axis=0)
    for i, (to, c) in enumerate(near):
        copy = remote(over_plane.at[me], over_plane.at[me], psend.at[i], precv.at[me], to, c)
        copy.start()
        copies.append(copy)
    for to, c in near:
        slot = to * 2 + c
        remote(over_plane.at[me], over_plane.at[slot], psend.at[0], precv.at[slot], to, c).wait_recv()
    for copy in copies:
        copy.wait_send()
    o_ref[...] = jnp.sum(over_plane[...], axis=0)


def total(x, grps, chips, call_id):
    devs = 2 * chips
    return pl.pallas_call(
        functools.partial(total_kernel, grps, chips),
        out_shape=jax.ShapeDtypeStruct(x.shape, F32),
        in_specs=[VMEM],
        out_specs=VMEM,
        scratch_shapes=[
            pltpu.VMEM((grps,) + x.shape, F32),
            pltpu.VMEM((devs,) + x.shape, F32),
            pltpu.SemaphoreType.DMA((grps,)),
            pltpu.SemaphoreType.DMA((grps,)),
            pltpu.SemaphoreType.DMA((devs,)),
            pltpu.SemaphoreType.DMA((devs,)),
        ],
        cost_estimate=BRIEF,
        compiler_params=pltpu.CompilerParams(collective_id=call_id, has_side_effects=True),
    )(x)


def params(axes, mib=56):
    return pltpu.CompilerParams(
        dimension_semantics=("arbitrary",) * axes, vmem_limit_bytes=mib << 20
    )


def tile_rows(count, limit):
    while count % limit:
        limit //= 2
    return limit


def widen_kernel(n_ref, w_ref, h_ref, ht_ref, s_ref, t_ref, nt_ref):
    values = n_ref[...]
    gate, up = matmul(values, w_ref[0, 0]), matmul(values, w_ref[0, 1])
    sig = 1.0 / (1.0 + jnp.exp(-gate))
    silu = gate * sig
    hidden = (silu * up).astype(BF16)
    h_ref[0] = hidden
    ht_ref[0] = hidden.T
    s_ref[0] = silu.astype(BF16)
    t_ref[0] = (up * (sig * (1.0 + gate * (1.0 - sig)))).astype(BF16)

    @pl.when(pl.program_id(1) == 0)
    def _():
        nt_ref[...] = values.T


def widen(normed, weights):
    tokens, depth = normed.shape
    shards, _, _, width = weights.shape
    rows = tile_rows(tokens, 1024)
    tall = jax.ShapeDtypeStruct((shards, tokens, width), BF16)
    tall_spec = pl.BlockSpec((1, rows, width), lambda r, s: (s, r, 0))
    return pl.pallas_call(
        widen_kernel,
        out_shape=(
            tall,
            jax.ShapeDtypeStruct((shards, width, tokens), BF16),
            tall,
            tall,
            jax.ShapeDtypeStruct((depth, tokens), BF16),
        ),
        grid=(tokens // rows, shards),
        in_specs=[
            pl.BlockSpec((rows, depth), lambda r, s: (r, 0)),
            pl.BlockSpec((1, 2, depth, width), lambda r, s: (s, 0, 0, 0)),
        ],
        out_specs=(
            tall_spec,
            pl.BlockSpec((1, width, rows), lambda r, s: (s, 0, r)),
            tall_spec,
            tall_spec,
            pl.BlockSpec((depth, rows), lambda r, s: (0, r)),
        ),
        cost_estimate=BRIEF,
        compiler_params=params(2),
    )(normed, weights)


def down_part_kernel(ht_ref, d_ref, o_ref):
    o_ref[0] = matmul(ht_ref[0], d_ref[...]).astype(BF16)


def down_part(hidden_t, upstream):
    shards, width, tokens = hidden_t.shape
    depth = upstream.shape[1]
    cols = tile_rows(depth, 1024)
    return pl.pallas_call(
        down_part_kernel,
        out_shape=jax.ShapeDtypeStruct((shards, width, depth), BF16),
        grid=(depth // cols, shards),
        in_specs=[
            pl.BlockSpec((1, width, tokens), lambda c, s: (s, 0, 0)),
            pl.BlockSpec((tokens, cols), lambda c, s: (0, c)),
        ],
        out_specs=pl.BlockSpec((1, width, cols), lambda c, s: (s, 0, c)),
        cost_estimate=BRIEF,
        compiler_params=params(2),
    )(hidden_t, upstream)


def mix_kernel(h_ref, w_ref, m_ref):
    mixed = None
    for i in range(w_ref.shape[0]):
        part = matmul(h_ref[i], w_ref[i])
        mixed = part if mixed is None else mixed + part
    m_ref[...] = mixed.astype(BF16)


def narrow_specs(hidden, weights):
    shards, tokens, width = hidden.shape
    depth = weights.shape[2]
    rows = tile_rows(tokens, 512)
    return (
        tokens // rows,
        pl.BlockSpec((shards, rows, width), lambda r: (0, r, 0)),
        pl.BlockSpec((rows, depth), lambda r: (r, 0)),
        pl.BlockSpec(weights.shape, lambda r: (0, 0, 0), pipeline_mode=pl.Buffered(1)),
    )


def mix(hidden, weights):
    steps, tall_spec, flat_spec, weight_spec = narrow_specs(hidden, weights)
    return pl.pallas_call(
        mix_kernel,
        out_shape=jax.ShapeDtypeStruct((hidden.shape[1], weights.shape[2]), BF16),
        grid=(steps,),
        in_specs=[tall_spec, weight_spec],
        out_specs=flat_spec,
        cost_estimate=BRIEF,
        compiler_params=params(1),
    )(hidden, weights)


def narrow_back_kernel(s_ref, t_ref, d_ref, w_ref, dg_ref, du_ref):
    upstream = d_ref[...]
    for i in range(w_ref.shape[0]):
        d_hidden = dot_nt(upstream, w_ref[i])
        dg_ref[i] = (d_hidden * t_ref[i].astype(F32)).astype(BF16)
        du_ref[i] = (d_hidden * s_ref[i].astype(F32)).astype(BF16)


def narrow_back(silu, slope, upstream, weights):
    steps, tall_spec, flat_spec, weight_spec = narrow_specs(silu, weights)
    tall = jax.ShapeDtypeStruct(silu.shape, BF16)
    return pl.pallas_call(
        narrow_back_kernel,
        out_shape=(tall, tall),
        grid=(steps,),
        in_specs=[tall_spec, tall_spec, flat_spec, weight_spec],
        out_specs=(tall_spec, tall_spec),
        cost_estimate=BRIEF,
        compiler_params=params(1),
    )(silu, slope, upstream, weights)


def widen_part_kernel(nt_ref, dg_ref, du_ref, o_ref):
    values = nt_ref[...]
    o_ref[0, 0] = matmul(values, dg_ref[0]).astype(BF16)
    o_ref[0, 1] = matmul(values, du_ref[0]).astype(BF16)


def widen_part(normed_t, d_gate, d_up):
    depth, tokens = normed_t.shape
    shards, _, width = d_gate.shape
    rows = tile_rows(depth, 1024)
    tall_spec = pl.BlockSpec((1, tokens, width), lambda r, s: (s, 0, 0))
    return pl.pallas_call(
        widen_part_kernel,
        out_shape=jax.ShapeDtypeStruct((shards, 2, depth, width), BF16),
        grid=(depth // rows, shards),
        in_specs=[pl.BlockSpec((rows, tokens), lambda r, s: (r, 0)), tall_spec, tall_spec],
        out_specs=pl.BlockSpec((1, 2, rows, width), lambda r, s: (s, 0, r, 0)),
        cost_estimate=BRIEF,
        compiler_params=params(2),
    )(normed_t, d_gate, d_up)


def widen_back_kernel(dg_ref, du_ref, w_ref, o_ref):
    total = None
    for i in range(w_ref.shape[0]):
        part = dot_nt(dg_ref[i], w_ref[i, 0]) + dot_nt(du_ref[i], w_ref[i, 1])
        total = part if total is None else total + part
    o_ref[...] = total.astype(BF16)


def widen_back(d_gate, d_up, weights):
    shards, tokens, width = d_gate.shape
    depth = weights.shape[2]
    rows = tile_rows(tokens, 512)
    tall_spec = pl.BlockSpec((shards, rows, width), lambda r: (0, r, 0))
    return pl.pallas_call(
        widen_back_kernel,
        out_shape=jax.ShapeDtypeStruct((tokens, depth), BF16),
        grid=(tokens // rows,),
        in_specs=[
            tall_spec,
            tall_spec,
            pl.BlockSpec(weights.shape, lambda r: (0, 0, 0, 0), pipeline_mode=pl.Buffered(1)),
        ],
        out_specs=pl.BlockSpec((rows, depth), lambda r: (r, 0)),
        cost_estimate=BRIEF,
        compiler_params=params(1),
    )(d_gate, d_up, weights)


def stage_step(stage):
    return jnp.where(stage == 0, 3, jnp.where(stage == 3, 0, stage))


class Square:
    def __init__(self, acc, mine, away, twin, moved, corner, landed, tsend, trecv, msend, mrecv, csend, crecv):
        self.acc, self.mine, self.away, self.twin = acc, mine, away, twin
        self.moved, self.corner, self.landed = moved, corner, landed
        self.tsend, self.trecv, self.msend, self.mrecv = tsend, trecv, msend, mrecv
        self.csend, self.crecv = csend, crecv
        self.chip, self.core = place()
        self.rows = mine.shape[1]
        self.half = self.rows // 2

    def greet(self):
        peers = [(flip(self.chip, s, 4), self.core) for s in (1, 2)]
        greet(peers + [(self.chip, 1 - self.core)])

    def twin_copy(self, stage):
        return remote(
            self.away.at[stage], self.twin.at[stage], self.tsend.at[stage], self.trecv.at[stage],
            self.chip, 1 - self.core,
        )

    def offer(self, stage):
        own, other = self.core * self.rows, (1 - self.core) * self.rows
        self.mine[stage] = self.acc[pl.ds(pl.multiple_of(own, self.rows), self.rows)].astype(BF16)
        self.away[stage] = self.acc[pl.ds(pl.multiple_of(other, self.rows), self.rows)].astype(BF16)
        self.twin_copy(stage).start()

    def at(self, h):
        return pl.ds(h * self.half, self.half)

    def both(self, stage, h):
        return self.mine[stage, self.at(h)].astype(F32) + self.twin[stage, self.at(h)].astype(F32)

    def corner_copy(self, h):
        return remote(
            self.moved.at[0, self.at(h)], self.corner.at[h], self.csend.at[h], self.crecv.at[h],
            flip(self.chip, h + 1, 4), self.core,
        )

    def copy(self, stage, h):
        return remote(
            self.moved.at[stage, self.at(h)], self.landed.at[stage - 1, self.at(h)],
            self.msend.at[stage - 1, h], self.mrecv.at[stage - 1, h],
            flip(self.chip, stage, 4), self.core,
        )

    def corners(self):
        self.twin_copy(0).wait_recv()
        for h in range(2):
            self.moved[0, self.at(h)] = self.both(0, h).astype(BF16)
            self.corner_copy(h).start()

    def plain(self, stage):
        self.twin_copy(stage).wait_recv()
        h = stage - 1
        self.moved[stage, self.at(h)] = self.both(stage, h).astype(BF16)
        self.copy(stage, h).start()

    def joined(self, stage):
        h = 2 - stage
        self.corner_copy(h).wait_recv()
        total = self.both(stage, h) + self.corner[h].astype(F32)
        self.moved[stage, self.at(h)] = total.astype(BF16)
        self.copy(stage, h).start()

    def finish(self, o_ref):
        self.twin_copy(3).wait_recv()
        for h in range(2):
            o_ref[self.at(h)] = self.both(3, h)
        for stage, h in ((1, 0), (2, 1), (2, 0), (1, 1)):
            self.copy(stage, h).wait_recv()
            o_ref[self.at(h)] += self.landed[stage - 1, self.at(h)].astype(F32)
        for stage in (1, 2):
            for h in range(2):
                self.copy(stage, h).wait_send()
        for h in range(2):
            self.corner_copy(h).wait_send()
        for stage in range(4):
            self.twin_copy(stage).wait_send()


def square_kernel(compute, count, *refs):
    operands, o_ref, scratch = refs[:count], refs[count], refs[count + 1 :]
    run = Square(*scratch)
    stage = pl.program_id(0)

    @pl.when(stage == 0)
    def _():
        run.greet()

    target = jnp.bitwise_xor(run.chip, stage_step(stage))
    width = 2 * run.rows
    run.acc[...] = compute(operands, pl.ds(pl.multiple_of(target * width, width), width))
    run.offer(stage)

    @pl.when(stage == 1)
    def _():
        run.corners()

    @pl.when(stage == 2)
    def _():
        run.plain(1)

    @pl.when(stage == 3)
    def _():
        run.plain(2)
        run.joined(2)
        run.joined(1)
        run.finish(o_ref)


def square_reduce(compute, operands, rows, call_id):
    block = (rows, D)

    def held(shape):
        return pl.BlockSpec(shape, lambda s: (0,) * len(shape), pipeline_mode=pl.Buffered(1))

    return pl.pallas_call(
        functools.partial(square_kernel, compute, len(operands)),
        out_shape=jax.ShapeDtypeStruct(block, F32),
        grid=(4,),
        in_specs=[held(x.shape) for x in operands],
        out_specs=held(block),
        scratch_shapes=[
            pltpu.VMEM((2 * rows, D), F32),
            pltpu.VMEM((4,) + block, BF16),
            pltpu.VMEM((4,) + block, BF16),
            pltpu.VMEM((4,) + block, BF16),
            pltpu.VMEM((3,) + block, BF16),
            pltpu.VMEM((2, rows // 2, D), BF16),
            pltpu.VMEM((2,) + block, BF16),
            pltpu.SemaphoreType.DMA((4,)),
            pltpu.SemaphoreType.DMA((4,)),
            pltpu.SemaphoreType.DMA((2, 2)),
            pltpu.SemaphoreType.DMA((2, 2)),
            pltpu.SemaphoreType.DMA((2,)),
            pltpu.SemaphoreType.DMA((2,)),
        ],
        cost_estimate=BRIEF,
        compiler_params=pltpu.CompilerParams(
            collective_id=call_id, has_side_effects=True, vmem_limit_bytes=60 << 20
        ),
    )(*operands)


def widen_back_rows(refs, rows):
    dg_ref, du_ref, w_ref = refs
    total = None
    for i in range(w_ref.shape[0]):
        part = dot_nt(dg_ref[i, rows], w_ref[i, 0]) + dot_nt(du_ref[i, rows], w_ref[i, 1])
        total = part if total is None else total + part
    return total


def project_back_rows(refs, rows):
    d_ref, w_ref = refs
    return dot_nt(d_ref[rows], w_ref[...])


def twin_kernel(h_ref, w_ref, o_ref, corner_ref, x_ref, y_ref, acc, mine, away, twin, tsend, trecv):
    chip, core = place()
    stage = pl.program_id(0)
    rows = o_ref.shape[0]

    def copy(s):
        return remote(away.at[s], twin.at[s], tsend.at[s], trecv.at[s], chip, 1 - core)

    def both(s):
        copy(s).wait_recv()
        return mine[s].astype(F32) + twin[s].astype(F32)

    @pl.when(stage == 0)
    def _():
        greet([(chip, 1 - core)])

    target = jnp.bitwise_xor(chip, stage_step(stage)) * 2 * rows
    total = None
    for i in range(w_ref.shape[0]):
        part = matmul(h_ref[i, pl.ds(pl.multiple_of(target, 2 * rows), 2 * rows)], w_ref[i])
        total = part if total is None else total + part
    acc[...] = total
    mine[stage] = acc[pl.ds(pl.multiple_of(core * rows, rows), rows)].astype(BF16)
    away[stage] = acc[pl.ds(pl.multiple_of((1 - core) * rows, rows), rows)].astype(BF16)
    copy(stage).start()

    for s, part_ref in enumerate((corner_ref, x_ref, y_ref)):

        @pl.when(stage == s + 1)
        def _(s=s, part_ref=part_ref):
            part_ref[...] = both(s).astype(BF16)

    @pl.when(stage == 3)
    def _():
        o_ref[...] = both(3)
        for s in range(4):
            copy(s).wait_send()


def mix_twin(hidden, weights, rows, call_id):
    block = (rows, D)

    def held(shape):
        return pl.BlockSpec(shape, lambda s: (0,) * len(shape), pipeline_mode=pl.Buffered(1))

    return pl.pallas_call(
        twin_kernel,
        out_shape=(jax.ShapeDtypeStruct(block, F32),) + (jax.ShapeDtypeStruct(block, BF16),) * 3,
        grid=(4,),
        in_specs=[held(hidden.shape), held(weights.shape)],
        out_specs=(held(block),) * 4,
        scratch_shapes=[
            pltpu.VMEM((2 * rows, D), F32),
            pltpu.VMEM((4,) + block, BF16),
            pltpu.VMEM((4,) + block, BF16),
            pltpu.VMEM((4,) + block, BF16),
            pltpu.SemaphoreType.DMA((4,)),
            pltpu.SemaphoreType.DMA((4,)),
        ],
        cost_estimate=BRIEF,
        compiler_params=pltpu.CompilerParams(
            collective_id=call_id, has_side_effects=True, vmem_limit_bytes=60 << 20
        ),
    )(hidden, weights)


def norm_parts(values):
    factor = lax.rsqrt(jnp.mean(values * values, axis=-1, keepdims=True) + EPSILON)
    return factor


def norm_back(values, factor, gain, grad):
    scaled = gain * grad
    inner = jnp.mean(values * scaled, axis=-1, keepdims=True)
    return factor * scaled - values * (factor * factor * factor * inner), jnp.sum(
        grad * values * factor, axis=0
    )


def on_device(
    tokens,
    block_group,
    block_slot,
    attn_gain,
    w_query,
    w_key,
    w_value,
    w_out,
    mlp_gain,
    w_gate,
    w_up,
    w_down,
    cotangent,
):
    grps = lax.axis_size("grp")
    devs = lax.axis_size(PLANE)
    chips = devs // 2
    rows = tokens.shape[0]
    w_rows = w_query.shape[0]
    q_heads = HEADS // devs
    kv_heads = 1
    assert devs % KV_HEADS == 0
    kv_copies = max(1, devs // KV_HEADS)
    q_cols, kv_cols = q_heads * HEAD_DIM, kv_heads * HEAD_DIM
    row_blocks = rows // BLOCK * devs
    row_groups = row_blocks // GROUP_BLOCKS

    row_first = lax.axis_index("grp") * row_blocks
    keys = lax.dynamic_slice_in_dim(block_group, row_first, row_blocks) * GROUP_BLOCKS
    keys = keys + lax.dynamic_slice_in_dim(block_slot, row_first, row_blocks)
    rank = jnp.sum((keys[None, :] < keys[:, None]).astype(jnp.int32), axis=1)
    ids = jnp.arange(row_blocks, dtype=jnp.int32)
    order = jnp.sum(jnp.where(rank[None, :] == ids[:, None], ids[None, :], 0), axis=1)

    def kv_split(w):
        w = w.reshape(w_rows, devs // kv_copies, kv_cols)
        return jnp.repeat(w, kv_copies, axis=1) if kv_copies > 1 else w

    gains = jnp.stack([attn_gain, mlp_gain], axis=1)
    cols = D // 4
    room = cols - q_cols - 2 * kv_cols
    gains = jnp.pad(gains, ((0, 0), (0, room - 2)))
    gains = jnp.broadcast_to(gains[:, None, :], (w_rows, devs, room))
    packed = jnp.concatenate(
        [w_query.reshape(w_rows, devs, q_cols), kv_split(w_key), kv_split(w_value), gains], axis=2
    )
    packed = jnp.swapaxes(packed, 0, 1)
    packed = plane_exchange(packed, packed.shape, by_slot, by_slot, chips, 1)
    packed = jnp.concatenate([packed.reshape(devs * w_rows, cols), w_out.reshape(-1, cols)])
    packed = gather(packed[None], "grp")
    out_full = packed[:, devs * w_rows :].reshape(grps, w_rows, D)
    packed = packed[:, : devs * w_rows].reshape(D, cols)
    w_qkv = packed[:, : q_cols + 2 * kv_cols]
    gain_one = packed[:, q_cols + 2 * kv_cols].astype(F32)
    gain_two = packed[:, q_cols + 2 * kv_cols + 1].astype(F32)

    all_tokens = plane_gather(tokens, chips, 2).reshape(devs * rows, D)
    layer_all = all_tokens.astype(F32)
    normed_one = (layer_all * norm_parts(layer_all) * gain_one).astype(BF16)
    qkv = matmul(normed_one, w_qkv).astype(BF16)
    attended = attend(qkv, order, q_heads)
    attended = plane_exchange(
        attended, (rows, D), by_rows(rows), by_cols(q_cols), chips, 3
    )

    out_full = plane_gather(out_full, chips, 4, inner=True).reshape(D, D)
    layer_in = tokens.astype(F32)
    branch_attn = matmul(attended, out_full)
    residual = layer_in + RESID_MULT * branch_attn
    factor_two = norm_parts(residual)
    normed_two = (residual * factor_two * gain_two).astype(BF16)
    normed_two = plane_gather(normed_two, chips, 2).reshape(devs * rows, D)
    upstream = cotangent.astype(F32)
    d_branch_mlp = (RESID_MULT * upstream).astype(BF16)
    d_branch_mlp, normed_two = lax.optimization_barrier((d_branch_mlp, normed_two))
    d_branch_mlp = plane_gather(d_branch_mlp, chips, 2)
    d_branch_mlp = d_branch_mlp.reshape(devs * rows, D)

    wide_w = gather(jnp.stack([w_gate, w_up])[None], "grp")
    down_w = gather(w_down[None], "grp")
    normed_two, d_branch_mlp = lax.optimization_barrier((normed_two, d_branch_mlp))
    hidden, hidden_t, silu, slope, normed_t = widen(normed_two, wide_w)
    part_down = down_part(hidden_t, d_branch_mlp)
    part_down, hidden, silu = lax.optimization_barrier((part_down, hidden, silu))
    grad_down = scatter(part_down, "grp")
    if chips == 4:
        branch_mlp, *others = mix_twin(hidden, down_w, rows, 11)
        others, silu = lax.optimization_barrier((others, silu))
        others = [swap_chips(part, step) for step, part in zip((3, 1, 2), others)]
    else:
        branch_mlp = mix(hidden, down_w)
    d_gate, d_up = narrow_back(silu, slope, d_branch_mlp, down_w)
    part_wide = widen_part(normed_t, d_gate, d_up)
    if chips == 4:
        part_wide, others, d_gate, d_up = lax.optimization_barrier(
            (part_wide, others, d_gate, d_up)
        )
    else:
        part_wide, d_gate, d_up = lax.optimization_barrier((part_wide, d_gate, d_up))
    grad_wide = scatter(part_wide, "grp")
    if chips == 4:
        for part in others:
            branch_mlp = branch_mlp + part.astype(F32)
        d_normed_two = square_reduce(widen_back_rows, (d_gate, d_up, wide_w), rows, 10)
    else:
        branch_mlp = plane_reduce(branch_mlp.reshape(devs, rows, D), chips, 5)
        d_normed_two = widen_back(d_gate, d_up, wide_w)
        d_normed_two = plane_reduce(d_normed_two.reshape(devs, rows, D), chips, 5)
    layer_out = residual + RESID_MULT * branch_mlp

    d_residual_norm, d_gain_two = norm_back(residual, factor_two, gain_two, d_normed_two)
    d_residual = upstream + d_residual_norm
    d_branch_attn = (RESID_MULT * d_residual).astype(BF16)
    grad_out = over_rows(attended, d_branch_attn).astype(BF16)
    grad_out, d_branch_attn = lax.optimization_barrier((grad_out, d_branch_attn))
    if chips == 4:
        drift_out = Drift(grad_out.reshape(grps, 4, 2, w_rows, D), 1)
    d_attended = over_cols(d_branch_attn, out_full).astype(BF16)
    d_attended = plane_exchange(
        d_attended, (devs * rows, q_cols), by_cols(q_cols), by_rows(rows), chips, 7
    )
    if chips == 4:
        sent_out, d_attended = lax.optimization_barrier((drift_out.parts(), d_attended))
        sent_out = Drift.send(sent_out)
    d_attended, grad_down = lax.optimization_barrier((d_attended, grad_down))
    d_qkv = attend_back(qkv, d_attended, order, q_heads)
    if chips == 4:
        sent_out, d_qkv, grad_wide = lax.optimization_barrier((sent_out, d_qkv, grad_wide))
        grad_out = drift_out.finish(sent_out).astype(BF16)
    else:
        grad_out = plane_reduce(
            grad_out.reshape(grps, devs, w_rows, D), chips, 6, dtype=BF16, inner=True
        )
    grad_out = scatter(grad_out, "grp").reshape(w_rows, D).astype(F32)
    sent = over_rows(normed_one, d_qkv).astype(BF16)
    sent, d_qkv = lax.optimization_barrier((sent, d_qkv))
    sent = scatter(sent, "grp")

    d_normed_one = over_cols(d_qkv, w_qkv).astype(BF16).reshape(devs, rows, D)
    d_normed_one = plane_reduce(d_normed_one, chips, 5)
    d_normed_one, sent = lax.optimization_barrier((d_normed_one, sent))
    d_input_norm, d_gain_one = norm_back(layer_in, norm_parts(layer_in), gain_one, d_normed_one)
    tokens_grad = (d_residual + d_input_norm).astype(BF16)

    sent = sent.reshape(devs, w_rows, q_cols + 2 * kv_cols)
    sent = plane_exchange(sent, sent.shape, by_slot, by_slot, chips, 9).astype(F32)

    def kv_join(g):
        g = g.reshape(devs // kv_copies, kv_copies, w_rows, kv_cols)
        g = jnp.sum(g, axis=1) if kv_copies > 1 else g[:, 0]
        return jnp.swapaxes(g, 0, 1).reshape(w_rows, KV_HEADS * HEAD_DIM)

    grad_query = jnp.swapaxes(sent[:, :, :q_cols], 0, 1).reshape(w_rows, D)
    grad_key = kv_join(sent[:, :, q_cols : q_cols + kv_cols])
    grad_value = kv_join(sent[:, :, q_cols + kv_cols : q_cols + 2 * kv_cols])

    scaled_attn = RESID_MULT * branch_attn
    scaled_mlp = RESID_MULT * branch_mlp
    squares = jnp.stack(
        [
            jnp.sum(layer_out * layer_out),
            jnp.sum(scaled_attn * scaled_attn),
            jnp.sum(scaled_mlp * scaled_mlp),
        ]
    )
    totals = jnp.concatenate([d_gain_one, d_gain_two, squares, jnp.zeros((1021,), F32)])
    totals = total(totals.reshape(8, 5 * D // 16), grps, chips, 8).reshape(-1)
    rms_stats = jnp.sqrt(totals[2 * D : 2 * D + 3] / (rows * grps * devs * D))
    gain_first = (lax.axis_index("grp") * devs + lax.axis_index(PLANE)) * w_rows
    gain_one_grad = lax.dynamic_slice(totals, (gain_first,), (w_rows,))
    gain_two_grad = lax.dynamic_slice(totals, (gain_first + D,), (w_rows,))
    return (
        layer_out.astype(BF16),
        tokens_grad,
        gain_one_grad,
        grad_query,
        grad_key,
        grad_value,
        grad_out,
        gain_two_grad,
        grad_wide[0, 0].astype(F32),
        grad_wide[0, 1].astype(F32),
        grad_down[0].astype(F32),
        rms_stats,
    )


def solution(mesh):
    shape = (mesh.shape["grp"], mesh.shape["blk"] // 2, 2)
    mesh = Mesh(mesh.devices.reshape(shape), EVERY)
    row, col, vec = P(EVERY, None), P(None, EVERY), P(EVERY)
    return jax.shard_map(
        on_device,
        mesh=mesh,
        in_specs=(row, P(), P(), vec, row, row, row, row, vec, col, col, row, row),
        out_specs=(row, row, vec, row, row, row, row, vec, col, col, row, P()),
        check_vma=False,
    )
```

```python
import functools

import jax
import jax.numpy as jnp
from jax import lax
from jax.experimental import pallas as pl
from jax.experimental.pallas import tpu as pltpu
from jax.sharding import Mesh
from jax.sharding import PartitionSpec as P

D = 2048
HEADS = 32
KV_HEADS = 8
HEAD_DIM = 64
BLOCK = 128
PROMPT_BLOCKS = 8
GROUP_BLOCKS = 16
PER_GROUP = HEADS // KV_HEADS

ATTN_MULT = 0.015625
RESID_MULT = 0.22
EPSILON = 1e-05
MASKED = -1e30

PLANE = ("chip", "core")
EVERY = ("grp", "chip", "core")
BF16 = jnp.bfloat16
F32 = jnp.float32


MESH = pl.DeviceIdType.MESH
BRIEF = pl.CostEstimate(flops=1000, bytes_accessed=1000, transcendentals=0)
ANY = pl.BlockSpec(memory_space=pl.ANY)
VMEM = pl.BlockSpec(memory_space=pltpu.VMEM)


def place():
    return lax.axis_index("chip"), lax.axis_index("core")


def flip(chip, step, chips):
    return jnp.bitwise_xor(chip, step) if chips == 4 else lax.rem(chip + step, chips)


def unflip(chip, step, chips):
    return jnp.bitwise_xor(chip, step) if chips == 4 else lax.rem(chip + chips - step, chips)


def greet(peers):
    barrier = pltpu.get_barrier_semaphore()
    for chip, core in peers:
        pl.semaphore_signal(
            barrier, inc=1, device_id={"chip": chip, "core": core}, device_id_type=MESH
        )
    pl.semaphore_wait(barrier, len(peers))


def remote(src, dst, send, recv, chip, core):
    return pltpu.make_async_remote_copy(
        src_ref=src,
        dst_ref=dst,
        send_sem=send,
        recv_sem=recv,
        device_id={"chip": chip, "core": core},
        device_id_type=MESH,
    )


class Gather:
    def __init__(self, chips, inner, x_ref, o_ref, send, recv, local):
        self.chips, self.inner, self.x, self.o = chips, inner, x_ref, o_ref
        self.send, self.recv, self.local = send, recv, local
        self.chip, self.core = place()
        self.half = x_ref.shape[0] // 2
        self.started = []

    def greet(self):
        steps = (1, 2) if self.chips == 4 else range(1, self.chips)
        peers = [(flip(self.chip, s, self.chips), self.core) for s in steps]
        greet(peers + [(self.chip, 1 - self.core)])

    def piece(self, slot, h):
        at = pl.ds(h * self.half, self.half)
        return self.o.at[at, slot] if self.inner else self.o.at[slot, at]

    def own(self, h):
        return self.x.at[pl.ds(h * self.half, self.half)]

    def slot(self, chip, core):
        return chip * 2 + core

    def push(self, src, slot, h, chip, core):
        i = len(self.started)
        copy = remote(src, self.piece(slot, h), self.send.at[i], self.recv.at[slot, h], chip, core)
        copy.start()
        self.started.append(copy)

    def wait_for(self, slot, h):
        remote(
            self.own(h), self.piece(slot, h), self.send.at[0], self.recv.at[slot, h],
            self.chip, 1 - self.core,
        ).wait_recv()

    def start(self):
        me = self.slot(self.chip, self.core)
        if self.chips == 4:
            for h, s in ((0, 1), (1, 2), (1, 1), (0, 2)):
                self.push(self.own(h), me, h, flip(self.chip, s, 4), self.core)
        else:
            for s in range(1, self.chips):
                for h in range(2):
                    self.push(self.own(h), me, h, flip(self.chip, s, self.chips), self.core)
        for h in range(2):
            self.push(self.own(h), me, h, self.chip, 1 - self.core)
        whole = self.o.at[:, me] if self.inner else self.o.at[me]
        self.mine = pltpu.make_async_copy(self.x, whole, self.local)
        self.mine.start()

    def relay(self, first=0, last=None):
        if self.chips == 4:
            plan = ((1, 0, 2), (2, 1, 1), (1, 1, 0), (2, 0, 0), (3, 0, 0), (3, 1, 0))
        else:
            plan = tuple((s, h, 0) for s in range(1, self.chips) for h in range(2))
        for s, h, onward in plan[first:last]:
            slot = self.slot(unflip(self.chip, s, self.chips), self.core)
            self.wait_for(slot, h)
            if onward:
                self.push(self.piece(slot, h), slot, h, flip(self.chip, onward, 4), self.core)
            self.push(self.piece(slot, h), slot, h, self.chip, 1 - self.core)

    def finish(self):
        for s in range(self.chips):
            slot = self.slot(unflip(self.chip, s, self.chips), 1 - self.core)
            for h in range(2):
                self.wait_for(slot, h)
        for copy in self.started:
            copy.wait_send()
        self.mine.wait()


def gather_sems(chips):
    return [
        pltpu.SemaphoreType.DMA((4 * chips + 4,)),
        pltpu.SemaphoreType.DMA((2 * chips, 2)),
        pltpu.SemaphoreType.DMA,
    ]


def gather_kernel(chips, inner, x_ref, o_ref, *sems):
    run = Gather(chips, inner, x_ref, o_ref, *sems)
    run.greet()
    run.start()
    run.relay()
    run.finish()


def plane_gather(x, chips, call_id, inner=False):
    devs = 2 * chips
    shape = (x.shape[0], devs) + x.shape[1:] if inner else (devs,) + x.shape
    return pl.pallas_call(
        functools.partial(gather_kernel, chips, inner),
        out_shape=jax.ShapeDtypeStruct(shape, x.dtype),
        in_specs=[ANY],
        out_specs=ANY,
        scratch_shapes=gather_sems(chips),
        cost_estimate=BRIEF,
        compiler_params=pltpu.CompilerParams(collective_id=call_id, has_side_effects=True),
    )(x)


def reduce_kernel(chips, inner, p_ref, o_ref, total, mine, twin, moved, corner, landed, lsem, tsend, trecv, msend, mrecv, csend, crecv):
    chip, core = place()
    sib = 1 - core
    half = (p_ref.shape[0] if inner else p_ref.shape[1]) // 2
    block = (lambda slot: p_ref.at[:, slot]) if inner else (lambda slot: p_ref.at[slot])
    steps = (1, 2) if chips == 4 else tuple(range(1, chips))
    peers = [(flip(chip, s, chips), core) for s in steps]
    greet(peers + [(chip, sib)])
    order = (3, 1, 2, 0) if chips == 4 else tuple(range(1, chips)) + (0,)
    loads, twins = {}, {}
    for s in order:
        to = flip(chip, s, chips) * 2
        twins[s] = remote(block(to + sib), twin.at[s], tsend.at[s], trecv.at[s], chip, sib)
        twins[s].start()
        loads[s] = pltpu.make_async_copy(block(to + core), mine.at[s], lsem.at[s])
        loads[s].start()

    def part(s, h):
        at = pl.ds(h * half, half)
        return mine[s, at].astype(F32) + twin[s, at].astype(F32)

    def ready(s):
        loads[s].wait()
        twins[s].wait_recv()

    sent = []
    if chips == 4:
        corners = []
        ready(3)
        for h, s in ((0, 1), (1, 2)):
            moved[3, pl.ds(h * half, half)] = part(3, h).astype(BF16)
            copy = remote(moved.at[3, pl.ds(h * half, half)], corner.at[h], csend.at[h], crecv.at[h], flip(chip, s, 4), core)
            copy.start()
            corners.append(copy)

        def send(s, h):
            at = pl.ds(h * half, half)
            copy = remote(moved.at[s, at], landed.at[s - 1, at], msend.at[s - 1, h], mrecv.at[s - 1, h], flip(chip, s, 4), core)
            copy.start()
            sent.append(copy)

        for s, h in ((1, 0), (2, 1)):
            ready(s)
            moved[s, pl.ds(h * half, half)] = part(s, h).astype(BF16)
            send(s, h)
        for s, h in ((2, 0), (1, 1)):
            corners[h].wait_recv()
            moved[s, pl.ds(h * half, half)] = (part(s, h) + corner[h].astype(F32)).astype(BF16)
            send(s, h)
        for copy in corners:
            copy.wait_send()
    else:
        for s in steps:
            ready(s)
            for h in range(2):
                at = pl.ds(h * half, half)
                moved[s, at] = part(s, h).astype(BF16)
                copy = remote(moved.at[s, at], landed.at[s - 1, at], msend.at[s - 1, h], mrecv.at[s - 1, h], flip(chip, s, chips), core)
                copy.start()
                sent.append(copy)
    ready(0)
    for h in range(2):
        total[pl.ds(h * half, half)] = part(0, h)
    for copy in sent:
        copy.wait()
    for s in steps[:-1]:
        total[...] += landed[s - 1].astype(F32)
    o_ref[...] = (total[...] + landed[steps[-1] - 1].astype(F32)).astype(o_ref.dtype)
    for s in order:
        twins[s].wait_send()


def plane_reduce(p, chips, call_id, dtype=F32, inner=False):
    block = (p.shape[0],) + p.shape[2:] if inner else p.shape[1:]
    steps = 2 if chips == 4 else chips - 1
    return pl.pallas_call(
        functools.partial(reduce_kernel, chips, inner),
        out_shape=jax.ShapeDtypeStruct(block, dtype),
        in_specs=[ANY],
        out_specs=VMEM,
        scratch_shapes=[
            pltpu.VMEM(block, F32),
            pltpu.VMEM((chips,) + block, BF16),
            pltpu.VMEM((chips,) + block, BF16),
            pltpu.VMEM((chips,) + block, BF16),
            pltpu.VMEM((2, block[0] // 2) + block[1:], BF16),
            pltpu.VMEM((steps,) + block, BF16),
            pltpu.SemaphoreType.DMA((chips,)),
            pltpu.SemaphoreType.DMA((chips,)),
            pltpu.SemaphoreType.DMA((chips,)),
            pltpu.SemaphoreType.DMA((steps, 2)),
            pltpu.SemaphoreType.DMA((steps, 2)),
            pltpu.SemaphoreType.DMA((2,)),
            pltpu.SemaphoreType.DMA((2,)),
        ],
        cost_estimate=BRIEF,
        compiler_params=pltpu.CompilerParams(
            collective_id=call_id, has_side_effects=True, vmem_limit_bytes=56 << 20
        ),
    )(p)


def swap_chips(values, step):
    return lax.ppermute(values, "chip", [(c, c ^ step) for c in range(4)])


class Drift:
    def __init__(self, pairs, axis):
        self.axis = axis
        self.chip, self.core = place()
        away = lax.dynamic_index_in_dim(pairs, 1 - self.core, axis + 1, keepdims=False)
        self.mine = lax.dynamic_index_in_dim(pairs, self.core, axis + 1, keepdims=False)
        self.twin = lax.ppermute(away, "core", [(0, 1), (1, 0)])

    def part(self, step):
        at = jnp.bitwise_xor(self.chip, step)
        mine = lax.dynamic_index_in_dim(self.mine, at, self.axis, keepdims=False)
        twin = lax.dynamic_index_in_dim(self.twin, at, self.axis, keepdims=False)
        return mine.astype(F32) + twin.astype(F32)

    def parts(self):
        return tuple(self.part(step).astype(BF16) for step in (1, 2, 3))

    @staticmethod
    def send(parts):
        return tuple(
            swap_chips(part, step)
            for step, part in zip((3, 1, 2), (parts[2], parts[0], parts[1]))
        )

    def finish(self, came):
        total = self.part(0)
        for part in came:
            total = total + part.astype(F32)
        return total


def exchange_kernel(chips, cut, paste, x_ref, o_ref, send, recv, local):
    chip, core = place()
    me = chip * 2 + core
    peers = [(flip(chip, s, chips), c) for s in range(1, chips) for c in (core, 1 - core)]
    peers = peers + [(chip, 1 - core)]
    greet(peers)
    far = [p for p in ([3, 1, 2] if chips == 4 else range(1, chips))]
    order = [(flip(chip, s, chips), c) for s in far for c in (core, 1 - core)] + [(chip, 1 - core)]
    copies = []
    for i, (to, c) in enumerate(order):
        copy = remote(cut(x_ref, to * 2 + c), paste(o_ref, me), send.at[i], recv.at[me], to, c)
        copy.start()
        copies.append(copy)
    mine = pltpu.make_async_copy(cut(x_ref, me), paste(o_ref, me), local)
    mine.start()
    for s in far:
        for c in (core, 1 - core):
            slot = unflip(chip, s, chips) * 2 + c
            remote(cut(x_ref, me), paste(o_ref, slot), send.at[0], recv.at[slot], chip, 1 - core).wait_recv()
    slot = chip * 2 + 1 - core
    remote(cut(x_ref, me), paste(o_ref, slot), send.at[0], recv.at[slot], chip, 1 - core).wait_recv()
    for copy in copies:
        copy.wait_send()
    mine.wait()


def plane_exchange(x, shape, cut, paste, chips, call_id):
    return pl.pallas_call(
        functools.partial(exchange_kernel, chips, cut, paste),
        out_shape=jax.ShapeDtypeStruct(shape, x.dtype),
        in_specs=[ANY],
        out_specs=ANY,
        scratch_shapes=[
            pltpu.SemaphoreType.DMA((2 * chips,)),
            pltpu.SemaphoreType.DMA((2 * chips,)),
            pltpu.SemaphoreType.DMA,
        ],
        cost_estimate=BRIEF,
        compiler_params=pltpu.CompilerParams(collective_id=call_id, has_side_effects=True),
    )(x)


def by_slot(ref, dev):
    return ref.at[dev]


def by_rows(rows):
    return lambda ref, dev: ref.at[pl.ds(pl.multiple_of(dev * rows, rows), rows)]


def by_cols(cols):
    return lambda ref, dev: ref.at[:, pl.ds(pl.multiple_of(dev * cols, cols), cols)]


def matmul(left, right):
    return jnp.dot(left, right, preferred_element_type=F32)


def over_rows(left, right):
    return lax.dot_general(left, right, (((0,), (0,)), ((), ())), preferred_element_type=F32)


def over_cols(left, right):
    return lax.dot_general(left, right, (((1,), (1,)), ((), ())), preferred_element_type=F32)


def gather(values, axes, axis=0):
    return lax.all_gather(values, axes, axis=axis, tiled=True)


def scatter(values, axes, axis=0):
    return lax.psum_scatter(values, axes, scatter_dimension=axis, tiled=True)


def dot_nt(left, right):
    return lax.dot_general(left, right, (((1,), (1,)), ((), ())), preferred_element_type=F32)


def head_stack(values, heads):
    col_head = lax.broadcasted_iota(jnp.int32, values.shape, 1) // HEAD_DIM
    return jnp.concatenate(
        [jnp.where(col_head == h, values, jnp.zeros_like(values)) for h in range(heads)], axis=0
    )


def head_pick(stacked, heads):
    rows = stacked.shape[0] // heads
    col_head = lax.broadcasted_iota(jnp.int32, (rows, stacked.shape[1]), 1) // HEAD_DIM
    total = jnp.zeros((rows, stacked.shape[1]), F32)
    for h in range(heads):
        total = jnp.where(col_head == h, stacked[h * rows : (h + 1) * rows], total)
    return total


def head_fold(values, heads):
    total = values[:, :HEAD_DIM]
    for h in range(1, heads):
        total = total + values[:, h * HEAD_DIM : (h + 1) * HEAD_DIM]
    return total


def repeat_heads(values, heads):
    return jnp.concatenate([values] * heads, axis=1)


def own_rows(order_ref, slot):
    return pl.ds(pl.multiple_of(order_ref[slot] * BLOCK, BLOCK), BLOCK)


def load_prompt(heads, order_ref, qkv_ref, k_ref, v_ref, first):
    q_cols = heads * HEAD_DIM
    for s in range(PROMPT_BLOCKS):
        pair = qkv_ref[own_rows(order_ref, first + s), q_cols:]
        at = pl.ds(s * BLOCK, BLOCK)
        k_ref[at] = repeat_heads(pair[:, :HEAD_DIM], heads)
        v_ref[at] = repeat_heads(pair[:, HEAD_DIM:], heads)


def soft_parts(heads, slot, q_stack, k_far, k_own):
    far = dot_nt(k_far, q_stack)
    own = dot_nt(k_own, q_stack)
    limit = jnp.minimum(slot, PROMPT_BLOCKS) * BLOCK
    far = jnp.where(lax.broadcasted_iota(jnp.int32, far.shape, 0) < limit, far, MASKED)
    key = lax.broadcasted_iota(jnp.int32, own.shape, 0)
    row = lax.broadcasted_iota(jnp.int32, own.shape, 1) % BLOCK
    own = jnp.where(key <= row, own, MASKED)
    peak = jnp.maximum(jnp.max(far, axis=0, keepdims=True), jnp.max(own, axis=0, keepdims=True))
    far, own = jnp.exp(far - peak), jnp.exp(own - peak)
    scale = 1.0 / (jnp.sum(far, axis=0, keepdims=True) + jnp.sum(own, axis=0, keepdims=True))
    return far * scale, own * scale


def scaled_stack(q, heads):
    return head_stack((q.astype(F32) * ATTN_MULT).astype(BF16), heads)


def attend_kernel(heads, order_ref, qkv_ref, o_ref, k_ref, v_ref, vt_ref):
    first, slot = pl.program_id(0) * GROUP_BLOCKS, pl.program_id(1)
    q_cols = heads * HEAD_DIM

    @pl.when(slot == 0)
    def _():
        load_prompt(heads, order_ref, qkv_ref, k_ref, v_ref, first)
        vt_ref[...] = v_ref[...].astype(F32).T.astype(BF16)

    rows = own_rows(order_ref, first + slot)
    mine = qkv_ref[rows, :]
    k_own = repeat_heads(mine[:, q_cols : q_cols + HEAD_DIM], heads)
    v_own = repeat_heads(mine[:, q_cols + HEAD_DIM :], heads)
    far, own = soft_parts(heads, slot, scaled_stack(mine[:, :q_cols], heads), k_ref[...], k_own)
    mixed = matmul(vt_ref[...], far.astype(BF16))
    mixed += matmul(v_own.astype(F32).T.astype(BF16), own.astype(BF16))
    o_ref[rows, :] = head_pick(mixed.T, heads).astype(BF16)


def attend_back_kernel(
    heads, order_ref, qkv_ref, d_ref, o_ref, k_ref, v_ref, kt_ref, dk_ref, dv_ref
):
    first, slot = pl.program_id(0) * GROUP_BLOCKS, pl.program_id(1)
    q_cols = heads * HEAD_DIM

    @pl.when(slot == 0)
    def _():
        load_prompt(heads, order_ref, qkv_ref, k_ref, v_ref, first)
        kt_ref[...] = k_ref[...].astype(F32).T.astype(BF16)
        dk_ref[...] = jnp.zeros_like(dk_ref)
        dv_ref[...] = jnp.zeros_like(dv_ref)

    rows = own_rows(order_ref, first + slot)
    mine = qkv_ref[rows, :]
    k_own = repeat_heads(mine[:, q_cols : q_cols + HEAD_DIM], heads)
    v_own = repeat_heads(mine[:, q_cols + HEAD_DIM :], heads)
    q_stack = scaled_stack(mine[:, :q_cols], heads)
    d_stack = head_stack(d_ref[rows, :], heads)
    far, own = soft_parts(heads, slot, q_stack, k_ref[...], k_own)
    d_far, d_own = dot_nt(v_ref[...], d_stack), dot_nt(v_own, d_stack)
    mean = jnp.sum(far * d_far, axis=0, keepdims=True) + jnp.sum(own * d_own, axis=0, keepdims=True)
    d_far = (far * (d_far - mean)).astype(BF16)
    d_own = (own * (d_own - mean)).astype(BF16)
    dv_ref[...] += matmul(far.astype(BF16), d_stack)
    dk_ref[...] += matmul(d_far, q_stack)
    dv_own = matmul(own.astype(BF16), d_stack)
    dk_own = matmul(d_own, q_stack)
    d_q = matmul(kt_ref[...], d_far) + matmul(k_own.astype(F32).T.astype(BF16), d_own)
    o_ref[rows, :q_cols] = (head_pick(d_q.T, heads) * ATTN_MULT).astype(BF16)

    def fold(d_k, d_v):
        return jnp.concatenate([head_fold(d_k, heads), head_fold(d_v, heads)], axis=1).astype(BF16)

    @pl.when(slot < PROMPT_BLOCKS)
    def _():
        at = pl.ds(pl.multiple_of(slot * BLOCK, BLOCK), BLOCK)
        dk_ref[at] += dk_own
        dv_ref[at] += dv_own

    @pl.when(slot >= PROMPT_BLOCKS)
    def _():
        o_ref[rows, q_cols:] = fold(dk_own, dv_own)

    @pl.when(slot == GROUP_BLOCKS - 1)
    def _():
        for s in range(PROMPT_BLOCKS):
            at = pl.ds(s * BLOCK, BLOCK)
            o_ref[own_rows(order_ref, first + s), q_cols:] = fold(dk_ref[at], dv_ref[at])


def whole(shape):
    return pl.BlockSpec(shape, lambda g, s, order: (0,) * len(shape))


def attend(qkv, order, heads):
    tokens, cols = qkv.shape
    prompt, q_cols = PROMPT_BLOCKS * BLOCK, heads * HEAD_DIM
    return pl.pallas_call(
        functools.partial(attend_kernel, heads),
        out_shape=jax.ShapeDtypeStruct((tokens, q_cols), BF16),
        grid_spec=pltpu.PrefetchScalarGridSpec(
            num_scalar_prefetch=1,
            grid=(tokens // (GROUP_BLOCKS * BLOCK), GROUP_BLOCKS),
            in_specs=[whole((tokens, cols))],
            out_specs=whole((tokens, q_cols)),
            scratch_shapes=[
                pltpu.VMEM((prompt, q_cols), BF16),
                pltpu.VMEM((prompt, q_cols), BF16),
                pltpu.VMEM((q_cols, prompt), BF16),
            ],
        ),
        cost_estimate=BRIEF,
        compiler_params=pltpu.CompilerParams(vmem_limit_bytes=40 << 20),
    )(order, qkv)


def attend_back(qkv, d_attended, order, heads):
    tokens, cols = qkv.shape
    prompt, q_cols = PROMPT_BLOCKS * BLOCK, heads * HEAD_DIM
    return pl.pallas_call(
        functools.partial(attend_back_kernel, heads),
        out_shape=jax.ShapeDtypeStruct((tokens, cols), BF16),
        grid_spec=pltpu.PrefetchScalarGridSpec(
            num_scalar_prefetch=1,
            grid=(tokens // (GROUP_BLOCKS * BLOCK), GROUP_BLOCKS),
            in_specs=[whole((tokens, cols)), whole((tokens, q_cols))],
            out_specs=whole((tokens, cols)),
            scratch_shapes=[
                pltpu.VMEM((prompt, q_cols), BF16),
                pltpu.VMEM((prompt, q_cols), BF16),
                pltpu.VMEM((q_cols, prompt), BF16),
                pltpu.VMEM((prompt, q_cols), F32),
                pltpu.VMEM((prompt, q_cols), F32),
            ],
        ),
        cost_estimate=BRIEF,
        compiler_params=pltpu.CompilerParams(vmem_limit_bytes=40 << 20),
    )(order, qkv, d_attended)


def total_kernel(grps, chips, x_ref, o_ref, over_z, over_plane, send, recv, psend, precv):
    grp = lax.axis_index("grp")
    chip, core = place()
    me = chip * 2 + core
    far = [lax.rem(grp + s, grps) for s in range(1, grps)]
    near = [(flip(chip, s, chips), c) for s in range(1, chips) for c in (core, 1 - core)]
    near = near + [(chip, 1 - core)]
    barrier = pltpu.get_barrier_semaphore()
    for g in far:
        pl.semaphore_signal(barrier, inc=1, device_id={"grp": g}, device_id_type=MESH)
    for to, c in near:
        pl.semaphore_signal(
            barrier, inc=1, device_id={"chip": to, "core": c}, device_id_type=MESH
        )
    pl.semaphore_wait(barrier, len(far) + len(near))
    copies = []
    for i, g in enumerate(far):
        copy = pltpu.make_async_remote_copy(
            src_ref=x_ref,
            dst_ref=over_z.at[grp],
            send_sem=send.at[i],
            recv_sem=recv.at[grp],
            device_id={"grp": g},
            device_id_type=MESH,
        )
        copy.start()
        copies.append(copy)
    over_z[grp] = x_ref[...]
    for g in far:
        pltpu.make_async_remote_copy(
            src_ref=x_ref,
            dst_ref=over_z.at[g],
            send_sem=send.at[0],
            recv_sem=recv.at[g],
            device_id={"grp": g},
            device_id_type=MESH,
        ).wait_recv()
    over_plane[me] = jnp.sum(over_z[...], axis=0)
    for i, (to, c) in enumerate(near):
        copy = remote(over_plane.at[me], over_plane.at[me], psend.at[i], precv.at[me], to, c)
        copy.start()
        copies.append(copy)
    for to, c in near:
        slot = to * 2 + c
        remote(over_plane.at[me], over_plane.at[slot], psend.at[0], precv.at[slot], to, c).wait_recv()
    for copy in copies:
        copy.wait_send()
    o_ref[...] = jnp.sum(over_plane[...], axis=0)


def total(x, grps, chips, call_id):
    devs = 2 * chips
    return pl.pallas_call(
        functools.partial(total_kernel, grps, chips),
        out_shape=jax.ShapeDtypeStruct(x.shape, F32),
        in_specs=[VMEM],
        out_specs=VMEM,
        scratch_shapes=[
            pltpu.VMEM((grps,) + x.shape, F32),
            pltpu.VMEM((devs,) + x.shape, F32),
            pltpu.SemaphoreType.DMA((grps,)),
            pltpu.SemaphoreType.DMA((grps,)),
            pltpu.SemaphoreType.DMA((devs,)),
            pltpu.SemaphoreType.DMA((devs,)),
        ],
        cost_estimate=BRIEF,
        compiler_params=pltpu.CompilerParams(collective_id=call_id, has_side_effects=True),
    )(x)


def params(axes, mib=56):
    return pltpu.CompilerParams(
        dimension_semantics=("arbitrary",) * axes, vmem_limit_bytes=mib << 20
    )


def tile_rows(count, limit):
    while count % limit:
        limit //= 2
    return limit


def widen_kernel(n_ref, w_ref, h_ref, ht_ref, s_ref, t_ref, nt_ref):
    values = n_ref[...]
    gate, up = matmul(values, w_ref[0, 0]), matmul(values, w_ref[0, 1])
    sig = 1.0 / (1.0 + jnp.exp(-gate))
    silu = gate * sig
    hidden = (silu * up).astype(BF16)
    h_ref[0] = hidden
    ht_ref[0] = hidden.T
    s_ref[0] = silu.astype(BF16)
    t_ref[0] = (up * (sig * (1.0 + gate * (1.0 - sig)))).astype(BF16)

    @pl.when(pl.program_id(1) == 0)
    def _():
        nt_ref[...] = values.T


def widen(normed, weights):
    tokens, depth = normed.shape
    shards, _, _, width = weights.shape
    rows = tile_rows(tokens, 1024)
    tall = jax.ShapeDtypeStruct((shards, tokens, width), BF16)
    tall_spec = pl.BlockSpec((1, rows, width), lambda r, s: (s, r, 0))
    return pl.pallas_call(
        widen_kernel,
        out_shape=(
            tall,
            jax.ShapeDtypeStruct((shards, width, tokens), BF16),
            tall,
            tall,
            jax.ShapeDtypeStruct((depth, tokens), BF16),
        ),
        grid=(tokens // rows, shards),
        in_specs=[
            pl.BlockSpec((rows, depth), lambda r, s: (r, 0)),
            pl.BlockSpec((1, 2, depth, width), lambda r, s: (s, 0, 0, 0)),
        ],
        out_specs=(
            tall_spec,
            pl.BlockSpec((1, width, rows), lambda r, s: (s, 0, r)),
            tall_spec,
            tall_spec,
            pl.BlockSpec((depth, rows), lambda r, s: (0, r)),
        ),
        cost_estimate=BRIEF,
        compiler_params=params(2),
    )(normed, weights)


def down_part_kernel(ht_ref, d_ref, o_ref):
    o_ref[0] = matmul(ht_ref[0], d_ref[...]).astype(BF16)


def down_part(hidden_t, upstream):
    shards, width, tokens = hidden_t.shape
    depth = upstream.shape[1]
    cols = tile_rows(depth, 1024)
    return pl.pallas_call(
        down_part_kernel,
        out_shape=jax.ShapeDtypeStruct((shards, width, depth), BF16),
        grid=(depth // cols, shards),
        in_specs=[
            pl.BlockSpec((1, width, tokens), lambda c, s: (s, 0, 0)),
            pl.BlockSpec((tokens, cols), lambda c, s: (0, c)),
        ],
        out_specs=pl.BlockSpec((1, width, cols), lambda c, s: (s, 0, c)),
        cost_estimate=BRIEF,
        compiler_params=params(2),
    )(hidden_t, upstream)


def mix_kernel(h_ref, w_ref, m_ref):
    mixed = None
    for i in range(w_ref.shape[0]):
        part = matmul(h_ref[i], w_ref[i])
        mixed = part if mixed is None else mixed + part
    m_ref[...] = mixed.astype(BF16)


def narrow_specs(hidden, weights):
    shards, tokens, width = hidden.shape
    depth = weights.shape[2]
    rows = tile_rows(tokens, 512)
    return (
        tokens // rows,
        pl.BlockSpec((shards, rows, width), lambda r: (0, r, 0)),
        pl.BlockSpec((rows, depth), lambda r: (r, 0)),
        pl.BlockSpec(weights.shape, lambda r: (0, 0, 0), pipeline_mode=pl.Buffered(1)),
    )


def mix(hidden, weights):
    steps, tall_spec, flat_spec, weight_spec = narrow_specs(hidden, weights)
    return pl.pallas_call(
        mix_kernel,
        out_shape=jax.ShapeDtypeStruct((hidden.shape[1], weights.shape[2]), BF16),
        grid=(steps,),
        in_specs=[tall_spec, weight_spec],
        out_specs=flat_spec,
        cost_estimate=BRIEF,
        compiler_params=params(1),
    )(hidden, weights)


def narrow_back_kernel(s_ref, t_ref, d_ref, w_ref, dg_ref, du_ref):
    upstream = d_ref[...]
    for i in range(w_ref.shape[0]):
        d_hidden = dot_nt(upstream, w_ref[i])
        dg_ref[i] = (d_hidden * t_ref[i].astype(F32)).astype(BF16)
        du_ref[i] = (d_hidden * s_ref[i].astype(F32)).astype(BF16)


def narrow_back(silu, slope, upstream, weights):
    steps, tall_spec, flat_spec, weight_spec = narrow_specs(silu, weights)
    tall = jax.ShapeDtypeStruct(silu.shape, BF16)
    return pl.pallas_call(
        narrow_back_kernel,
        out_shape=(tall, tall),
        grid=(steps,),
        in_specs=[tall_spec, tall_spec, flat_spec, weight_spec],
        out_specs=(tall_spec, tall_spec),
        cost_estimate=BRIEF,
        compiler_params=params(1),
    )(silu, slope, upstream, weights)


def widen_part_kernel(nt_ref, dg_ref, du_ref, o_ref):
    values = nt_ref[...]
    o_ref[0, 0] = matmul(values, dg_ref[0]).astype(BF16)
    o_ref[0, 1] = matmul(values, du_ref[0]).astype(BF16)


def widen_part(normed_t, d_gate, d_up):
    depth, tokens = normed_t.shape
    shards, _, width = d_gate.shape
    rows = tile_rows(depth, 1024)
    tall_spec = pl.BlockSpec((1, tokens, width), lambda r, s: (s, 0, 0))
    return pl.pallas_call(
        widen_part_kernel,
        out_shape=jax.ShapeDtypeStruct((shards, 2, depth, width), BF16),
        grid=(depth // rows, shards),
        in_specs=[pl.BlockSpec((rows, tokens), lambda r, s: (r, 0)), tall_spec, tall_spec],
        out_specs=pl.BlockSpec((1, 2, rows, width), lambda r, s: (s, 0, r, 0)),
        cost_estimate=BRIEF,
        compiler_params=params(2),
    )(normed_t, d_gate, d_up)


def widen_back_kernel(dg_ref, du_ref, w_ref, o_ref):
    total = None
    for i in range(w_ref.shape[0]):
        part = dot_nt(dg_ref[i], w_ref[i, 0]) + dot_nt(du_ref[i], w_ref[i, 1])
        total = part if total is None else total + part
    o_ref[...] = total.astype(BF16)


def widen_back(d_gate, d_up, weights):
    shards, tokens, width = d_gate.shape
    depth = weights.shape[2]
    rows = tile_rows(tokens, 512)
    tall_spec = pl.BlockSpec((shards, rows, width), lambda r: (0, r, 0))
    return pl.pallas_call(
        widen_back_kernel,
        out_shape=jax.ShapeDtypeStruct((tokens, depth), BF16),
        grid=(tokens // rows,),
        in_specs=[
            tall_spec,
            tall_spec,
            pl.BlockSpec(weights.shape, lambda r: (0, 0, 0, 0), pipeline_mode=pl.Buffered(1)),
        ],
        out_specs=pl.BlockSpec((rows, depth), lambda r: (r, 0)),
        cost_estimate=BRIEF,
        compiler_params=params(1),
    )(d_gate, d_up, weights)


def stage_step(stage):
    return jnp.where(stage == 0, 3, jnp.where(stage == 3, 0, stage))


class Square:
    def __init__(self, acc, mine, away, twin, moved, corner, landed, tsend, trecv, msend, mrecv, csend, crecv):
        self.acc, self.mine, self.away, self.twin = acc, mine, away, twin
        self.moved, self.corner, self.landed = moved, corner, landed
        self.tsend, self.trecv, self.msend, self.mrecv = tsend, trecv, msend, mrecv
        self.csend, self.crecv = csend, crecv
        self.chip, self.core = place()
        self.rows = mine.shape[1]
        self.half = self.rows // 2

    def greet(self):
        peers = [(flip(self.chip, s, 4), self.core) for s in (1, 2)]
        greet(peers + [(self.chip, 1 - self.core)])

    def twin_copy(self, stage):
        return remote(
            self.away.at[stage], self.twin.at[stage], self.tsend.at[stage], self.trecv.at[stage],
            self.chip, 1 - self.core,
        )

    def offer(self, stage):
        own, other = self.core * self.rows, (1 - self.core) * self.rows
        self.mine[stage] = self.acc[pl.ds(pl.multiple_of(own, self.rows), self.rows)].astype(BF16)
        self.away[stage] = self.acc[pl.ds(pl.multiple_of(other, self.rows), self.rows)].astype(BF16)
        self.twin_copy(stage).start()

    def at(self, h):
        return pl.ds(h * self.half, self.half)

    def both(self, stage, h):
        return self.mine[stage, self.at(h)].astype(F32) + self.twin[stage, self.at(h)].astype(F32)

    def corner_copy(self, h):
        return remote(
            self.moved.at[0, self.at(h)], self.corner.at[h], self.csend.at[h], self.crecv.at[h],
            flip(self.chip, h + 1, 4), self.core,
        )

    def copy(self, stage, h):
        return remote(
            self.moved.at[stage, self.at(h)], self.landed.at[stage - 1, self.at(h)],
            self.msend.at[stage - 1, h], self.mrecv.at[stage - 1, h],
            flip(self.chip, stage, 4), self.core,
        )

    def corners(self):
        self.twin_copy(0).wait_recv()
        for h in range(2):
            self.moved[0, self.at(h)] = self.both(0, h).astype(BF16)
            self.corner_copy(h).start()

    def plain(self, stage):
        self.twin_copy(stage).wait_recv()
        h = stage - 1
        self.moved[stage, self.at(h)] = self.both(stage, h).astype(BF16)
        self.copy(stage, h).start()

    def joined(self, stage):
        h = 2 - stage
        self.corner_copy(h).wait_recv()
        total = self.both(stage, h) + self.corner[h].astype(F32)
        self.moved[stage, self.at(h)] = total.astype(BF16)
        self.copy(stage, h).start()

    def finish(self, o_ref):
        self.twin_copy(3).wait_recv()
        for h in range(2):
            o_ref[self.at(h)] = self.both(3, h)
        for stage, h in ((1, 0), (2, 1), (2, 0), (1, 1)):
            self.copy(stage, h).wait_recv()
            o_ref[self.at(h)] += self.landed[stage - 1, self.at(h)].astype(F32)
        for stage in (1, 2):
            for h in range(2):
                self.copy(stage, h).wait_send()
        for h in range(2):
            self.corner_copy(h).wait_send()
        for stage in range(4):
            self.twin_copy(stage).wait_send()


def square_kernel(compute, count, *refs):
    operands, o_ref, scratch = refs[:count], refs[count], refs[count + 1 :]
    run = Square(*scratch)
    stage = pl.program_id(0)

    @pl.when(stage == 0)
    def _():
        run.greet()

    target = jnp.bitwise_xor(run.chip, stage_step(stage))
    width = 2 * run.rows
    run.acc[...] = compute(operands, pl.ds(pl.multiple_of(target * width, width), width))
    run.offer(stage)

    @pl.when(stage == 1)
    def _():
        run.corners()

    @pl.when(stage == 2)
    def _():
        run.plain(1)

    @pl.when(stage == 3)
    def _():
        run.plain(2)
        run.joined(2)
        run.joined(1)
        run.finish(o_ref)


def square_reduce(compute, operands, rows, call_id):
    block = (rows, D)

    def held(shape):
        return pl.BlockSpec(shape, lambda s: (0,) * len(shape), pipeline_mode=pl.Buffered(1))

    return pl.pallas_call(
        functools.partial(square_kernel, compute, len(operands)),
        out_shape=jax.ShapeDtypeStruct(block, F32),
        grid=(4,),
        in_specs=[held(x.shape) for x in operands],
        out_specs=held(block),
        scratch_shapes=[
            pltpu.VMEM((2 * rows, D), F32),
            pltpu.VMEM((4,) + block, BF16),
            pltpu.VMEM((4,) + block, BF16),
            pltpu.VMEM((4,) + block, BF16),
            pltpu.VMEM((3,) + block, BF16),
            pltpu.VMEM((2, rows // 2, D), BF16),
            pltpu.VMEM((2,) + block, BF16),
            pltpu.SemaphoreType.DMA((4,)),
            pltpu.SemaphoreType.DMA((4,)),
            pltpu.SemaphoreType.DMA((2, 2)),
            pltpu.SemaphoreType.DMA((2, 2)),
            pltpu.SemaphoreType.DMA((2,)),
            pltpu.SemaphoreType.DMA((2,)),
        ],
        cost_estimate=BRIEF,
        compiler_params=pltpu.CompilerParams(
            collective_id=call_id, has_side_effects=True, vmem_limit_bytes=60 << 20
        ),
    )(*operands)


def widen_back_rows(refs, rows):
    dg_ref, du_ref, w_ref = refs
    total = None
    for i in range(w_ref.shape[0]):
        part = dot_nt(dg_ref[i, rows], w_ref[i, 0]) + dot_nt(du_ref[i, rows], w_ref[i, 1])
        total = part if total is None else total + part
    return total


def project_back_rows(refs, rows):
    d_ref, w_ref = refs
    return dot_nt(d_ref[rows], w_ref[...])


def twin_kernel(h_ref, w_ref, o_ref, corner_ref, x_ref, y_ref, acc, mine, away, twin, tsend, trecv):
    chip, core = place()
    stage = pl.program_id(0)
    rows = o_ref.shape[0]

    def copy(s):
        return remote(away.at[s], twin.at[s], tsend.at[s], trecv.at[s], chip, 1 - core)

    def both(s):
        copy(s).wait_recv()
        return mine[s].astype(F32) + twin[s].astype(F32)

    @pl.when(stage == 0)
    def _():
        greet([(chip, 1 - core)])

    target = jnp.bitwise_xor(chip, stage_step(stage)) * 2 * rows
    total = None
    for i in range(w_ref.shape[0]):
        part = matmul(h_ref[i, pl.ds(pl.multiple_of(target, 2 * rows), 2 * rows)], w_ref[i])
        total = part if total is None else total + part
    acc[...] = total
    mine[stage] = acc[pl.ds(pl.multiple_of(core * rows, rows), rows)].astype(BF16)
    away[stage] = acc[pl.ds(pl.multiple_of((1 - core) * rows, rows), rows)].astype(BF16)
    copy(stage).start()

    for s, part_ref in enumerate((corner_ref, x_ref, y_ref)):

        @pl.when(stage == s + 1)
        def _(s=s, part_ref=part_ref):
            part_ref[...] = both(s).astype(BF16)

    @pl.when(stage == 3)
    def _():
        o_ref[...] = both(3)
        for s in range(4):
            copy(s).wait_send()


def mix_twin(hidden, weights, rows, call_id):
    block = (rows, D)

    def held(shape):
        return pl.BlockSpec(shape, lambda s: (0,) * len(shape), pipeline_mode=pl.Buffered(1))

    return pl.pallas_call(
        twin_kernel,
        out_shape=(jax.ShapeDtypeStruct(block, F32),) + (jax.ShapeDtypeStruct(block, BF16),) * 3,
        grid=(4,),
        in_specs=[held(hidden.shape), held(weights.shape)],
        out_specs=(held(block),) * 4,
        scratch_shapes=[
            pltpu.VMEM((2 * rows, D), F32),
            pltpu.VMEM((4,) + block, BF16),
            pltpu.VMEM((4,) + block, BF16),
            pltpu.VMEM((4,) + block, BF16),
            pltpu.SemaphoreType.DMA((4,)),
            pltpu.SemaphoreType.DMA((4,)),
        ],
        cost_estimate=BRIEF,
        compiler_params=pltpu.CompilerParams(
            collective_id=call_id, has_side_effects=True, vmem_limit_bytes=60 << 20
        ),
    )(hidden, weights)


def entry_kernel(
    grps, chips, tok_ref, cot_ref, pack_ref, all_tok, all_cot, all_pack,
    tsend, trecv, tlocal, csend, crecv, clocal, psend, precv, plocal, zsend, zrecv, usend, dsend,
):
    grp = lax.axis_index("grp")
    chip, core = place()
    me = chip * 2 + core
    above, below = lax.rem(grp + 1, grps), lax.rem(grp + grps - 1, grps)
    near = [(flip(chip, s, chips), c) for s in range(1, chips) for c in (core, 1 - core)]
    near = near + [(chip, 1 - core)]
    barrier = pltpu.get_barrier_semaphore()
    for g in (above, below):
        pl.semaphore_signal(barrier, inc=1, device_id={"grp": g}, device_id_type=MESH)
    for to, c in near:
        pl.semaphore_signal(
            barrier, inc=1, device_id={"chip": to, "core": c}, device_id_type=MESH
        )
    pl.semaphore_wait(barrier, len(near) + 2)

    tok = Gather(chips, False, tok_ref, all_tok, tsend, trecv, tlocal)
    cot = Gather(chips, False, cot_ref, all_cot, csend, crecv, clocal)
    packs = []
    for i, (to, c) in enumerate(near):
        copy = remote(
            pack_ref.at[to * 2 + c], all_pack.at[grp, me], psend.at[i], precv.at[me], to, c
        )
        copy.start()
        packs.append(copy)
    mine = pltpu.make_async_copy(pack_ref.at[me], all_pack.at[grp, me], plocal)
    mine.start()
    tok.start()
    for to, c in near:
        slot = to * 2 + c
        remote(
            pack_ref.at[me], all_pack.at[grp, slot], psend.at[0], precv.at[slot], to, c
        ).wait_recv()
    mine.wait()

    def z_copy(block, sem, to):
        return pltpu.make_async_remote_copy(
            src_ref=all_pack.at[block],
            dst_ref=all_pack.at[block],
            send_sem=sem,
            recv_sem=zrecv.at[block],
            device_id={"grp": to},
            device_id_type=MESH,
        )

    has_above, has_below = grp + 1 < grps, grp > 0

    def send(step, block, up):
        @pl.when(has_above if up else has_below)
        def _():
            z_copy(block, (usend if up else dsend).at[step], above if up else below).start()

    def relay(step):
        low, high = grp - step, grp + step

        @pl.when(low >= 0)
        def _():
            z_copy(low, zsend, below).wait_recv()
            send(step, low, True)

        @pl.when(high < grps)
        def _():
            z_copy(high, zsend, above).wait_recv()
            send(step, high, False)

    send(0, grp, True)
    send(0, grp, False)
    tok.relay(0, 4)
    relay(1)
    cot.start()
    tok.relay(4, None)
    for step in range(2, grps - 1):
        relay(step)
    cot.relay(0, 4)
    if grps > 2:
        relay(grps - 1)
    cot.relay(4, None)
    tok.finish()
    cot.finish()
    for copy in packs:
        copy.wait_send()
    for step in range(grps):
        for up in (True, False):
            held = grp - step >= 0 if up else grp + step < grps

            @pl.when(held & (has_above if up else has_below))
            def _(step=step, up=up):
                block = grp - step if up else grp + step
                z_copy(block, (usend if up else dsend).at[step], above if up else below).wait_send()


def entry(tokens, cotangent, packed, grps, chips, call_id):
    devs = 2 * chips
    return pl.pallas_call(
        functools.partial(entry_kernel, grps, chips),
        out_shape=(
            jax.ShapeDtypeStruct((devs,) + tokens.shape, BF16),
            jax.ShapeDtypeStruct((devs,) + cotangent.shape, BF16),
            jax.ShapeDtypeStruct((grps,) + packed.shape, BF16),
        ),
        in_specs=[ANY] * 3,
        out_specs=(ANY,) * 3,
        scratch_shapes=gather_sems(chips)
        + gather_sems(chips)
        + [
            pltpu.SemaphoreType.DMA((devs,)),
            pltpu.SemaphoreType.DMA((devs,)),
            pltpu.SemaphoreType.DMA,
            pltpu.SemaphoreType.DMA,
            pltpu.SemaphoreType.DMA((grps,)),
            pltpu.SemaphoreType.DMA((grps,)),
            pltpu.SemaphoreType.DMA((grps,)),
        ],
        cost_estimate=BRIEF,
        compiler_params=pltpu.CompilerParams(collective_id=call_id, has_side_effects=True),
    )(tokens, cotangent, packed)


def project_kernel(used, x_ref, w_ref, n_ref, qkv_ref, gain_ref):
    @pl.when(pl.program_id(0) == 0)
    def _():
        gain_ref[...] = w_ref[:, used:].astype(F32).T[:8]

    values = x_ref[...].astype(F32)
    factor = lax.rsqrt(jnp.mean(values * values, axis=-1, keepdims=True) + EPSILON)
    normed = (values * factor * gain_ref[0:1]).astype(BF16)
    n_ref[...] = normed
    qkv_ref[...] = matmul(normed, w_ref[:, :used]).astype(BF16)


def project(tokens, packed, used):
    count, depth = tokens.shape
    rows = tile_rows(count, 256)
    return pl.pallas_call(
        functools.partial(project_kernel, used),
        out_shape=(
            jax.ShapeDtypeStruct((count, depth), BF16),
            jax.ShapeDtypeStruct((count, used), BF16),
            jax.ShapeDtypeStruct((8, depth), F32),
        ),
        grid=(count // rows,),
        in_specs=[
            pl.BlockSpec((rows, depth), lambda r: (r, 0)),
            pl.BlockSpec(packed.shape, lambda r: (0, 0)),
        ],
        out_specs=(
            pl.BlockSpec((rows, depth), lambda r: (r, 0)),
            pl.BlockSpec((rows, used), lambda r: (r, 0)),
            pl.BlockSpec((8, depth), lambda r: (0, 0)),
        ),
        cost_estimate=BRIEF,
        compiler_params=params(1),
    )(tokens, packed)


def norm_parts(values):
    factor = lax.rsqrt(jnp.mean(values * values, axis=-1, keepdims=True) + EPSILON)
    return factor


def norm_back(values, factor, gain, grad):
    scaled = gain * grad
    inner = jnp.mean(values * scaled, axis=-1, keepdims=True)
    return factor * scaled - values * (factor * factor * factor * inner), jnp.sum(
        grad * values * factor, axis=0
    )


def on_device(
    tokens,
    block_group,
    block_slot,
    attn_gain,
    w_query,
    w_key,
    w_value,
    w_out,
    mlp_gain,
    w_gate,
    w_up,
    w_down,
    cotangent,
):
    grps = lax.axis_size("grp")
    devs = lax.axis_size(PLANE)
    chips = devs // 2
    rows = tokens.shape[0]
    w_rows = w_query.shape[0]
    q_heads = HEADS // devs
    kv_heads = 1
    assert devs % KV_HEADS == 0
    kv_copies = max(1, devs // KV_HEADS)
    q_cols, kv_cols = q_heads * HEAD_DIM, kv_heads * HEAD_DIM
    row_blocks = rows // BLOCK * devs
    row_groups = row_blocks // GROUP_BLOCKS

    row_first = lax.axis_index("grp") * row_blocks
    keys = lax.dynamic_slice_in_dim(block_group, row_first, row_blocks) * GROUP_BLOCKS
    keys = keys + lax.dynamic_slice_in_dim(block_slot, row_first, row_blocks)
    rank = jnp.sum((keys[None, :] < keys[:, None]).astype(jnp.int32), axis=1)
    ids = jnp.arange(row_blocks, dtype=jnp.int32)
    order = jnp.sum(jnp.where(rank[None, :] == ids[:, None], ids[None, :], 0), axis=1)

    def kv_split(w):
        w = w.reshape(w_rows, devs // kv_copies, kv_cols)
        return jnp.repeat(w, kv_copies, axis=1) if kv_copies > 1 else w

    gains = jnp.stack([attn_gain, mlp_gain], axis=1)
    cols = D // 4
    room = cols - q_cols - 2 * kv_cols
    gains = jnp.pad(gains, ((0, 0), (0, room - 2)))
    gains = jnp.broadcast_to(gains[:, None, :], (w_rows, devs, room))
    packed = jnp.concatenate(
        [w_query.reshape(w_rows, devs, q_cols), kv_split(w_key), kv_split(w_value), gains], axis=2
    )
    packed = jnp.swapaxes(packed, 0, 1)
    used = q_cols + 2 * kv_cols
    out_full = gather(w_out[None], "grp")
    upstream = cotangent.astype(F32)
    d_branch_mlp = (RESID_MULT * upstream).astype(BF16)
    all_tokens, d_branch_mlp, packed = entry(tokens, d_branch_mlp, packed, grps, chips, 2)
    packed = packed.reshape(D, cols)
    normed_one, qkv, gains = project(all_tokens.reshape(devs * rows, D), packed, used)
    gain_one, gain_two, w_qkv = gains[0], gains[1], packed[:, :used]
    d_branch_mlp = d_branch_mlp.reshape(devs * rows, D)
    attended = attend(qkv, order, q_heads)
    attended = plane_exchange(
        attended, (rows, D), by_rows(rows), by_cols(q_cols), chips, 3
    )

    out_full = plane_gather(out_full, chips, 4, inner=True).reshape(D, D)
    layer_in = tokens.astype(F32)
    branch_attn = matmul(attended, out_full)
    residual = layer_in + RESID_MULT * branch_attn
    factor_two = norm_parts(residual)
    normed_two = (residual * factor_two * gain_two).astype(BF16)
    normed_two = plane_gather(normed_two, chips, 1).reshape(devs * rows, D)
    wide_w = gather(jnp.stack([w_gate, w_up])[None], "grp")
    down_w = gather(w_down[None], "grp")
    hidden, hidden_t, silu, slope, normed_t = widen(normed_two, wide_w)
    part_down = down_part(hidden_t, d_branch_mlp)
    part_down, hidden, silu = lax.optimization_barrier((part_down, hidden, silu))
    grad_down = scatter(part_down, "grp")
    if chips == 4:
        branch_mlp, *others = mix_twin(hidden, down_w, rows, 11)
        others, silu = lax.optimization_barrier((others, silu))
        others = [swap_chips(part, step) for step, part in zip((3, 1, 2), others)]
    else:
        branch_mlp = mix(hidden, down_w)
    d_gate, d_up = narrow_back(silu, slope, d_branch_mlp, down_w)
    part_wide = widen_part(normed_t, d_gate, d_up)
    if chips == 4:
        part_wide, others, d_gate, d_up = lax.optimization_barrier(
            (part_wide, others, d_gate, d_up)
        )
    else:
        part_wide, d_gate, d_up = lax.optimization_barrier((part_wide, d_gate, d_up))
    grad_wide = scatter(part_wide, "grp")
    if chips == 4:
        for part in others:
            branch_mlp = branch_mlp + part.astype(F32)
        d_normed_two = square_reduce(widen_back_rows, (d_gate, d_up, wide_w), rows, 10)
    else:
        branch_mlp = plane_reduce(branch_mlp.reshape(devs, rows, D), chips, 5)
        d_normed_two = widen_back(d_gate, d_up, wide_w)
        d_normed_two = plane_reduce(d_normed_two.reshape(devs, rows, D), chips, 5)
    layer_out = residual + RESID_MULT * branch_mlp

    d_residual_norm, d_gain_two = norm_back(residual, factor_two, gain_two, d_normed_two)
    d_residual = upstream + d_residual_norm
    d_branch_attn = (RESID_MULT * d_residual).astype(BF16)
    grad_out = over_rows(attended, d_branch_attn).astype(BF16)
    grad_out, d_branch_attn = lax.optimization_barrier((grad_out, d_branch_attn))
    if chips == 4:
        drift_out = Drift(grad_out.reshape(grps, 4, 2, w_rows, D), 1)
    d_attended = over_cols(d_branch_attn, out_full).astype(BF16)
    d_attended = plane_exchange(
        d_attended, (devs * rows, q_cols), by_cols(q_cols), by_rows(rows), chips, 7
    )
    if chips == 4:
        sent_out, d_attended = lax.optimization_barrier((drift_out.parts(), d_attended))
        sent_out = Drift.send(sent_out)
    d_attended, grad_down = lax.optimization_barrier((d_attended, grad_down))
    d_qkv = attend_back(qkv, d_attended, order, q_heads)
    if chips == 4:
        sent_out, d_qkv, grad_wide = lax.optimization_barrier((sent_out, d_qkv, grad_wide))
        grad_out = drift_out.finish(sent_out).astype(BF16)
    else:
        grad_out = plane_reduce(
            grad_out.reshape(grps, devs, w_rows, D), chips, 6, dtype=BF16, inner=True
        )
    grad_out = scatter(grad_out, "grp").reshape(w_rows, D).astype(F32)
    sent = over_rows(normed_one, d_qkv).astype(BF16)
    sent, d_qkv = lax.optimization_barrier((sent, d_qkv))
    sent = scatter(sent, "grp")

    d_normed_one = over_cols(d_qkv, w_qkv).astype(BF16).reshape(devs, rows, D)
    d_normed_one = plane_reduce(d_normed_one, chips, 5)
    d_normed_one, sent = lax.optimization_barrier((d_normed_one, sent))
    d_input_norm, d_gain_one = norm_back(layer_in, norm_parts(layer_in), gain_one, d_normed_one)
    tokens_grad = (d_residual + d_input_norm).astype(BF16)

    sent = sent.reshape(devs, w_rows, q_cols + 2 * kv_cols)
    sent = plane_exchange(sent, sent.shape, by_slot, by_slot, chips, 9).astype(F32)

    def kv_join(g):
        g = g.reshape(devs // kv_copies, kv_copies, w_rows, kv_cols)
        g = jnp.sum(g, axis=1) if kv_copies > 1 else g[:, 0]
        return jnp.swapaxes(g, 0, 1).reshape(w_rows, KV_HEADS * HEAD_DIM)

    grad_query = jnp.swapaxes(sent[:, :, :q_cols], 0, 1).reshape(w_rows, D)
    grad_key = kv_join(sent[:, :, q_cols : q_cols + kv_cols])
    grad_value = kv_join(sent[:, :, q_cols + kv_cols : q_cols + 2 * kv_cols])

    scaled_attn = RESID_MULT * branch_attn
    scaled_mlp = RESID_MULT * branch_mlp
    squares = jnp.stack(
        [
            jnp.sum(layer_out * layer_out),
            jnp.sum(scaled_attn * scaled_attn),
            jnp.sum(scaled_mlp * scaled_mlp),
        ]
    )
    totals = jnp.concatenate([d_gain_one, d_gain_two, squares, jnp.zeros((1021,), F32)])
    totals = total(totals.reshape(8, 5 * D // 16), grps, chips, 8).reshape(-1)
    rms_stats = jnp.sqrt(totals[2 * D : 2 * D + 3] / (rows * grps * devs * D))
    gain_first = (lax.axis_index("grp") * devs + lax.axis_index(PLANE)) * w_rows
    gain_one_grad = lax.dynamic_slice(totals, (gain_first,), (w_rows,))
    gain_two_grad = lax.dynamic_slice(totals, (gain_first + D,), (w_rows,))
    return (
        layer_out.astype(BF16),
        tokens_grad,
        gain_one_grad,
        grad_query,
        grad_key,
        grad_value,
        grad_out,
        gain_two_grad,
        grad_wide[0, 0].astype(F32),
        grad_wide[0, 1].astype(F32),
        grad_down[0].astype(F32),
        rms_stats,
    )


def solution(mesh):
    shape = (mesh.shape["grp"], mesh.shape["blk"] // 2, 2)
    mesh = Mesh(mesh.devices.reshape(shape), EVERY)
    row, col, vec = P(EVERY, None), P(None, EVERY), P(EVERY)
    return jax.shard_map(
        on_device,
        mesh=mesh,
        in_specs=(row, P(), P(), vec, row, row, row, row, vec, col, col, row, row),
        out_specs=(row, row, vec, row, row, row, row, vec, col, col, row, P()),
        check_vma=False,
    )
```

```python
import functools

import jax
import jax.numpy as jnp
from jax import lax
from jax.experimental import pallas as pl
from jax.experimental.pallas import tpu as pltpu
from jax.sharding import Mesh
from jax.sharding import PartitionSpec as P

D = 2048
HEADS = 32
KV_HEADS = 8
HEAD_DIM = 64
BLOCK = 128
PROMPT_BLOCKS = 8
GROUP_BLOCKS = 16
PER_GROUP = HEADS // KV_HEADS

ATTN_MULT = 0.015625
RESID_MULT = 0.22
EPSILON = 1e-05
MASKED = -1e30

PLANE = ("chip", "core")
EVERY = ("grp", "chip", "core")
BF16 = jnp.bfloat16
F32 = jnp.float32


MESH = pl.DeviceIdType.MESH
BRIEF = pl.CostEstimate(flops=1000, bytes_accessed=1000, transcendentals=0)
ANY = pl.BlockSpec(memory_space=pl.ANY)
VMEM = pl.BlockSpec(memory_space=pltpu.VMEM)


def place():
    return lax.axis_index("chip"), lax.axis_index("core")


def flip(chip, step, chips):
    return jnp.bitwise_xor(chip, step) if chips == 4 else lax.rem(chip + step, chips)


def unflip(chip, step, chips):
    return jnp.bitwise_xor(chip, step) if chips == 4 else lax.rem(chip + chips - step, chips)


def greet(peers):
    barrier = pltpu.get_barrier_semaphore()
    for chip, core in peers:
        pl.semaphore_signal(
            barrier, inc=1, device_id={"chip": chip, "core": core}, device_id_type=MESH
        )
    pl.semaphore_wait(barrier, len(peers))


def remote(src, dst, send, recv, chip, core):
    return pltpu.make_async_remote_copy(
        src_ref=src,
        dst_ref=dst,
        send_sem=send,
        recv_sem=recv,
        device_id={"chip": chip, "core": core},
        device_id_type=MESH,
    )


class Gather:
    def __init__(self, chips, inner, x_ref, o_ref, send, recv, local):
        self.chips, self.inner, self.x, self.o = chips, inner, x_ref, o_ref
        self.send, self.recv, self.local = send, recv, local
        self.chip, self.core = place()
        self.half = x_ref.shape[0] // 2
        self.started = []

    def greet(self):
        steps = (1, 2) if self.chips == 4 else range(1, self.chips)
        peers = [(flip(self.chip, s, self.chips), self.core) for s in steps]
        greet(peers + [(self.chip, 1 - self.core)])

    def piece(self, slot, h):
        at = pl.ds(h * self.half, self.half)
        return self.o.at[at, slot] if self.inner else self.o.at[slot, at]

    def own(self, h):
        return self.x.at[pl.ds(h * self.half, self.half)]

    def slot(self, chip, core):
        return chip * 2 + core

    def push(self, src, slot, h, chip, core):
        i = len(self.started)
        copy = remote(src, self.piece(slot, h), self.send.at[i], self.recv.at[slot, h], chip, core)
        copy.start()
        self.started.append(copy)

    def wait_for(self, slot, h):
        remote(
            self.own(h), self.piece(slot, h), self.send.at[0], self.recv.at[slot, h],
            self.chip, 1 - self.core,
        ).wait_recv()

    def start(self):
        me = self.slot(self.chip, self.core)
        if self.chips == 4:
            for h, s in ((0, 1), (1, 2), (1, 1), (0, 2)):
                self.push(self.own(h), me, h, flip(self.chip, s, 4), self.core)
        else:
            for s in range(1, self.chips):
                for h in range(2):
                    self.push(self.own(h), me, h, flip(self.chip, s, self.chips), self.core)
        for h in range(2):
            self.push(self.own(h), me, h, self.chip, 1 - self.core)
        whole = self.o.at[:, me] if self.inner else self.o.at[me]
        self.mine = pltpu.make_async_copy(self.x, whole, self.local)
        self.mine.start()

    def relay(self, first=0, last=None):
        if self.chips == 4:
            plan = ((1, 0, 2), (2, 1, 1), (1, 1, 0), (2, 0, 0), (3, 0, 0), (3, 1, 0))
        else:
            plan = tuple((s, h, 0) for s in range(1, self.chips) for h in range(2))
        for s, h, onward in plan[first:last]:
            slot = self.slot(unflip(self.chip, s, self.chips), self.core)
            self.wait_for(slot, h)
            if onward:
                self.push(self.piece(slot, h), slot, h, flip(self.chip, onward, 4), self.core)
            self.push(self.piece(slot, h), slot, h, self.chip, 1 - self.core)

    def finish(self):
        for s in range(self.chips):
            slot = self.slot(unflip(self.chip, s, self.chips), 1 - self.core)
            for h in range(2):
                self.wait_for(slot, h)
        for copy in self.started:
            copy.wait_send()
        self.mine.wait()


def gather_sems(chips):
    return [
        pltpu.SemaphoreType.DMA((4 * chips + 4,)),
        pltpu.SemaphoreType.DMA((2 * chips, 2)),
        pltpu.SemaphoreType.DMA,
    ]


def gather_kernel(chips, inner, x_ref, o_ref, *sems):
    run = Gather(chips, inner, x_ref, o_ref, *sems)
    run.greet()
    run.start()
    run.relay()
    run.finish()


def plane_gather(x, chips, call_id, inner=False):
    devs = 2 * chips
    shape = (x.shape[0], devs) + x.shape[1:] if inner else (devs,) + x.shape
    return pl.pallas_call(
        functools.partial(gather_kernel, chips, inner),
        out_shape=jax.ShapeDtypeStruct(shape, x.dtype),
        in_specs=[ANY],
        out_specs=ANY,
        scratch_shapes=gather_sems(chips),
        cost_estimate=BRIEF,
        compiler_params=pltpu.CompilerParams(collective_id=call_id, has_side_effects=True),
    )(x)


def reduce_kernel(chips, inner, p_ref, o_ref, total, mine, twin, moved, corner, landed, lsem, tsend, trecv, msend, mrecv, csend, crecv):
    chip, core = place()
    sib = 1 - core
    half = (p_ref.shape[0] if inner else p_ref.shape[1]) // 2
    block = (lambda slot: p_ref.at[:, slot]) if inner else (lambda slot: p_ref.at[slot])
    steps = (1, 2) if chips == 4 else tuple(range(1, chips))
    peers = [(flip(chip, s, chips), core) for s in steps]
    greet(peers + [(chip, sib)])
    order = (3, 1, 2, 0) if chips == 4 else tuple(range(1, chips)) + (0,)
    loads, twins = {}, {}
    for s in order:
        to = flip(chip, s, chips) * 2
        twins[s] = remote(block(to + sib), twin.at[s], tsend.at[s], trecv.at[s], chip, sib)
        twins[s].start()
        loads[s] = pltpu.make_async_copy(block(to + core), mine.at[s], lsem.at[s])
        loads[s].start()

    def part(s, h):
        at = pl.ds(h * half, half)
        return mine[s, at].astype(F32) + twin[s, at].astype(F32)

    def ready(s):
        loads[s].wait()
        twins[s].wait_recv()

    sent = []
    if chips == 4:
        corners = []
        ready(3)
        for h, s in ((0, 1), (1, 2)):
            moved[3, pl.ds(h * half, half)] = part(3, h).astype(BF16)
            copy = remote(moved.at[3, pl.ds(h * half, half)], corner.at[h], csend.at[h], crecv.at[h], flip(chip, s, 4), core)
            copy.start()
            corners.append(copy)

        def send(s, h):
            at = pl.ds(h * half, half)
            copy = remote(moved.at[s, at], landed.at[s - 1, at], msend.at[s - 1, h], mrecv.at[s - 1, h], flip(chip, s, 4), core)
            copy.start()
            sent.append(copy)

        for s, h in ((1, 0), (2, 1)):
            ready(s)
            moved[s, pl.ds(h * half, half)] = part(s, h).astype(BF16)
            send(s, h)
        for s, h in ((2, 0), (1, 1)):
            corners[h].wait_recv()
            moved[s, pl.ds(h * half, half)] = (part(s, h) + corner[h].astype(F32)).astype(BF16)
            send(s, h)
        for copy in corners:
            copy.wait_send()
    else:
        for s in steps:
            ready(s)
            for h in range(2):
                at = pl.ds(h * half, half)
                moved[s, at] = part(s, h).astype(BF16)
                copy = remote(moved.at[s, at], landed.at[s - 1, at], msend.at[s - 1, h], mrecv.at[s - 1, h], flip(chip, s, chips), core)
                copy.start()
                sent.append(copy)
    ready(0)
    for h in range(2):
        total[pl.ds(h * half, half)] = part(0, h)
    for copy in sent:
        copy.wait()
    for s in steps[:-1]:
        total[...] += landed[s - 1].astype(F32)
    o_ref[...] = (total[...] + landed[steps[-1] - 1].astype(F32)).astype(o_ref.dtype)
    for s in order:
        twins[s].wait_send()


def plane_reduce(p, chips, call_id, dtype=F32, inner=False):
    block = (p.shape[0],) + p.shape[2:] if inner else p.shape[1:]
    steps = 2 if chips == 4 else chips - 1
    return pl.pallas_call(
        functools.partial(reduce_kernel, chips, inner),
        out_shape=jax.ShapeDtypeStruct(block, dtype),
        in_specs=[ANY],
        out_specs=VMEM,
        scratch_shapes=[
            pltpu.VMEM(block, F32),
            pltpu.VMEM((chips,) + block, BF16),
            pltpu.VMEM((chips,) + block, BF16),
            pltpu.VMEM((chips,) + block, BF16),
            pltpu.VMEM((2, block[0] // 2) + block[1:], BF16),
            pltpu.VMEM((steps,) + block, BF16),
            pltpu.SemaphoreType.DMA((chips,)),
            pltpu.SemaphoreType.DMA((chips,)),
            pltpu.SemaphoreType.DMA((chips,)),
            pltpu.SemaphoreType.DMA((steps, 2)),
            pltpu.SemaphoreType.DMA((steps, 2)),
            pltpu.SemaphoreType.DMA((2,)),
            pltpu.SemaphoreType.DMA((2,)),
        ],
        cost_estimate=BRIEF,
        compiler_params=pltpu.CompilerParams(
            collective_id=call_id, has_side_effects=True, vmem_limit_bytes=56 << 20
        ),
    )(p)


def swap_chips(values, step):
    return lax.ppermute(values, "chip", [(c, c ^ step) for c in range(4)])


class Drift:
    def __init__(self, pairs, axis):
        self.axis = axis
        self.chip, self.core = place()
        away = lax.dynamic_index_in_dim(pairs, 1 - self.core, axis + 1, keepdims=False)
        self.mine = lax.dynamic_index_in_dim(pairs, self.core, axis + 1, keepdims=False)
        self.twin = lax.ppermute(away, "core", [(0, 1), (1, 0)])

    def part(self, step):
        at = jnp.bitwise_xor(self.chip, step)
        mine = lax.dynamic_index_in_dim(self.mine, at, self.axis, keepdims=False)
        twin = lax.dynamic_index_in_dim(self.twin, at, self.axis, keepdims=False)
        return mine.astype(F32) + twin.astype(F32)

    def parts(self):
        return tuple(self.part(step).astype(BF16) for step in (1, 2, 3))

    @staticmethod
    def send(parts):
        return tuple(
            swap_chips(part, step)
            for step, part in zip((3, 1, 2), (parts[2], parts[0], parts[1]))
        )

    def finish(self, came):
        total = self.part(0)
        for part in came:
            total = total + part.astype(F32)
        return total


def exchange_kernel(chips, cut, paste, x_ref, o_ref, send, recv, local):
    chip, core = place()
    me = chip * 2 + core
    peers = [(flip(chip, s, chips), c) for s in range(1, chips) for c in (core, 1 - core)]
    peers = peers + [(chip, 1 - core)]
    greet(peers)
    far = [p for p in ([3, 1, 2] if chips == 4 else range(1, chips))]
    order = [(flip(chip, s, chips), c) for s in far for c in (core, 1 - core)] + [(chip, 1 - core)]
    copies = []
    for i, (to, c) in enumerate(order):
        copy = remote(cut(x_ref, to * 2 + c), paste(o_ref, me), send.at[i], recv.at[me], to, c)
        copy.start()
        copies.append(copy)
    mine = pltpu.make_async_copy(cut(x_ref, me), paste(o_ref, me), local)
    mine.start()
    for s in far:
        for c in (core, 1 - core):
            slot = unflip(chip, s, chips) * 2 + c
            remote(cut(x_ref, me), paste(o_ref, slot), send.at[0], recv.at[slot], chip, 1 - core).wait_recv()
    slot = chip * 2 + 1 - core
    remote(cut(x_ref, me), paste(o_ref, slot), send.at[0], recv.at[slot], chip, 1 - core).wait_recv()
    for copy in copies:
        copy.wait_send()
    mine.wait()


def plane_exchange(x, shape, cut, paste, chips, call_id):
    return pl.pallas_call(
        functools.partial(exchange_kernel, chips, cut, paste),
        out_shape=jax.ShapeDtypeStruct(shape, x.dtype),
        in_specs=[ANY],
        out_specs=ANY,
        scratch_shapes=[
            pltpu.SemaphoreType.DMA((2 * chips,)),
            pltpu.SemaphoreType.DMA((2 * chips,)),
            pltpu.SemaphoreType.DMA,
        ],
        cost_estimate=BRIEF,
        compiler_params=pltpu.CompilerParams(collective_id=call_id, has_side_effects=True),
    )(x)


def by_slot(ref, dev):
    return ref.at[dev]


def by_rows(rows):
    return lambda ref, dev: ref.at[pl.ds(pl.multiple_of(dev * rows, rows), rows)]


def by_cols(cols):
    return lambda ref, dev: ref.at[:, pl.ds(pl.multiple_of(dev * cols, cols), cols)]


def matmul(left, right):
    return jnp.dot(left, right, preferred_element_type=F32)


def over_rows(left, right):
    return lax.dot_general(left, right, (((0,), (0,)), ((), ())), preferred_element_type=F32)


def over_cols(left, right):
    return lax.dot_general(left, right, (((1,), (1,)), ((), ())), preferred_element_type=F32)


def gather(values, axes, axis=0):
    return lax.all_gather(values, axes, axis=axis, tiled=True)


def scatter(values, axes, axis=0):
    return lax.psum_scatter(values, axes, scatter_dimension=axis, tiled=True)


def dot_nt(left, right):
    return lax.dot_general(left, right, (((1,), (1,)), ((), ())), preferred_element_type=F32)


def head_stack(values, heads):
    col_head = lax.broadcasted_iota(jnp.int32, values.shape, 1) // HEAD_DIM
    return jnp.concatenate(
        [jnp.where(col_head == h, values, jnp.zeros_like(values)) for h in range(heads)], axis=0
    )


def head_pick(stacked, heads):
    rows = stacked.shape[0] // heads
    col_head = lax.broadcasted_iota(jnp.int32, (rows, stacked.shape[1]), 1) // HEAD_DIM
    total = jnp.zeros((rows, stacked.shape[1]), F32)
    for h in range(heads):
        total = jnp.where(col_head == h, stacked[h * rows : (h + 1) * rows], total)
    return total


def head_fold(values, heads):
    total = values[:, :HEAD_DIM]
    for h in range(1, heads):
        total = total + values[:, h * HEAD_DIM : (h + 1) * HEAD_DIM]
    return total


def repeat_heads(values, heads):
    return jnp.concatenate([values] * heads, axis=1)


def own_rows(order_ref, slot):
    return pl.ds(pl.multiple_of(order_ref[slot] * BLOCK, BLOCK), BLOCK)


def load_prompt(heads, order_ref, qkv_ref, k_ref, v_ref, first):
    q_cols = heads * HEAD_DIM
    for s in range(PROMPT_BLOCKS):
        pair = qkv_ref[own_rows(order_ref, first + s), q_cols:]
        at = pl.ds(s * BLOCK, BLOCK)
        k_ref[at] = repeat_heads(pair[:, :HEAD_DIM], heads)
        v_ref[at] = repeat_heads(pair[:, HEAD_DIM:], heads)


def soft_parts(heads, slot, q_stack, k_far, k_own):
    far = dot_nt(k_far, q_stack)
    own = dot_nt(k_own, q_stack)
    limit = jnp.minimum(slot, PROMPT_BLOCKS) * BLOCK
    far = jnp.where(lax.broadcasted_iota(jnp.int32, far.shape, 0) < limit, far, MASKED)
    key = lax.broadcasted_iota(jnp.int32, own.shape, 0)
    row = lax.broadcasted_iota(jnp.int32, own.shape, 1) % BLOCK
    own = jnp.where(key <= row, own, MASKED)
    peak = jnp.maximum(jnp.max(far, axis=0, keepdims=True), jnp.max(own, axis=0, keepdims=True))
    far, own = jnp.exp(far - peak), jnp.exp(own - peak)
    scale = 1.0 / (jnp.sum(far, axis=0, keepdims=True) + jnp.sum(own, axis=0, keepdims=True))
    return far * scale, own * scale


def scaled_stack(q, heads):
    return head_stack((q.astype(F32) * ATTN_MULT).astype(BF16), heads)


def attend_kernel(heads, order_ref, qkv_ref, o_ref, k_ref, v_ref, vt_ref):
    first, slot = pl.program_id(0) * GROUP_BLOCKS, pl.program_id(1)
    q_cols = heads * HEAD_DIM

    @pl.when(slot == 0)
    def _():
        load_prompt(heads, order_ref, qkv_ref, k_ref, v_ref, first)
        vt_ref[...] = v_ref[...].astype(F32).T.astype(BF16)

    rows = own_rows(order_ref, first + slot)
    mine = qkv_ref[rows, :]
    k_own = repeat_heads(mine[:, q_cols : q_cols + HEAD_DIM], heads)
    v_own = repeat_heads(mine[:, q_cols + HEAD_DIM :], heads)
    far, own = soft_parts(heads, slot, scaled_stack(mine[:, :q_cols], heads), k_ref[...], k_own)
    mixed = matmul(vt_ref[...], far.astype(BF16))
    mixed += matmul(v_own.astype(F32).T.astype(BF16), own.astype(BF16))
    o_ref[rows, :] = head_pick(mixed.T, heads).astype(BF16)


def attend_back_kernel(
    heads, order_ref, qkv_ref, d_ref, o_ref, k_ref, v_ref, kt_ref, dk_ref, dv_ref
):
    first, slot = pl.program_id(0) * GROUP_BLOCKS, pl.program_id(1)
    q_cols = heads * HEAD_DIM

    @pl.when(slot == 0)
    def _():
        load_prompt(heads, order_ref, qkv_ref, k_ref, v_ref, first)
        kt_ref[...] = k_ref[...].astype(F32).T.astype(BF16)
        dk_ref[...] = jnp.zeros_like(dk_ref)
        dv_ref[...] = jnp.zeros_like(dv_ref)

    rows = own_rows(order_ref, first + slot)
    mine = qkv_ref[rows, :]
    k_own = repeat_heads(mine[:, q_cols : q_cols + HEAD_DIM], heads)
    v_own = repeat_heads(mine[:, q_cols + HEAD_DIM :], heads)
    q_stack = scaled_stack(mine[:, :q_cols], heads)
    d_stack = head_stack(d_ref[rows, :], heads)
    far, own = soft_parts(heads, slot, q_stack, k_ref[...], k_own)
    d_far, d_own = dot_nt(v_ref[...], d_stack), dot_nt(v_own, d_stack)
    mean = jnp.sum(far * d_far, axis=0, keepdims=True) + jnp.sum(own * d_own, axis=0, keepdims=True)
    d_far = (far * (d_far - mean)).astype(BF16)
    d_own = (own * (d_own - mean)).astype(BF16)
    dv_ref[...] += matmul(far.astype(BF16), d_stack)
    dk_ref[...] += matmul(d_far, q_stack)
    dv_own = matmul(own.astype(BF16), d_stack)
    dk_own = matmul(d_own, q_stack)
    d_q = matmul(kt_ref[...], d_far) + matmul(k_own.astype(F32).T.astype(BF16), d_own)
    o_ref[rows, :q_cols] = (head_pick(d_q.T, heads) * ATTN_MULT).astype(BF16)

    def fold(d_k, d_v):
        return jnp.concatenate([head_fold(d_k, heads), head_fold(d_v, heads)], axis=1).astype(BF16)

    @pl.when(slot < PROMPT_BLOCKS)
    def _():
        at = pl.ds(pl.multiple_of(slot * BLOCK, BLOCK), BLOCK)
        dk_ref[at] += dk_own
        dv_ref[at] += dv_own

    @pl.when(slot >= PROMPT_BLOCKS)
    def _():
        o_ref[rows, q_cols:] = fold(dk_own, dv_own)

    @pl.when(slot == GROUP_BLOCKS - 1)
    def _():
        for s in range(PROMPT_BLOCKS):
            at = pl.ds(s * BLOCK, BLOCK)
            o_ref[own_rows(order_ref, first + s), q_cols:] = fold(dk_ref[at], dv_ref[at])


def whole(shape):
    return pl.BlockSpec(shape, lambda g, s, order: (0,) * len(shape))


def attend(qkv, order, heads):
    tokens, cols = qkv.shape
    prompt, q_cols = PROMPT_BLOCKS * BLOCK, heads * HEAD_DIM
    return pl.pallas_call(
        functools.partial(attend_kernel, heads),
        out_shape=jax.ShapeDtypeStruct((tokens, q_cols), BF16),
        grid_spec=pltpu.PrefetchScalarGridSpec(
            num_scalar_prefetch=1,
            grid=(tokens // (GROUP_BLOCKS * BLOCK), GROUP_BLOCKS),
            in_specs=[whole((tokens, cols))],
            out_specs=whole((tokens, q_cols)),
            scratch_shapes=[
                pltpu.VMEM((prompt, q_cols), BF16),
                pltpu.VMEM((prompt, q_cols), BF16),
                pltpu.VMEM((q_cols, prompt), BF16),
            ],
        ),
        cost_estimate=BRIEF,
        compiler_params=pltpu.CompilerParams(vmem_limit_bytes=40 << 20),
    )(order, qkv)


def attend_back(qkv, d_attended, order, heads):
    tokens, cols = qkv.shape
    prompt, q_cols = PROMPT_BLOCKS * BLOCK, heads * HEAD_DIM
    return pl.pallas_call(
        functools.partial(attend_back_kernel, heads),
        out_shape=jax.ShapeDtypeStruct((tokens, cols), BF16),
        grid_spec=pltpu.PrefetchScalarGridSpec(
            num_scalar_prefetch=1,
            grid=(tokens // (GROUP_BLOCKS * BLOCK), GROUP_BLOCKS),
            in_specs=[whole((tokens, cols)), whole((tokens, q_cols))],
            out_specs=whole((tokens, cols)),
            scratch_shapes=[
                pltpu.VMEM((prompt, q_cols), BF16),
                pltpu.VMEM((prompt, q_cols), BF16),
                pltpu.VMEM((q_cols, prompt), BF16),
                pltpu.VMEM((prompt, q_cols), F32),
                pltpu.VMEM((prompt, q_cols), F32),
            ],
        ),
        cost_estimate=BRIEF,
        compiler_params=pltpu.CompilerParams(vmem_limit_bytes=40 << 20),
    )(order, qkv, d_attended)


def total_kernel(grps, chips, x_ref, o_ref, over_z, over_plane, send, recv, psend, precv):
    grp = lax.axis_index("grp")
    chip, core = place()
    me = chip * 2 + core
    far = [lax.rem(grp + s, grps) for s in range(1, grps)]
    near = [(flip(chip, s, chips), c) for s in range(1, chips) for c in (core, 1 - core)]
    near = near + [(chip, 1 - core)]
    barrier = pltpu.get_barrier_semaphore()
    for g in far:
        pl.semaphore_signal(barrier, inc=1, device_id={"grp": g}, device_id_type=MESH)
    for to, c in near:
        pl.semaphore_signal(
            barrier, inc=1, device_id={"chip": to, "core": c}, device_id_type=MESH
        )
    pl.semaphore_wait(barrier, len(far) + len(near))
    copies = []
    for i, g in enumerate(far):
        copy = pltpu.make_async_remote_copy(
            src_ref=x_ref,
            dst_ref=over_z.at[grp],
            send_sem=send.at[i],
            recv_sem=recv.at[grp],
            device_id={"grp": g},
            device_id_type=MESH,
        )
        copy.start()
        copies.append(copy)
    over_z[grp] = x_ref[...]
    for g in far:
        pltpu.make_async_remote_copy(
            src_ref=x_ref,
            dst_ref=over_z.at[g],
            send_sem=send.at[0],
            recv_sem=recv.at[g],
            device_id={"grp": g},
            device_id_type=MESH,
        ).wait_recv()
    over_plane[me] = jnp.sum(over_z[...], axis=0)
    for i, (to, c) in enumerate(near):
        copy = remote(over_plane.at[me], over_plane.at[me], psend.at[i], precv.at[me], to, c)
        copy.start()
        copies.append(copy)
    for to, c in near:
        slot = to * 2 + c
        remote(over_plane.at[me], over_plane.at[slot], psend.at[0], precv.at[slot], to, c).wait_recv()
    for copy in copies:
        copy.wait_send()
    o_ref[...] = jnp.sum(over_plane[...], axis=0)


def total(x, grps, chips, call_id):
    devs = 2 * chips
    return pl.pallas_call(
        functools.partial(total_kernel, grps, chips),
        out_shape=jax.ShapeDtypeStruct(x.shape, F32),
        in_specs=[VMEM],
        out_specs=VMEM,
        scratch_shapes=[
            pltpu.VMEM((grps,) + x.shape, F32),
            pltpu.VMEM((devs,) + x.shape, F32),
            pltpu.SemaphoreType.DMA((grps,)),
            pltpu.SemaphoreType.DMA((grps,)),
            pltpu.SemaphoreType.DMA((devs,)),
            pltpu.SemaphoreType.DMA((devs,)),
        ],
        cost_estimate=BRIEF,
        compiler_params=pltpu.CompilerParams(collective_id=call_id, has_side_effects=True),
    )(x)


def params(axes, mib=56):
    return pltpu.CompilerParams(
        dimension_semantics=("arbitrary",) * axes, vmem_limit_bytes=mib << 20
    )


def tile_rows(count, limit):
    while count % limit:
        limit //= 2
    return limit


def widen_kernel(n_ref, w_ref, h_ref, ht_ref, s_ref, t_ref, nt_ref):
    values = n_ref[...]
    gate, up = matmul(values, w_ref[0, 0]), matmul(values, w_ref[0, 1])
    sig = 1.0 / (1.0 + jnp.exp(-gate))
    silu = gate * sig
    hidden = (silu * up).astype(BF16)
    h_ref[0] = hidden
    ht_ref[0] = hidden.T
    s_ref[0] = silu.astype(BF16)
    t_ref[0] = (up * (sig * (1.0 + gate * (1.0 - sig)))).astype(BF16)

    @pl.when(pl.program_id(1) == 0)
    def _():
        nt_ref[...] = values.T


def widen(normed, weights):
    tokens, depth = normed.shape
    shards, _, _, width = weights.shape
    rows = tile_rows(tokens, 1024)
    tall = jax.ShapeDtypeStruct((shards, tokens, width), BF16)
    tall_spec = pl.BlockSpec((1, rows, width), lambda r, s: (s, r, 0))
    return pl.pallas_call(
        widen_kernel,
        out_shape=(
            tall,
            jax.ShapeDtypeStruct((shards, width, tokens), BF16),
            tall,
            tall,
            jax.ShapeDtypeStruct((depth, tokens), BF16),
        ),
        grid=(tokens // rows, shards),
        in_specs=[
            pl.BlockSpec((rows, depth), lambda r, s: (r, 0)),
            pl.BlockSpec((1, 2, depth, width), lambda r, s: (s, 0, 0, 0)),
        ],
        out_specs=(
            tall_spec,
            pl.BlockSpec((1, width, rows), lambda r, s: (s, 0, r)),
            tall_spec,
            tall_spec,
            pl.BlockSpec((depth, rows), lambda r, s: (0, r)),
        ),
        cost_estimate=BRIEF,
        compiler_params=params(2),
    )(normed, weights)


def down_part_kernel(ht_ref, d_ref, o_ref):
    o_ref[0] = matmul(ht_ref[0], d_ref[...]).astype(BF16)


def down_part(hidden_t, upstream):
    shards, width, tokens = hidden_t.shape
    depth = upstream.shape[1]
    cols = tile_rows(depth, 1024)
    return pl.pallas_call(
        down_part_kernel,
        out_shape=jax.ShapeDtypeStruct((shards, width, depth), BF16),
        grid=(depth // cols, shards),
        in_specs=[
            pl.BlockSpec((1, width, tokens), lambda c, s: (s, 0, 0)),
            pl.BlockSpec((tokens, cols), lambda c, s: (0, c)),
        ],
        out_specs=pl.BlockSpec((1, width, cols), lambda c, s: (s, 0, c)),
        cost_estimate=BRIEF,
        compiler_params=params(2),
    )(hidden_t, upstream)


def mix_kernel(h_ref, w_ref, m_ref):
    mixed = None
    for i in range(w_ref.shape[0]):
        part = matmul(h_ref[i], w_ref[i])
        mixed = part if mixed is None else mixed + part
    m_ref[...] = mixed.astype(BF16)


def narrow_specs(hidden, weights):
    shards, tokens, width = hidden.shape
    depth = weights.shape[2]
    rows = tile_rows(tokens, 512)
    return (
        tokens // rows,
        pl.BlockSpec((shards, rows, width), lambda r: (0, r, 0)),
        pl.BlockSpec((rows, depth), lambda r: (r, 0)),
        pl.BlockSpec(weights.shape, lambda r: (0, 0, 0), pipeline_mode=pl.Buffered(1)),
    )


def mix(hidden, weights):
    steps, tall_spec, flat_spec, weight_spec = narrow_specs(hidden, weights)
    return pl.pallas_call(
        mix_kernel,
        out_shape=jax.ShapeDtypeStruct((hidden.shape[1], weights.shape[2]), BF16),
        grid=(steps,),
        in_specs=[tall_spec, weight_spec],
        out_specs=flat_spec,
        cost_estimate=BRIEF,
        compiler_params=params(1),
    )(hidden, weights)


def narrow_back_kernel(s_ref, t_ref, d_ref, w_ref, dg_ref, du_ref):
    upstream = d_ref[...]
    for i in range(w_ref.shape[0]):
        d_hidden = dot_nt(upstream, w_ref[i])
        dg_ref[i] = (d_hidden * t_ref[i].astype(F32)).astype(BF16)
        du_ref[i] = (d_hidden * s_ref[i].astype(F32)).astype(BF16)


def narrow_back(silu, slope, upstream, weights):
    steps, tall_spec, flat_spec, weight_spec = narrow_specs(silu, weights)
    tall = jax.ShapeDtypeStruct(silu.shape, BF16)
    return pl.pallas_call(
        narrow_back_kernel,
        out_shape=(tall, tall),
        grid=(steps,),
        in_specs=[tall_spec, tall_spec, flat_spec, weight_spec],
        out_specs=(tall_spec, tall_spec),
        cost_estimate=BRIEF,
        compiler_params=params(1),
    )(silu, slope, upstream, weights)


def widen_part_kernel(nt_ref, dg_ref, du_ref, o_ref):
    values = nt_ref[...]
    o_ref[0, 0] = matmul(values, dg_ref[0]).astype(BF16)
    o_ref[0, 1] = matmul(values, du_ref[0]).astype(BF16)


def widen_part(normed_t, d_gate, d_up):
    depth, tokens = normed_t.shape
    shards, _, width = d_gate.shape
    rows = tile_rows(depth, 1024)
    tall_spec = pl.BlockSpec((1, tokens, width), lambda r, s: (s, 0, 0))
    return pl.pallas_call(
        widen_part_kernel,
        out_shape=jax.ShapeDtypeStruct((shards, 2, depth, width), BF16),
        grid=(depth // rows, shards),
        in_specs=[pl.BlockSpec((rows, tokens), lambda r, s: (r, 0)), tall_spec, tall_spec],
        out_specs=pl.BlockSpec((1, 2, rows, width), lambda r, s: (s, 0, r, 0)),
        cost_estimate=BRIEF,
        compiler_params=params(2),
    )(normed_t, d_gate, d_up)


def widen_back_kernel(dg_ref, du_ref, w_ref, o_ref):
    total = None
    for i in range(w_ref.shape[0]):
        part = dot_nt(dg_ref[i], w_ref[i, 0]) + dot_nt(du_ref[i], w_ref[i, 1])
        total = part if total is None else total + part
    o_ref[...] = total.astype(BF16)


def widen_back(d_gate, d_up, weights):
    shards, tokens, width = d_gate.shape
    depth = weights.shape[2]
    rows = tile_rows(tokens, 512)
    tall_spec = pl.BlockSpec((shards, rows, width), lambda r: (0, r, 0))
    return pl.pallas_call(
        widen_back_kernel,
        out_shape=jax.ShapeDtypeStruct((tokens, depth), BF16),
        grid=(tokens // rows,),
        in_specs=[
            tall_spec,
            tall_spec,
            pl.BlockSpec(weights.shape, lambda r: (0, 0, 0, 0), pipeline_mode=pl.Buffered(1)),
        ],
        out_specs=pl.BlockSpec((rows, depth), lambda r: (r, 0)),
        cost_estimate=BRIEF,
        compiler_params=params(1),
    )(d_gate, d_up, weights)


def stage_step(stage):
    return jnp.where(stage == 0, 3, jnp.where(stage == 3, 0, stage))


def widen_back_rows(refs, rows):
    dg_ref, du_ref, w_ref = refs
    total = None
    for i in range(w_ref.shape[0]):
        part = dot_nt(dg_ref[i, rows], w_ref[i, 0]) + dot_nt(du_ref[i, rows], w_ref[i, 1])
        total = part if total is None else total + part
    return total


def project_back_rows(refs, rows):
    d_ref, w_ref = refs
    return dot_nt(d_ref[rows], w_ref[...])


def mix_rows(refs, rows):
    h_ref, w_ref = refs
    total = None
    for i in range(w_ref.shape[0]):
        part = matmul(h_ref[i, rows], w_ref[i])
        total = part if total is None else total + part
    return total


def twin_kernel(compute, count, *refs):
    operands, (o_ref, corner_ref, x_ref, y_ref) = refs[:count], refs[count : count + 4]
    acc, mine, away, twin, tsend, trecv = refs[count + 4 :]
    chip, core = place()
    stage = pl.program_id(0)
    rows = o_ref.shape[0]

    def copy(s):
        return remote(away.at[s], twin.at[s], tsend.at[s], trecv.at[s], chip, 1 - core)

    def both(s):
        copy(s).wait_recv()
        return mine[s].astype(F32) + twin[s].astype(F32)

    @pl.when(stage == 0)
    def _():
        greet([(chip, 1 - core)])

    target = jnp.bitwise_xor(chip, stage_step(stage)) * 2 * rows
    acc[...] = compute(operands, pl.ds(pl.multiple_of(target, 2 * rows), 2 * rows))
    mine[stage] = acc[pl.ds(pl.multiple_of(core * rows, rows), rows)].astype(BF16)
    away[stage] = acc[pl.ds(pl.multiple_of((1 - core) * rows, rows), rows)].astype(BF16)
    copy(stage).start()

    for s, part_ref in enumerate((corner_ref, x_ref, y_ref)):

        @pl.when(stage == s + 1)
        def _(s=s, part_ref=part_ref):
            part_ref[...] = both(s).astype(BF16)

    @pl.when(stage == 3)
    def _():
        o_ref[...] = both(3)
        for s in range(4):
            copy(s).wait_send()


def twin_reduce(compute, operands, rows, call_id):
    block = (rows, D)

    def held(shape):
        return pl.BlockSpec(shape, lambda s: (0,) * len(shape), pipeline_mode=pl.Buffered(1))

    return pl.pallas_call(
        functools.partial(twin_kernel, compute, len(operands)),
        out_shape=(jax.ShapeDtypeStruct(block, F32),) + (jax.ShapeDtypeStruct(block, BF16),) * 3,
        grid=(4,),
        in_specs=[held(x.shape) for x in operands],
        out_specs=(held(block),) * 4,
        scratch_shapes=[
            pltpu.VMEM((2 * rows, D), F32),
            pltpu.VMEM((4,) + block, BF16),
            pltpu.VMEM((4,) + block, BF16),
            pltpu.VMEM((4,) + block, BF16),
            pltpu.SemaphoreType.DMA((4,)),
            pltpu.SemaphoreType.DMA((4,)),
        ],
        cost_estimate=BRIEF,
        compiler_params=pltpu.CompilerParams(
            collective_id=call_id, has_side_effects=True, vmem_limit_bytes=60 << 20
        ),
    )(*operands)


def swap_others(parts):
    return tuple(swap_chips(part, step) for step, part in zip((3, 1, 2), parts))


def join(own, came):
    for part in came:
        own = own + part.astype(F32)
    return own


def entry_kernel(
    grps, chips, tok_ref, cot_ref, pack_ref, all_tok, all_cot, all_pack,
    tsend, trecv, tlocal, csend, crecv, clocal, psend, precv, plocal, zsend, zrecv, usend, dsend,
):
    grp = lax.axis_index("grp")
    chip, core = place()
    me = chip * 2 + core
    above, below = lax.rem(grp + 1, grps), lax.rem(grp + grps - 1, grps)
    near = [(flip(chip, s, chips), c) for s in range(1, chips) for c in (core, 1 - core)]
    near = near + [(chip, 1 - core)]
    barrier = pltpu.get_barrier_semaphore()
    for g in (above, below):
        pl.semaphore_signal(barrier, inc=1, device_id={"grp": g}, device_id_type=MESH)
    for to, c in near:
        pl.semaphore_signal(
            barrier, inc=1, device_id={"chip": to, "core": c}, device_id_type=MESH
        )
    pl.semaphore_wait(barrier, len(near) + 2)

    tok = Gather(chips, False, tok_ref, all_tok, tsend, trecv, tlocal)
    cot = Gather(chips, False, cot_ref, all_cot, csend, crecv, clocal)
    packs = []
    for i, (to, c) in enumerate(near):
        copy = remote(
            pack_ref.at[to * 2 + c], all_pack.at[grp, me], psend.at[i], precv.at[me], to, c
        )
        copy.start()
        packs.append(copy)
    mine = pltpu.make_async_copy(pack_ref.at[me], all_pack.at[grp, me], plocal)
    mine.start()
    tok.start()
    for to, c in near:
        slot = to * 2 + c
        remote(
            pack_ref.at[me], all_pack.at[grp, slot], psend.at[0], precv.at[slot], to, c
        ).wait_recv()
    mine.wait()

    def z_copy(block, sem, to):
        return pltpu.make_async_remote_copy(
            src_ref=all_pack.at[block],
            dst_ref=all_pack.at[block],
            send_sem=sem,
            recv_sem=zrecv.at[block],
            device_id={"grp": to},
            device_id_type=MESH,
        )

    has_above, has_below = grp + 1 < grps, grp > 0

    def send(step, block, up):
        @pl.when(has_above if up else has_below)
        def _():
            z_copy(block, (usend if up else dsend).at[step], above if up else below).start()

    def relay(step):
        low, high = grp - step, grp + step

        @pl.when(low >= 0)
        def _():
            z_copy(low, zsend, below).wait_recv()
            send(step, low, True)

        @pl.when(high < grps)
        def _():
            z_copy(high, zsend, above).wait_recv()
            send(step, high, False)

    send(0, grp, True)
    send(0, grp, False)
    tok.relay(0, 4)
    relay(1)
    cot.start()
    tok.relay(4, None)
    for step in range(2, grps - 1):
        relay(step)
    cot.relay(0, 4)
    if grps > 2:
        relay(grps - 1)
    cot.relay(4, None)
    tok.finish()
    cot.finish()
    for copy in packs:
        copy.wait_send()
    for step in range(grps):
        for up in (True, False):
            held = grp - step >= 0 if up else grp + step < grps

            @pl.when(held & (has_above if up else has_below))
            def _(step=step, up=up):
                block = grp - step if up else grp + step
                z_copy(block, (usend if up else dsend).at[step], above if up else below).wait_send()


def entry(tokens, cotangent, packed, grps, chips, call_id):
    devs = 2 * chips
    return pl.pallas_call(
        functools.partial(entry_kernel, grps, chips),
        out_shape=(
            jax.ShapeDtypeStruct((devs,) + tokens.shape, BF16),
            jax.ShapeDtypeStruct((devs,) + cotangent.shape, BF16),
            jax.ShapeDtypeStruct((grps,) + packed.shape, BF16),
        ),
        in_specs=[ANY] * 3,
        out_specs=(ANY,) * 3,
        scratch_shapes=gather_sems(chips)
        + gather_sems(chips)
        + [
            pltpu.SemaphoreType.DMA((devs,)),
            pltpu.SemaphoreType.DMA((devs,)),
            pltpu.SemaphoreType.DMA,
            pltpu.SemaphoreType.DMA,
            pltpu.SemaphoreType.DMA((grps,)),
            pltpu.SemaphoreType.DMA((grps,)),
            pltpu.SemaphoreType.DMA((grps,)),
        ],
        cost_estimate=BRIEF,
        compiler_params=pltpu.CompilerParams(collective_id=call_id, has_side_effects=True),
    )(tokens, cotangent, packed)


def project_kernel(used, x_ref, w_ref, n_ref, qkv_ref, gain_ref):
    @pl.when(pl.program_id(0) == 0)
    def _():
        gain_ref[...] = w_ref[:, used:].astype(F32).T[:8]

    values = x_ref[...].astype(F32)
    factor = lax.rsqrt(jnp.mean(values * values, axis=-1, keepdims=True) + EPSILON)
    normed = (values * factor * gain_ref[0:1]).astype(BF16)
    n_ref[...] = normed
    qkv_ref[...] = matmul(normed, w_ref[:, :used]).astype(BF16)


def project(tokens, packed, used):
    count, depth = tokens.shape
    rows = tile_rows(count, 256)
    return pl.pallas_call(
        functools.partial(project_kernel, used),
        out_shape=(
            jax.ShapeDtypeStruct((count, depth), BF16),
            jax.ShapeDtypeStruct((count, used), BF16),
            jax.ShapeDtypeStruct((8, depth), F32),
        ),
        grid=(count // rows,),
        in_specs=[
            pl.BlockSpec((rows, depth), lambda r: (r, 0)),
            pl.BlockSpec(packed.shape, lambda r: (0, 0)),
        ],
        out_specs=(
            pl.BlockSpec((rows, depth), lambda r: (r, 0)),
            pl.BlockSpec((rows, used), lambda r: (r, 0)),
            pl.BlockSpec((8, depth), lambda r: (0, 0)),
        ),
        cost_estimate=BRIEF,
        compiler_params=params(1),
    )(tokens, packed)


def norm_parts(values):
    factor = lax.rsqrt(jnp.mean(values * values, axis=-1, keepdims=True) + EPSILON)
    return factor


def norm_back(values, factor, gain, grad):
    scaled = gain * grad
    inner = jnp.mean(values * scaled, axis=-1, keepdims=True)
    return factor * scaled - values * (factor * factor * factor * inner), jnp.sum(
        grad * values * factor, axis=0
    )


def on_device(
    tokens,
    block_group,
    block_slot,
    attn_gain,
    w_query,
    w_key,
    w_value,
    w_out,
    mlp_gain,
    w_gate,
    w_up,
    w_down,
    cotangent,
):
    grps = lax.axis_size("grp")
    devs = lax.axis_size(PLANE)
    chips = devs // 2
    rows = tokens.shape[0]
    w_rows = w_query.shape[0]
    q_heads = HEADS // devs
    kv_heads = 1
    assert devs % KV_HEADS == 0
    kv_copies = max(1, devs // KV_HEADS)
    q_cols, kv_cols = q_heads * HEAD_DIM, kv_heads * HEAD_DIM
    row_blocks = rows // BLOCK * devs
    row_groups = row_blocks // GROUP_BLOCKS

    row_first = lax.axis_index("grp") * row_blocks
    keys = lax.dynamic_slice_in_dim(block_group, row_first, row_blocks) * GROUP_BLOCKS
    keys = keys + lax.dynamic_slice_in_dim(block_slot, row_first, row_blocks)
    rank = jnp.sum((keys[None, :] < keys[:, None]).astype(jnp.int32), axis=1)
    ids = jnp.arange(row_blocks, dtype=jnp.int32)
    order = jnp.sum(jnp.where(rank[None, :] == ids[:, None], ids[None, :], 0), axis=1)

    def kv_split(w):
        w = w.reshape(w_rows, devs // kv_copies, kv_cols)
        return jnp.repeat(w, kv_copies, axis=1) if kv_copies > 1 else w

    gains = jnp.stack([attn_gain, mlp_gain], axis=1)
    cols = D // 4
    room = cols - q_cols - 2 * kv_cols
    gains = jnp.pad(gains, ((0, 0), (0, room - 2)))
    gains = jnp.broadcast_to(gains[:, None, :], (w_rows, devs, room))
    packed = jnp.concatenate(
        [w_query.reshape(w_rows, devs, q_cols), kv_split(w_key), kv_split(w_value), gains], axis=2
    )
    packed = jnp.swapaxes(packed, 0, 1)
    used = q_cols + 2 * kv_cols
    out_full = gather(w_out[None], "grp")
    upstream = cotangent.astype(F32)
    d_branch_mlp = (RESID_MULT * upstream).astype(BF16)
    all_tokens, d_branch_mlp, packed = entry(tokens, d_branch_mlp, packed, grps, chips, 2)
    packed = packed.reshape(D, cols)
    normed_one, qkv, gains = project(all_tokens.reshape(devs * rows, D), packed, used)
    gain_one, gain_two, w_qkv = gains[0], gains[1], packed[:, :used]
    d_branch_mlp = d_branch_mlp.reshape(devs * rows, D)
    attended = attend(qkv, order, q_heads)
    attended = plane_exchange(
        attended, (rows, D), by_rows(rows), by_cols(q_cols), chips, 3
    )

    out_full = plane_gather(out_full, chips, 4, inner=True).reshape(D, D)
    layer_in = tokens.astype(F32)
    branch_attn = matmul(attended, out_full)
    residual = layer_in + RESID_MULT * branch_attn
    factor_two = norm_parts(residual)
    normed_two = (residual * factor_two * gain_two).astype(BF16)
    normed_two = plane_gather(normed_two, chips, 1).reshape(devs * rows, D)
    wide_w = gather(jnp.stack([w_gate, w_up])[None], "grp")
    down_w = gather(w_down[None], "grp")
    hidden, hidden_t, silu, slope, normed_t = widen(normed_two, wide_w)
    part_down = down_part(hidden_t, d_branch_mlp)
    part_down, hidden, silu = lax.optimization_barrier((part_down, hidden, silu))
    grad_down = scatter(part_down, "grp")
    d_gate, d_up = narrow_back(silu, slope, d_branch_mlp, down_w)
    if chips == 4:
        d_normed_two, *others = twin_reduce(widen_back_rows, (d_gate, d_up, wide_w), rows, 10)
        others, d_gate, d_up = lax.optimization_barrier((others, d_gate, d_up))
        others = swap_others(others)
        part_wide = widen_part(normed_t, d_gate, d_up)
        part_wide, hidden = lax.optimization_barrier((part_wide, hidden))
        branch_mlp, *shares = twin_reduce(mix_rows, (hidden, down_w), rows, 11)
        others, shares, part_wide = lax.optimization_barrier((others, shares, part_wide))
        grad_wide = scatter(part_wide, "grp")
        d_normed_two = join(d_normed_two, others)
        shares = swap_others(shares)
    else:
        part_wide = widen_part(normed_t, d_gate, d_up)
        part_wide, d_gate, d_up = lax.optimization_barrier((part_wide, d_gate, d_up))
        grad_wide = scatter(part_wide, "grp")
        d_normed_two = widen_back(d_gate, d_up, wide_w)
        d_normed_two = plane_reduce(d_normed_two.reshape(devs, rows, D), chips, 5)
        branch_mlp = mix(hidden, down_w)
        branch_mlp = plane_reduce(branch_mlp.reshape(devs, rows, D), chips, 5)

    d_residual_norm, d_gain_two = norm_back(residual, factor_two, gain_two, d_normed_two)
    d_residual = upstream + d_residual_norm
    d_branch_attn = (RESID_MULT * d_residual).astype(BF16)
    grad_out = over_rows(attended, d_branch_attn).astype(BF16)
    grad_out, d_branch_attn = lax.optimization_barrier((grad_out, d_branch_attn))
    if chips == 4:
        drift_out = Drift(grad_out.reshape(grps, 4, 2, w_rows, D), 1)
    d_attended = over_cols(d_branch_attn, out_full).astype(BF16)
    d_attended = plane_exchange(
        d_attended, (devs * rows, q_cols), by_cols(q_cols), by_rows(rows), chips, 7
    )
    if chips == 4:
        sent_out, d_attended, shares = lax.optimization_barrier(
            (drift_out.parts(), d_attended, shares)
        )
        branch_mlp = join(branch_mlp, shares)
        sent_out = Drift.send(sent_out)
    d_attended, grad_down = lax.optimization_barrier((d_attended, grad_down))
    d_qkv = attend_back(qkv, d_attended, order, q_heads)
    if chips == 4:
        sent_out, d_qkv = lax.optimization_barrier((sent_out, d_qkv))
        grad_out = drift_out.finish(sent_out).astype(BF16)
    else:
        grad_out = plane_reduce(
            grad_out.reshape(grps, devs, w_rows, D), chips, 6, dtype=BF16, inner=True
        )
    layer_out = residual + RESID_MULT * branch_mlp
    sent = over_rows(normed_one, d_qkv).astype(BF16)
    d_gain_one = jnp.sum(w_qkv.astype(F32) * sent.astype(F32), axis=1) / gain_one
    scaled_attn = RESID_MULT * branch_attn
    scaled_mlp = RESID_MULT * branch_mlp
    squares = jnp.stack(
        [
            jnp.sum(layer_out * layer_out),
            jnp.sum(scaled_attn * scaled_attn),
            jnp.sum(scaled_mlp * scaled_mlp),
        ]
    )
    totals = jnp.concatenate([d_gain_one, d_gain_two, squares, jnp.zeros((1021,), F32)])
    sent, d_qkv, totals = lax.optimization_barrier((sent, d_qkv, totals))
    totals = totals.reshape(8, 5 * D // 16)
    if chips == 4:
        d_normed_one, *others = twin_reduce(project_back_rows, (d_qkv, w_qkv), rows, 5)
        sent, grad_out, _ = lax.optimization_barrier((sent, grad_out, others[0]))
    sent, grad_out, grad_wide = lax.optimization_barrier((sent, grad_out, grad_wide))
    sent = scatter(sent, "grp")
    grad_out = scatter(grad_out, "grp").reshape(w_rows, D).astype(F32)
    if chips == 4:
        others, totals = lax.optimization_barrier((others, totals))
        others = swap_others(others)
        totals = total(totals, grps, chips, 8)
        others, totals = lax.optimization_barrier((others, totals))
        d_normed_one = join(d_normed_one, others)
    else:
        totals = total(totals, grps, chips, 8)
        d_normed_one = over_cols(d_qkv, w_qkv).astype(BF16).reshape(devs, rows, D)
        d_normed_one = plane_reduce(d_normed_one, chips, 5)
    d_input_norm, _ = norm_back(layer_in, norm_parts(layer_in), gain_one, d_normed_one)
    tokens_grad = (d_residual + d_input_norm).astype(BF16)
    sent = sent.reshape(devs, w_rows, q_cols + 2 * kv_cols)
    sent = plane_exchange(sent, sent.shape, by_slot, by_slot, chips, 9).astype(F32)

    def kv_join(g):
        g = g.reshape(devs // kv_copies, kv_copies, w_rows, kv_cols)
        g = jnp.sum(g, axis=1) if kv_copies > 1 else g[:, 0]
        return jnp.swapaxes(g, 0, 1).reshape(w_rows, KV_HEADS * HEAD_DIM)

    grad_query = jnp.swapaxes(sent[:, :, :q_cols], 0, 1).reshape(w_rows, D)
    grad_key = kv_join(sent[:, :, q_cols : q_cols + kv_cols])
    grad_value = kv_join(sent[:, :, q_cols + kv_cols : q_cols + 2 * kv_cols])

    totals = totals.reshape(-1)
    rms_stats = jnp.sqrt(totals[2 * D : 2 * D + 3] / (rows * grps * devs * D))
    gain_first = (lax.axis_index("grp") * devs + lax.axis_index(PLANE)) * w_rows
    gain_one_grad = lax.dynamic_slice(totals, (gain_first,), (w_rows,))
    gain_two_grad = lax.dynamic_slice(totals, (gain_first + D,), (w_rows,))
    return (
        layer_out.astype(BF16),
        tokens_grad,
        gain_one_grad,
        grad_query,
        grad_key,
        grad_value,
        grad_out,
        gain_two_grad,
        grad_wide[0, 0].astype(F32),
        grad_wide[0, 1].astype(F32),
        grad_down[0].astype(F32),
        rms_stats,
    )


def solution(mesh):
    shape = (mesh.shape["grp"], mesh.shape["blk"] // 2, 2)
    mesh = Mesh(mesh.devices.reshape(shape), EVERY)
    row, col, vec = P(EVERY, None), P(None, EVERY), P(EVERY)
    return jax.shard_map(
        on_device,
        mesh=mesh,
        in_specs=(row, P(), P(), vec, row, row, row, row, vec, col, col, row, row),
        out_specs=(row, row, vec, row, row, row, row, vec, col, col, row, P()),
        check_vma=False,
    )
```

```python
import functools

import jax
import jax.numpy as jnp
from jax import lax
from jax.experimental import pallas as pl
from jax.experimental.pallas import tpu as pltpu
from jax.sharding import Mesh
from jax.sharding import PartitionSpec as P

D = 2048
HEADS = 32
KV_HEADS = 8
HEAD_DIM = 64
BLOCK = 128
PROMPT_BLOCKS = 8
GROUP_BLOCKS = 16
PER_GROUP = HEADS // KV_HEADS

ATTN_MULT = 0.015625
RESID_MULT = 0.22
EPSILON = 1e-05
MASKED = -1e30

PLANE = ("chip", "core")
EVERY = ("grp", "chip", "core")
BF16 = jnp.bfloat16
F32 = jnp.float32


MESH = pl.DeviceIdType.MESH
BRIEF = pl.CostEstimate(flops=1000, bytes_accessed=1000, transcendentals=0)
ANY = pl.BlockSpec(memory_space=pl.ANY)
VMEM = pl.BlockSpec(memory_space=pltpu.VMEM)


def place():
    return lax.axis_index("chip"), lax.axis_index("core")


def flip(chip, step, chips):
    return jnp.bitwise_xor(chip, step) if chips == 4 else lax.rem(chip + step, chips)


def unflip(chip, step, chips):
    return jnp.bitwise_xor(chip, step) if chips == 4 else lax.rem(chip + chips - step, chips)


def greet(peers):
    barrier = pltpu.get_barrier_semaphore()
    for chip, core in peers:
        pl.semaphore_signal(
            barrier, inc=1, device_id={"chip": chip, "core": core}, device_id_type=MESH
        )
    pl.semaphore_wait(barrier, len(peers))


def remote(src, dst, send, recv, chip, core):
    return pltpu.make_async_remote_copy(
        src_ref=src,
        dst_ref=dst,
        send_sem=send,
        recv_sem=recv,
        device_id={"chip": chip, "core": core},
        device_id_type=MESH,
    )


class Gather:
    def __init__(self, chips, inner, x_ref, o_ref, send, recv, local):
        self.chips, self.inner, self.x, self.o = chips, inner, x_ref, o_ref
        self.send, self.recv, self.local = send, recv, local
        self.chip, self.core = place()
        self.half = x_ref.shape[0] // 2
        self.started = []

    def greet(self):
        steps = (1, 2) if self.chips == 4 else range(1, self.chips)
        peers = [(flip(self.chip, s, self.chips), self.core) for s in steps]
        greet(peers + [(self.chip, 1 - self.core)])

    def piece(self, slot, h):
        at = pl.ds(h * self.half, self.half)
        return self.o.at[at, slot] if self.inner else self.o.at[slot, at]

    def own(self, h):
        return self.x.at[pl.ds(h * self.half, self.half)]

    def slot(self, chip, core):
        return chip * 2 + core

    def push(self, src, slot, h, chip, core):
        i = len(self.started)
        copy = remote(src, self.piece(slot, h), self.send.at[i], self.recv.at[slot, h], chip, core)
        copy.start()
        self.started.append(copy)

    def wait_for(self, slot, h):
        remote(
            self.own(h), self.piece(slot, h), self.send.at[0], self.recv.at[slot, h],
            self.chip, 1 - self.core,
        ).wait_recv()

    def start(self):
        me = self.slot(self.chip, self.core)
        if self.chips == 4:
            for h, s in ((0, 1), (1, 2), (1, 1), (0, 2)):
                self.push(self.own(h), me, h, flip(self.chip, s, 4), self.core)
        else:
            for s in range(1, self.chips):
                for h in range(2):
                    self.push(self.own(h), me, h, flip(self.chip, s, self.chips), self.core)
        for h in range(2):
            self.push(self.own(h), me, h, self.chip, 1 - self.core)
        whole = self.o.at[:, me] if self.inner else self.o.at[me]
        self.mine = pltpu.make_async_copy(self.x, whole, self.local)
        self.mine.start()

    def relay(self, first=0, last=None):
        if self.chips == 4:
            plan = ((1, 0, 2), (2, 1, 1), (1, 1, 0), (2, 0, 0), (3, 0, 0), (3, 1, 0))
        else:
            plan = tuple((s, h, 0) for s in range(1, self.chips) for h in range(2))
        for s, h, onward in plan[first:last]:
            slot = self.slot(unflip(self.chip, s, self.chips), self.core)
            self.wait_for(slot, h)
            if onward:
                self.push(self.piece(slot, h), slot, h, flip(self.chip, onward, 4), self.core)
            self.push(self.piece(slot, h), slot, h, self.chip, 1 - self.core)

    def finish(self):
        for s in range(self.chips):
            slot = self.slot(unflip(self.chip, s, self.chips), 1 - self.core)
            for h in range(2):
                self.wait_for(slot, h)
        for copy in self.started:
            copy.wait_send()
        self.mine.wait()


def gather_sems(chips):
    return [
        pltpu.SemaphoreType.DMA((4 * chips + 4,)),
        pltpu.SemaphoreType.DMA((2 * chips, 2)),
        pltpu.SemaphoreType.DMA,
    ]


def gather_kernel(chips, inner, x_ref, o_ref, *sems):
    run = Gather(chips, inner, x_ref, o_ref, *sems)
    run.greet()
    run.start()
    run.relay()
    run.finish()


def plane_gather(x, chips, call_id, inner=False):
    devs = 2 * chips
    shape = (x.shape[0], devs) + x.shape[1:] if inner else (devs,) + x.shape
    return pl.pallas_call(
        functools.partial(gather_kernel, chips, inner),
        out_shape=jax.ShapeDtypeStruct(shape, x.dtype),
        in_specs=[ANY],
        out_specs=ANY,
        scratch_shapes=gather_sems(chips),
        cost_estimate=BRIEF,
        compiler_params=pltpu.CompilerParams(collective_id=call_id, has_side_effects=True),
    )(x)


def reduce_kernel(chips, inner, p_ref, o_ref, total, mine, twin, moved, corner, landed, lsem, tsend, trecv, msend, mrecv, csend, crecv):
    chip, core = place()
    sib = 1 - core
    half = (p_ref.shape[0] if inner else p_ref.shape[1]) // 2
    block = (lambda slot: p_ref.at[:, slot]) if inner else (lambda slot: p_ref.at[slot])
    steps = (1, 2) if chips == 4 else tuple(range(1, chips))
    peers = [(flip(chip, s, chips), core) for s in steps]
    greet(peers + [(chip, sib)])
    order = (3, 1, 2, 0) if chips == 4 else tuple(range(1, chips)) + (0,)
    loads, twins = {}, {}
    for s in order:
        to = flip(chip, s, chips) * 2
        twins[s] = remote(block(to + sib), twin.at[s], tsend.at[s], trecv.at[s], chip, sib)
        twins[s].start()
        loads[s] = pltpu.make_async_copy(block(to + core), mine.at[s], lsem.at[s])
        loads[s].start()

    def part(s, h):
        at = pl.ds(h * half, half)
        return mine[s, at].astype(F32) + twin[s, at].astype(F32)

    def ready(s):
        loads[s].wait()
        twins[s].wait_recv()

    sent = []
    if chips == 4:
        corners = []
        ready(3)
        for h, s in ((0, 1), (1, 2)):
            moved[3, pl.ds(h * half, half)] = part(3, h).astype(BF16)
            copy = remote(moved.at[3, pl.ds(h * half, half)], corner.at[h], csend.at[h], crecv.at[h], flip(chip, s, 4), core)
            copy.start()
            corners.append(copy)

        def send(s, h):
            at = pl.ds(h * half, half)
            copy = remote(moved.at[s, at], landed.at[s - 1, at], msend.at[s - 1, h], mrecv.at[s - 1, h], flip(chip, s, 4), core)
            copy.start()
            sent.append(copy)

        for s, h in ((1, 0), (2, 1)):
            ready(s)
            moved[s, pl.ds(h * half, half)] = part(s, h).astype(BF16)
            send(s, h)
        for s, h in ((2, 0), (1, 1)):
            corners[h].wait_recv()
            moved[s, pl.ds(h * half, half)] = (part(s, h) + corner[h].astype(F32)).astype(BF16)
            send(s, h)
        for copy in corners:
            copy.wait_send()
    else:
        for s in steps:
            ready(s)
            for h in range(2):
                at = pl.ds(h * half, half)
                moved[s, at] = part(s, h).astype(BF16)
                copy = remote(moved.at[s, at], landed.at[s - 1, at], msend.at[s - 1, h], mrecv.at[s - 1, h], flip(chip, s, chips), core)
                copy.start()
                sent.append(copy)
    ready(0)
    for h in range(2):
        total[pl.ds(h * half, half)] = part(0, h)
    for copy in sent:
        copy.wait()
    for s in steps[:-1]:
        total[...] += landed[s - 1].astype(F32)
    o_ref[...] = (total[...] + landed[steps[-1] - 1].astype(F32)).astype(o_ref.dtype)
    for s in order:
        twins[s].wait_send()


def plane_reduce(p, chips, call_id, dtype=F32, inner=False):
    block = (p.shape[0],) + p.shape[2:] if inner else p.shape[1:]
    steps = 2 if chips == 4 else chips - 1
    return pl.pallas_call(
        functools.partial(reduce_kernel, chips, inner),
        out_shape=jax.ShapeDtypeStruct(block, dtype),
        in_specs=[ANY],
        out_specs=VMEM,
        scratch_shapes=[
            pltpu.VMEM(block, F32),
            pltpu.VMEM((chips,) + block, BF16),
            pltpu.VMEM((chips,) + block, BF16),
            pltpu.VMEM((chips,) + block, BF16),
            pltpu.VMEM((2, block[0] // 2) + block[1:], BF16),
            pltpu.VMEM((steps,) + block, BF16),
            pltpu.SemaphoreType.DMA((chips,)),
            pltpu.SemaphoreType.DMA((chips,)),
            pltpu.SemaphoreType.DMA((chips,)),
            pltpu.SemaphoreType.DMA((steps, 2)),
            pltpu.SemaphoreType.DMA((steps, 2)),
            pltpu.SemaphoreType.DMA((2,)),
            pltpu.SemaphoreType.DMA((2,)),
        ],
        cost_estimate=BRIEF,
        compiler_params=pltpu.CompilerParams(
            collective_id=call_id, has_side_effects=True, vmem_limit_bytes=56 << 20
        ),
    )(p)


def swap_chips(values, step):
    return lax.ppermute(values, "chip", [(c, c ^ step) for c in range(4)])


class Drift:
    def __init__(self, pairs, axis):
        self.axis = axis
        self.chip, self.core = place()
        away = lax.dynamic_index_in_dim(pairs, 1 - self.core, axis + 1, keepdims=False)
        self.mine = lax.dynamic_index_in_dim(pairs, self.core, axis + 1, keepdims=False)
        self.twin = lax.ppermute(away, "core", [(0, 1), (1, 0)])

    def part(self, step):
        at = jnp.bitwise_xor(self.chip, step)
        mine = lax.dynamic_index_in_dim(self.mine, at, self.axis, keepdims=False)
        twin = lax.dynamic_index_in_dim(self.twin, at, self.axis, keepdims=False)
        return mine.astype(F32) + twin.astype(F32)

    def parts(self):
        return tuple(self.part(step).astype(BF16) for step in (1, 2, 3))

    def finish(self, came):
        total = self.part(0)
        for part in came:
            total = total + part.astype(F32)
        return total


def exchange_kernel(chips, cut, paste, x_ref, o_ref, send, recv, local):
    chip, core = place()
    me = chip * 2 + core
    peers = [(flip(chip, s, chips), c) for s in range(1, chips) for c in (core, 1 - core)]
    peers = peers + [(chip, 1 - core)]
    greet(peers)
    far = [p for p in ([3, 1, 2] if chips == 4 else range(1, chips))]
    order = [(flip(chip, s, chips), c) for s in far for c in (core, 1 - core)] + [(chip, 1 - core)]
    copies = []
    for i, (to, c) in enumerate(order):
        copy = remote(cut(x_ref, to * 2 + c), paste(o_ref, me), send.at[i], recv.at[me], to, c)
        copy.start()
        copies.append(copy)
    mine = pltpu.make_async_copy(cut(x_ref, me), paste(o_ref, me), local)
    mine.start()
    for s in far:
        for c in (core, 1 - core):
            slot = unflip(chip, s, chips) * 2 + c
            remote(cut(x_ref, me), paste(o_ref, slot), send.at[0], recv.at[slot], chip, 1 - core).wait_recv()
    slot = chip * 2 + 1 - core
    remote(cut(x_ref, me), paste(o_ref, slot), send.at[0], recv.at[slot], chip, 1 - core).wait_recv()
    for copy in copies:
        copy.wait_send()
    mine.wait()


def plane_exchange(x, shape, cut, paste, chips, call_id):
    return pl.pallas_call(
        functools.partial(exchange_kernel, chips, cut, paste),
        out_shape=jax.ShapeDtypeStruct(shape, x.dtype),
        in_specs=[ANY],
        out_specs=ANY,
        scratch_shapes=[
            pltpu.SemaphoreType.DMA((2 * chips,)),
            pltpu.SemaphoreType.DMA((2 * chips,)),
            pltpu.SemaphoreType.DMA,
        ],
        cost_estimate=BRIEF,
        compiler_params=pltpu.CompilerParams(collective_id=call_id, has_side_effects=True),
    )(x)


def by_slot(ref, dev):
    return ref.at[dev]


def by_rows(rows):
    return lambda ref, dev: ref.at[pl.ds(pl.multiple_of(dev * rows, rows), rows)]


def by_cols(cols):
    return lambda ref, dev: ref.at[:, pl.ds(pl.multiple_of(dev * cols, cols), cols)]


def matmul(left, right):
    return jnp.dot(left, right, preferred_element_type=F32)


def over_rows(left, right):
    return lax.dot_general(left, right, (((0,), (0,)), ((), ())), preferred_element_type=F32)


def over_cols(left, right):
    return lax.dot_general(left, right, (((1,), (1,)), ((), ())), preferred_element_type=F32)


def gather(values, axes, axis=0):
    return lax.all_gather(values, axes, axis=axis, tiled=True)


def scatter(values, axes, axis=0):
    return lax.psum_scatter(values, axes, scatter_dimension=axis, tiled=True)


def dot_nt(left, right):
    return lax.dot_general(left, right, (((1,), (1,)), ((), ())), preferred_element_type=F32)


def head_stack(values, heads):
    col_head = lax.broadcasted_iota(jnp.int32, values.shape, 1) // HEAD_DIM
    return jnp.concatenate(
        [jnp.where(col_head == h, values, jnp.zeros_like(values)) for h in range(heads)], axis=0
    )


def head_pick(stacked, heads):
    rows = stacked.shape[0] // heads
    col_head = lax.broadcasted_iota(jnp.int32, (rows, stacked.shape[1]), 1) // HEAD_DIM
    total = jnp.zeros((rows, stacked.shape[1]), F32)
    for h in range(heads):
        total = jnp.where(col_head == h, stacked[h * rows : (h + 1) * rows], total)
    return total


def head_fold(values, heads):
    total = values[:, :HEAD_DIM]
    for h in range(1, heads):
        total = total + values[:, h * HEAD_DIM : (h + 1) * HEAD_DIM]
    return total


def repeat_heads(values, heads):
    return jnp.concatenate([values] * heads, axis=1)


def own_rows(order_ref, slot):
    return pl.ds(pl.multiple_of(order_ref[slot] * BLOCK, BLOCK), BLOCK)


def load_prompt(heads, order_ref, qkv_ref, k_ref, v_ref, first):
    q_cols = heads * HEAD_DIM
    for s in range(PROMPT_BLOCKS):
        pair = qkv_ref[own_rows(order_ref, first + s), q_cols:]
        at = pl.ds(s * BLOCK, BLOCK)
        k_ref[at] = repeat_heads(pair[:, :HEAD_DIM], heads)
        v_ref[at] = repeat_heads(pair[:, HEAD_DIM:], heads)


def soft_parts(heads, slot, q_stack, k_far, k_own):
    far = dot_nt(k_far, q_stack)
    own = dot_nt(k_own, q_stack)
    limit = jnp.minimum(slot, PROMPT_BLOCKS) * BLOCK
    far = jnp.where(lax.broadcasted_iota(jnp.int32, far.shape, 0) < limit, far, MASKED)
    key = lax.broadcasted_iota(jnp.int32, own.shape, 0)
    row = lax.broadcasted_iota(jnp.int32, own.shape, 1) % BLOCK
    own = jnp.where(key <= row, own, MASKED)
    peak = jnp.maximum(jnp.max(far, axis=0, keepdims=True), jnp.max(own, axis=0, keepdims=True))
    far, own = jnp.exp(far - peak), jnp.exp(own - peak)
    scale = 1.0 / (jnp.sum(far, axis=0, keepdims=True) + jnp.sum(own, axis=0, keepdims=True))
    return far * scale, own * scale


def scaled_stack(q, heads):
    return head_stack((q.astype(F32) * ATTN_MULT).astype(BF16), heads)


def attend_kernel(heads, order_ref, qkv_ref, o_ref, k_ref, v_ref, vt_ref):
    first, slot = pl.program_id(0) * GROUP_BLOCKS, pl.program_id(1)
    q_cols = heads * HEAD_DIM

    @pl.when(slot == 0)
    def _():
        load_prompt(heads, order_ref, qkv_ref, k_ref, v_ref, first)
        vt_ref[...] = v_ref[...].astype(F32).T.astype(BF16)

    rows = own_rows(order_ref, first + slot)
    mine = qkv_ref[rows, :]
    k_own = repeat_heads(mine[:, q_cols : q_cols + HEAD_DIM], heads)
    v_own = repeat_heads(mine[:, q_cols + HEAD_DIM :], heads)
    far, own = soft_parts(heads, slot, scaled_stack(mine[:, :q_cols], heads), k_ref[...], k_own)
    mixed = matmul(vt_ref[...], far.astype(BF16))
    mixed += matmul(v_own.astype(F32).T.astype(BF16), own.astype(BF16))
    o_ref[rows, :] = head_pick(mixed.T, heads).astype(BF16)


def attend_back_kernel(
    heads, order_ref, qkv_ref, d_ref, o_ref, k_ref, v_ref, kt_ref, dk_ref, dv_ref
):
    first, slot = pl.program_id(0) * GROUP_BLOCKS, pl.program_id(1)
    q_cols = heads * HEAD_DIM

    @pl.when(slot == 0)
    def _():
        load_prompt(heads, order_ref, qkv_ref, k_ref, v_ref, first)
        kt_ref[...] = k_ref[...].astype(F32).T.astype(BF16)
        dk_ref[...] = jnp.zeros_like(dk_ref)
        dv_ref[...] = jnp.zeros_like(dv_ref)

    rows = own_rows(order_ref, first + slot)
    mine = qkv_ref[rows, :]
    k_own = repeat_heads(mine[:, q_cols : q_cols + HEAD_DIM], heads)
    v_own = repeat_heads(mine[:, q_cols + HEAD_DIM :], heads)
    q_stack = scaled_stack(mine[:, :q_cols], heads)
    d_stack = head_stack(d_ref[rows, :], heads)
    far, own = soft_parts(heads, slot, q_stack, k_ref[...], k_own)
    d_far, d_own = dot_nt(v_ref[...], d_stack), dot_nt(v_own, d_stack)
    mean = jnp.sum(far * d_far, axis=0, keepdims=True) + jnp.sum(own * d_own, axis=0, keepdims=True)
    d_far = (far * (d_far - mean)).astype(BF16)
    d_own = (own * (d_own - mean)).astype(BF16)
    dv_ref[...] += matmul(far.astype(BF16), d_stack)
    dk_ref[...] += matmul(d_far, q_stack)
    dv_own = matmul(own.astype(BF16), d_stack)
    dk_own = matmul(d_own, q_stack)
    d_q = matmul(kt_ref[...], d_far) + matmul(k_own.astype(F32).T.astype(BF16), d_own)
    o_ref[rows, :q_cols] = (head_pick(d_q.T, heads) * ATTN_MULT).astype(BF16)

    def fold(d_k, d_v):
        return jnp.concatenate([head_fold(d_k, heads), head_fold(d_v, heads)], axis=1).astype(BF16)

    @pl.when(slot < PROMPT_BLOCKS)
    def _():
        at = pl.ds(pl.multiple_of(slot * BLOCK, BLOCK), BLOCK)
        dk_ref[at] += dk_own
        dv_ref[at] += dv_own

    @pl.when(slot >= PROMPT_BLOCKS)
    def _():
        o_ref[rows, q_cols:] = fold(dk_own, dv_own)

    @pl.when(slot == GROUP_BLOCKS - 1)
    def _():
        for s in range(PROMPT_BLOCKS):
            at = pl.ds(s * BLOCK, BLOCK)
            o_ref[own_rows(order_ref, first + s), q_cols:] = fold(dk_ref[at], dv_ref[at])


def whole(shape):
    return pl.BlockSpec(shape, lambda g, s, order: (0,) * len(shape))


def attend(qkv, order, heads):
    tokens, cols = qkv.shape
    prompt, q_cols = PROMPT_BLOCKS * BLOCK, heads * HEAD_DIM
    return pl.pallas_call(
        functools.partial(attend_kernel, heads),
        out_shape=jax.ShapeDtypeStruct((tokens, q_cols), BF16),
        grid_spec=pltpu.PrefetchScalarGridSpec(
            num_scalar_prefetch=1,
            grid=(tokens // (GROUP_BLOCKS * BLOCK), GROUP_BLOCKS),
            in_specs=[whole((tokens, cols))],
            out_specs=whole((tokens, q_cols)),
            scratch_shapes=[
                pltpu.VMEM((prompt, q_cols), BF16),
                pltpu.VMEM((prompt, q_cols), BF16),
                pltpu.VMEM((q_cols, prompt), BF16),
            ],
        ),
        cost_estimate=BRIEF,
        compiler_params=pltpu.CompilerParams(vmem_limit_bytes=40 << 20),
    )(order, qkv)


def attend_back(qkv, d_attended, order, heads):
    tokens, cols = qkv.shape
    prompt, q_cols = PROMPT_BLOCKS * BLOCK, heads * HEAD_DIM
    return pl.pallas_call(
        functools.partial(attend_back_kernel, heads),
        out_shape=jax.ShapeDtypeStruct((tokens, cols), BF16),
        grid_spec=pltpu.PrefetchScalarGridSpec(
            num_scalar_prefetch=1,
            grid=(tokens // (GROUP_BLOCKS * BLOCK), GROUP_BLOCKS),
            in_specs=[whole((tokens, cols)), whole((tokens, q_cols))],
            out_specs=whole((tokens, cols)),
            scratch_shapes=[
                pltpu.VMEM((prompt, q_cols), BF16),
                pltpu.VMEM((prompt, q_cols), BF16),
                pltpu.VMEM((q_cols, prompt), BF16),
                pltpu.VMEM((prompt, q_cols), F32),
                pltpu.VMEM((prompt, q_cols), F32),
            ],
        ),
        cost_estimate=BRIEF,
        compiler_params=pltpu.CompilerParams(vmem_limit_bytes=40 << 20),
    )(order, qkv, d_attended)


def total_kernel(grps, chips, x_ref, o_ref, over_z, over_plane, send, recv, psend, precv):
    grp = lax.axis_index("grp")
    chip, core = place()
    me = chip * 2 + core
    far = [lax.rem(grp + s, grps) for s in range(1, grps)]
    near = [(flip(chip, s, chips), c) for s in range(1, chips) for c in (core, 1 - core)]
    near = near + [(chip, 1 - core)]
    barrier = pltpu.get_barrier_semaphore()
    for g in far:
        pl.semaphore_signal(barrier, inc=1, device_id={"grp": g}, device_id_type=MESH)
    for to, c in near:
        pl.semaphore_signal(
            barrier, inc=1, device_id={"chip": to, "core": c}, device_id_type=MESH
        )
    pl.semaphore_wait(barrier, len(far) + len(near))
    copies = []
    for i, g in enumerate(far):
        copy = pltpu.make_async_remote_copy(
            src_ref=x_ref,
            dst_ref=over_z.at[grp],
            send_sem=send.at[i],
            recv_sem=recv.at[grp],
            device_id={"grp": g},
            device_id_type=MESH,
        )
        copy.start()
        copies.append(copy)
    over_z[grp] = x_ref[...]
    for g in far:
        pltpu.make_async_remote_copy(
            src_ref=x_ref,
            dst_ref=over_z.at[g],
            send_sem=send.at[0],
            recv_sem=recv.at[g],
            device_id={"grp": g},
            device_id_type=MESH,
        ).wait_recv()
    over_plane[me] = jnp.sum(over_z[...], axis=0)
    for i, (to, c) in enumerate(near):
        copy = remote(over_plane.at[me], over_plane.at[me], psend.at[i], precv.at[me], to, c)
        copy.start()
        copies.append(copy)
    for to, c in near:
        slot = to * 2 + c
        remote(over_plane.at[me], over_plane.at[slot], psend.at[0], precv.at[slot], to, c).wait_recv()
    for copy in copies:
        copy.wait_send()
    o_ref[...] = jnp.sum(over_plane[...], axis=0)


def total(x, grps, chips, call_id):
    devs = 2 * chips
    return pl.pallas_call(
        functools.partial(total_kernel, grps, chips),
        out_shape=jax.ShapeDtypeStruct(x.shape, F32),
        in_specs=[VMEM],
        out_specs=VMEM,
        scratch_shapes=[
            pltpu.VMEM((grps,) + x.shape, F32),
            pltpu.VMEM((devs,) + x.shape, F32),
            pltpu.SemaphoreType.DMA((grps,)),
            pltpu.SemaphoreType.DMA((grps,)),
            pltpu.SemaphoreType.DMA((devs,)),
            pltpu.SemaphoreType.DMA((devs,)),
        ],
        cost_estimate=BRIEF,
        compiler_params=pltpu.CompilerParams(collective_id=call_id, has_side_effects=True),
    )(x)


def params(axes, mib=56):
    return pltpu.CompilerParams(
        dimension_semantics=("arbitrary",) * axes, vmem_limit_bytes=mib << 20
    )


def tile_rows(count, limit):
    while count % limit:
        limit //= 2
    return limit


def widen_kernel(n_ref, w_ref, h_ref, ht_ref, s_ref, t_ref, nt_ref):
    values = n_ref[...]
    gate, up = matmul(values, w_ref[0, 0]), matmul(values, w_ref[0, 1])
    sig = 1.0 / (1.0 + jnp.exp(-gate))
    silu = gate * sig
    hidden = (silu * up).astype(BF16)
    h_ref[0] = hidden
    ht_ref[0] = hidden.T
    s_ref[0] = silu.astype(BF16)
    t_ref[0] = (up * (sig * (1.0 + gate * (1.0 - sig)))).astype(BF16)

    @pl.when(pl.program_id(1) == 0)
    def _():
        nt_ref[...] = values.T


def widen(normed, weights):
    tokens, depth = normed.shape
    shards, _, _, width = weights.shape
    rows = tile_rows(tokens, 1024)
    tall = jax.ShapeDtypeStruct((shards, tokens, width), BF16)
    tall_spec = pl.BlockSpec((1, rows, width), lambda r, s: (s, r, 0))
    return pl.pallas_call(
        widen_kernel,
        out_shape=(
            tall,
            jax.ShapeDtypeStruct((shards, width, tokens), BF16),
            tall,
            tall,
            jax.ShapeDtypeStruct((depth, tokens), BF16),
        ),
        grid=(tokens // rows, shards),
        in_specs=[
            pl.BlockSpec((rows, depth), lambda r, s: (r, 0)),
            pl.BlockSpec((1, 2, depth, width), lambda r, s: (s, 0, 0, 0)),
        ],
        out_specs=(
            tall_spec,
            pl.BlockSpec((1, width, rows), lambda r, s: (s, 0, r)),
            tall_spec,
            tall_spec,
            pl.BlockSpec((depth, rows), lambda r, s: (0, r)),
        ),
        cost_estimate=BRIEF,
        compiler_params=params(2),
    )(normed, weights)


def down_part_kernel(ht_ref, d_ref, o_ref):
    o_ref[0] = matmul(ht_ref[0], d_ref[...]).astype(BF16)


def down_part(hidden_t, upstream):
    shards, width, tokens = hidden_t.shape
    depth = upstream.shape[1]
    cols = tile_rows(depth, 1024)
    return pl.pallas_call(
        down_part_kernel,
        out_shape=jax.ShapeDtypeStruct((shards, width, depth), BF16),
        grid=(depth // cols, shards),
        in_specs=[
            pl.BlockSpec((1, width, tokens), lambda c, s: (s, 0, 0)),
            pl.BlockSpec((tokens, cols), lambda c, s: (0, c)),
        ],
        out_specs=pl.BlockSpec((1, width, cols), lambda c, s: (s, 0, c)),
        cost_estimate=BRIEF,
        compiler_params=params(2),
    )(hidden_t, upstream)


def mix_kernel(h_ref, w_ref, m_ref):
    mixed = None
    for i in range(w_ref.shape[0]):
        part = matmul(h_ref[i], w_ref[i])
        mixed = part if mixed is None else mixed + part
    m_ref[...] = mixed.astype(BF16)


def narrow_specs(hidden, weights):
    shards, tokens, width = hidden.shape
    depth = weights.shape[2]
    rows = tile_rows(tokens, 512)
    return (
        tokens // rows,
        pl.BlockSpec((shards, rows, width), lambda r: (0, r, 0)),
        pl.BlockSpec((rows, depth), lambda r: (r, 0)),
        pl.BlockSpec(weights.shape, lambda r: (0, 0, 0), pipeline_mode=pl.Buffered(1)),
    )


def mix(hidden, weights):
    steps, tall_spec, flat_spec, weight_spec = narrow_specs(hidden, weights)
    return pl.pallas_call(
        mix_kernel,
        out_shape=jax.ShapeDtypeStruct((hidden.shape[1], weights.shape[2]), BF16),
        grid=(steps,),
        in_specs=[tall_spec, weight_spec],
        out_specs=flat_spec,
        cost_estimate=BRIEF,
        compiler_params=params(1),
    )(hidden, weights)


def narrow_back_kernel(s_ref, t_ref, d_ref, w_ref, dg_ref, du_ref):
    upstream = d_ref[...]
    for i in range(w_ref.shape[0]):
        d_hidden = dot_nt(upstream, w_ref[i])
        dg_ref[i] = (d_hidden * t_ref[i].astype(F32)).astype(BF16)
        du_ref[i] = (d_hidden * s_ref[i].astype(F32)).astype(BF16)


def narrow_back(silu, slope, upstream, weights):
    steps, tall_spec, flat_spec, weight_spec = narrow_specs(silu, weights)
    tall = jax.ShapeDtypeStruct(silu.shape, BF16)
    return pl.pallas_call(
        narrow_back_kernel,
        out_shape=(tall, tall),
        grid=(steps,),
        in_specs=[tall_spec, tall_spec, flat_spec, weight_spec],
        out_specs=(tall_spec, tall_spec),
        cost_estimate=BRIEF,
        compiler_params=params(1),
    )(silu, slope, upstream, weights)


def widen_part_kernel(nt_ref, dg_ref, du_ref, o_ref):
    values = nt_ref[...]
    o_ref[0, 0] = matmul(values, dg_ref[0]).astype(BF16)
    o_ref[0, 1] = matmul(values, du_ref[0]).astype(BF16)


def widen_part(normed_t, d_gate, d_up):
    depth, tokens = normed_t.shape
    shards, _, width = d_gate.shape
    rows = tile_rows(depth, 1024)
    tall_spec = pl.BlockSpec((1, tokens, width), lambda r, s: (s, 0, 0))
    return pl.pallas_call(
        widen_part_kernel,
        out_shape=jax.ShapeDtypeStruct((shards, 2, depth, width), BF16),
        grid=(depth // rows, shards),
        in_specs=[pl.BlockSpec((rows, tokens), lambda r, s: (r, 0)), tall_spec, tall_spec],
        out_specs=pl.BlockSpec((1, 2, rows, width), lambda r, s: (s, 0, r, 0)),
        cost_estimate=BRIEF,
        compiler_params=params(2),
    )(normed_t, d_gate, d_up)


def widen_back_kernel(dg_ref, du_ref, w_ref, o_ref):
    total = None
    for i in range(w_ref.shape[0]):
        part = dot_nt(dg_ref[i], w_ref[i, 0]) + dot_nt(du_ref[i], w_ref[i, 1])
        total = part if total is None else total + part
    o_ref[...] = total.astype(BF16)


def widen_back(d_gate, d_up, weights):
    shards, tokens, width = d_gate.shape
    depth = weights.shape[2]
    rows = tile_rows(tokens, 512)
    tall_spec = pl.BlockSpec((shards, rows, width), lambda r: (0, r, 0))
    return pl.pallas_call(
        widen_back_kernel,
        out_shape=jax.ShapeDtypeStruct((tokens, depth), BF16),
        grid=(tokens // rows,),
        in_specs=[
            tall_spec,
            tall_spec,
            pl.BlockSpec(weights.shape, lambda r: (0, 0, 0, 0), pipeline_mode=pl.Buffered(1)),
        ],
        out_specs=pl.BlockSpec((rows, depth), lambda r: (r, 0)),
        cost_estimate=BRIEF,
        compiler_params=params(1),
    )(d_gate, d_up, weights)


def stage_step(stage):
    return jnp.where(stage == 0, 3, jnp.where(stage == 3, 0, stage))


def widen_back_rows(refs, rows):
    dg_ref, du_ref, w_ref = refs
    total = None
    for i in range(w_ref.shape[0]):
        part = dot_nt(dg_ref[i, rows], w_ref[i, 0]) + dot_nt(du_ref[i, rows], w_ref[i, 1])
        total = part if total is None else total + part
    return total


def project_back_rows(refs, rows):
    d_ref, w_ref = refs
    return dot_nt(d_ref[rows], w_ref[...])


def mix_rows(refs, rows):
    h_ref, w_ref = refs
    total = None
    for i in range(w_ref.shape[0]):
        part = matmul(h_ref[i, rows], w_ref[i])
        total = part if total is None else total + part
    return total


def twin_kernel(compute, count, *refs):
    operands, (o_ref, corner_ref, x_ref, y_ref) = refs[:count], refs[count : count + 4]
    acc, mine, away, twin, tsend, trecv = refs[count + 4 :]
    chip, core = place()
    stage = pl.program_id(0)
    rows = o_ref.shape[0]

    def copy(s):
        return remote(away.at[s], twin.at[s], tsend.at[s], trecv.at[s], chip, 1 - core)

    def both(s):
        copy(s).wait_recv()
        return mine[s].astype(F32) + twin[s].astype(F32)

    @pl.when(stage == 0)
    def _():
        greet([(chip, 1 - core)])

    target = jnp.bitwise_xor(chip, stage_step(stage)) * 2 * rows
    acc[...] = compute(operands, pl.ds(pl.multiple_of(target, 2 * rows), 2 * rows))
    mine[stage] = acc[pl.ds(pl.multiple_of(core * rows, rows), rows)].astype(BF16)
    away[stage] = acc[pl.ds(pl.multiple_of((1 - core) * rows, rows), rows)].astype(BF16)
    copy(stage).start()

    for s, part_ref in enumerate((corner_ref, x_ref, y_ref)):

        @pl.when(stage == s + 1)
        def _(s=s, part_ref=part_ref):
            part_ref[...] = both(s).astype(BF16)

    @pl.when(stage == 3)
    def _():
        o_ref[...] = both(3)
        for s in range(4):
            copy(s).wait_send()


def twin_reduce(compute, operands, rows, call_id):
    block = (rows, D)

    def held(shape):
        return pl.BlockSpec(shape, lambda s: (0,) * len(shape), pipeline_mode=pl.Buffered(1))

    return pl.pallas_call(
        functools.partial(twin_kernel, compute, len(operands)),
        out_shape=(jax.ShapeDtypeStruct(block, F32),) + (jax.ShapeDtypeStruct(block, BF16),) * 3,
        grid=(4,),
        in_specs=[held(x.shape) for x in operands],
        out_specs=(held(block),) * 4,
        scratch_shapes=[
            pltpu.VMEM((2 * rows, D), F32),
            pltpu.VMEM((4,) + block, BF16),
            pltpu.VMEM((4,) + block, BF16),
            pltpu.VMEM((4,) + block, BF16),
            pltpu.SemaphoreType.DMA((4,)),
            pltpu.SemaphoreType.DMA((4,)),
        ],
        cost_estimate=BRIEF,
        compiler_params=pltpu.CompilerParams(
            collective_id=call_id, has_side_effects=True, vmem_limit_bytes=60 << 20
        ),
    )(*operands)


def swap_others(parts):
    return tuple(swap_chips(part, step) for step, part in zip((3, 1, 2), parts))


def join(own, came):
    for part in came:
        own = own + part.astype(F32)
    return own


def entry_kernel(
    grps, chips, tok_ref, cot_ref, pack_ref, all_tok, all_cot, all_pack,
    tsend, trecv, tlocal, csend, crecv, clocal, psend, precv, plocal, zsend, zrecv, usend, dsend,
):
    grp = lax.axis_index("grp")
    chip, core = place()
    me = chip * 2 + core
    above, below = lax.rem(grp + 1, grps), lax.rem(grp + grps - 1, grps)
    near = [(flip(chip, s, chips), c) for s in range(1, chips) for c in (core, 1 - core)]
    near = near + [(chip, 1 - core)]
    barrier = pltpu.get_barrier_semaphore()
    for g in (above, below):
        pl.semaphore_signal(barrier, inc=1, device_id={"grp": g}, device_id_type=MESH)
    for to, c in near:
        pl.semaphore_signal(
            barrier, inc=1, device_id={"chip": to, "core": c}, device_id_type=MESH
        )
    pl.semaphore_wait(barrier, len(near) + 2)

    tok = Gather(chips, False, tok_ref, all_tok, tsend, trecv, tlocal)
    cot = Gather(chips, False, cot_ref, all_cot, csend, crecv, clocal)
    packs = []
    for i, (to, c) in enumerate(near):
        copy = remote(
            pack_ref.at[to * 2 + c], all_pack.at[grp, me], psend.at[i], precv.at[me], to, c
        )
        copy.start()
        packs.append(copy)
    mine = pltpu.make_async_copy(pack_ref.at[me], all_pack.at[grp, me], plocal)
    mine.start()
    tok.start()
    for to, c in near:
        slot = to * 2 + c
        remote(
            pack_ref.at[me], all_pack.at[grp, slot], psend.at[0], precv.at[slot], to, c
        ).wait_recv()
    mine.wait()

    def z_copy(block, sem, to):
        return pltpu.make_async_remote_copy(
            src_ref=all_pack.at[block],
            dst_ref=all_pack.at[block],
            send_sem=sem,
            recv_sem=zrecv.at[block],
            device_id={"grp": to},
            device_id_type=MESH,
        )

    has_above, has_below = grp + 1 < grps, grp > 0

    def send(step, block, up):
        @pl.when(has_above if up else has_below)
        def _():
            z_copy(block, (usend if up else dsend).at[step], above if up else below).start()

    def relay(step):
        low, high = grp - step, grp + step

        @pl.when(low >= 0)
        def _():
            z_copy(low, zsend, below).wait_recv()
            send(step, low, True)

        @pl.when(high < grps)
        def _():
            z_copy(high, zsend, above).wait_recv()
            send(step, high, False)

    send(0, grp, True)
    send(0, grp, False)
    tok.relay(0, 4)
    relay(1)
    cot.start()
    tok.relay(4, None)
    for step in range(2, grps - 1):
        relay(step)
    cot.relay(0, 4)
    if grps > 2:
        relay(grps - 1)
    cot.relay(4, None)
    tok.finish()
    cot.finish()
    for copy in packs:
        copy.wait_send()
    for step in range(grps):
        for up in (True, False):
            held = grp - step >= 0 if up else grp + step < grps

            @pl.when(held & (has_above if up else has_below))
            def _(step=step, up=up):
                block = grp - step if up else grp + step
                z_copy(block, (usend if up else dsend).at[step], above if up else below).wait_send()


def entry(tokens, cotangent, packed, grps, chips, call_id):
    devs = 2 * chips
    return pl.pallas_call(
        functools.partial(entry_kernel, grps, chips),
        out_shape=(
            jax.ShapeDtypeStruct((devs,) + tokens.shape, BF16),
            jax.ShapeDtypeStruct((devs,) + cotangent.shape, BF16),
            jax.ShapeDtypeStruct((grps,) + packed.shape, BF16),
        ),
        in_specs=[ANY] * 3,
        out_specs=(ANY,) * 3,
        scratch_shapes=gather_sems(chips)
        + gather_sems(chips)
        + [
            pltpu.SemaphoreType.DMA((devs,)),
            pltpu.SemaphoreType.DMA((devs,)),
            pltpu.SemaphoreType.DMA,
            pltpu.SemaphoreType.DMA,
            pltpu.SemaphoreType.DMA((grps,)),
            pltpu.SemaphoreType.DMA((grps,)),
            pltpu.SemaphoreType.DMA((grps,)),
        ],
        cost_estimate=BRIEF,
        compiler_params=pltpu.CompilerParams(collective_id=call_id, has_side_effects=True),
    )(tokens, cotangent, packed)


def project_kernel(used, x_ref, w_ref, n_ref, qkv_ref, gain_ref):
    @pl.when(pl.program_id(0) == 0)
    def _():
        gain_ref[...] = w_ref[:, used:].astype(F32).T[:8]

    values = x_ref[...].astype(F32)
    factor = lax.rsqrt(jnp.mean(values * values, axis=-1, keepdims=True) + EPSILON)
    normed = (values * factor * gain_ref[0:1]).astype(BF16)
    n_ref[...] = normed
    qkv_ref[...] = matmul(normed, w_ref[:, :used]).astype(BF16)


def project(tokens, packed, used):
    count, depth = tokens.shape
    rows = tile_rows(count, 256)
    return pl.pallas_call(
        functools.partial(project_kernel, used),
        out_shape=(
            jax.ShapeDtypeStruct((count, depth), BF16),
            jax.ShapeDtypeStruct((count, used), BF16),
            jax.ShapeDtypeStruct((8, depth), F32),
        ),
        grid=(count // rows,),
        in_specs=[
            pl.BlockSpec((rows, depth), lambda r: (r, 0)),
            pl.BlockSpec(packed.shape, lambda r: (0, 0)),
        ],
        out_specs=(
            pl.BlockSpec((rows, depth), lambda r: (r, 0)),
            pl.BlockSpec((rows, used), lambda r: (r, 0)),
            pl.BlockSpec((8, depth), lambda r: (0, 0)),
        ),
        cost_estimate=BRIEF,
        compiler_params=params(1),
    )(tokens, packed)


def norm_parts(values):
    factor = lax.rsqrt(jnp.mean(values * values, axis=-1, keepdims=True) + EPSILON)
    return factor


def norm_back(values, factor, gain, grad):
    scaled = gain * grad
    inner = jnp.mean(values * scaled, axis=-1, keepdims=True)
    return factor * scaled - values * (factor * factor * factor * inner), jnp.sum(
        grad * values * factor, axis=0
    )


def on_device(
    tokens,
    block_group,
    block_slot,
    attn_gain,
    w_query,
    w_key,
    w_value,
    w_out,
    mlp_gain,
    w_gate,
    w_up,
    w_down,
    cotangent,
):
    grps = lax.axis_size("grp")
    devs = lax.axis_size(PLANE)
    chips = devs // 2
    rows = tokens.shape[0]
    w_rows = w_query.shape[0]
    q_heads = HEADS // devs
    kv_heads = 1
    assert devs % KV_HEADS == 0
    kv_copies = max(1, devs // KV_HEADS)
    q_cols, kv_cols = q_heads * HEAD_DIM, kv_heads * HEAD_DIM
    row_blocks = rows // BLOCK * devs
    row_groups = row_blocks // GROUP_BLOCKS

    row_first = lax.axis_index("grp") * row_blocks
    keys = lax.dynamic_slice_in_dim(block_group, row_first, row_blocks) * GROUP_BLOCKS
    keys = keys + lax.dynamic_slice_in_dim(block_slot, row_first, row_blocks)
    rank = jnp.sum((keys[None, :] < keys[:, None]).astype(jnp.int32), axis=1)
    ids = jnp.arange(row_blocks, dtype=jnp.int32)
    order = jnp.sum(jnp.where(rank[None, :] == ids[:, None], ids[None, :], 0), axis=1)

    def kv_split(w):
        w = w.reshape(w_rows, devs // kv_copies, kv_cols)
        return jnp.repeat(w, kv_copies, axis=1) if kv_copies > 1 else w

    gains = jnp.stack([attn_gain, mlp_gain], axis=1)
    cols = D // 4
    room = cols - q_cols - 2 * kv_cols
    gains = jnp.pad(gains, ((0, 0), (0, room - 2)))
    gains = jnp.broadcast_to(gains[:, None, :], (w_rows, devs, room))
    packed = jnp.concatenate(
        [w_query.reshape(w_rows, devs, q_cols), kv_split(w_key), kv_split(w_value), gains], axis=2
    )
    packed = jnp.swapaxes(packed, 0, 1)
    used = q_cols + 2 * kv_cols
    out_full = gather(w_out[None], "grp")
    upstream = cotangent.astype(F32)
    d_branch_mlp = (RESID_MULT * upstream).astype(BF16)
    all_tokens, d_branch_mlp, packed = entry(tokens, d_branch_mlp, packed, grps, chips, 2)
    packed = packed.reshape(D, cols)
    normed_one, qkv, gains = project(all_tokens.reshape(devs * rows, D), packed, used)
    gain_one, gain_two, w_qkv = gains[0], gains[1], packed[:, :used]
    d_branch_mlp = d_branch_mlp.reshape(devs * rows, D)
    attended = attend(qkv, order, q_heads)
    attended = plane_exchange(
        attended, (rows, D), by_rows(rows), by_cols(q_cols), chips, 3
    )

    out_full = plane_gather(out_full, chips, 4, inner=True).reshape(D, D)
    layer_in = tokens.astype(F32)
    branch_attn = matmul(attended, out_full)
    residual = layer_in + RESID_MULT * branch_attn
    factor_two = norm_parts(residual)
    normed_two = (residual * factor_two * gain_two).astype(BF16)
    normed_two = plane_gather(normed_two, chips, 1).reshape(devs * rows, D)
    wide_w = gather(jnp.stack([w_gate, w_up])[None], "grp")
    down_w = gather(w_down[None], "grp")
    hidden, hidden_t, silu, slope, normed_t = widen(normed_two, wide_w)
    part_down = down_part(hidden_t, d_branch_mlp)
    part_down, hidden, silu = lax.optimization_barrier((part_down, hidden, silu))
    grad_down = scatter(part_down, "grp")
    d_gate, d_up = narrow_back(silu, slope, d_branch_mlp, down_w)
    if chips == 4:
        d_normed_two, *others = twin_reduce(widen_back_rows, (d_gate, d_up, wide_w), rows, 10)
        others, d_gate, d_up = lax.optimization_barrier((others, d_gate, d_up))
        others = swap_others(others)
        part_wide = widen_part(normed_t, d_gate, d_up)
        part_wide, hidden = lax.optimization_barrier((part_wide, hidden))
        branch_mlp, *shares = twin_reduce(mix_rows, (hidden, down_w), rows, 11)
        others, shares, part_wide = lax.optimization_barrier((others, shares, part_wide))
        grad_wide = scatter(part_wide, "grp")
        d_normed_two = join(d_normed_two, others)
    else:
        part_wide = widen_part(normed_t, d_gate, d_up)
        part_wide, d_gate, d_up = lax.optimization_barrier((part_wide, d_gate, d_up))
        grad_wide = scatter(part_wide, "grp")
        d_normed_two = widen_back(d_gate, d_up, wide_w)
        d_normed_two = plane_reduce(d_normed_two.reshape(devs, rows, D), chips, 5)
        branch_mlp = mix(hidden, down_w)
        branch_mlp = plane_reduce(branch_mlp.reshape(devs, rows, D), chips, 5)

    d_residual_norm, d_gain_two = norm_back(residual, factor_two, gain_two, d_normed_two)
    d_residual = upstream + d_residual_norm
    d_branch_attn = (RESID_MULT * d_residual).astype(BF16)
    grad_out = over_rows(attended, d_branch_attn).astype(BF16)
    grad_out, d_branch_attn = lax.optimization_barrier((grad_out, d_branch_attn))
    if chips == 4:
        drift_out = Drift(grad_out.reshape(grps, 4, 2, w_rows, D), 1)
    d_attended = over_cols(d_branch_attn, out_full).astype(BF16)
    d_attended = plane_exchange(
        d_attended, (devs * rows, q_cols), by_cols(q_cols), by_rows(rows), chips, 7
    )
    if chips == 4:
        sent_out, d_attended, shares = lax.optimization_barrier(
            (drift_out.parts(), d_attended, shares)
        )
        sent_out = (sent_out[2], sent_out[0], sent_out[1])
        shares = [
            jnp.concatenate([share, part.reshape(rows, D)]) for share, part in zip(shares, sent_out)
        ]
        shares = swap_others(shares)
    d_attended, grad_down = lax.optimization_barrier((d_attended, grad_down))
    d_qkv = attend_back(qkv, d_attended, order, q_heads)
    if chips == 4:
        d_normed_one, *others = twin_reduce(project_back_rows, (d_qkv, w_qkv), rows, 5)
        shares, others, d_qkv = lax.optimization_barrier((shares, others, d_qkv))
        others = swap_others(others)
        branch_mlp = join(branch_mlp, [share[:rows] for share in shares])
        sent_out = [share[rows:].reshape(grps, w_rows, D) for share in shares]
        grad_out = drift_out.finish(sent_out).astype(BF16)
    else:
        grad_out = plane_reduce(
            grad_out.reshape(grps, devs, w_rows, D), chips, 6, dtype=BF16, inner=True
        )
    sent = over_rows(normed_one, d_qkv).astype(BF16)
    sent, grad_wide = lax.optimization_barrier((sent, grad_wide))
    sent = scatter(sent, "grp")
    grad_out = scatter(grad_out, "grp").reshape(w_rows, D).astype(F32)
    if chips == 4:
        d_normed_one = join(d_normed_one, others)
    else:
        d_normed_one = over_cols(d_qkv, w_qkv).astype(BF16).reshape(devs, rows, D)
        d_normed_one = plane_reduce(d_normed_one, chips, 5)
    d_input_norm, _ = norm_back(layer_in, norm_parts(layer_in), gain_one, d_normed_one)
    tokens_grad = (d_residual + d_input_norm).astype(BF16)
    layer_out = residual + RESID_MULT * branch_mlp
    scaled_attn = RESID_MULT * branch_attn
    scaled_mlp = RESID_MULT * branch_mlp
    squares = jnp.stack(
        [
            jnp.sum(layer_out * layer_out),
            jnp.sum(scaled_attn * scaled_attn),
            jnp.sum(scaled_mlp * scaled_mlp),
        ]
    )
    totals = jnp.concatenate([d_gain_two, squares, jnp.zeros((1021,), F32)])
    totals, tokens_grad = lax.optimization_barrier((totals, tokens_grad))
    totals = total(totals.reshape(8, 3 * D // 16), grps, chips, 8)
    sent = sent.reshape(devs, w_rows, q_cols + 2 * kv_cols)
    sent = plane_exchange(sent, sent.shape, by_slot, by_slot, chips, 9).astype(F32)

    def kv_join(g):
        g = g.reshape(devs // kv_copies, kv_copies, w_rows, kv_cols)
        g = jnp.sum(g, axis=1) if kv_copies > 1 else g[:, 0]
        return jnp.swapaxes(g, 0, 1).reshape(w_rows, KV_HEADS * HEAD_DIM)

    grad_query = jnp.swapaxes(sent[:, :, :q_cols], 0, 1).reshape(w_rows, D)
    grad_key = kv_join(sent[:, :, q_cols : q_cols + kv_cols])
    grad_value = kv_join(sent[:, :, q_cols + kv_cols : q_cols + 2 * kv_cols])

    gain_one_grad = sum(
        jnp.sum(weight.astype(F32) * grad, axis=1)
        for weight, grad in ((w_query, grad_query), (w_key, grad_key), (w_value, grad_value))
    ) / attn_gain.astype(F32)
    totals = totals.reshape(-1)
    rms_stats = jnp.sqrt(totals[D : D + 3] / (rows * grps * devs * D))
    gain_first = (lax.axis_index("grp") * devs + lax.axis_index(PLANE)) * w_rows
    gain_two_grad = lax.dynamic_slice(totals, (gain_first,), (w_rows,))
    return (
        layer_out.astype(BF16),
        tokens_grad,
        gain_one_grad,
        grad_query,
        grad_key,
        grad_value,
        grad_out,
        gain_two_grad,
        grad_wide[0, 0].astype(F32),
        grad_wide[0, 1].astype(F32),
        grad_down[0].astype(F32),
        rms_stats,
    )


def solution(mesh):
    shape = (mesh.shape["grp"], mesh.shape["blk"] // 2, 2)
    mesh = Mesh(mesh.devices.reshape(shape), EVERY)
    row, col, vec = P(EVERY, None), P(None, EVERY), P(EVERY)
    return jax.shard_map(
        on_device,
        mesh=mesh,
        in_specs=(row, P(), P(), vec, row, row, row, row, vec, col, col, row, row),
        out_specs=(row, row, vec, row, row, row, row, vec, col, col, row, P()),
        check_vma=False,
    )
```

```python
import functools

import jax
import jax.numpy as jnp
from jax import lax
from jax.experimental import pallas as pl
from jax.experimental.pallas import tpu as pltpu
from jax.sharding import Mesh
from jax.sharding import PartitionSpec as P

D = 2048
HEADS = 32
KV_HEADS = 8
HEAD_DIM = 64
BLOCK = 128
PROMPT_BLOCKS = 8
GROUP_BLOCKS = 16
PER_GROUP = HEADS // KV_HEADS

ATTN_MULT = 0.015625
RESID_MULT = 0.22
EPSILON = 1e-05
MASKED = -1e30

PLANE = ("chip", "core")
EVERY = ("grp", "chip", "core")
BF16 = jnp.bfloat16
F32 = jnp.float32


MESH = pl.DeviceIdType.MESH
BRIEF = pl.CostEstimate(flops=1000, bytes_accessed=1000, transcendentals=0)
ANY = pl.BlockSpec(memory_space=pl.ANY)
VMEM = pl.BlockSpec(memory_space=pltpu.VMEM)


def place():
    return lax.axis_index("chip"), lax.axis_index("core")


def flip(chip, step, chips):
    return jnp.bitwise_xor(chip, step) if chips == 4 else lax.rem(chip + step, chips)


def unflip(chip, step, chips):
    return jnp.bitwise_xor(chip, step) if chips == 4 else lax.rem(chip + chips - step, chips)


def greet(peers):
    barrier = pltpu.get_barrier_semaphore()
    for chip, core in peers:
        pl.semaphore_signal(
            barrier, inc=1, device_id={"chip": chip, "core": core}, device_id_type=MESH
        )
    pl.semaphore_wait(barrier, len(peers))


def remote(src, dst, send, recv, chip, core):
    return pltpu.make_async_remote_copy(
        src_ref=src,
        dst_ref=dst,
        send_sem=send,
        recv_sem=recv,
        device_id={"chip": chip, "core": core},
        device_id_type=MESH,
    )


class Gather:
    def __init__(self, chips, inner, x_ref, o_ref, send, recv, local):
        self.chips, self.inner, self.x, self.o = chips, inner, x_ref, o_ref
        self.send, self.recv, self.local = send, recv, local
        self.chip, self.core = place()
        self.half = x_ref.shape[0] // 2
        self.started = []

    def greet(self):
        steps = (1, 2) if self.chips == 4 else range(1, self.chips)
        peers = [(flip(self.chip, s, self.chips), self.core) for s in steps]
        greet(peers + [(self.chip, 1 - self.core)])

    def piece(self, slot, h):
        at = pl.ds(h * self.half, self.half)
        return self.o.at[at, slot] if self.inner else self.o.at[slot, at]

    def own(self, h):
        return self.x.at[pl.ds(h * self.half, self.half)]

    def slot(self, chip, core):
        return chip * 2 + core

    def push(self, src, slot, h, chip, core):
        i = len(self.started)
        copy = remote(src, self.piece(slot, h), self.send.at[i], self.recv.at[slot, h], chip, core)
        copy.start()
        self.started.append(copy)

    def wait_for(self, slot, h):
        remote(
            self.own(h), self.piece(slot, h), self.send.at[0], self.recv.at[slot, h],
            self.chip, 1 - self.core,
        ).wait_recv()

    def start(self):
        me = self.slot(self.chip, self.core)
        if self.chips == 4:
            for h, s in ((0, 1), (1, 2), (1, 1), (0, 2)):
                self.push(self.own(h), me, h, flip(self.chip, s, 4), self.core)
        else:
            for s in range(1, self.chips):
                for h in range(2):
                    self.push(self.own(h), me, h, flip(self.chip, s, self.chips), self.core)
        for h in range(2):
            self.push(self.own(h), me, h, self.chip, 1 - self.core)
        whole = self.o.at[:, me] if self.inner else self.o.at[me]
        self.mine = pltpu.make_async_copy(self.x, whole, self.local)
        self.mine.start()

    def relay(self, first=0, last=None):
        if self.chips == 4:
            plan = ((1, 0, 2), (2, 1, 1), (1, 1, 0), (2, 0, 0), (3, 0, 0), (3, 1, 0))
        else:
            plan = tuple((s, h, 0) for s in range(1, self.chips) for h in range(2))
        for s, h, onward in plan[first:last]:
            slot = self.slot(unflip(self.chip, s, self.chips), self.core)
            self.wait_for(slot, h)
            if onward:
                self.push(self.piece(slot, h), slot, h, flip(self.chip, onward, 4), self.core)
            self.push(self.piece(slot, h), slot, h, self.chip, 1 - self.core)

    def finish(self):
        for s in range(self.chips):
            slot = self.slot(unflip(self.chip, s, self.chips), 1 - self.core)
            for h in range(2):
                self.wait_for(slot, h)
        for copy in self.started:
            copy.wait_send()
        self.mine.wait()


def gather_sems(chips):
    return [
        pltpu.SemaphoreType.DMA((4 * chips + 4,)),
        pltpu.SemaphoreType.DMA((2 * chips, 2)),
        pltpu.SemaphoreType.DMA,
    ]


def gather_kernel(chips, inner, x_ref, o_ref, *sems):
    run = Gather(chips, inner, x_ref, o_ref, *sems)
    run.greet()
    run.start()
    run.relay()
    run.finish()


def plane_gather(x, chips, call_id, inner=False):
    devs = 2 * chips
    shape = (x.shape[0], devs) + x.shape[1:] if inner else (devs,) + x.shape
    return pl.pallas_call(
        functools.partial(gather_kernel, chips, inner),
        out_shape=jax.ShapeDtypeStruct(shape, x.dtype),
        in_specs=[ANY],
        out_specs=ANY,
        scratch_shapes=gather_sems(chips),
        cost_estimate=BRIEF,
        compiler_params=pltpu.CompilerParams(collective_id=call_id, has_side_effects=True),
    )(x)


def reduce_kernel(chips, inner, p_ref, o_ref, total, mine, twin, moved, corner, landed, lsem, tsend, trecv, msend, mrecv, csend, crecv):
    chip, core = place()
    sib = 1 - core
    half = (p_ref.shape[0] if inner else p_ref.shape[1]) // 2
    block = (lambda slot: p_ref.at[:, slot]) if inner else (lambda slot: p_ref.at[slot])
    steps = (1, 2) if chips == 4 else tuple(range(1, chips))
    peers = [(flip(chip, s, chips), core) for s in steps]
    greet(peers + [(chip, sib)])
    order = (3, 1, 2, 0) if chips == 4 else tuple(range(1, chips)) + (0,)
    loads, twins = {}, {}
    for s in order:
        to = flip(chip, s, chips) * 2
        twins[s] = remote(block(to + sib), twin.at[s], tsend.at[s], trecv.at[s], chip, sib)
        twins[s].start()
        loads[s] = pltpu.make_async_copy(block(to + core), mine.at[s], lsem.at[s])
        loads[s].start()

    def part(s, h):
        at = pl.ds(h * half, half)
        return mine[s, at].astype(F32) + twin[s, at].astype(F32)

    def ready(s):
        loads[s].wait()
        twins[s].wait_recv()

    sent = []
    if chips == 4:
        corners = []
        ready(3)
        for h, s in ((0, 1), (1, 2)):
            moved[3, pl.ds(h * half, half)] = part(3, h).astype(BF16)
            copy = remote(moved.at[3, pl.ds(h * half, half)], corner.at[h], csend.at[h], crecv.at[h], flip(chip, s, 4), core)
            copy.start()
            corners.append(copy)

        def send(s, h):
            at = pl.ds(h * half, half)
            copy = remote(moved.at[s, at], landed.at[s - 1, at], msend.at[s - 1, h], mrecv.at[s - 1, h], flip(chip, s, 4), core)
            copy.start()
            sent.append(copy)

        for s, h in ((1, 0), (2, 1)):
            ready(s)
            moved[s, pl.ds(h * half, half)] = part(s, h).astype(BF16)
            send(s, h)
        for s, h in ((2, 0), (1, 1)):
            corners[h].wait_recv()
            moved[s, pl.ds(h * half, half)] = (part(s, h) + corner[h].astype(F32)).astype(BF16)
            send(s, h)
        for copy in corners:
            copy.wait_send()
    else:
        for s in steps:
            ready(s)
            for h in range(2):
                at = pl.ds(h * half, half)
                moved[s, at] = part(s, h).astype(BF16)
                copy = remote(moved.at[s, at], landed.at[s - 1, at], msend.at[s - 1, h], mrecv.at[s - 1, h], flip(chip, s, chips), core)
                copy.start()
                sent.append(copy)
    ready(0)
    for h in range(2):
        total[pl.ds(h * half, half)] = part(0, h)
    for copy in sent:
        copy.wait()
    for s in steps[:-1]:
        total[...] += landed[s - 1].astype(F32)
    o_ref[...] = (total[...] + landed[steps[-1] - 1].astype(F32)).astype(o_ref.dtype)
    for s in order:
        twins[s].wait_send()


def plane_reduce(p, chips, call_id, dtype=F32, inner=False):
    block = (p.shape[0],) + p.shape[2:] if inner else p.shape[1:]
    steps = 2 if chips == 4 else chips - 1
    return pl.pallas_call(
        functools.partial(reduce_kernel, chips, inner),
        out_shape=jax.ShapeDtypeStruct(block, dtype),
        in_specs=[ANY],
        out_specs=VMEM,
        scratch_shapes=[
            pltpu.VMEM(block, F32),
            pltpu.VMEM((chips,) + block, BF16),
            pltpu.VMEM((chips,) + block, BF16),
            pltpu.VMEM((chips,) + block, BF16),
            pltpu.VMEM((2, block[0] // 2) + block[1:], BF16),
            pltpu.VMEM((steps,) + block, BF16),
            pltpu.SemaphoreType.DMA((chips,)),
            pltpu.SemaphoreType.DMA((chips,)),
            pltpu.SemaphoreType.DMA((chips,)),
            pltpu.SemaphoreType.DMA((steps, 2)),
            pltpu.SemaphoreType.DMA((steps, 2)),
            pltpu.SemaphoreType.DMA((2,)),
            pltpu.SemaphoreType.DMA((2,)),
        ],
        cost_estimate=BRIEF,
        compiler_params=pltpu.CompilerParams(
            collective_id=call_id, has_side_effects=True, vmem_limit_bytes=56 << 20
        ),
    )(p)


def swap_chips(values, step):
    return lax.ppermute(values, "chip", [(c, c ^ step) for c in range(4)])


class Drift:
    def __init__(self, pairs, axis):
        self.axis = axis
        self.chip, self.core = place()
        away = lax.dynamic_index_in_dim(pairs, 1 - self.core, axis + 1, keepdims=False)
        self.mine = lax.dynamic_index_in_dim(pairs, self.core, axis + 1, keepdims=False)
        self.twin = lax.ppermute(away, "core", [(0, 1), (1, 0)])

    def part(self, step):
        at = jnp.bitwise_xor(self.chip, step)
        mine = lax.dynamic_index_in_dim(self.mine, at, self.axis, keepdims=False)
        twin = lax.dynamic_index_in_dim(self.twin, at, self.axis, keepdims=False)
        return mine.astype(F32) + twin.astype(F32)

    def parts(self):
        return tuple(self.part(step).astype(BF16) for step in (1, 2, 3))

    def finish(self, came):
        total = self.part(0)
        for part in came:
            total = total + part.astype(F32)
        return total


def exchange_kernel(chips, cut, paste, x_ref, o_ref, send, recv, local):
    chip, core = place()
    me = chip * 2 + core
    peers = [(flip(chip, s, chips), c) for s in range(1, chips) for c in (core, 1 - core)]
    peers = peers + [(chip, 1 - core)]
    greet(peers)
    far = [p for p in ([3, 1, 2] if chips == 4 else range(1, chips))]
    order = [(flip(chip, s, chips), c) for s in far for c in (core, 1 - core)] + [(chip, 1 - core)]
    copies = []
    for i, (to, c) in enumerate(order):
        copy = remote(cut(x_ref, to * 2 + c), paste(o_ref, me), send.at[i], recv.at[me], to, c)
        copy.start()
        copies.append(copy)
    mine = pltpu.make_async_copy(cut(x_ref, me), paste(o_ref, me), local)
    mine.start()
    for s in far:
        for c in (core, 1 - core):
            slot = unflip(chip, s, chips) * 2 + c
            remote(cut(x_ref, me), paste(o_ref, slot), send.at[0], recv.at[slot], chip, 1 - core).wait_recv()
    slot = chip * 2 + 1 - core
    remote(cut(x_ref, me), paste(o_ref, slot), send.at[0], recv.at[slot], chip, 1 - core).wait_recv()
    for copy in copies:
        copy.wait_send()
    mine.wait()


def plane_exchange(x, shape, cut, paste, chips, call_id):
    return pl.pallas_call(
        functools.partial(exchange_kernel, chips, cut, paste),
        out_shape=jax.ShapeDtypeStruct(shape, x.dtype),
        in_specs=[ANY],
        out_specs=ANY,
        scratch_shapes=[
            pltpu.SemaphoreType.DMA((2 * chips,)),
            pltpu.SemaphoreType.DMA((2 * chips,)),
            pltpu.SemaphoreType.DMA,
        ],
        cost_estimate=BRIEF,
        compiler_params=pltpu.CompilerParams(collective_id=call_id, has_side_effects=True),
    )(x)


def by_slot(ref, dev):
    return ref.at[dev]


def by_rows(rows):
    return lambda ref, dev: ref.at[pl.ds(pl.multiple_of(dev * rows, rows), rows)]


def by_cols(cols):
    return lambda ref, dev: ref.at[:, pl.ds(pl.multiple_of(dev * cols, cols), cols)]


def matmul(left, right):
    return jnp.dot(left, right, preferred_element_type=F32)


def over_rows(left, right):
    return lax.dot_general(left, right, (((0,), (0,)), ((), ())), preferred_element_type=F32)


def over_cols(left, right):
    return lax.dot_general(left, right, (((1,), (1,)), ((), ())), preferred_element_type=F32)


def gather(values, axes, axis=0):
    return lax.all_gather(values, axes, axis=axis, tiled=True)


def scatter(values, axes, axis=0):
    return lax.psum_scatter(values, axes, scatter_dimension=axis, tiled=True)


def dot_nt(left, right):
    return lax.dot_general(left, right, (((1,), (1,)), ((), ())), preferred_element_type=F32)


def head_stack(values, heads):
    col_head = lax.broadcasted_iota(jnp.int32, values.shape, 1) // HEAD_DIM
    return jnp.concatenate(
        [jnp.where(col_head == h, values, jnp.zeros_like(values)) for h in range(heads)], axis=0
    )


def head_pick(stacked, heads):
    rows = stacked.shape[0] // heads
    col_head = lax.broadcasted_iota(jnp.int32, (rows, stacked.shape[1]), 1) // HEAD_DIM
    total = jnp.zeros((rows, stacked.shape[1]), F32)
    for h in range(heads):
        total = jnp.where(col_head == h, stacked[h * rows : (h + 1) * rows], total)
    return total


def head_fold(values, heads):
    total = values[:, :HEAD_DIM]
    for h in range(1, heads):
        total = total + values[:, h * HEAD_DIM : (h + 1) * HEAD_DIM]
    return total


def repeat_heads(values, heads):
    return jnp.concatenate([values] * heads, axis=1)


def own_rows(order_ref, slot):
    return pl.ds(pl.multiple_of(order_ref[slot] * BLOCK, BLOCK), BLOCK)


def load_prompt(heads, order_ref, qkv_ref, k_ref, v_ref, first):
    q_cols = heads * HEAD_DIM
    for s in range(PROMPT_BLOCKS):
        pair = qkv_ref[own_rows(order_ref, first + s), q_cols:]
        at = pl.ds(s * BLOCK, BLOCK)
        k_ref[at] = repeat_heads(pair[:, :HEAD_DIM], heads)
        v_ref[at] = repeat_heads(pair[:, HEAD_DIM:], heads)


def soft_parts(heads, slot, q_stack, k_far, k_own):
    far = dot_nt(k_far, q_stack)
    own = dot_nt(k_own, q_stack)
    limit = jnp.minimum(slot, PROMPT_BLOCKS) * BLOCK
    far = jnp.where(lax.broadcasted_iota(jnp.int32, far.shape, 0) < limit, far, MASKED)
    key = lax.broadcasted_iota(jnp.int32, own.shape, 0)
    row = lax.broadcasted_iota(jnp.int32, own.shape, 1) % BLOCK
    own = jnp.where(key <= row, own, MASKED)
    peak = jnp.maximum(jnp.max(far, axis=0, keepdims=True), jnp.max(own, axis=0, keepdims=True))
    far, own = jnp.exp(far - peak), jnp.exp(own - peak)
    scale = 1.0 / (jnp.sum(far, axis=0, keepdims=True) + jnp.sum(own, axis=0, keepdims=True))
    return far * scale, own * scale


def scaled_stack(q, heads):
    return head_stack((q.astype(F32) * ATTN_MULT).astype(BF16), heads)


def attend_kernel(heads, order_ref, qkv_ref, o_ref, k_ref, v_ref, vt_ref):
    first, slot = pl.program_id(0) * GROUP_BLOCKS, pl.program_id(1)
    q_cols = heads * HEAD_DIM

    @pl.when(slot == 0)
    def _():
        load_prompt(heads, order_ref, qkv_ref, k_ref, v_ref, first)
        vt_ref[...] = v_ref[...].astype(F32).T.astype(BF16)

    rows = own_rows(order_ref, first + slot)
    mine = qkv_ref[rows, :]
    k_own = repeat_heads(mine[:, q_cols : q_cols + HEAD_DIM], heads)
    v_own = repeat_heads(mine[:, q_cols + HEAD_DIM :], heads)
    far, own = soft_parts(heads, slot, scaled_stack(mine[:, :q_cols], heads), k_ref[...], k_own)
    mixed = matmul(vt_ref[...], far.astype(BF16))
    mixed += matmul(v_own.astype(F32).T.astype(BF16), own.astype(BF16))
    o_ref[rows, :] = head_pick(mixed.T, heads).astype(BF16)


def attend_back_kernel(
    heads, order_ref, qkv_ref, d_ref, o_ref, k_ref, v_ref, kt_ref, dk_ref, dv_ref
):
    first, slot = pl.program_id(0) * GROUP_BLOCKS, pl.program_id(1)
    q_cols = heads * HEAD_DIM

    @pl.when(slot == 0)
    def _():
        load_prompt(heads, order_ref, qkv_ref, k_ref, v_ref, first)
        kt_ref[...] = k_ref[...].astype(F32).T.astype(BF16)
        dk_ref[...] = jnp.zeros_like(dk_ref)
        dv_ref[...] = jnp.zeros_like(dv_ref)

    rows = own_rows(order_ref, first + slot)
    mine = qkv_ref[rows, :]
    k_own = repeat_heads(mine[:, q_cols : q_cols + HEAD_DIM], heads)
    v_own = repeat_heads(mine[:, q_cols + HEAD_DIM :], heads)
    q_stack = scaled_stack(mine[:, :q_cols], heads)
    d_stack = head_stack(d_ref[rows, :], heads)
    far, own = soft_parts(heads, slot, q_stack, k_ref[...], k_own)
    d_far, d_own = dot_nt(v_ref[...], d_stack), dot_nt(v_own, d_stack)
    mean = jnp.sum(far * d_far, axis=0, keepdims=True) + jnp.sum(own * d_own, axis=0, keepdims=True)
    d_far = (far * (d_far - mean)).astype(BF16)
    d_own = (own * (d_own - mean)).astype(BF16)
    dv_ref[...] += matmul(far.astype(BF16), d_stack)
    dk_ref[...] += matmul(d_far, q_stack)
    dv_own = matmul(own.astype(BF16), d_stack)
    dk_own = matmul(d_own, q_stack)
    d_q = matmul(kt_ref[...], d_far) + matmul(k_own.astype(F32).T.astype(BF16), d_own)
    o_ref[rows, :q_cols] = (head_pick(d_q.T, heads) * ATTN_MULT).astype(BF16)

    def fold(d_k, d_v):
        return jnp.concatenate([head_fold(d_k, heads), head_fold(d_v, heads)], axis=1).astype(BF16)

    @pl.when(slot < PROMPT_BLOCKS)
    def _():
        at = pl.ds(pl.multiple_of(slot * BLOCK, BLOCK), BLOCK)
        dk_ref[at] += dk_own
        dv_ref[at] += dv_own

    @pl.when(slot >= PROMPT_BLOCKS)
    def _():
        o_ref[rows, q_cols:] = fold(dk_own, dv_own)

    @pl.when(slot == GROUP_BLOCKS - 1)
    def _():
        for s in range(PROMPT_BLOCKS):
            at = pl.ds(s * BLOCK, BLOCK)
            o_ref[own_rows(order_ref, first + s), q_cols:] = fold(dk_ref[at], dv_ref[at])


def whole(shape):
    return pl.BlockSpec(shape, lambda g, s, order: (0,) * len(shape))


def attend(qkv, order, heads):
    tokens, cols = qkv.shape
    prompt, q_cols = PROMPT_BLOCKS * BLOCK, heads * HEAD_DIM
    return pl.pallas_call(
        functools.partial(attend_kernel, heads),
        out_shape=jax.ShapeDtypeStruct((tokens, q_cols), BF16),
        grid_spec=pltpu.PrefetchScalarGridSpec(
            num_scalar_prefetch=1,
            grid=(tokens // (GROUP_BLOCKS * BLOCK), GROUP_BLOCKS),
            in_specs=[whole((tokens, cols))],
            out_specs=whole((tokens, q_cols)),
            scratch_shapes=[
                pltpu.VMEM((prompt, q_cols), BF16),
                pltpu.VMEM((prompt, q_cols), BF16),
                pltpu.VMEM((q_cols, prompt), BF16),
            ],
        ),
        cost_estimate=BRIEF,
        compiler_params=pltpu.CompilerParams(vmem_limit_bytes=40 << 20),
    )(order, qkv)


def attend_back(qkv, d_attended, order, heads):
    tokens, cols = qkv.shape
    prompt, q_cols = PROMPT_BLOCKS * BLOCK, heads * HEAD_DIM
    return pl.pallas_call(
        functools.partial(attend_back_kernel, heads),
        out_shape=jax.ShapeDtypeStruct((tokens, cols), BF16),
        grid_spec=pltpu.PrefetchScalarGridSpec(
            num_scalar_prefetch=1,
            grid=(tokens // (GROUP_BLOCKS * BLOCK), GROUP_BLOCKS),
            in_specs=[whole((tokens, cols)), whole((tokens, q_cols))],
            out_specs=whole((tokens, cols)),
            scratch_shapes=[
                pltpu.VMEM((prompt, q_cols), BF16),
                pltpu.VMEM((prompt, q_cols), BF16),
                pltpu.VMEM((q_cols, prompt), BF16),
                pltpu.VMEM((prompt, q_cols), F32),
                pltpu.VMEM((prompt, q_cols), F32),
            ],
        ),
        cost_estimate=BRIEF,
        compiler_params=pltpu.CompilerParams(vmem_limit_bytes=40 << 20),
    )(order, qkv, d_attended)


def exchange_total_kernel(
    grps, chips, cut, paste, x_ref, t_ref, o_ref, sum_ref,
    over_z, over_plane, send, recv, local, zsend, zrecv, psend, precv,
):
    grp = lax.axis_index("grp")
    chip, core = place()
    me = chip * 2 + core
    far = [lax.rem(grp + s, grps) for s in range(1, grps)]
    steps = (3, 1, 2) if chips == 4 else tuple(range(1, chips))
    near = [(flip(chip, s, chips), c) for s in steps for c in (core, 1 - core)]
    near = near + [(chip, 1 - core)]
    barrier = pltpu.get_barrier_semaphore()
    for g in far:
        pl.semaphore_signal(barrier, inc=1, device_id={"grp": g}, device_id_type=MESH)
    for to, c in near:
        pl.semaphore_signal(
            barrier, inc=1, device_id={"chip": to, "core": c}, device_id_type=MESH
        )
    pl.semaphore_wait(barrier, len(far) + len(near))

    def z_copy(slot, sem, to):
        return pltpu.make_async_remote_copy(
            src_ref=t_ref,
            dst_ref=over_z.at[slot],
            send_sem=sem,
            recv_sem=zrecv.at[slot],
            device_id={"grp": to},
            device_id_type=MESH,
        )

    copies = []
    for i, g in enumerate(far):
        copy = z_copy(grp, zsend.at[i], g)
        copy.start()
        copies.append(copy)
    for i, (to, c) in enumerate(near):
        copy = remote(cut(x_ref, to * 2 + c), paste(o_ref, me), send.at[i], recv.at[me], to, c)
        copy.start()
        copies.append(copy)
    mine = pltpu.make_async_copy(cut(x_ref, me), paste(o_ref, me), local)
    mine.start()
    over_z[grp] = t_ref[...]
    for g in far:
        z_copy(g, zsend.at[0], g).wait_recv()
    over_plane[me] = jnp.sum(over_z[...], axis=0)
    for i, (to, c) in enumerate(near):
        copy = remote(over_plane.at[me], over_plane.at[me], psend.at[i], precv.at[me], to, c)
        copy.start()
        copies.append(copy)
    for to, c in near:
        slot = to * 2 + c
        remote(cut(x_ref, me), paste(o_ref, slot), send.at[0], recv.at[slot], to, c).wait_recv()
        remote(over_plane.at[me], over_plane.at[slot], psend.at[0], precv.at[slot], to, c).wait_recv()
    for copy in copies:
        copy.wait_send()
    mine.wait()
    sum_ref[...] = jnp.sum(over_plane[...], axis=0)


def exchange_total(x, t, shape, rows, cols, grps, chips, call_id):
    devs = 2 * chips
    return pl.pallas_call(
        functools.partial(exchange_total_kernel, grps, chips, by_cols(cols), by_rows(rows)),
        out_shape=(
            jax.ShapeDtypeStruct(shape, x.dtype),
            jax.ShapeDtypeStruct(t.shape, F32),
        ),
        in_specs=[ANY, VMEM],
        out_specs=(ANY, VMEM),
        scratch_shapes=[
            pltpu.VMEM((grps,) + t.shape, F32),
            pltpu.VMEM((devs,) + t.shape, F32),
            pltpu.SemaphoreType.DMA((devs,)),
            pltpu.SemaphoreType.DMA((devs,)),
            pltpu.SemaphoreType.DMA,
            pltpu.SemaphoreType.DMA((grps,)),
            pltpu.SemaphoreType.DMA((grps,)),
            pltpu.SemaphoreType.DMA((devs,)),
            pltpu.SemaphoreType.DMA((devs,)),
        ],
        cost_estimate=BRIEF,
        compiler_params=pltpu.CompilerParams(collective_id=call_id, has_side_effects=True),
    )(x, t)


def params(axes, mib=56):
    return pltpu.CompilerParams(
        dimension_semantics=("arbitrary",) * axes, vmem_limit_bytes=mib << 20
    )


def tile_rows(count, limit):
    while count % limit:
        limit //= 2
    return limit


def widen_kernel(n_ref, w_ref, h_ref, ht_ref, s_ref, t_ref, nt_ref):
    values = n_ref[...]
    gate, up = matmul(values, w_ref[0, 0]), matmul(values, w_ref[0, 1])
    sig = 1.0 / (1.0 + jnp.exp(-gate))
    silu = gate * sig
    hidden = (silu * up).astype(BF16)
    h_ref[0] = hidden
    ht_ref[0] = hidden.T
    s_ref[0] = silu.astype(BF16)
    t_ref[0] = (up * (sig * (1.0 + gate * (1.0 - sig)))).astype(BF16)

    @pl.when(pl.program_id(1) == 0)
    def _():
        nt_ref[...] = values.T


def widen(normed, weights):
    tokens, depth = normed.shape
    shards, _, _, width = weights.shape
    rows = tile_rows(tokens, 1024)
    tall = jax.ShapeDtypeStruct((shards, tokens, width), BF16)
    tall_spec = pl.BlockSpec((1, rows, width), lambda r, s: (s, r, 0))
    return pl.pallas_call(
        widen_kernel,
        out_shape=(
            tall,
            jax.ShapeDtypeStruct((shards, width, tokens), BF16),
            tall,
            tall,
            jax.ShapeDtypeStruct((depth, tokens), BF16),
        ),
        grid=(tokens // rows, shards),
        in_specs=[
            pl.BlockSpec((rows, depth), lambda r, s: (r, 0)),
            pl.BlockSpec((1, 2, depth, width), lambda r, s: (s, 0, 0, 0)),
        ],
        out_specs=(
            tall_spec,
            pl.BlockSpec((1, width, rows), lambda r, s: (s, 0, r)),
            tall_spec,
            tall_spec,
            pl.BlockSpec((depth, rows), lambda r, s: (0, r)),
        ),
        cost_estimate=BRIEF,
        compiler_params=params(2),
    )(normed, weights)


def down_part_kernel(ht_ref, d_ref, o_ref):
    o_ref[0] = matmul(ht_ref[0], d_ref[...]).astype(BF16)


def down_part(hidden_t, upstream):
    shards, width, tokens = hidden_t.shape
    depth = upstream.shape[1]
    cols = tile_rows(depth, 1024)
    return pl.pallas_call(
        down_part_kernel,
        out_shape=jax.ShapeDtypeStruct((shards, width, depth), BF16),
        grid=(depth // cols, shards),
        in_specs=[
            pl.BlockSpec((1, width, tokens), lambda c, s: (s, 0, 0)),
            pl.BlockSpec((tokens, cols), lambda c, s: (0, c)),
        ],
        out_specs=pl.BlockSpec((1, width, cols), lambda c, s: (s, 0, c)),
        cost_estimate=BRIEF,
        compiler_params=params(2),
    )(hidden_t, upstream)


def mix_kernel(h_ref, w_ref, m_ref):
    mixed = None
    for i in range(w_ref.shape[0]):
        part = matmul(h_ref[i], w_ref[i])
        mixed = part if mixed is None else mixed + part
    m_ref[...] = mixed.astype(BF16)


def narrow_specs(hidden, weights):
    shards, tokens, width = hidden.shape
    depth = weights.shape[2]
    rows = tile_rows(tokens, 512)
    return (
        tokens // rows,
        pl.BlockSpec((shards, rows, width), lambda r: (0, r, 0)),
        pl.BlockSpec((rows, depth), lambda r: (r, 0)),
        pl.BlockSpec(weights.shape, lambda r: (0, 0, 0), pipeline_mode=pl.Buffered(1)),
    )


def mix(hidden, weights):
    steps, tall_spec, flat_spec, weight_spec = narrow_specs(hidden, weights)
    return pl.pallas_call(
        mix_kernel,
        out_shape=jax.ShapeDtypeStruct((hidden.shape[1], weights.shape[2]), BF16),
        grid=(steps,),
        in_specs=[tall_spec, weight_spec],
        out_specs=flat_spec,
        cost_estimate=BRIEF,
        compiler_params=params(1),
    )(hidden, weights)


def narrow_back_kernel(s_ref, t_ref, d_ref, w_ref, dg_ref, du_ref):
    upstream = d_ref[...]
    for i in range(w_ref.shape[0]):
        d_hidden = dot_nt(upstream, w_ref[i])
        dg_ref[i] = (d_hidden * t_ref[i].astype(F32)).astype(BF16)
        du_ref[i] = (d_hidden * s_ref[i].astype(F32)).astype(BF16)


def narrow_back(silu, slope, upstream, weights):
    steps, tall_spec, flat_spec, weight_spec = narrow_specs(silu, weights)
    tall = jax.ShapeDtypeStruct(silu.shape, BF16)
    return pl.pallas_call(
        narrow_back_kernel,
        out_shape=(tall, tall),
        grid=(steps,),
        in_specs=[tall_spec, tall_spec, flat_spec, weight_spec],
        out_specs=(tall_spec, tall_spec),
        cost_estimate=BRIEF,
        compiler_params=params(1),
    )(silu, slope, upstream, weights)


def widen_part_kernel(nt_ref, dg_ref, du_ref, o_ref):
    values = nt_ref[...]
    o_ref[0, 0] = matmul(values, dg_ref[0]).astype(BF16)
    o_ref[0, 1] = matmul(values, du_ref[0]).astype(BF16)


def widen_part(normed_t, d_gate, d_up):
    depth, tokens = normed_t.shape
    shards, _, width = d_gate.shape
    rows = tile_rows(depth, 1024)
    tall_spec = pl.BlockSpec((1, tokens, width), lambda r, s: (s, 0, 0))
    return pl.pallas_call(
        widen_part_kernel,
        out_shape=jax.ShapeDtypeStruct((shards, 2, depth, width), BF16),
        grid=(depth // rows, shards),
        in_specs=[pl.BlockSpec((rows, tokens), lambda r, s: (r, 0)), tall_spec, tall_spec],
        out_specs=pl.BlockSpec((1, 2, rows, width), lambda r, s: (s, 0, r, 0)),
        cost_estimate=BRIEF,
        compiler_params=params(2),
    )(normed_t, d_gate, d_up)


def widen_back_kernel(dg_ref, du_ref, w_ref, o_ref):
    total = None
    for i in range(w_ref.shape[0]):
        part = dot_nt(dg_ref[i], w_ref[i, 0]) + dot_nt(du_ref[i], w_ref[i, 1])
        total = part if total is None else total + part
    o_ref[...] = total.astype(BF16)


def widen_back(d_gate, d_up, weights):
    shards, tokens, width = d_gate.shape
    depth = weights.shape[2]
    rows = tile_rows(tokens, 512)
    tall_spec = pl.BlockSpec((shards, rows, width), lambda r: (0, r, 0))
    return pl.pallas_call(
        widen_back_kernel,
        out_shape=jax.ShapeDtypeStruct((tokens, depth), BF16),
        grid=(tokens // rows,),
        in_specs=[
            tall_spec,
            tall_spec,
            pl.BlockSpec(weights.shape, lambda r: (0, 0, 0, 0), pipeline_mode=pl.Buffered(1)),
        ],
        out_specs=pl.BlockSpec((rows, depth), lambda r: (r, 0)),
        cost_estimate=BRIEF,
        compiler_params=params(1),
    )(d_gate, d_up, weights)


def stage_step(stage):
    return jnp.where(stage == 0, 3, jnp.where(stage == 3, 0, stage))


class Square:
    def __init__(self, acc, mine, away, twin, moved, corner, landed, tsend, trecv, msend, mrecv, csend, crecv):
        self.acc, self.mine, self.away, self.twin = acc, mine, away, twin
        self.moved, self.corner, self.landed = moved, corner, landed
        self.tsend, self.trecv, self.msend, self.mrecv = tsend, trecv, msend, mrecv
        self.csend, self.crecv = csend, crecv
        self.chip, self.core = place()
        self.rows = mine.shape[1]
        self.half = self.rows // 2

    def greet(self):
        peers = [(flip(self.chip, s, 4), self.core) for s in (1, 2)]
        greet(peers + [(self.chip, 1 - self.core)])

    def twin_copy(self, stage):
        return remote(
            self.away.at[stage], self.twin.at[stage], self.tsend.at[stage], self.trecv.at[stage],
            self.chip, 1 - self.core,
        )

    def offer(self, stage):
        own, other = self.core * self.rows, (1 - self.core) * self.rows
        self.mine[stage] = self.acc[pl.ds(pl.multiple_of(own, self.rows), self.rows)].astype(BF16)
        self.away[stage] = self.acc[pl.ds(pl.multiple_of(other, self.rows), self.rows)].astype(BF16)
        self.twin_copy(stage).start()

    def at(self, h):
        return pl.ds(h * self.half, self.half)

    def both(self, stage, h):
        return self.mine[stage, self.at(h)].astype(F32) + self.twin[stage, self.at(h)].astype(F32)

    def corner_copy(self, h):
        return remote(
            self.moved.at[0, self.at(h)], self.corner.at[h], self.csend.at[h], self.crecv.at[h],
            flip(self.chip, h + 1, 4), self.core,
        )

    def copy(self, stage, h):
        return remote(
            self.moved.at[stage, self.at(h)], self.landed.at[stage - 1, self.at(h)],
            self.msend.at[stage - 1, h], self.mrecv.at[stage - 1, h],
            flip(self.chip, stage, 4), self.core,
        )

    def corners(self):
        self.twin_copy(0).wait_recv()
        for h in range(2):
            self.moved[0, self.at(h)] = self.both(0, h).astype(BF16)
            self.corner_copy(h).start()

    def plain(self, stage):
        self.twin_copy(stage).wait_recv()
        h = stage - 1
        self.moved[stage, self.at(h)] = self.both(stage, h).astype(BF16)
        self.copy(stage, h).start()

    def joined(self, stage):
        h = 2 - stage
        self.corner_copy(h).wait_recv()
        total = self.both(stage, h) + self.corner[h].astype(F32)
        self.moved[stage, self.at(h)] = total.astype(BF16)
        self.copy(stage, h).start()

    def finish(self, o_ref):
        self.twin_copy(3).wait_recv()
        for h in range(2):
            o_ref[self.at(h)] = self.both(3, h)
        for stage, h in ((1, 0), (2, 1), (2, 0), (1, 1)):
            self.copy(stage, h).wait_recv()
            o_ref[self.at(h)] += self.landed[stage - 1, self.at(h)].astype(F32)
        for stage in (1, 2):
            for h in range(2):
                self.copy(stage, h).wait_send()
        for h in range(2):
            self.corner_copy(h).wait_send()
        for stage in range(4):
            self.twin_copy(stage).wait_send()


def square_kernel(compute, count, *refs):
    operands, o_ref, scratch = refs[:count], refs[count], refs[count + 1 :]
    run = Square(*scratch)
    stage = pl.program_id(0)

    @pl.when(stage == 0)
    def _():
        run.greet()

    target = jnp.bitwise_xor(run.chip, stage_step(stage))
    width = 2 * run.rows
    run.acc[...] = compute(operands, pl.ds(pl.multiple_of(target * width, width), width))
    run.offer(stage)

    @pl.when(stage == 1)
    def _():
        run.corners()

    @pl.when(stage == 2)
    def _():
        run.plain(1)

    @pl.when(stage == 3)
    def _():
        run.plain(2)
        run.joined(2)
        run.joined(1)
        run.finish(o_ref)


def square_reduce(compute, operands, rows, call_id):
    block = (rows, D)

    def held(shape):
        return pl.BlockSpec(shape, lambda s: (0,) * len(shape), pipeline_mode=pl.Buffered(1))

    return pl.pallas_call(
        functools.partial(square_kernel, compute, len(operands)),
        out_shape=jax.ShapeDtypeStruct(block, F32),
        grid=(4,),
        in_specs=[held(x.shape) for x in operands],
        out_specs=held(block),
        scratch_shapes=[
            pltpu.VMEM((2 * rows, D), F32),
            pltpu.VMEM((4,) + block, BF16),
            pltpu.VMEM((4,) + block, BF16),
            pltpu.VMEM((4,) + block, BF16),
            pltpu.VMEM((3,) + block, BF16),
            pltpu.VMEM((2, rows // 2, D), BF16),
            pltpu.VMEM((2,) + block, BF16),
            pltpu.SemaphoreType.DMA((4,)),
            pltpu.SemaphoreType.DMA((4,)),
            pltpu.SemaphoreType.DMA((2, 2)),
            pltpu.SemaphoreType.DMA((2, 2)),
            pltpu.SemaphoreType.DMA((2,)),
            pltpu.SemaphoreType.DMA((2,)),
        ],
        cost_estimate=BRIEF,
        compiler_params=pltpu.CompilerParams(
            collective_id=call_id, has_side_effects=True, vmem_limit_bytes=60 << 20
        ),
    )(*operands)


def widen_back_rows(refs, rows):
    dg_ref, du_ref, w_ref = refs
    total = None
    for i in range(w_ref.shape[0]):
        part = dot_nt(dg_ref[i, rows], w_ref[i, 0]) + dot_nt(du_ref[i, rows], w_ref[i, 1])
        total = part if total is None else total + part
    return total


def project_back_rows(refs, rows):
    d_ref, w_ref = refs
    return dot_nt(d_ref[rows], w_ref[...])


def mix_rows(refs, rows):
    h_ref, w_ref = refs
    total = None
    for i in range(w_ref.shape[0]):
        part = matmul(h_ref[i, rows], w_ref[i])
        total = part if total is None else total + part
    return total


def twin_kernel(compute, count, *refs):
    operands, (o_ref, corner_ref, x_ref, y_ref) = refs[:count], refs[count : count + 4]
    acc, mine, away, twin, tsend, trecv = refs[count + 4 :]
    chip, core = place()
    stage = pl.program_id(0)
    rows = o_ref.shape[0]

    def copy(s):
        return remote(away.at[s], twin.at[s], tsend.at[s], trecv.at[s], chip, 1 - core)

    def both(s):
        copy(s).wait_recv()
        return mine[s].astype(F32) + twin[s].astype(F32)

    @pl.when(stage == 0)
    def _():
        greet([(chip, 1 - core)])

    target = jnp.bitwise_xor(chip, stage_step(stage)) * 2 * rows
    acc[...] = compute(operands, pl.ds(pl.multiple_of(target, 2 * rows), 2 * rows))
    mine[stage] = acc[pl.ds(pl.multiple_of(core * rows, rows), rows)].astype(BF16)
    away[stage] = acc[pl.ds(pl.multiple_of((1 - core) * rows, rows), rows)].astype(BF16)
    copy(stage).start()

    for s, part_ref in enumerate((corner_ref, x_ref, y_ref)):

        @pl.when(stage == s + 1)
        def _(s=s, part_ref=part_ref):
            part_ref[...] = both(s).astype(BF16)

    @pl.when(stage == 3)
    def _():
        o_ref[...] = both(3)
        for s in range(4):
            copy(s).wait_send()


def twin_reduce(compute, operands, rows, call_id):
    block = (rows, D)

    def held(shape):
        return pl.BlockSpec(shape, lambda s: (0,) * len(shape), pipeline_mode=pl.Buffered(1))

    return pl.pallas_call(
        functools.partial(twin_kernel, compute, len(operands)),
        out_shape=(jax.ShapeDtypeStruct(block, F32),) + (jax.ShapeDtypeStruct(block, BF16),) * 3,
        grid=(4,),
        in_specs=[held(x.shape) for x in operands],
        out_specs=(held(block),) * 4,
        scratch_shapes=[
            pltpu.VMEM((2 * rows, D), F32),
            pltpu.VMEM((4,) + block, BF16),
            pltpu.VMEM((4,) + block, BF16),
            pltpu.VMEM((4,) + block, BF16),
            pltpu.SemaphoreType.DMA((4,)),
            pltpu.SemaphoreType.DMA((4,)),
        ],
        cost_estimate=BRIEF,
        compiler_params=pltpu.CompilerParams(
            collective_id=call_id, has_side_effects=True, vmem_limit_bytes=60 << 20
        ),
    )(*operands)


def swap_others(parts):
    return tuple(swap_chips(part, step) for step, part in zip((3, 1, 2), parts))


def join(own, came):
    for part in came:
        own = own + part.astype(F32)
    return own


def entry_kernel(
    grps, chips, tok_ref, cot_ref, pack_ref, all_tok, all_cot, all_pack,
    tsend, trecv, tlocal, csend, crecv, clocal, psend, precv, plocal, zsend, zrecv, usend, dsend,
):
    grp = lax.axis_index("grp")
    chip, core = place()
    me = chip * 2 + core
    above, below = lax.rem(grp + 1, grps), lax.rem(grp + grps - 1, grps)
    near = [(flip(chip, s, chips), c) for s in range(1, chips) for c in (core, 1 - core)]
    near = near + [(chip, 1 - core)]
    barrier = pltpu.get_barrier_semaphore()
    for g in (above, below):
        pl.semaphore_signal(barrier, inc=1, device_id={"grp": g}, device_id_type=MESH)
    for to, c in near:
        pl.semaphore_signal(
            barrier, inc=1, device_id={"chip": to, "core": c}, device_id_type=MESH
        )
    pl.semaphore_wait(barrier, len(near) + 2)

    tok = Gather(chips, False, tok_ref, all_tok, tsend, trecv, tlocal)
    cot = Gather(chips, False, cot_ref, all_cot, csend, crecv, clocal)
    packs = []
    for i, (to, c) in enumerate(near):
        copy = remote(
            pack_ref.at[to * 2 + c], all_pack.at[grp, me], psend.at[i], precv.at[me], to, c
        )
        copy.start()
        packs.append(copy)
    mine = pltpu.make_async_copy(pack_ref.at[me], all_pack.at[grp, me], plocal)
    mine.start()
    tok.start()
    for to, c in near:
        slot = to * 2 + c
        remote(
            pack_ref.at[me], all_pack.at[grp, slot], psend.at[0], precv.at[slot], to, c
        ).wait_recv()
    mine.wait()

    def z_copy(block, sem, to):
        return pltpu.make_async_remote_copy(
            src_ref=all_pack.at[block],
            dst_ref=all_pack.at[block],
            send_sem=sem,
            recv_sem=zrecv.at[block],
            device_id={"grp": to},
            device_id_type=MESH,
        )

    has_above, has_below = grp + 1 < grps, grp > 0

    def send(step, block, up):
        @pl.when(has_above if up else has_below)
        def _():
            z_copy(block, (usend if up else dsend).at[step], above if up else below).start()

    def relay(step):
        low, high = grp - step, grp + step

        @pl.when(low >= 0)
        def _():
            z_copy(low, zsend, below).wait_recv()
            send(step, low, True)

        @pl.when(high < grps)
        def _():
            z_copy(high, zsend, above).wait_recv()
            send(step, high, False)

    send(0, grp, True)
    send(0, grp, False)
    tok.relay(0, 4)
    relay(1)
    cot.start()
    tok.relay(4, None)
    for step in range(2, grps - 1):
        relay(step)
    cot.relay(0, 4)
    if grps > 2:
        relay(grps - 1)
    cot.relay(4, None)
    tok.finish()
    cot.finish()
    for copy in packs:
        copy.wait_send()
    for step in range(grps):
        for up in (True, False):
            held = grp - step >= 0 if up else grp + step < grps

            @pl.when(held & (has_above if up else has_below))
            def _(step=step, up=up):
                block = grp - step if up else grp + step
                z_copy(block, (usend if up else dsend).at[step], above if up else below).wait_send()


def entry(tokens, cotangent, packed, grps, chips, call_id):
    devs = 2 * chips
    return pl.pallas_call(
        functools.partial(entry_kernel, grps, chips),
        out_shape=(
            jax.ShapeDtypeStruct((devs,) + tokens.shape, BF16),
            jax.ShapeDtypeStruct((devs,) + cotangent.shape, BF16),
            jax.ShapeDtypeStruct((grps,) + packed.shape, BF16),
        ),
        in_specs=[ANY] * 3,
        out_specs=(ANY,) * 3,
        scratch_shapes=gather_sems(chips)
        + gather_sems(chips)
        + [
            pltpu.SemaphoreType.DMA((devs,)),
            pltpu.SemaphoreType.DMA((devs,)),
            pltpu.SemaphoreType.DMA,
            pltpu.SemaphoreType.DMA,
            pltpu.SemaphoreType.DMA((grps,)),
            pltpu.SemaphoreType.DMA((grps,)),
            pltpu.SemaphoreType.DMA((grps,)),
        ],
        cost_estimate=BRIEF,
        compiler_params=pltpu.CompilerParams(collective_id=call_id, has_side_effects=True),
    )(tokens, cotangent, packed)


def project_kernel(used, x_ref, w_ref, n_ref, qkv_ref, gain_ref):
    @pl.when(pl.program_id(0) == 0)
    def _():
        gain_ref[...] = w_ref[:, used:].astype(F32).T[:8]

    values = x_ref[...].astype(F32)
    factor = lax.rsqrt(jnp.mean(values * values, axis=-1, keepdims=True) + EPSILON)
    normed = (values * factor * gain_ref[0:1]).astype(BF16)
    n_ref[...] = normed
    qkv_ref[...] = matmul(normed, w_ref[:, :used]).astype(BF16)


def project(tokens, packed, used):
    count, depth = tokens.shape
    rows = tile_rows(count, 256)
    return pl.pallas_call(
        functools.partial(project_kernel, used),
        out_shape=(
            jax.ShapeDtypeStruct((count, depth), BF16),
            jax.ShapeDtypeStruct((count, used), BF16),
            jax.ShapeDtypeStruct((8, depth), F32),
        ),
        grid=(count // rows,),
        in_specs=[
            pl.BlockSpec((rows, depth), lambda r: (r, 0)),
            pl.BlockSpec(packed.shape, lambda r: (0, 0)),
        ],
        out_specs=(
            pl.BlockSpec((rows, depth), lambda r: (r, 0)),
            pl.BlockSpec((rows, used), lambda r: (r, 0)),
            pl.BlockSpec((8, depth), lambda r: (0, 0)),
        ),
        cost_estimate=BRIEF,
        compiler_params=params(1),
    )(tokens, packed)


def norm_parts(values):
    factor = lax.rsqrt(jnp.mean(values * values, axis=-1, keepdims=True) + EPSILON)
    return factor


def norm_back(values, factor, gain, grad):
    scaled = gain * grad
    inner = jnp.mean(values * scaled, axis=-1, keepdims=True)
    return factor * scaled - values * (factor * factor * factor * inner), jnp.sum(
        grad * values * factor, axis=0
    )


def on_device(
    tokens,
    block_group,
    block_slot,
    attn_gain,
    w_query,
    w_key,
    w_value,
    w_out,
    mlp_gain,
    w_gate,
    w_up,
    w_down,
    cotangent,
):
    grps = lax.axis_size("grp")
    devs = lax.axis_size(PLANE)
    chips = devs // 2
    rows = tokens.shape[0]
    w_rows = w_query.shape[0]
    q_heads = HEADS // devs
    kv_heads = 1
    assert devs % KV_HEADS == 0
    kv_copies = max(1, devs // KV_HEADS)
    q_cols, kv_cols = q_heads * HEAD_DIM, kv_heads * HEAD_DIM
    row_blocks = rows // BLOCK * devs
    row_groups = row_blocks // GROUP_BLOCKS

    row_first = lax.axis_index("grp") * row_blocks
    keys = lax.dynamic_slice_in_dim(block_group, row_first, row_blocks) * GROUP_BLOCKS
    keys = keys + lax.dynamic_slice_in_dim(block_slot, row_first, row_blocks)
    rank = jnp.sum((keys[None, :] < keys[:, None]).astype(jnp.int32), axis=1)
    ids = jnp.arange(row_blocks, dtype=jnp.int32)
    order = jnp.sum(jnp.where(rank[None, :] == ids[:, None], ids[None, :], 0), axis=1)

    def kv_split(w):
        w = w.reshape(w_rows, devs // kv_copies, kv_cols)
        return jnp.repeat(w, kv_copies, axis=1) if kv_copies > 1 else w

    gains = jnp.stack([attn_gain, mlp_gain], axis=1)
    cols = D // 4
    room = cols - q_cols - 2 * kv_cols
    gains = jnp.pad(gains, ((0, 0), (0, room - 2)))
    gains = jnp.broadcast_to(gains[:, None, :], (w_rows, devs, room))
    packed = jnp.concatenate(
        [w_query.reshape(w_rows, devs, q_cols), kv_split(w_key), kv_split(w_value), gains], axis=2
    )
    packed = jnp.swapaxes(packed, 0, 1)
    used = q_cols + 2 * kv_cols
    out_full = gather(w_out[None], "grp")
    upstream = cotangent.astype(F32)
    d_branch_mlp = (RESID_MULT * upstream).astype(BF16)
    all_tokens, d_branch_mlp, packed = entry(tokens, d_branch_mlp, packed, grps, chips, 2)
    packed = packed.reshape(D, cols)
    normed_one, qkv, gains = project(all_tokens.reshape(devs * rows, D), packed, used)
    gain_one, gain_two, w_qkv = gains[0], gains[1], packed[:, :used]
    d_branch_mlp = d_branch_mlp.reshape(devs * rows, D)
    attended = attend(qkv, order, q_heads)
    attended = plane_exchange(
        attended, (rows, D), by_rows(rows), by_cols(q_cols), chips, 3
    )

    out_full = plane_gather(out_full, chips, 4, inner=True).reshape(D, D)
    layer_in = tokens.astype(F32)
    branch_attn = matmul(attended, out_full)
    residual = layer_in + RESID_MULT * branch_attn
    factor_two = norm_parts(residual)
    normed_two = (residual * factor_two * gain_two).astype(BF16)
    normed_two = plane_gather(normed_two, chips, 1).reshape(devs * rows, D)
    wide_w = gather(jnp.stack([w_gate, w_up])[None], "grp")
    down_w = gather(w_down[None], "grp")
    hidden, hidden_t, silu, slope, normed_t = widen(normed_two, wide_w)
    part_down = down_part(hidden_t, d_branch_mlp)
    part_down, hidden, silu = lax.optimization_barrier((part_down, hidden, silu))
    grad_down = scatter(part_down, "grp")
    if chips == 4:
        branch_mlp, *shares = twin_reduce(mix_rows, (hidden, down_w), rows, 11)
        shares, silu = lax.optimization_barrier((shares, silu))
        shares = swap_others(shares)
    d_gate, d_up = narrow_back(silu, slope, d_branch_mlp, down_w)
    if chips == 4:
        part_wide = widen_part(normed_t, d_gate, d_up)
        part_wide, shares, d_gate, d_up = lax.optimization_barrier(
            (part_wide, shares, d_gate, d_up)
        )
        grad_wide = scatter(part_wide, "grp")
        branch_mlp = join(branch_mlp, shares)
        d_normed_two = square_reduce(widen_back_rows, (d_gate, d_up, wide_w), rows, 10)
    else:
        part_wide = widen_part(normed_t, d_gate, d_up)
        part_wide, d_gate, d_up = lax.optimization_barrier((part_wide, d_gate, d_up))
        grad_wide = scatter(part_wide, "grp")
        d_normed_two = widen_back(d_gate, d_up, wide_w)
        d_normed_two = plane_reduce(d_normed_two.reshape(devs, rows, D), chips, 5)
        branch_mlp = mix(hidden, down_w)
        branch_mlp = plane_reduce(branch_mlp.reshape(devs, rows, D), chips, 5)

    d_residual_norm, d_gain_two = norm_back(residual, factor_two, gain_two, d_normed_two)
    d_residual = upstream + d_residual_norm
    d_branch_attn = (RESID_MULT * d_residual).astype(BF16)
    grad_out = over_rows(attended, d_branch_attn).astype(BF16)
    grad_out, d_branch_attn = lax.optimization_barrier((grad_out, d_branch_attn))
    if chips == 4:
        drift_out = Drift(grad_out.reshape(grps, 4, 2, w_rows, D), 1)
    d_attended = over_cols(d_branch_attn, out_full).astype(BF16)
    layer_out = residual + RESID_MULT * branch_mlp
    scaled_attn = RESID_MULT * branch_attn
    scaled_mlp = RESID_MULT * branch_mlp
    squares = jnp.stack(
        [
            jnp.sum(layer_out * layer_out),
            jnp.sum(scaled_attn * scaled_attn),
            jnp.sum(scaled_mlp * scaled_mlp),
        ]
    )
    totals = jnp.concatenate([d_gain_two, squares, jnp.zeros((1021,), F32)])
    d_attended, totals = exchange_total(
        d_attended, totals.reshape(8, 3 * D // 16), (devs * rows, q_cols), rows, q_cols, grps, chips, 7
    )
    if chips == 4:
        sent_out, d_attended = lax.optimization_barrier((drift_out.parts(), d_attended))
        sent_out = swap_others((sent_out[2], sent_out[0], sent_out[1]))
    d_attended, grad_down = lax.optimization_barrier((d_attended, grad_down))
    d_qkv = attend_back(qkv, d_attended, order, q_heads)
    if chips == 4:
        sent_out, d_qkv = lax.optimization_barrier((sent_out, d_qkv))
        d_normed_one, *others = twin_reduce(project_back_rows, (d_qkv, w_qkv), rows, 5)
        others, d_qkv = lax.optimization_barrier((others, d_qkv))
        others = swap_others(others)
        grad_out = drift_out.finish(sent_out).astype(BF16)
    else:
        grad_out = plane_reduce(
            grad_out.reshape(grps, devs, w_rows, D), chips, 6, dtype=BF16, inner=True
        )
    sent = over_rows(normed_one, d_qkv).astype(BF16)
    sent, grad_wide = lax.optimization_barrier((sent, grad_wide))
    sent = scatter(sent, "grp")
    grad_out = scatter(grad_out, "grp").reshape(w_rows, D).astype(F32)
    if chips == 4:
        d_normed_one = join(d_normed_one, others)
    else:
        d_normed_one = over_cols(d_qkv, w_qkv).astype(BF16).reshape(devs, rows, D)
        d_normed_one = plane_reduce(d_normed_one, chips, 5)
    d_input_norm, _ = norm_back(layer_in, norm_parts(layer_in), gain_one, d_normed_one)
    tokens_grad = (d_residual + d_input_norm).astype(BF16)
    sent = sent.reshape(devs, w_rows, q_cols + 2 * kv_cols)
    sent = plane_exchange(sent, sent.shape, by_slot, by_slot, chips, 9).astype(F32)

    def kv_join(g):
        g = g.reshape(devs // kv_copies, kv_copies, w_rows, kv_cols)
        g = jnp.sum(g, axis=1) if kv_copies > 1 else g[:, 0]
        return jnp.swapaxes(g, 0, 1).reshape(w_rows, KV_HEADS * HEAD_DIM)

    grad_query = jnp.swapaxes(sent[:, :, :q_cols], 0, 1).reshape(w_rows, D)
    grad_key = kv_join(sent[:, :, q_cols : q_cols + kv_cols])
    grad_value = kv_join(sent[:, :, q_cols + kv_cols : q_cols + 2 * kv_cols])

    gain_one_grad = sum(
        jnp.sum(weight.astype(F32) * grad, axis=1)
        for weight, grad in ((w_query, grad_query), (w_key, grad_key), (w_value, grad_value))
    ) / attn_gain.astype(F32)
    totals = totals.reshape(-1)
    rms_stats = jnp.sqrt(totals[D : D + 3] / (rows * grps * devs * D))
    gain_first = (lax.axis_index("grp") * devs + lax.axis_index(PLANE)) * w_rows
    gain_two_grad = lax.dynamic_slice(totals, (gain_first,), (w_rows,))
    return (
        layer_out.astype(BF16),
        tokens_grad,
        gain_one_grad,
        grad_query,
        grad_key,
        grad_value,
        grad_out,
        gain_two_grad,
        grad_wide[0, 0].astype(F32),
        grad_wide[0, 1].astype(F32),
        grad_down[0].astype(F32),
        rms_stats,
    )


def solution(mesh):
    shape = (mesh.shape["grp"], mesh.shape["blk"] // 2, 2)
    mesh = Mesh(mesh.devices.reshape(shape), EVERY)
    row, col, vec = P(EVERY, None), P(None, EVERY), P(EVERY)
    return jax.shard_map(
        on_device,
        mesh=mesh,
        in_specs=(row, P(), P(), vec, row, row, row, row, vec, col, col, row, row),
        out_specs=(row, row, vec, row, row, row, row, vec, col, col, row, P()),
        check_vma=False,
    )
```

```python
import functools

import jax
import jax.numpy as jnp
from jax import lax
from jax.experimental import pallas as pl
from jax.experimental.pallas import tpu as pltpu
from jax.sharding import Mesh
from jax.sharding import PartitionSpec as P

D = 2048
HEADS = 32
KV_HEADS = 8
HEAD_DIM = 64
BLOCK = 128
PROMPT_BLOCKS = 8
GROUP_BLOCKS = 16
PER_GROUP = HEADS // KV_HEADS

ATTN_MULT = 0.015625
RESID_MULT = 0.22
EPSILON = 1e-05
MASKED = -1e30

PLANE = ("chip", "core")
EVERY = ("grp", "chip", "core")
BF16 = jnp.bfloat16
F32 = jnp.float32


MESH = pl.DeviceIdType.MESH
BRIEF = pl.CostEstimate(flops=1000, bytes_accessed=1000, transcendentals=0)
ANY = pl.BlockSpec(memory_space=pl.ANY)
VMEM = pl.BlockSpec(memory_space=pltpu.VMEM)


def place():
    return lax.axis_index("chip"), lax.axis_index("core")


def flip(chip, step, chips):
    return jnp.bitwise_xor(chip, step) if chips == 4 else lax.rem(chip + step, chips)


def unflip(chip, step, chips):
    return jnp.bitwise_xor(chip, step) if chips == 4 else lax.rem(chip + chips - step, chips)


def greet(peers):
    barrier = pltpu.get_barrier_semaphore()
    for chip, core in peers:
        pl.semaphore_signal(
            barrier, inc=1, device_id={"chip": chip, "core": core}, device_id_type=MESH
        )
    pl.semaphore_wait(barrier, len(peers))


def remote(src, dst, send, recv, chip, core):
    return pltpu.make_async_remote_copy(
        src_ref=src,
        dst_ref=dst,
        send_sem=send,
        recv_sem=recv,
        device_id={"chip": chip, "core": core},
        device_id_type=MESH,
    )


class Gather:
    def __init__(self, chips, inner, x_ref, o_ref, send, recv, local):
        self.chips, self.inner, self.x, self.o = chips, inner, x_ref, o_ref
        self.send, self.recv, self.local = send, recv, local
        self.chip, self.core = place()
        self.half = x_ref.shape[0] // 2
        self.started = []

    def greet(self):
        steps = (1, 2) if self.chips == 4 else range(1, self.chips)
        peers = [(flip(self.chip, s, self.chips), self.core) for s in steps]
        greet(peers + [(self.chip, 1 - self.core)])

    def piece(self, slot, h):
        at = pl.ds(h * self.half, self.half)
        return self.o.at[at, slot] if self.inner else self.o.at[slot, at]

    def own(self, h):
        return self.x.at[pl.ds(h * self.half, self.half)]

    def slot(self, chip, core):
        return chip * 2 + core

    def push(self, src, slot, h, chip, core):
        i = len(self.started)
        copy = remote(src, self.piece(slot, h), self.send.at[i], self.recv.at[slot, h], chip, core)
        copy.start()
        self.started.append(copy)

    def wait_for(self, slot, h):
        remote(
            self.own(h), self.piece(slot, h), self.send.at[0], self.recv.at[slot, h],
            self.chip, 1 - self.core,
        ).wait_recv()

    def start(self):
        me = self.slot(self.chip, self.core)
        if self.chips == 4:
            for h, s in ((0, 1), (1, 2), (1, 1), (0, 2)):
                self.push(self.own(h), me, h, flip(self.chip, s, 4), self.core)
        else:
            for s in range(1, self.chips):
                for h in range(2):
                    self.push(self.own(h), me, h, flip(self.chip, s, self.chips), self.core)
        for h in range(2):
            self.push(self.own(h), me, h, self.chip, 1 - self.core)
        whole = self.o.at[:, me] if self.inner else self.o.at[me]
        self.mine = pltpu.make_async_copy(self.x, whole, self.local)
        self.mine.start()

    def relay(self, first=0, last=None):
        if self.chips == 4:
            plan = ((1, 0, 2), (2, 1, 1), (1, 1, 0), (2, 0, 0), (3, 0, 0), (3, 1, 0))
        else:
            plan = tuple((s, h, 0) for s in range(1, self.chips) for h in range(2))
        for s, h, onward in plan[first:last]:
            slot = self.slot(unflip(self.chip, s, self.chips), self.core)
            self.wait_for(slot, h)
            if onward:
                self.push(self.piece(slot, h), slot, h, flip(self.chip, onward, 4), self.core)
            self.push(self.piece(slot, h), slot, h, self.chip, 1 - self.core)

    def finish(self):
        for s in range(self.chips):
            slot = self.slot(unflip(self.chip, s, self.chips), 1 - self.core)
            for h in range(2):
                self.wait_for(slot, h)
        for copy in self.started:
            copy.wait_send()
        self.mine.wait()


def gather_sems(chips):
    return [
        pltpu.SemaphoreType.DMA((4 * chips + 4,)),
        pltpu.SemaphoreType.DMA((2 * chips, 2)),
        pltpu.SemaphoreType.DMA,
    ]


def gather_kernel(chips, inner, x_ref, o_ref, *sems):
    run = Gather(chips, inner, x_ref, o_ref, *sems)
    run.greet()
    run.start()
    run.relay()
    run.finish()


def plane_gather(x, chips, call_id, inner=False):
    devs = 2 * chips
    shape = (x.shape[0], devs) + x.shape[1:] if inner else (devs,) + x.shape
    return pl.pallas_call(
        functools.partial(gather_kernel, chips, inner),
        out_shape=jax.ShapeDtypeStruct(shape, x.dtype),
        in_specs=[ANY],
        out_specs=ANY,
        scratch_shapes=gather_sems(chips),
        cost_estimate=BRIEF,
        compiler_params=pltpu.CompilerParams(collective_id=call_id, has_side_effects=True),
    )(x)


def reduce_kernel(chips, inner, p_ref, o_ref, total, mine, twin, moved, corner, landed, lsem, tsend, trecv, msend, mrecv, csend, crecv):
    chip, core = place()
    sib = 1 - core
    half = (p_ref.shape[0] if inner else p_ref.shape[1]) // 2
    block = (lambda slot: p_ref.at[:, slot]) if inner else (lambda slot: p_ref.at[slot])
    steps = (1, 2) if chips == 4 else tuple(range(1, chips))
    peers = [(flip(chip, s, chips), core) for s in steps]
    greet(peers + [(chip, sib)])
    order = (3, 1, 2, 0) if chips == 4 else tuple(range(1, chips)) + (0,)
    loads, twins = {}, {}
    for s in order:
        to = flip(chip, s, chips) * 2
        twins[s] = remote(block(to + sib), twin.at[s], tsend.at[s], trecv.at[s], chip, sib)
        twins[s].start()
        loads[s] = pltpu.make_async_copy(block(to + core), mine.at[s], lsem.at[s])
        loads[s].start()

    def part(s, h):
        at = pl.ds(h * half, half)
        return mine[s, at].astype(F32) + twin[s, at].astype(F32)

    def ready(s):
        loads[s].wait()
        twins[s].wait_recv()

    sent = []
    if chips == 4:
        corners = []
        ready(3)
        for h, s in ((0, 1), (1, 2)):
            moved[3, pl.ds(h * half, half)] = part(3, h).astype(BF16)
            copy = remote(moved.at[3, pl.ds(h * half, half)], corner.at[h], csend.at[h], crecv.at[h], flip(chip, s, 4), core)
            copy.start()
            corners.append(copy)

        def send(s, h):
            at = pl.ds(h * half, half)
            copy = remote(moved.at[s, at], landed.at[s - 1, at], msend.at[s - 1, h], mrecv.at[s - 1, h], flip(chip, s, 4), core)
            copy.start()
            sent.append(copy)

        for s, h in ((1, 0), (2, 1)):
            ready(s)
            moved[s, pl.ds(h * half, half)] = part(s, h).astype(BF16)
            send(s, h)
        for s, h in ((2, 0), (1, 1)):
            corners[h].wait_recv()
            moved[s, pl.ds(h * half, half)] = (part(s, h) + corner[h].astype(F32)).astype(BF16)
            send(s, h)
        for copy in corners:
            copy.wait_send()
    else:
        for s in steps:
            ready(s)
            for h in range(2):
                at = pl.ds(h * half, half)
                moved[s, at] = part(s, h).astype(BF16)
                copy = remote(moved.at[s, at], landed.at[s - 1, at], msend.at[s - 1, h], mrecv.at[s - 1, h], flip(chip, s, chips), core)
                copy.start()
                sent.append(copy)
    ready(0)
    for h in range(2):
        total[pl.ds(h * half, half)] = part(0, h)
    for copy in sent:
        copy.wait()
    for s in steps[:-1]:
        total[...] += landed[s - 1].astype(F32)
    o_ref[...] = (total[...] + landed[steps[-1] - 1].astype(F32)).astype(o_ref.dtype)
    for s in order:
        twins[s].wait_send()


def plane_reduce(p, chips, call_id, dtype=F32, inner=False):
    block = (p.shape[0],) + p.shape[2:] if inner else p.shape[1:]
    steps = 2 if chips == 4 else chips - 1
    return pl.pallas_call(
        functools.partial(reduce_kernel, chips, inner),
        out_shape=jax.ShapeDtypeStruct(block, dtype),
        in_specs=[ANY],
        out_specs=VMEM,
        scratch_shapes=[
            pltpu.VMEM(block, F32),
            pltpu.VMEM((chips,) + block, BF16),
            pltpu.VMEM((chips,) + block, BF16),
            pltpu.VMEM((chips,) + block, BF16),
            pltpu.VMEM((2, block[0] // 2) + block[1:], BF16),
            pltpu.VMEM((steps,) + block, BF16),
            pltpu.SemaphoreType.DMA((chips,)),
            pltpu.SemaphoreType.DMA((chips,)),
            pltpu.SemaphoreType.DMA((chips,)),
            pltpu.SemaphoreType.DMA((steps, 2)),
            pltpu.SemaphoreType.DMA((steps, 2)),
            pltpu.SemaphoreType.DMA((2,)),
            pltpu.SemaphoreType.DMA((2,)),
        ],
        cost_estimate=BRIEF,
        compiler_params=pltpu.CompilerParams(
            collective_id=call_id, has_side_effects=True, vmem_limit_bytes=56 << 20
        ),
    )(p)


def swap_chips(values, step):
    return lax.ppermute(values, "chip", [(c, c ^ step) for c in range(4)])


class Drift:
    def __init__(self, pairs, axis):
        self.axis = axis
        self.chip, self.core = place()
        away = lax.dynamic_index_in_dim(pairs, 1 - self.core, axis + 1, keepdims=False)
        self.mine = lax.dynamic_index_in_dim(pairs, self.core, axis + 1, keepdims=False)
        self.twin = lax.ppermute(away, "core", [(0, 1), (1, 0)])

    def part(self, step):
        at = jnp.bitwise_xor(self.chip, step)
        mine = lax.dynamic_index_in_dim(self.mine, at, self.axis, keepdims=False)
        twin = lax.dynamic_index_in_dim(self.twin, at, self.axis, keepdims=False)
        return mine.astype(F32) + twin.astype(F32)

    def parts(self):
        return tuple(self.part(step).astype(BF16) for step in (1, 2, 3))

    def finish(self, came):
        total = self.part(0)
        for part in came:
            total = total + part.astype(F32)
        return total


def exchange_kernel(chips, cut, paste, x_ref, o_ref, send, recv, local):
    chip, core = place()
    me = chip * 2 + core
    peers = [(flip(chip, s, chips), c) for s in range(1, chips) for c in (core, 1 - core)]
    peers = peers + [(chip, 1 - core)]
    greet(peers)
    far = [p for p in ([3, 1, 2] if chips == 4 else range(1, chips))]
    order = [(flip(chip, s, chips), c) for s in far for c in (core, 1 - core)] + [(chip, 1 - core)]
    copies = []
    for i, (to, c) in enumerate(order):
        copy = remote(cut(x_ref, to * 2 + c), paste(o_ref, me), send.at[i], recv.at[me], to, c)
        copy.start()
        copies.append(copy)
    mine = pltpu.make_async_copy(cut(x_ref, me), paste(o_ref, me), local)
    mine.start()
    for s in far:
        for c in (core, 1 - core):
            slot = unflip(chip, s, chips) * 2 + c
            remote(cut(x_ref, me), paste(o_ref, slot), send.at[0], recv.at[slot], chip, 1 - core).wait_recv()
    slot = chip * 2 + 1 - core
    remote(cut(x_ref, me), paste(o_ref, slot), send.at[0], recv.at[slot], chip, 1 - core).wait_recv()
    for copy in copies:
        copy.wait_send()
    mine.wait()


def plane_exchange(x, shape, cut, paste, chips, call_id):
    return pl.pallas_call(
        functools.partial(exchange_kernel, chips, cut, paste),
        out_shape=jax.ShapeDtypeStruct(shape, x.dtype),
        in_specs=[ANY],
        out_specs=ANY,
        scratch_shapes=[
            pltpu.SemaphoreType.DMA((2 * chips,)),
            pltpu.SemaphoreType.DMA((2 * chips,)),
            pltpu.SemaphoreType.DMA,
        ],
        cost_estimate=BRIEF,
        compiler_params=pltpu.CompilerParams(collective_id=call_id, has_side_effects=True),
    )(x)


def by_slot(ref, dev):
    return ref.at[dev]


def by_rows(rows):
    return lambda ref, dev: ref.at[pl.ds(pl.multiple_of(dev * rows, rows), rows)]


def by_cols(cols):
    return lambda ref, dev: ref.at[:, pl.ds(pl.multiple_of(dev * cols, cols), cols)]


def matmul(left, right):
    return jnp.dot(left, right, preferred_element_type=F32)


def over_rows(left, right):
    return lax.dot_general(left, right, (((0,), (0,)), ((), ())), preferred_element_type=F32)


def over_cols(left, right):
    return lax.dot_general(left, right, (((1,), (1,)), ((), ())), preferred_element_type=F32)


def gather(values, axes, axis=0):
    return lax.all_gather(values, axes, axis=axis, tiled=True)


def scatter(values, axes, axis=0):
    return lax.psum_scatter(values, axes, scatter_dimension=axis, tiled=True)


def dot_nt(left, right):
    return lax.dot_general(left, right, (((1,), (1,)), ((), ())), preferred_element_type=F32)


def head_stack(values, heads):
    col_head = lax.broadcasted_iota(jnp.int32, values.shape, 1) // HEAD_DIM
    return jnp.concatenate(
        [jnp.where(col_head == h, values, jnp.zeros_like(values)) for h in range(heads)], axis=0
    )


def head_pick(stacked, heads):
    rows = stacked.shape[0] // heads
    col_head = lax.broadcasted_iota(jnp.int32, (rows, stacked.shape[1]), 1) // HEAD_DIM
    total = jnp.zeros((rows, stacked.shape[1]), F32)
    for h in range(heads):
        total = jnp.where(col_head == h, stacked[h * rows : (h + 1) * rows], total)
    return total


def head_fold(values, heads):
    total = values[:, :HEAD_DIM]
    for h in range(1, heads):
        total = total + values[:, h * HEAD_DIM : (h + 1) * HEAD_DIM]
    return total


def repeat_heads(values, heads):
    return jnp.concatenate([values] * heads, axis=1)


def own_rows(order_ref, slot):
    return pl.ds(pl.multiple_of(order_ref[slot] * BLOCK, BLOCK), BLOCK)


def load_prompt(heads, order_ref, qkv_ref, k_ref, v_ref, first):
    q_cols = heads * HEAD_DIM
    for s in range(PROMPT_BLOCKS):
        pair = qkv_ref[own_rows(order_ref, first + s), q_cols:]
        at = pl.ds(s * BLOCK, BLOCK)
        k_ref[at] = repeat_heads(pair[:, :HEAD_DIM], heads)
        v_ref[at] = repeat_heads(pair[:, HEAD_DIM:], heads)


def by_keys(slot, body):
    prompt = PROMPT_BLOCKS * BLOCK
    quarter = prompt // 4
    seen = jnp.minimum(slot, PROMPT_BLOCKS) * BLOCK
    for n in range(1, 5):
        low = (n - 1) * quarter if n > 1 else -1

        @pl.when((seen > low) & (seen <= n * quarter))
        def _(n=n):
            body(n * quarter)


def soft_parts(heads, slot, q_stack, k_far, k_own):
    far = dot_nt(k_far, q_stack)
    own = dot_nt(k_own, q_stack)
    limit = jnp.minimum(slot, PROMPT_BLOCKS) * BLOCK
    far = jnp.where(lax.broadcasted_iota(jnp.int32, far.shape, 0) < limit, far, MASKED)
    key = lax.broadcasted_iota(jnp.int32, own.shape, 0)
    row = lax.broadcasted_iota(jnp.int32, own.shape, 1) % BLOCK
    own = jnp.where(key <= row, own, MASKED)
    peak = jnp.maximum(jnp.max(far, axis=0, keepdims=True), jnp.max(own, axis=0, keepdims=True))
    far, own = jnp.exp(far - peak), jnp.exp(own - peak)
    scale = 1.0 / (jnp.sum(far, axis=0, keepdims=True) + jnp.sum(own, axis=0, keepdims=True))
    return far * scale, own * scale


def scaled_stack(q, heads):
    return head_stack((q.astype(F32) * ATTN_MULT).astype(BF16), heads)


def attend_kernel(heads, order_ref, qkv_ref, o_ref, k_ref, v_ref, vt_ref):
    first, slot = pl.program_id(0) * GROUP_BLOCKS, pl.program_id(1)
    q_cols = heads * HEAD_DIM

    @pl.when(slot == 0)
    def _():
        load_prompt(heads, order_ref, qkv_ref, k_ref, v_ref, first)
        vt_ref[...] = v_ref[...].astype(F32).T.astype(BF16)

    rows = own_rows(order_ref, first + slot)
    mine = qkv_ref[rows, :]
    k_own = repeat_heads(mine[:, q_cols : q_cols + HEAD_DIM], heads)
    v_own = repeat_heads(mine[:, q_cols + HEAD_DIM :], heads)
    q_stack = scaled_stack(mine[:, :q_cols], heads)

    def body(count):
        far, own = soft_parts(heads, slot, q_stack, k_ref[:count], k_own)
        mixed = matmul(vt_ref[:, :count], far.astype(BF16))
        mixed += matmul(v_own.astype(F32).T.astype(BF16), own.astype(BF16))
        o_ref[rows, :] = head_pick(mixed.T, heads).astype(BF16)

    by_keys(slot, body)


def attend_back_kernel(
    heads, order_ref, qkv_ref, d_ref, o_ref, k_ref, v_ref, kt_ref, dk_ref, dv_ref
):
    first, slot = pl.program_id(0) * GROUP_BLOCKS, pl.program_id(1)
    q_cols = heads * HEAD_DIM

    @pl.when(slot == 0)
    def _():
        load_prompt(heads, order_ref, qkv_ref, k_ref, v_ref, first)
        kt_ref[...] = k_ref[...].astype(F32).T.astype(BF16)
        dk_ref[...] = jnp.zeros_like(dk_ref)
        dv_ref[...] = jnp.zeros_like(dv_ref)

    rows = own_rows(order_ref, first + slot)
    mine = qkv_ref[rows, :]
    k_own = repeat_heads(mine[:, q_cols : q_cols + HEAD_DIM], heads)
    v_own = repeat_heads(mine[:, q_cols + HEAD_DIM :], heads)
    q_stack = scaled_stack(mine[:, :q_cols], heads)
    d_stack = head_stack(d_ref[rows, :], heads)

    def fold(d_k, d_v):
        return jnp.concatenate([head_fold(d_k, heads), head_fold(d_v, heads)], axis=1).astype(BF16)

    def body(count):
        far, own = soft_parts(heads, slot, q_stack, k_ref[:count], k_own)
        d_far, d_own = dot_nt(v_ref[:count], d_stack), dot_nt(v_own, d_stack)
        mean = jnp.sum(far * d_far, axis=0, keepdims=True)
        mean += jnp.sum(own * d_own, axis=0, keepdims=True)
        d_far = (far * (d_far - mean)).astype(BF16)
        d_own = (own * (d_own - mean)).astype(BF16)
        dv_ref[:count] += matmul(far.astype(BF16), d_stack)
        dk_ref[:count] += matmul(d_far, q_stack)
        dv_own = matmul(own.astype(BF16), d_stack)
        dk_own = matmul(d_own, q_stack)
        d_q = matmul(kt_ref[:, :count], d_far) + matmul(k_own.astype(F32).T.astype(BF16), d_own)
        o_ref[rows, :q_cols] = (head_pick(d_q.T, heads) * ATTN_MULT).astype(BF16)

        @pl.when(slot < PROMPT_BLOCKS)
        def _():
            at = pl.ds(pl.multiple_of(slot * BLOCK, BLOCK), BLOCK)
            dk_ref[at] += dk_own
            dv_ref[at] += dv_own

        @pl.when(slot >= PROMPT_BLOCKS)
        def _():
            o_ref[rows, q_cols:] = fold(dk_own, dv_own)

    by_keys(slot, body)

    @pl.when(slot == GROUP_BLOCKS - 1)
    def _():
        for s in range(PROMPT_BLOCKS):
            at = pl.ds(s * BLOCK, BLOCK)
            o_ref[own_rows(order_ref, first + s), q_cols:] = fold(dk_ref[at], dv_ref[at])


def whole(shape):
    return pl.BlockSpec(shape, lambda g, s, order: (0,) * len(shape))


def attend(qkv, order, heads):
    tokens, cols = qkv.shape
    prompt, q_cols = PROMPT_BLOCKS * BLOCK, heads * HEAD_DIM
    return pl.pallas_call(
        functools.partial(attend_kernel, heads),
        out_shape=jax.ShapeDtypeStruct((tokens, q_cols), BF16),
        grid_spec=pltpu.PrefetchScalarGridSpec(
            num_scalar_prefetch=1,
            grid=(tokens // (GROUP_BLOCKS * BLOCK), GROUP_BLOCKS),
            in_specs=[whole((tokens, cols))],
            out_specs=whole((tokens, q_cols)),
            scratch_shapes=[
                pltpu.VMEM((prompt, q_cols), BF16),
                pltpu.VMEM((prompt, q_cols), BF16),
                pltpu.VMEM((q_cols, prompt), BF16),
            ],
        ),
        cost_estimate=BRIEF,
        compiler_params=pltpu.CompilerParams(vmem_limit_bytes=40 << 20),
    )(order, qkv)


def attend_back(qkv, d_attended, order, heads):
    tokens, cols = qkv.shape
    prompt, q_cols = PROMPT_BLOCKS * BLOCK, heads * HEAD_DIM
    return pl.pallas_call(
        functools.partial(attend_back_kernel, heads),
        out_shape=jax.ShapeDtypeStruct((tokens, cols), BF16),
        grid_spec=pltpu.PrefetchScalarGridSpec(
            num_scalar_prefetch=1,
            grid=(tokens // (GROUP_BLOCKS * BLOCK), GROUP_BLOCKS),
            in_specs=[whole((tokens, cols)), whole((tokens, q_cols))],
            out_specs=whole((tokens, cols)),
            scratch_shapes=[
                pltpu.VMEM((prompt, q_cols), BF16),
                pltpu.VMEM((prompt, q_cols), BF16),
                pltpu.VMEM((q_cols, prompt), BF16),
                pltpu.VMEM((prompt, q_cols), F32),
                pltpu.VMEM((prompt, q_cols), F32),
            ],
        ),
        cost_estimate=BRIEF,
        compiler_params=pltpu.CompilerParams(vmem_limit_bytes=40 << 20),
    )(order, qkv, d_attended)


def exchange_total_kernel(
    grps, chips, cut, paste, x_ref, t_ref, o_ref, sum_ref,
    over_z, over_plane, send, recv, local, zsend, zrecv, psend, precv,
):
    grp = lax.axis_index("grp")
    chip, core = place()
    me = chip * 2 + core
    far = [lax.rem(grp + s, grps) for s in range(1, grps)]
    steps = (3, 1, 2) if chips == 4 else tuple(range(1, chips))
    near = [(flip(chip, s, chips), c) for s in steps for c in (core, 1 - core)]
    near = near + [(chip, 1 - core)]
    barrier = pltpu.get_barrier_semaphore()
    for g in far:
        pl.semaphore_signal(barrier, inc=1, device_id={"grp": g}, device_id_type=MESH)
    for to, c in near:
        pl.semaphore_signal(
            barrier, inc=1, device_id={"chip": to, "core": c}, device_id_type=MESH
        )
    pl.semaphore_wait(barrier, len(far) + len(near))

    def z_copy(slot, sem, to):
        return pltpu.make_async_remote_copy(
            src_ref=t_ref,
            dst_ref=over_z.at[slot],
            send_sem=sem,
            recv_sem=zrecv.at[slot],
            device_id={"grp": to},
            device_id_type=MESH,
        )

    copies = []
    for i, g in enumerate(far):
        copy = z_copy(grp, zsend.at[i], g)
        copy.start()
        copies.append(copy)
    for i, (to, c) in enumerate(near):
        copy = remote(cut(x_ref, to * 2 + c), paste(o_ref, me), send.at[i], recv.at[me], to, c)
        copy.start()
        copies.append(copy)
    mine = pltpu.make_async_copy(cut(x_ref, me), paste(o_ref, me), local)
    mine.start()
    over_z[grp] = t_ref[...]
    for g in far:
        z_copy(g, zsend.at[0], g).wait_recv()
    over_plane[me] = jnp.sum(over_z[...], axis=0)
    for i, (to, c) in enumerate(near):
        copy = remote(over_plane.at[me], over_plane.at[me], psend.at[i], precv.at[me], to, c)
        copy.start()
        copies.append(copy)
    for to, c in near:
        slot = to * 2 + c
        remote(cut(x_ref, me), paste(o_ref, slot), send.at[0], recv.at[slot], to, c).wait_recv()
        remote(over_plane.at[me], over_plane.at[slot], psend.at[0], precv.at[slot], to, c).wait_recv()
    for copy in copies:
        copy.wait_send()
    mine.wait()
    sum_ref[...] = jnp.sum(over_plane[...], axis=0)


def exchange_total(x, t, shape, rows, cols, grps, chips, call_id):
    devs = 2 * chips
    return pl.pallas_call(
        functools.partial(exchange_total_kernel, grps, chips, by_cols(cols), by_rows(rows)),
        out_shape=(
            jax.ShapeDtypeStruct(shape, x.dtype),
            jax.ShapeDtypeStruct(t.shape, F32),
        ),
        in_specs=[ANY, VMEM],
        out_specs=(ANY, VMEM),
        scratch_shapes=[
            pltpu.VMEM((grps,) + t.shape, F32),
            pltpu.VMEM((devs,) + t.shape, F32),
            pltpu.SemaphoreType.DMA((devs,)),
            pltpu.SemaphoreType.DMA((devs,)),
            pltpu.SemaphoreType.DMA,
            pltpu.SemaphoreType.DMA((grps,)),
            pltpu.SemaphoreType.DMA((grps,)),
            pltpu.SemaphoreType.DMA((devs,)),
            pltpu.SemaphoreType.DMA((devs,)),
        ],
        cost_estimate=BRIEF,
        compiler_params=pltpu.CompilerParams(collective_id=call_id, has_side_effects=True),
    )(x, t)


def params(axes, mib=56):
    return pltpu.CompilerParams(
        dimension_semantics=("arbitrary",) * axes, vmem_limit_bytes=mib << 20
    )


def tile_rows(count, limit):
    while count % limit:
        limit //= 2
    return limit


def widen_kernel(n_ref, w_ref, h_ref, ht_ref, s_ref, t_ref, nt_ref):
    values = n_ref[...]
    gate, up = matmul(values, w_ref[0, 0]), matmul(values, w_ref[0, 1])
    sig = 1.0 / (1.0 + jnp.exp(-gate))
    silu = gate * sig
    hidden = (silu * up).astype(BF16)
    h_ref[0] = hidden
    ht_ref[0] = hidden.T
    s_ref[0] = silu.astype(BF16)
    t_ref[0] = (up * (sig * (1.0 + gate * (1.0 - sig)))).astype(BF16)

    @pl.when(pl.program_id(1) == 0)
    def _():
        nt_ref[...] = values.T


def widen(normed, weights):
    tokens, depth = normed.shape
    shards, _, _, width = weights.shape
    rows = tile_rows(tokens, 1024)
    tall = jax.ShapeDtypeStruct((shards, tokens, width), BF16)
    tall_spec = pl.BlockSpec((1, rows, width), lambda r, s: (s, r, 0))
    return pl.pallas_call(
        widen_kernel,
        out_shape=(
            tall,
            jax.ShapeDtypeStruct((shards, width, tokens), BF16),
            tall,
            tall,
            jax.ShapeDtypeStruct((depth, tokens), BF16),
        ),
        grid=(tokens // rows, shards),
        in_specs=[
            pl.BlockSpec((rows, depth), lambda r, s: (r, 0)),
            pl.BlockSpec((1, 2, depth, width), lambda r, s: (s, 0, 0, 0)),
        ],
        out_specs=(
            tall_spec,
            pl.BlockSpec((1, width, rows), lambda r, s: (s, 0, r)),
            tall_spec,
            tall_spec,
            pl.BlockSpec((depth, rows), lambda r, s: (0, r)),
        ),
        cost_estimate=BRIEF,
        compiler_params=params(2),
    )(normed, weights)


def down_part_kernel(ht_ref, d_ref, o_ref):
    o_ref[0] = matmul(ht_ref[0], d_ref[...]).astype(BF16)


def down_part(hidden_t, upstream):
    shards, width, tokens = hidden_t.shape
    depth = upstream.shape[1]
    cols = tile_rows(depth, 1024)
    return pl.pallas_call(
        down_part_kernel,
        out_shape=jax.ShapeDtypeStruct((shards, width, depth), BF16),
        grid=(depth // cols, shards),
        in_specs=[
            pl.BlockSpec((1, width, tokens), lambda c, s: (s, 0, 0)),
            pl.BlockSpec((tokens, cols), lambda c, s: (0, c)),
        ],
        out_specs=pl.BlockSpec((1, width, cols), lambda c, s: (s, 0, c)),
        cost_estimate=BRIEF,
        compiler_params=params(2),
    )(hidden_t, upstream)


def mix_kernel(h_ref, w_ref, m_ref):
    mixed = None
    for i in range(w_ref.shape[0]):
        part = matmul(h_ref[i], w_ref[i])
        mixed = part if mixed is None else mixed + part
    m_ref[...] = mixed.astype(BF16)


def narrow_specs(hidden, weights):
    shards, tokens, width = hidden.shape
    depth = weights.shape[2]
    rows = tile_rows(tokens, 512)
    return (
        tokens // rows,
        pl.BlockSpec((shards, rows, width), lambda r: (0, r, 0)),
        pl.BlockSpec((rows, depth), lambda r: (r, 0)),
        pl.BlockSpec(weights.shape, lambda r: (0, 0, 0), pipeline_mode=pl.Buffered(1)),
    )


def mix(hidden, weights):
    steps, tall_spec, flat_spec, weight_spec = narrow_specs(hidden, weights)
    return pl.pallas_call(
        mix_kernel,
        out_shape=jax.ShapeDtypeStruct((hidden.shape[1], weights.shape[2]), BF16),
        grid=(steps,),
        in_specs=[tall_spec, weight_spec],
        out_specs=flat_spec,
        cost_estimate=BRIEF,
        compiler_params=params(1),
    )(hidden, weights)


def narrow_back_kernel(s_ref, t_ref, d_ref, w_ref, dg_ref, du_ref):
    upstream = d_ref[...]
    for i in range(w_ref.shape[0]):
        d_hidden = dot_nt(upstream, w_ref[i])
        dg_ref[i] = (d_hidden * t_ref[i].astype(F32)).astype(BF16)
        du_ref[i] = (d_hidden * s_ref[i].astype(F32)).astype(BF16)


def narrow_back(silu, slope, upstream, weights):
    steps, tall_spec, flat_spec, weight_spec = narrow_specs(silu, weights)
    tall = jax.ShapeDtypeStruct(silu.shape, BF16)
    return pl.pallas_call(
        narrow_back_kernel,
        out_shape=(tall, tall),
        grid=(steps,),
        in_specs=[tall_spec, tall_spec, flat_spec, weight_spec],
        out_specs=(tall_spec, tall_spec),
        cost_estimate=BRIEF,
        compiler_params=params(1),
    )(silu, slope, upstream, weights)


def widen_part_kernel(nt_ref, dg_ref, du_ref, o_ref):
    values = nt_ref[...]
    o_ref[0, 0] = matmul(values, dg_ref[0]).astype(BF16)
    o_ref[0, 1] = matmul(values, du_ref[0]).astype(BF16)


def widen_part(normed_t, d_gate, d_up):
    depth, tokens = normed_t.shape
    shards, _, width = d_gate.shape
    rows = tile_rows(depth, 1024)
    tall_spec = pl.BlockSpec((1, tokens, width), lambda r, s: (s, 0, 0))
    return pl.pallas_call(
        widen_part_kernel,
        out_shape=jax.ShapeDtypeStruct((shards, 2, depth, width), BF16),
        grid=(depth // rows, shards),
        in_specs=[pl.BlockSpec((rows, tokens), lambda r, s: (r, 0)), tall_spec, tall_spec],
        out_specs=pl.BlockSpec((1, 2, rows, width), lambda r, s: (s, 0, r, 0)),
        cost_estimate=BRIEF,
        compiler_params=params(2),
    )(normed_t, d_gate, d_up)


def widen_back_kernel(dg_ref, du_ref, w_ref, o_ref):
    total = None
    for i in range(w_ref.shape[0]):
        part = dot_nt(dg_ref[i], w_ref[i, 0]) + dot_nt(du_ref[i], w_ref[i, 1])
        total = part if total is None else total + part
    o_ref[...] = total.astype(BF16)


def widen_back(d_gate, d_up, weights):
    shards, tokens, width = d_gate.shape
    depth = weights.shape[2]
    rows = tile_rows(tokens, 512)
    tall_spec = pl.BlockSpec((shards, rows, width), lambda r: (0, r, 0))
    return pl.pallas_call(
        widen_back_kernel,
        out_shape=jax.ShapeDtypeStruct((tokens, depth), BF16),
        grid=(tokens // rows,),
        in_specs=[
            tall_spec,
            tall_spec,
            pl.BlockSpec(weights.shape, lambda r: (0, 0, 0, 0), pipeline_mode=pl.Buffered(1)),
        ],
        out_specs=pl.BlockSpec((rows, depth), lambda r: (r, 0)),
        cost_estimate=BRIEF,
        compiler_params=params(1),
    )(d_gate, d_up, weights)


def stage_step(stage):
    return jnp.where(stage == 0, 3, jnp.where(stage == 3, 0, stage))


class Square:
    def __init__(self, acc, mine, away, twin, moved, corner, landed, tsend, trecv, msend, mrecv, csend, crecv):
        self.acc, self.mine, self.away, self.twin = acc, mine, away, twin
        self.moved, self.corner, self.landed = moved, corner, landed
        self.tsend, self.trecv, self.msend, self.mrecv = tsend, trecv, msend, mrecv
        self.csend, self.crecv = csend, crecv
        self.chip, self.core = place()
        self.rows = mine.shape[1]
        self.half = self.rows // 2

    def greet(self):
        peers = [(flip(self.chip, s, 4), self.core) for s in (1, 2)]
        greet(peers + [(self.chip, 1 - self.core)])

    def twin_copy(self, stage):
        return remote(
            self.away.at[stage], self.twin.at[stage], self.tsend.at[stage], self.trecv.at[stage],
            self.chip, 1 - self.core,
        )

    def offer(self, stage):
        own, other = self.core * self.rows, (1 - self.core) * self.rows
        self.mine[stage] = self.acc[pl.ds(pl.multiple_of(own, self.rows), self.rows)].astype(BF16)
        self.away[stage] = self.acc[pl.ds(pl.multiple_of(other, self.rows), self.rows)].astype(BF16)
        self.twin_copy(stage).start()

    def at(self, h):
        return pl.ds(h * self.half, self.half)

    def both(self, stage, h):
        return self.mine[stage, self.at(h)].astype(F32) + self.twin[stage, self.at(h)].astype(F32)

    def corner_copy(self, h):
        return remote(
            self.moved.at[0, self.at(h)], self.corner.at[h], self.csend.at[h], self.crecv.at[h],
            flip(self.chip, h + 1, 4), self.core,
        )

    def copy(self, stage, h):
        return remote(
            self.moved.at[stage, self.at(h)], self.landed.at[stage - 1, self.at(h)],
            self.msend.at[stage - 1, h], self.mrecv.at[stage - 1, h],
            flip(self.chip, stage, 4), self.core,
        )

    def corners(self):
        self.twin_copy(0).wait_recv()
        for h in range(2):
            self.moved[0, self.at(h)] = self.both(0, h).astype(BF16)
            self.corner_copy(h).start()

    def plain(self, stage):
        self.twin_copy(stage).wait_recv()
        h = stage - 1
        self.moved[stage, self.at(h)] = self.both(stage, h).astype(BF16)
        self.copy(stage, h).start()

    def joined(self, stage):
        h = 2 - stage
        self.corner_copy(h).wait_recv()
        total = self.both(stage, h) + self.corner[h].astype(F32)
        self.moved[stage, self.at(h)] = total.astype(BF16)
        self.copy(stage, h).start()

    def finish(self, o_ref):
        self.twin_copy(3).wait_recv()
        for h in range(2):
            o_ref[self.at(h)] = self.both(3, h)
        for stage, h in ((1, 0), (2, 1), (2, 0), (1, 1)):
            self.copy(stage, h).wait_recv()
            o_ref[self.at(h)] += self.landed[stage - 1, self.at(h)].astype(F32)
        for stage in (1, 2):
            for h in range(2):
                self.copy(stage, h).wait_send()
        for h in range(2):
            self.corner_copy(h).wait_send()
        for stage in range(4):
            self.twin_copy(stage).wait_send()


def square_kernel(compute, count, *refs):
    operands, o_ref, scratch = refs[:count], refs[count], refs[count + 1 :]
    run = Square(*scratch)
    stage = pl.program_id(0)

    @pl.when(stage == 0)
    def _():
        run.greet()

    @pl.when(stage == 3)
    def _():
        run.plain(2)
        run.joined(2)
        run.joined(1)

    target = jnp.bitwise_xor(run.chip, stage_step(stage))
    width = 2 * run.rows
    run.acc[...] = compute(operands, pl.ds(pl.multiple_of(target * width, width), width))
    run.offer(stage)

    @pl.when(stage == 1)
    def _():
        run.corners()

    @pl.when(stage == 2)
    def _():
        run.plain(1)

    @pl.when(stage == 3)
    def _():
        run.finish(o_ref)


def square_reduce(compute, operands, rows, call_id):
    block = (rows, D)

    def held(shape):
        return pl.BlockSpec(shape, lambda s: (0,) * len(shape), pipeline_mode=pl.Buffered(1))

    return pl.pallas_call(
        functools.partial(square_kernel, compute, len(operands)),
        out_shape=jax.ShapeDtypeStruct(block, F32),
        grid=(4,),
        in_specs=[held(x.shape) for x in operands],
        out_specs=held(block),
        scratch_shapes=[
            pltpu.VMEM((2 * rows, D), F32),
            pltpu.VMEM((4,) + block, BF16),
            pltpu.VMEM((4,) + block, BF16),
            pltpu.VMEM((4,) + block, BF16),
            pltpu.VMEM((3,) + block, BF16),
            pltpu.VMEM((2, rows // 2, D), BF16),
            pltpu.VMEM((2,) + block, BF16),
            pltpu.SemaphoreType.DMA((4,)),
            pltpu.SemaphoreType.DMA((4,)),
            pltpu.SemaphoreType.DMA((2, 2)),
            pltpu.SemaphoreType.DMA((2, 2)),
            pltpu.SemaphoreType.DMA((2,)),
            pltpu.SemaphoreType.DMA((2,)),
        ],
        cost_estimate=BRIEF,
        compiler_params=pltpu.CompilerParams(
            collective_id=call_id, has_side_effects=True, vmem_limit_bytes=60 << 20
        ),
    )(*operands)


def widen_back_rows(refs, rows):
    dg_ref, du_ref, w_ref = refs
    total = None
    for i in range(w_ref.shape[0]):
        part = dot_nt(dg_ref[i, rows], w_ref[i, 0]) + dot_nt(du_ref[i, rows], w_ref[i, 1])
        total = part if total is None else total + part
    return total


def project_back_rows(refs, rows):
    d_ref, w_ref = refs
    return dot_nt(d_ref[rows], w_ref[...])


def mix_rows(refs, rows):
    h_ref, w_ref = refs
    total = None
    for i in range(w_ref.shape[0]):
        part = matmul(h_ref[i, rows], w_ref[i])
        total = part if total is None else total + part
    return total


def twin_kernel(compute, count, *refs):
    operands, (o_ref, corner_ref, x_ref, y_ref) = refs[:count], refs[count : count + 4]
    acc, mine, away, twin, tsend, trecv = refs[count + 4 :]
    chip, core = place()
    stage = pl.program_id(0)
    rows = o_ref.shape[0]

    def copy(s):
        return remote(away.at[s], twin.at[s], tsend.at[s], trecv.at[s], chip, 1 - core)

    def both(s):
        copy(s).wait_recv()
        return mine[s].astype(F32) + twin[s].astype(F32)

    @pl.when(stage == 0)
    def _():
        greet([(chip, 1 - core)])

    target = jnp.bitwise_xor(chip, stage_step(stage)) * 2 * rows
    acc[...] = compute(operands, pl.ds(pl.multiple_of(target, 2 * rows), 2 * rows))
    mine[stage] = acc[pl.ds(pl.multiple_of(core * rows, rows), rows)].astype(BF16)
    away[stage] = acc[pl.ds(pl.multiple_of((1 - core) * rows, rows), rows)].astype(BF16)
    copy(stage).start()

    for s, part_ref in enumerate((corner_ref, x_ref, y_ref)):

        @pl.when(stage == s + 1)
        def _(s=s, part_ref=part_ref):
            part_ref[...] = both(s).astype(BF16)

    @pl.when(stage == 3)
    def _():
        o_ref[...] = both(3)
        for s in range(4):
            copy(s).wait_send()


def twin_reduce(compute, operands, rows, call_id):
    block = (rows, D)

    def held(shape):
        return pl.BlockSpec(shape, lambda s: (0,) * len(shape), pipeline_mode=pl.Buffered(1))

    return pl.pallas_call(
        functools.partial(twin_kernel, compute, len(operands)),
        out_shape=(jax.ShapeDtypeStruct(block, F32),) + (jax.ShapeDtypeStruct(block, BF16),) * 3,
        grid=(4,),
        in_specs=[held(x.shape) for x in operands],
        out_specs=(held(block),) * 4,
        scratch_shapes=[
            pltpu.VMEM((2 * rows, D), F32),
            pltpu.VMEM((4,) + block, BF16),
            pltpu.VMEM((4,) + block, BF16),
            pltpu.VMEM((4,) + block, BF16),
            pltpu.SemaphoreType.DMA((4,)),
            pltpu.SemaphoreType.DMA((4,)),
        ],
        cost_estimate=BRIEF,
        compiler_params=pltpu.CompilerParams(
            collective_id=call_id, has_side_effects=True, vmem_limit_bytes=60 << 20
        ),
    )(*operands)


def swap_others(parts):
    return tuple(swap_chips(part, step) for step, part in zip((3, 1, 2), parts))


def join(own, came):
    for part in came:
        own = own + part.astype(F32)
    return own


def entry_kernel(
    grps, chips, tok_ref, cot_ref, pack_ref, all_tok, all_cot, all_pack,
    tsend, trecv, tlocal, csend, crecv, clocal, psend, precv, plocal, zsend, zrecv, usend, dsend,
):
    grp = lax.axis_index("grp")
    chip, core = place()
    me = chip * 2 + core
    above, below = lax.rem(grp + 1, grps), lax.rem(grp + grps - 1, grps)
    near = [(flip(chip, s, chips), c) for s in range(1, chips) for c in (core, 1 - core)]
    near = near + [(chip, 1 - core)]
    barrier = pltpu.get_barrier_semaphore()
    for g in (above, below):
        pl.semaphore_signal(barrier, inc=1, device_id={"grp": g}, device_id_type=MESH)
    for to, c in near:
        pl.semaphore_signal(
            barrier, inc=1, device_id={"chip": to, "core": c}, device_id_type=MESH
        )
    pl.semaphore_wait(barrier, len(near) + 2)

    tok = Gather(chips, False, tok_ref, all_tok, tsend, trecv, tlocal)
    cot = Gather(chips, False, cot_ref, all_cot, csend, crecv, clocal)
    packs = []
    for i, (to, c) in enumerate(near):
        copy = remote(
            pack_ref.at[to * 2 + c], all_pack.at[grp, me], psend.at[i], precv.at[me], to, c
        )
        copy.start()
        packs.append(copy)
    mine = pltpu.make_async_copy(pack_ref.at[me], all_pack.at[grp, me], plocal)
    mine.start()
    tok.start()
    for to, c in near:
        slot = to * 2 + c
        remote(
            pack_ref.at[me], all_pack.at[grp, slot], psend.at[0], precv.at[slot], to, c
        ).wait_recv()
    mine.wait()

    def z_copy(block, sem, to):
        return pltpu.make_async_remote_copy(
            src_ref=all_pack.at[block],
            dst_ref=all_pack.at[block],
            send_sem=sem,
            recv_sem=zrecv.at[block],
            device_id={"grp": to},
            device_id_type=MESH,
        )

    has_above, has_below = grp + 1 < grps, grp > 0

    def send(step, block, up):
        @pl.when(has_above if up else has_below)
        def _():
            z_copy(block, (usend if up else dsend).at[step], above if up else below).start()

    def relay(step):
        low, high = grp - step, grp + step

        @pl.when(low >= 0)
        def _():
            z_copy(low, zsend, below).wait_recv()
            send(step, low, True)

        @pl.when(high < grps)
        def _():
            z_copy(high, zsend, above).wait_recv()
            send(step, high, False)

    send(0, grp, True)
    send(0, grp, False)
    tok.relay(0, 4)
    relay(1)
    cot.start()
    tok.relay(4, None)
    for step in range(2, grps - 1):
        relay(step)
    cot.relay(0, 4)
    if grps > 2:
        relay(grps - 1)
    cot.relay(4, None)
    tok.finish()
    cot.finish()
    for copy in packs:
        copy.wait_send()
    for step in range(grps):
        for up in (True, False):
            held = grp - step >= 0 if up else grp + step < grps

            @pl.when(held & (has_above if up else has_below))
            def _(step=step, up=up):
                block = grp - step if up else grp + step
                z_copy(block, (usend if up else dsend).at[step], above if up else below).wait_send()


def entry(tokens, cotangent, packed, grps, chips, call_id):
    devs = 2 * chips
    return pl.pallas_call(
        functools.partial(entry_kernel, grps, chips),
        out_shape=(
            jax.ShapeDtypeStruct((devs,) + tokens.shape, BF16),
            jax.ShapeDtypeStruct((devs,) + cotangent.shape, BF16),
            jax.ShapeDtypeStruct((grps,) + packed.shape, BF16),
        ),
        in_specs=[ANY] * 3,
        out_specs=(ANY,) * 3,
        scratch_shapes=gather_sems(chips)
        + gather_sems(chips)
        + [
            pltpu.SemaphoreType.DMA((devs,)),
            pltpu.SemaphoreType.DMA((devs,)),
            pltpu.SemaphoreType.DMA,
            pltpu.SemaphoreType.DMA,
            pltpu.SemaphoreType.DMA((grps,)),
            pltpu.SemaphoreType.DMA((grps,)),
            pltpu.SemaphoreType.DMA((grps,)),
        ],
        cost_estimate=BRIEF,
        compiler_params=pltpu.CompilerParams(collective_id=call_id, has_side_effects=True),
    )(tokens, cotangent, packed)


def project_kernel(used, x_ref, w_ref, n_ref, qkv_ref, gain_ref):
    @pl.when(pl.program_id(0) == 0)
    def _():
        gain_ref[...] = w_ref[:, used:].astype(F32).T[:8]

    values = x_ref[...].astype(F32)
    factor = lax.rsqrt(jnp.mean(values * values, axis=-1, keepdims=True) + EPSILON)
    normed = (values * factor * gain_ref[0:1]).astype(BF16)
    n_ref[...] = normed
    qkv_ref[...] = matmul(normed, w_ref[:, :used]).astype(BF16)


def project(tokens, packed, used):
    count, depth = tokens.shape
    rows = tile_rows(count, 256)
    return pl.pallas_call(
        functools.partial(project_kernel, used),
        out_shape=(
            jax.ShapeDtypeStruct((count, depth), BF16),
            jax.ShapeDtypeStruct((count, used), BF16),
            jax.ShapeDtypeStruct((8, depth), F32),
        ),
        grid=(count // rows,),
        in_specs=[
            pl.BlockSpec((rows, depth), lambda r: (r, 0)),
            pl.BlockSpec(packed.shape, lambda r: (0, 0)),
        ],
        out_specs=(
            pl.BlockSpec((rows, depth), lambda r: (r, 0)),
            pl.BlockSpec((rows, used), lambda r: (r, 0)),
            pl.BlockSpec((8, depth), lambda r: (0, 0)),
        ),
        cost_estimate=BRIEF,
        compiler_params=params(1),
    )(tokens, packed)


def norm_parts(values):
    factor = lax.rsqrt(jnp.mean(values * values, axis=-1, keepdims=True) + EPSILON)
    return factor


def norm_back(values, factor, gain, grad):
    scaled = gain * grad
    inner = jnp.mean(values * scaled, axis=-1, keepdims=True)
    return factor * scaled - values * (factor * factor * factor * inner), jnp.sum(
        grad * values * factor, axis=0
    )


def on_device(
    tokens,
    block_group,
    block_slot,
    attn_gain,
    w_query,
    w_key,
    w_value,
    w_out,
    mlp_gain,
    w_gate,
    w_up,
    w_down,
    cotangent,
):
    grps = lax.axis_size("grp")
    devs = lax.axis_size(PLANE)
    chips = devs // 2
    rows = tokens.shape[0]
    w_rows = w_query.shape[0]
    q_heads = HEADS // devs
    kv_heads = 1
    assert devs % KV_HEADS == 0
    kv_copies = max(1, devs // KV_HEADS)
    q_cols, kv_cols = q_heads * HEAD_DIM, kv_heads * HEAD_DIM
    row_blocks = rows // BLOCK * devs
    row_groups = row_blocks // GROUP_BLOCKS

    row_first = lax.axis_index("grp") * row_blocks
    keys = lax.dynamic_slice_in_dim(block_group, row_first, row_blocks) * GROUP_BLOCKS
    keys = keys + lax.dynamic_slice_in_dim(block_slot, row_first, row_blocks)
    rank = jnp.sum((keys[None, :] < keys[:, None]).astype(jnp.int32), axis=1)
    ids = jnp.arange(row_blocks, dtype=jnp.int32)
    order = jnp.sum(jnp.where(rank[None, :] == ids[:, None], ids[None, :], 0), axis=1)

    def kv_split(w):
        w = w.reshape(w_rows, devs // kv_copies, kv_cols)
        return jnp.repeat(w, kv_copies, axis=1) if kv_copies > 1 else w

    gains = jnp.stack([attn_gain, mlp_gain], axis=1)
    cols = D // 4
    room = cols - q_cols - 2 * kv_cols
    gains = jnp.pad(gains, ((0, 0), (0, room - 2)))
    gains = jnp.broadcast_to(gains[:, None, :], (w_rows, devs, room))
    packed = jnp.concatenate(
        [w_query.reshape(w_rows, devs, q_cols), kv_split(w_key), kv_split(w_value), gains], axis=2
    )
    packed = jnp.swapaxes(packed, 0, 1)
    used = q_cols + 2 * kv_cols
    out_full = gather(w_out[None], "grp")
    upstream = cotangent.astype(F32)
    d_branch_mlp = (RESID_MULT * upstream).astype(BF16)
    all_tokens, d_branch_mlp, packed = entry(tokens, d_branch_mlp, packed, grps, chips, 2)
    packed = packed.reshape(D, cols)
    normed_one, qkv, gains = project(all_tokens.reshape(devs * rows, D), packed, used)
    gain_one, gain_two, w_qkv = gains[0], gains[1], packed[:, :used]
    d_branch_mlp = d_branch_mlp.reshape(devs * rows, D)
    attended = attend(qkv, order, q_heads)
    attended = plane_exchange(
        attended, (rows, D), by_rows(rows), by_cols(q_cols), chips, 3
    )

    out_full = plane_gather(out_full, chips, 4, inner=True).reshape(D, D)
    layer_in = tokens.astype(F32)
    branch_attn = matmul(attended, out_full)
    residual = layer_in + RESID_MULT * branch_attn
    factor_two = norm_parts(residual)
    normed_two = (residual * factor_two * gain_two).astype(BF16)
    normed_two = plane_gather(normed_two, chips, 1).reshape(devs * rows, D)
    wide_w = gather(jnp.stack([w_gate, w_up])[None], "grp")
    down_w = gather(w_down[None], "grp")
    hidden, hidden_t, silu, slope, normed_t = widen(normed_two, wide_w)
    part_down = down_part(hidden_t, d_branch_mlp)
    part_down, hidden, silu = lax.optimization_barrier((part_down, hidden, silu))
    grad_down = scatter(part_down, "grp")
    if chips == 4:
        branch_mlp, *shares = twin_reduce(mix_rows, (hidden, down_w), rows, 11)
        shares, silu = lax.optimization_barrier((shares, silu))
        shares = swap_others(shares)
    d_gate, d_up = narrow_back(silu, slope, d_branch_mlp, down_w)
    if chips == 4:
        part_wide = widen_part(normed_t, d_gate, d_up)
        part_wide, shares, d_gate, d_up = lax.optimization_barrier(
            (part_wide, shares, d_gate, d_up)
        )
        grad_wide = scatter(part_wide, "grp")
        branch_mlp = join(branch_mlp, shares)
        d_normed_two = square_reduce(widen_back_rows, (d_gate, d_up, wide_w), rows, 10)
    else:
        part_wide = widen_part(normed_t, d_gate, d_up)
        part_wide, d_gate, d_up = lax.optimization_barrier((part_wide, d_gate, d_up))
        grad_wide = scatter(part_wide, "grp")
        d_normed_two = widen_back(d_gate, d_up, wide_w)
        d_normed_two = plane_reduce(d_normed_two.reshape(devs, rows, D), chips, 5)
        branch_mlp = mix(hidden, down_w)
        branch_mlp = plane_reduce(branch_mlp.reshape(devs, rows, D), chips, 5)

    d_residual_norm, d_gain_two = norm_back(residual, factor_two, gain_two, d_normed_two)
    d_residual = upstream + d_residual_norm
    d_branch_attn = (RESID_MULT * d_residual).astype(BF16)
    grad_out = over_rows(attended, d_branch_attn).astype(BF16)
    grad_out, d_branch_attn = lax.optimization_barrier((grad_out, d_branch_attn))
    if chips == 4:
        drift_out = Drift(grad_out.reshape(grps, 4, 2, w_rows, D), 1)
    d_attended = over_cols(d_branch_attn, out_full).astype(BF16)
    layer_out = residual + RESID_MULT * branch_mlp
    scaled_attn = RESID_MULT * branch_attn
    scaled_mlp = RESID_MULT * branch_mlp
    squares = jnp.stack(
        [
            jnp.sum(layer_out * layer_out),
            jnp.sum(scaled_attn * scaled_attn),
            jnp.sum(scaled_mlp * scaled_mlp),
        ]
    )
    totals = jnp.concatenate([d_gain_two, squares, jnp.zeros((1021,), F32)])
    d_attended, totals = exchange_total(
        d_attended, totals.reshape(8, 3 * D // 16), (devs * rows, q_cols), rows, q_cols, grps, chips, 7
    )
    if chips == 4:
        sent_out, d_attended = lax.optimization_barrier((drift_out.parts(), d_attended))
        sent_out = swap_others((sent_out[2], sent_out[0], sent_out[1]))
    d_attended, grad_down = lax.optimization_barrier((d_attended, grad_down))
    d_qkv = attend_back(qkv, d_attended, order, q_heads)
    if chips == 4:
        sent_out, d_qkv = lax.optimization_barrier((sent_out, d_qkv))
    sent = over_rows(normed_one, d_qkv).astype(BF16)
    sent, d_qkv, grad_wide = lax.optimization_barrier((sent, d_qkv, grad_wide))
    sent = scatter(sent, "grp")
    d_normed_one = over_cols(d_qkv, w_qkv).astype(BF16).reshape(devs, rows, D)
    if chips == 4:
        sent_out, d_normed_one = lax.optimization_barrier((sent_out, d_normed_one))
        grad_out = drift_out.finish(sent_out).astype(BF16)
    else:
        grad_out = plane_reduce(
            grad_out.reshape(grps, devs, w_rows, D), chips, 6, dtype=BF16, inner=True
        )
    grad_out, d_normed_one = lax.optimization_barrier((grad_out, d_normed_one))
    grad_out = scatter(grad_out, "grp")
    d_normed_one = plane_reduce(d_normed_one, chips, 5)
    d_normed_one, sent = lax.optimization_barrier((d_normed_one, sent))
    d_input_norm, _ = norm_back(layer_in, norm_parts(layer_in), gain_one, d_normed_one)
    tokens_grad = (d_residual + d_input_norm).astype(BF16)
    sent = sent.reshape(devs, w_rows, q_cols + 2 * kv_cols)
    sent = plane_exchange(sent, sent.shape, by_slot, by_slot, chips, 9)
    sent, grad_out = lax.optimization_barrier((sent, grad_out))
    sent, grad_out = sent.astype(F32), grad_out.reshape(w_rows, D).astype(F32)

    def kv_join(g):
        g = g.reshape(devs // kv_copies, kv_copies, w_rows, kv_cols)
        g = jnp.sum(g, axis=1) if kv_copies > 1 else g[:, 0]
        return jnp.swapaxes(g, 0, 1).reshape(w_rows, KV_HEADS * HEAD_DIM)

    grad_query = jnp.swapaxes(sent[:, :, :q_cols], 0, 1).reshape(w_rows, D)
    grad_key = kv_join(sent[:, :, q_cols : q_cols + kv_cols])
    grad_value = kv_join(sent[:, :, q_cols + kv_cols : q_cols + 2 * kv_cols])

    gain_one_grad = sum(
        jnp.sum(weight.astype(F32) * grad, axis=1)
        for weight, grad in ((w_query, grad_query), (w_key, grad_key), (w_value, grad_value))
    ) / attn_gain.astype(F32)
    totals = totals.reshape(-1)
    rms_stats = jnp.sqrt(totals[D : D + 3] / (rows * grps * devs * D))
    gain_first = (lax.axis_index("grp") * devs + lax.axis_index(PLANE)) * w_rows
    gain_two_grad = lax.dynamic_slice(totals, (gain_first,), (w_rows,))
    return (
        layer_out.astype(BF16),
        tokens_grad,
        gain_one_grad,
        grad_query,
        grad_key,
        grad_value,
        grad_out,
        gain_two_grad,
        grad_wide[0, 0].astype(F32),
        grad_wide[0, 1].astype(F32),
        grad_down[0].astype(F32),
        rms_stats,
    )


def solution(mesh):
    shape = (mesh.shape["grp"], mesh.shape["blk"] // 2, 2)
    mesh = Mesh(mesh.devices.reshape(shape), EVERY)
    row, col, vec = P(EVERY, None), P(None, EVERY), P(EVERY)
    return jax.shard_map(
        on_device,
        mesh=mesh,
        in_specs=(row, P(), P(), vec, row, row, row, row, vec, col, col, row, row),
        out_specs=(row, row, vec, row, row, row, row, vec, col, col, row, P()),
        check_vma=False,
    )
```

```python
import functools

import jax
import jax.numpy as jnp
from jax import lax
from jax.experimental import pallas as pl
from jax.experimental.pallas import tpu as pltpu
from jax.sharding import Mesh
from jax.sharding import PartitionSpec as P

D = 2048
HEADS = 32
KV_HEADS = 8
HEAD_DIM = 64
BLOCK = 128
PROMPT_BLOCKS = 8
GROUP_BLOCKS = 16
PER_GROUP = HEADS // KV_HEADS

ATTN_MULT = 0.015625
RESID_MULT = 0.22
EPSILON = 1e-05
MASKED = -1e30

PLANE = ("chip", "core")
EVERY = ("grp", "chip", "core")
BF16 = jnp.bfloat16
F32 = jnp.float32


MESH = pl.DeviceIdType.MESH
BRIEF = pl.CostEstimate(flops=1000, bytes_accessed=1000, transcendentals=0)
ANY = pl.BlockSpec(memory_space=pl.ANY)
VMEM = pl.BlockSpec(memory_space=pltpu.VMEM)


def place():
    return lax.axis_index("chip"), lax.axis_index("core")


def flip(chip, step, chips):
    return jnp.bitwise_xor(chip, step) if chips == 4 else lax.rem(chip + step, chips)


def unflip(chip, step, chips):
    return jnp.bitwise_xor(chip, step) if chips == 4 else lax.rem(chip + chips - step, chips)


def greet(peers):
    barrier = pltpu.get_barrier_semaphore()
    for chip, core in peers:
        pl.semaphore_signal(
            barrier, inc=1, device_id={"chip": chip, "core": core}, device_id_type=MESH
        )
    pl.semaphore_wait(barrier, len(peers))


def remote(src, dst, send, recv, chip, core):
    return pltpu.make_async_remote_copy(
        src_ref=src,
        dst_ref=dst,
        send_sem=send,
        recv_sem=recv,
        device_id={"chip": chip, "core": core},
        device_id_type=MESH,
    )


class Gather:
    def __init__(self, chips, inner, x_ref, o_ref, send, recv, local):
        self.chips, self.inner, self.x, self.o = chips, inner, x_ref, o_ref
        self.send, self.recv, self.local = send, recv, local
        self.chip, self.core = place()
        self.half = x_ref.shape[0] // 2
        self.started = []

    def greet(self):
        steps = (1, 2) if self.chips == 4 else range(1, self.chips)
        peers = [(flip(self.chip, s, self.chips), self.core) for s in steps]
        greet(peers + [(self.chip, 1 - self.core)])

    def piece(self, slot, h):
        at = pl.ds(h * self.half, self.half)
        return self.o.at[at, slot] if self.inner else self.o.at[slot, at]

    def own(self, h):
        return self.x.at[pl.ds(h * self.half, self.half)]

    def slot(self, chip, core):
        return chip * 2 + core

    def push(self, src, slot, h, chip, core):
        i = len(self.started)
        copy = remote(src, self.piece(slot, h), self.send.at[i], self.recv.at[slot, h], chip, core)
        copy.start()
        self.started.append(copy)

    def wait_for(self, slot, h):
        remote(
            self.own(h), self.piece(slot, h), self.send.at[0], self.recv.at[slot, h],
            self.chip, 1 - self.core,
        ).wait_recv()

    def start(self):
        me = self.slot(self.chip, self.core)
        if self.chips == 4:
            for h, s in ((0, 1), (1, 2), (1, 1), (0, 2)):
                self.push(self.own(h), me, h, flip(self.chip, s, 4), self.core)
        else:
            for s in range(1, self.chips):
                for h in range(2):
                    self.push(self.own(h), me, h, flip(self.chip, s, self.chips), self.core)
        for h in range(2):
            self.push(self.own(h), me, h, self.chip, 1 - self.core)
        whole = self.o.at[:, me] if self.inner else self.o.at[me]
        self.mine = pltpu.make_async_copy(self.x, whole, self.local)
        self.mine.start()

    def relay(self, first=0, last=None):
        if self.chips == 4:
            plan = ((1, 0, 2), (2, 1, 1), (1, 1, 0), (2, 0, 0), (3, 0, 0), (3, 1, 0))
        else:
            plan = tuple((s, h, 0) for s in range(1, self.chips) for h in range(2))
        for s, h, onward in plan[first:last]:
            slot = self.slot(unflip(self.chip, s, self.chips), self.core)
            self.wait_for(slot, h)
            if onward:
                self.push(self.piece(slot, h), slot, h, flip(self.chip, onward, 4), self.core)
            self.push(self.piece(slot, h), slot, h, self.chip, 1 - self.core)

    def finish(self):
        for s in range(self.chips):
            slot = self.slot(unflip(self.chip, s, self.chips), 1 - self.core)
            for h in range(2):
                self.wait_for(slot, h)
        for copy in self.started:
            copy.wait_send()
        self.mine.wait()


def gather_sems(chips):
    return [
        pltpu.SemaphoreType.DMA((4 * chips + 4,)),
        pltpu.SemaphoreType.DMA((2 * chips, 2)),
        pltpu.SemaphoreType.DMA,
    ]


def gather_kernel(chips, inner, x_ref, o_ref, *sems):
    run = Gather(chips, inner, x_ref, o_ref, *sems)
    run.greet()
    run.start()
    run.relay()
    run.finish()


def plane_gather(x, chips, call_id, inner=False):
    devs = 2 * chips
    shape = (x.shape[0], devs) + x.shape[1:] if inner else (devs,) + x.shape
    return pl.pallas_call(
        functools.partial(gather_kernel, chips, inner),
        out_shape=jax.ShapeDtypeStruct(shape, x.dtype),
        in_specs=[ANY],
        out_specs=ANY,
        scratch_shapes=gather_sems(chips),
        cost_estimate=BRIEF,
        compiler_params=pltpu.CompilerParams(collective_id=call_id, has_side_effects=True),
    )(x)


def reduce_kernel(chips, inner, p_ref, o_ref, total, mine, twin, moved, corner, landed, lsem, tsend, trecv, msend, mrecv, csend, crecv):
    chip, core = place()
    sib = 1 - core
    half = (p_ref.shape[0] if inner else p_ref.shape[1]) // 2
    block = (lambda slot: p_ref.at[:, slot]) if inner else (lambda slot: p_ref.at[slot])
    steps = (1, 2) if chips == 4 else tuple(range(1, chips))
    peers = [(flip(chip, s, chips), core) for s in steps]
    greet(peers + [(chip, sib)])
    order = (3, 1, 2, 0) if chips == 4 else tuple(range(1, chips)) + (0,)
    loads, twins = {}, {}
    for s in order:
        to = flip(chip, s, chips) * 2
        twins[s] = remote(block(to + sib), twin.at[s], tsend.at[s], trecv.at[s], chip, sib)
        twins[s].start()
        loads[s] = pltpu.make_async_copy(block(to + core), mine.at[s], lsem.at[s])
        loads[s].start()

    def part(s, h):
        at = pl.ds(h * half, half)
        return mine[s, at].astype(F32) + twin[s, at].astype(F32)

    def ready(s):
        loads[s].wait()
        twins[s].wait_recv()

    sent = []
    if chips == 4:
        corners = []
        ready(3)
        for h, s in ((0, 1), (1, 2)):
            moved[3, pl.ds(h * half, half)] = part(3, h).astype(BF16)
            copy = remote(moved.at[3, pl.ds(h * half, half)], corner.at[h], csend.at[h], crecv.at[h], flip(chip, s, 4), core)
            copy.start()
            corners.append(copy)

        def send(s, h):
            at = pl.ds(h * half, half)
            copy = remote(moved.at[s, at], landed.at[s - 1, at], msend.at[s - 1, h], mrecv.at[s - 1, h], flip(chip, s, 4), core)
            copy.start()
            sent.append(copy)

        for s, h in ((1, 0), (2, 1)):
            ready(s)
            moved[s, pl.ds(h * half, half)] = part(s, h).astype(BF16)
            send(s, h)
        for s, h in ((2, 0), (1, 1)):
            corners[h].wait_recv()
            moved[s, pl.ds(h * half, half)] = (part(s, h) + corner[h].astype(F32)).astype(BF16)
            send(s, h)
        for copy in corners:
            copy.wait_send()
    else:
        for s in steps:
            ready(s)
            for h in range(2):
                at = pl.ds(h * half, half)
                moved[s, at] = part(s, h).astype(BF16)
                copy = remote(moved.at[s, at], landed.at[s - 1, at], msend.at[s - 1, h], mrecv.at[s - 1, h], flip(chip, s, chips), core)
                copy.start()
                sent.append(copy)
    ready(0)
    for h in range(2):
        total[pl.ds(h * half, half)] = part(0, h)
    for copy in sent:
        copy.wait()
    for s in steps[:-1]:
        total[...] += landed[s - 1].astype(F32)
    o_ref[...] = (total[...] + landed[steps[-1] - 1].astype(F32)).astype(o_ref.dtype)
    for s in order:
        twins[s].wait_send()


def plane_reduce(p, chips, call_id, dtype=F32, inner=False):
    block = (p.shape[0],) + p.shape[2:] if inner else p.shape[1:]
    steps = 2 if chips == 4 else chips - 1
    return pl.pallas_call(
        functools.partial(reduce_kernel, chips, inner),
        out_shape=jax.ShapeDtypeStruct(block, dtype),
        in_specs=[ANY],
        out_specs=VMEM,
        scratch_shapes=[
            pltpu.VMEM(block, F32),
            pltpu.VMEM((chips,) + block, BF16),
            pltpu.VMEM((chips,) + block, BF16),
            pltpu.VMEM((chips,) + block, BF16),
            pltpu.VMEM((2, block[0] // 2) + block[1:], BF16),
            pltpu.VMEM((steps,) + block, BF16),
            pltpu.SemaphoreType.DMA((chips,)),
            pltpu.SemaphoreType.DMA((chips,)),
            pltpu.SemaphoreType.DMA((chips,)),
            pltpu.SemaphoreType.DMA((steps, 2)),
            pltpu.SemaphoreType.DMA((steps, 2)),
            pltpu.SemaphoreType.DMA((2,)),
            pltpu.SemaphoreType.DMA((2,)),
        ],
        cost_estimate=BRIEF,
        compiler_params=pltpu.CompilerParams(
            collective_id=call_id, has_side_effects=True, vmem_limit_bytes=56 << 20
        ),
    )(p)


def swap_chips(values, step):
    return lax.ppermute(values, "chip", [(c, c ^ step) for c in range(4)])


class Drift:
    def __init__(self, pairs, axis):
        self.axis = axis
        self.chip, self.core = place()
        away = lax.dynamic_index_in_dim(pairs, 1 - self.core, axis + 1, keepdims=False)
        self.mine = lax.dynamic_index_in_dim(pairs, self.core, axis + 1, keepdims=False)
        self.twin = lax.ppermute(away, "core", [(0, 1), (1, 0)])

    def part(self, step):
        at = jnp.bitwise_xor(self.chip, step)
        mine = lax.dynamic_index_in_dim(self.mine, at, self.axis, keepdims=False)
        twin = lax.dynamic_index_in_dim(self.twin, at, self.axis, keepdims=False)
        return mine.astype(F32) + twin.astype(F32)

    def parts(self):
        return tuple(self.part(step).astype(BF16) for step in (1, 2, 3))

    def finish(self, came):
        total = self.part(0)
        for part in came:
            total = total + part.astype(F32)
        return total


def exchange_kernel(chips, cut, paste, x_ref, o_ref, send, recv, local):
    chip, core = place()
    me = chip * 2 + core
    peers = [(flip(chip, s, chips), c) for s in range(1, chips) for c in (core, 1 - core)]
    peers = peers + [(chip, 1 - core)]
    greet(peers)
    far = [p for p in ([3, 1, 2] if chips == 4 else range(1, chips))]
    order = [(flip(chip, s, chips), c) for s in far for c in (core, 1 - core)] + [(chip, 1 - core)]
    copies = []
    for i, (to, c) in enumerate(order):
        copy = remote(cut(x_ref, to * 2 + c), paste(o_ref, me), send.at[i], recv.at[me], to, c)
        copy.start()
        copies.append(copy)
    mine = pltpu.make_async_copy(cut(x_ref, me), paste(o_ref, me), local)
    mine.start()
    for s in far:
        for c in (core, 1 - core):
            slot = unflip(chip, s, chips) * 2 + c
            remote(cut(x_ref, me), paste(o_ref, slot), send.at[0], recv.at[slot], chip, 1 - core).wait_recv()
    slot = chip * 2 + 1 - core
    remote(cut(x_ref, me), paste(o_ref, slot), send.at[0], recv.at[slot], chip, 1 - core).wait_recv()
    for copy in copies:
        copy.wait_send()
    mine.wait()


def plane_exchange(x, shape, cut, paste, chips, call_id):
    return pl.pallas_call(
        functools.partial(exchange_kernel, chips, cut, paste),
        out_shape=jax.ShapeDtypeStruct(shape, x.dtype),
        in_specs=[ANY],
        out_specs=ANY,
        scratch_shapes=[
            pltpu.SemaphoreType.DMA((2 * chips,)),
            pltpu.SemaphoreType.DMA((2 * chips,)),
            pltpu.SemaphoreType.DMA,
        ],
        cost_estimate=BRIEF,
        compiler_params=pltpu.CompilerParams(collective_id=call_id, has_side_effects=True),
    )(x)


def by_slot(ref, dev):
    return ref.at[dev]


def by_rows(rows):
    return lambda ref, dev: ref.at[pl.ds(pl.multiple_of(dev * rows, rows), rows)]


def by_cols(cols):
    return lambda ref, dev: ref.at[:, pl.ds(pl.multiple_of(dev * cols, cols), cols)]


def matmul(left, right):
    return jnp.dot(left, right, preferred_element_type=F32)


def over_rows(left, right):
    return lax.dot_general(left, right, (((0,), (0,)), ((), ())), preferred_element_type=F32)


def over_cols(left, right):
    return lax.dot_general(left, right, (((1,), (1,)), ((), ())), preferred_element_type=F32)


def gather(values, axes, axis=0):
    return lax.all_gather(values, axes, axis=axis, tiled=True)


def scatter(values, axes, axis=0):
    return lax.psum_scatter(values, axes, scatter_dimension=axis, tiled=True)


def dot_nt(left, right):
    return lax.dot_general(left, right, (((1,), (1,)), ((), ())), preferred_element_type=F32)


def head_stack(values, heads):
    col_head = lax.broadcasted_iota(jnp.int32, values.shape, 1) // HEAD_DIM
    return jnp.concatenate(
        [jnp.where(col_head == h, values, jnp.zeros_like(values)) for h in range(heads)], axis=0
    )


def head_pick(stacked, heads):
    rows = stacked.shape[0] // heads
    col_head = lax.broadcasted_iota(jnp.int32, (rows, stacked.shape[1]), 1) // HEAD_DIM
    total = jnp.zeros((rows, stacked.shape[1]), F32)
    for h in range(heads):
        total = jnp.where(col_head == h, stacked[h * rows : (h + 1) * rows], total)
    return total


def head_fold(values, heads):
    total = values[:, :HEAD_DIM]
    for h in range(1, heads):
        total = total + values[:, h * HEAD_DIM : (h + 1) * HEAD_DIM]
    return total


def repeat_heads(values, heads):
    return jnp.concatenate([values] * heads, axis=1)


def own_rows(order_ref, slot):
    return pl.ds(pl.multiple_of(order_ref[slot] * BLOCK, BLOCK), BLOCK)


def load_prompt(heads, order_ref, qkv_ref, k_ref, v_ref, first):
    q_cols = heads * HEAD_DIM
    for s in range(PROMPT_BLOCKS):
        pair = qkv_ref[own_rows(order_ref, first + s), q_cols:]
        at = pl.ds(s * BLOCK, BLOCK)
        k_ref[at] = repeat_heads(pair[:, :HEAD_DIM], heads)
        v_ref[at] = repeat_heads(pair[:, HEAD_DIM:], heads)


def by_keys(slot, body):
    prompt = PROMPT_BLOCKS * BLOCK
    quarter = prompt // 4
    seen = jnp.minimum(slot, PROMPT_BLOCKS) * BLOCK
    for n in range(1, 5):
        low = (n - 1) * quarter if n > 1 else -1

        @pl.when((seen > low) & (seen <= n * quarter))
        def _(n=n):
            body(n * quarter)


def soft_parts(heads, slot, q_stack, k_far, k_own):
    far = dot_nt(k_far, q_stack)
    own = dot_nt(k_own, q_stack)
    limit = jnp.minimum(slot, PROMPT_BLOCKS) * BLOCK
    far = jnp.where(lax.broadcasted_iota(jnp.int32, far.shape, 0) < limit, far, MASKED)
    key = lax.broadcasted_iota(jnp.int32, own.shape, 0)
    row = lax.broadcasted_iota(jnp.int32, own.shape, 1) % BLOCK
    own = jnp.where(key <= row, own, MASKED)
    peak = jnp.maximum(jnp.max(far, axis=0, keepdims=True), jnp.max(own, axis=0, keepdims=True))
    far, own = jnp.exp(far - peak), jnp.exp(own - peak)
    scale = 1.0 / (jnp.sum(far, axis=0, keepdims=True) + jnp.sum(own, axis=0, keepdims=True))
    return far * scale, own * scale


def scaled_stack(q, heads):
    return head_stack((q.astype(F32) * ATTN_MULT).astype(BF16), heads)


def attend_kernel(heads, order_ref, qkv_ref, o_ref, k_ref, v_ref, vt_ref):
    first, slot = pl.program_id(0) * GROUP_BLOCKS, pl.program_id(1)
    q_cols = heads * HEAD_DIM

    @pl.when(slot == 0)
    def _():
        load_prompt(heads, order_ref, qkv_ref, k_ref, v_ref, first)
        vt_ref[...] = v_ref[...].astype(F32).T.astype(BF16)

    rows = own_rows(order_ref, first + slot)
    mine = qkv_ref[rows, :]
    k_own = repeat_heads(mine[:, q_cols : q_cols + HEAD_DIM], heads)
    v_own = repeat_heads(mine[:, q_cols + HEAD_DIM :], heads)
    q_stack = scaled_stack(mine[:, :q_cols], heads)

    def body(count):
        far, own = soft_parts(heads, slot, q_stack, k_ref[:count], k_own)
        mixed = matmul(vt_ref[:, :count], far.astype(BF16))
        mixed += matmul(v_own.astype(F32).T.astype(BF16), own.astype(BF16))
        o_ref[rows, :] = head_pick(mixed.T, heads).astype(BF16)

    by_keys(slot, body)


def attend_back_kernel(
    heads, order_ref, qkv_ref, d_ref, o_ref, k_ref, v_ref, kt_ref, dk_ref, dv_ref
):
    first, slot = pl.program_id(0) * GROUP_BLOCKS, pl.program_id(1)
    q_cols = heads * HEAD_DIM

    @pl.when(slot == 0)
    def _():
        load_prompt(heads, order_ref, qkv_ref, k_ref, v_ref, first)
        kt_ref[...] = k_ref[...].astype(F32).T.astype(BF16)
        dk_ref[...] = jnp.zeros_like(dk_ref)
        dv_ref[...] = jnp.zeros_like(dv_ref)

    rows = own_rows(order_ref, first + slot)
    mine = qkv_ref[rows, :]
    k_own = repeat_heads(mine[:, q_cols : q_cols + HEAD_DIM], heads)
    v_own = repeat_heads(mine[:, q_cols + HEAD_DIM :], heads)
    q_stack = scaled_stack(mine[:, :q_cols], heads)
    d_stack = head_stack(d_ref[rows, :], heads)

    def fold(d_k, d_v):
        return jnp.concatenate([head_fold(d_k, heads), head_fold(d_v, heads)], axis=1).astype(BF16)

    def body(count):
        far, own = soft_parts(heads, slot, q_stack, k_ref[:count], k_own)
        d_far, d_own = dot_nt(v_ref[:count], d_stack), dot_nt(v_own, d_stack)
        mean = jnp.sum(far * d_far, axis=0, keepdims=True)
        mean += jnp.sum(own * d_own, axis=0, keepdims=True)
        d_far = (far * (d_far - mean)).astype(BF16)
        d_own = (own * (d_own - mean)).astype(BF16)
        dv_ref[:count] += matmul(far.astype(BF16), d_stack)
        dk_ref[:count] += matmul(d_far, q_stack)
        dv_own = matmul(own.astype(BF16), d_stack)
        dk_own = matmul(d_own, q_stack)
        d_q = matmul(kt_ref[:, :count], d_far) + matmul(k_own.astype(F32).T.astype(BF16), d_own)
        o_ref[rows, :q_cols] = (head_pick(d_q.T, heads) * ATTN_MULT).astype(BF16)

        @pl.when(slot < PROMPT_BLOCKS)
        def _():
            at = pl.ds(pl.multiple_of(slot * BLOCK, BLOCK), BLOCK)
            dk_ref[at] += dk_own
            dv_ref[at] += dv_own

        @pl.when(slot >= PROMPT_BLOCKS)
        def _():
            o_ref[rows, q_cols:] = fold(dk_own, dv_own)

    by_keys(slot, body)

    @pl.when(slot == GROUP_BLOCKS - 1)
    def _():
        for s in range(PROMPT_BLOCKS):
            at = pl.ds(s * BLOCK, BLOCK)
            o_ref[own_rows(order_ref, first + s), q_cols:] = fold(dk_ref[at], dv_ref[at])


def whole(shape):
    return pl.BlockSpec(shape, lambda g, s, order: (0,) * len(shape))


def attend(qkv, order, heads):
    tokens, cols = qkv.shape
    prompt, q_cols = PROMPT_BLOCKS * BLOCK, heads * HEAD_DIM
    return pl.pallas_call(
        functools.partial(attend_kernel, heads),
        out_shape=jax.ShapeDtypeStruct((tokens, q_cols), BF16),
        grid_spec=pltpu.PrefetchScalarGridSpec(
            num_scalar_prefetch=1,
            grid=(tokens // (GROUP_BLOCKS * BLOCK), GROUP_BLOCKS),
            in_specs=[whole((tokens, cols))],
            out_specs=whole((tokens, q_cols)),
            scratch_shapes=[
                pltpu.VMEM((prompt, q_cols), BF16),
                pltpu.VMEM((prompt, q_cols), BF16),
                pltpu.VMEM((q_cols, prompt), BF16),
            ],
        ),
        cost_estimate=BRIEF,
        compiler_params=pltpu.CompilerParams(vmem_limit_bytes=40 << 20),
    )(order, qkv)


def attend_back(qkv, d_attended, order, heads):
    tokens, cols = qkv.shape
    prompt, q_cols = PROMPT_BLOCKS * BLOCK, heads * HEAD_DIM
    return pl.pallas_call(
        functools.partial(attend_back_kernel, heads),
        out_shape=jax.ShapeDtypeStruct((tokens, cols), BF16),
        grid_spec=pltpu.PrefetchScalarGridSpec(
            num_scalar_prefetch=1,
            grid=(tokens // (GROUP_BLOCKS * BLOCK), GROUP_BLOCKS),
            in_specs=[whole((tokens, cols)), whole((tokens, q_cols))],
            out_specs=whole((tokens, cols)),
            scratch_shapes=[
                pltpu.VMEM((prompt, q_cols), BF16),
                pltpu.VMEM((prompt, q_cols), BF16),
                pltpu.VMEM((q_cols, prompt), BF16),
                pltpu.VMEM((prompt, q_cols), F32),
                pltpu.VMEM((prompt, q_cols), F32),
            ],
        ),
        cost_estimate=BRIEF,
        compiler_params=pltpu.CompilerParams(vmem_limit_bytes=40 << 20),
    )(order, qkv, d_attended)


def exchange_total_kernel(
    grps, chips, cut, paste, x_ref, t_ref, o_ref, sum_ref,
    over_z, over_plane, send, recv, local, zsend, zrecv, psend, precv,
):
    grp = lax.axis_index("grp")
    chip, core = place()
    me = chip * 2 + core
    far = [lax.rem(grp + s, grps) for s in range(1, grps)]
    steps = (3, 1, 2) if chips == 4 else tuple(range(1, chips))
    near = [(flip(chip, s, chips), c) for s in steps for c in (core, 1 - core)]
    near = near + [(chip, 1 - core)]
    barrier = pltpu.get_barrier_semaphore()
    for g in far:
        pl.semaphore_signal(barrier, inc=1, device_id={"grp": g}, device_id_type=MESH)
    for to, c in near:
        pl.semaphore_signal(
            barrier, inc=1, device_id={"chip": to, "core": c}, device_id_type=MESH
        )
    pl.semaphore_wait(barrier, len(far) + len(near))

    def z_copy(slot, sem, to):
        return pltpu.make_async_remote_copy(
            src_ref=t_ref,
            dst_ref=over_z.at[slot],
            send_sem=sem,
            recv_sem=zrecv.at[slot],
            device_id={"grp": to},
            device_id_type=MESH,
        )

    copies = []
    for i, g in enumerate(far):
        copy = z_copy(grp, zsend.at[i], g)
        copy.start()
        copies.append(copy)
    for i, (to, c) in enumerate(near):
        copy = remote(cut(x_ref, to * 2 + c), paste(o_ref, me), send.at[i], recv.at[me], to, c)
        copy.start()
        copies.append(copy)
    mine = pltpu.make_async_copy(cut(x_ref, me), paste(o_ref, me), local)
    mine.start()
    over_z[grp] = t_ref[...]
    for g in far:
        z_copy(g, zsend.at[0], g).wait_recv()
    over_plane[me] = jnp.sum(over_z[...], axis=0)
    for i, (to, c) in enumerate(near):
        copy = remote(over_plane.at[me], over_plane.at[me], psend.at[i], precv.at[me], to, c)
        copy.start()
        copies.append(copy)
    for to, c in near:
        slot = to * 2 + c
        remote(cut(x_ref, me), paste(o_ref, slot), send.at[0], recv.at[slot], to, c).wait_recv()
        remote(over_plane.at[me], over_plane.at[slot], psend.at[0], precv.at[slot], to, c).wait_recv()
    for copy in copies:
        copy.wait_send()
    mine.wait()
    sum_ref[...] = jnp.sum(over_plane[...], axis=0)


def exchange_total(x, t, shape, rows, cols, grps, chips, call_id):
    devs = 2 * chips
    return pl.pallas_call(
        functools.partial(exchange_total_kernel, grps, chips, by_cols(cols), by_rows(rows)),
        out_shape=(
            jax.ShapeDtypeStruct(shape, x.dtype),
            jax.ShapeDtypeStruct(t.shape, F32),
        ),
        in_specs=[ANY, VMEM],
        out_specs=(ANY, VMEM),
        scratch_shapes=[
            pltpu.VMEM((grps,) + t.shape, F32),
            pltpu.VMEM((devs,) + t.shape, F32),
            pltpu.SemaphoreType.DMA((devs,)),
            pltpu.SemaphoreType.DMA((devs,)),
            pltpu.SemaphoreType.DMA,
            pltpu.SemaphoreType.DMA((grps,)),
            pltpu.SemaphoreType.DMA((grps,)),
            pltpu.SemaphoreType.DMA((devs,)),
            pltpu.SemaphoreType.DMA((devs,)),
        ],
        cost_estimate=BRIEF,
        compiler_params=pltpu.CompilerParams(collective_id=call_id, has_side_effects=True),
    )(x, t)


def params(axes, mib=56):
    return pltpu.CompilerParams(
        dimension_semantics=("arbitrary",) * axes, vmem_limit_bytes=mib << 20
    )


def tile_rows(count, limit):
    while count % limit:
        limit //= 2
    return limit


def widen_kernel(n_ref, w_ref, h_ref, ht_ref, s_ref, t_ref, nt_ref):
    values = n_ref[...]
    gate, up = matmul(values, w_ref[0, 0]), matmul(values, w_ref[0, 1])
    sig = 1.0 / (1.0 + jnp.exp(-gate))
    silu = gate * sig
    hidden = (silu * up).astype(BF16)
    h_ref[0] = hidden
    ht_ref[0] = hidden.T
    s_ref[0] = silu.astype(BF16)
    t_ref[0] = (up * (sig * (1.0 + gate * (1.0 - sig)))).astype(BF16)

    @pl.when(pl.program_id(1) == 0)
    def _():
        nt_ref[...] = values.T


def widen(normed, weights):
    tokens, depth = normed.shape
    shards, _, _, width = weights.shape
    rows = tile_rows(tokens, 1024)
    tall = jax.ShapeDtypeStruct((shards, tokens, width), BF16)
    tall_spec = pl.BlockSpec((1, rows, width), lambda r, s: (s, r, 0))
    return pl.pallas_call(
        widen_kernel,
        out_shape=(
            tall,
            jax.ShapeDtypeStruct((shards, width, tokens), BF16),
            tall,
            tall,
            jax.ShapeDtypeStruct((depth, tokens), BF16),
        ),
        grid=(tokens // rows, shards),
        in_specs=[
            pl.BlockSpec((rows, depth), lambda r, s: (r, 0)),
            pl.BlockSpec((1, 2, depth, width), lambda r, s: (s, 0, 0, 0)),
        ],
        out_specs=(
            tall_spec,
            pl.BlockSpec((1, width, rows), lambda r, s: (s, 0, r)),
            tall_spec,
            tall_spec,
            pl.BlockSpec((depth, rows), lambda r, s: (0, r)),
        ),
        cost_estimate=BRIEF,
        compiler_params=params(2),
    )(normed, weights)


def down_part_kernel(ht_ref, d_ref, o_ref):
    o_ref[0] = matmul(ht_ref[0], d_ref[...]).astype(BF16)


def down_part(hidden_t, upstream):
    shards, width, tokens = hidden_t.shape
    depth = upstream.shape[1]
    cols = tile_rows(depth, 1024)
    return pl.pallas_call(
        down_part_kernel,
        out_shape=jax.ShapeDtypeStruct((shards, width, depth), BF16),
        grid=(depth // cols, shards),
        in_specs=[
            pl.BlockSpec((1, width, tokens), lambda c, s: (s, 0, 0)),
            pl.BlockSpec((tokens, cols), lambda c, s: (0, c)),
        ],
        out_specs=pl.BlockSpec((1, width, cols), lambda c, s: (s, 0, c)),
        cost_estimate=BRIEF,
        compiler_params=params(2),
    )(hidden_t, upstream)


def mix_kernel(h_ref, w_ref, m_ref):
    mixed = None
    for i in range(w_ref.shape[0]):
        part = matmul(h_ref[i], w_ref[i])
        mixed = part if mixed is None else mixed + part
    m_ref[...] = mixed.astype(BF16)


def narrow_specs(hidden, weights):
    shards, tokens, width = hidden.shape
    depth = weights.shape[2]
    rows = tile_rows(tokens, 512)
    return (
        tokens // rows,
        pl.BlockSpec((shards, rows, width), lambda r: (0, r, 0)),
        pl.BlockSpec((rows, depth), lambda r: (r, 0)),
        pl.BlockSpec(weights.shape, lambda r: (0, 0, 0), pipeline_mode=pl.Buffered(1)),
    )


def mix(hidden, weights):
    steps, tall_spec, flat_spec, weight_spec = narrow_specs(hidden, weights)
    return pl.pallas_call(
        mix_kernel,
        out_shape=jax.ShapeDtypeStruct((hidden.shape[1], weights.shape[2]), BF16),
        grid=(steps,),
        in_specs=[tall_spec, weight_spec],
        out_specs=flat_spec,
        cost_estimate=BRIEF,
        compiler_params=params(1),
    )(hidden, weights)


def narrow_back_kernel(s_ref, t_ref, d_ref, w_ref, dg_ref, du_ref):
    upstream = d_ref[...]
    for i in range(w_ref.shape[0]):
        d_hidden = dot_nt(upstream, w_ref[i])
        dg_ref[i] = (d_hidden * t_ref[i].astype(F32)).astype(BF16)
        du_ref[i] = (d_hidden * s_ref[i].astype(F32)).astype(BF16)


def narrow_back(silu, slope, upstream, weights):
    steps, tall_spec, flat_spec, weight_spec = narrow_specs(silu, weights)
    tall = jax.ShapeDtypeStruct(silu.shape, BF16)
    return pl.pallas_call(
        narrow_back_kernel,
        out_shape=(tall, tall),
        grid=(steps,),
        in_specs=[tall_spec, tall_spec, flat_spec, weight_spec],
        out_specs=(tall_spec, tall_spec),
        cost_estimate=BRIEF,
        compiler_params=params(1),
    )(silu, slope, upstream, weights)


def widen_part_kernel(nt_ref, dg_ref, du_ref, o_ref):
    values = nt_ref[...]
    o_ref[0, 0] = matmul(values, dg_ref[0]).astype(BF16)
    o_ref[0, 1] = matmul(values, du_ref[0]).astype(BF16)


def widen_part(normed_t, d_gate, d_up):
    depth, tokens = normed_t.shape
    shards, _, width = d_gate.shape
    rows = tile_rows(depth, 1024)
    tall_spec = pl.BlockSpec((1, tokens, width), lambda r, s: (s, 0, 0))
    return pl.pallas_call(
        widen_part_kernel,
        out_shape=jax.ShapeDtypeStruct((shards, 2, depth, width), BF16),
        grid=(depth // rows, shards),
        in_specs=[pl.BlockSpec((rows, tokens), lambda r, s: (r, 0)), tall_spec, tall_spec],
        out_specs=pl.BlockSpec((1, 2, rows, width), lambda r, s: (s, 0, r, 0)),
        cost_estimate=BRIEF,
        compiler_params=params(2),
    )(normed_t, d_gate, d_up)


def widen_back_kernel(dg_ref, du_ref, w_ref, o_ref):
    total = None
    for i in range(w_ref.shape[0]):
        part = dot_nt(dg_ref[i], w_ref[i, 0]) + dot_nt(du_ref[i], w_ref[i, 1])
        total = part if total is None else total + part
    o_ref[...] = total.astype(BF16)


def widen_back(d_gate, d_up, weights):
    shards, tokens, width = d_gate.shape
    depth = weights.shape[2]
    rows = tile_rows(tokens, 512)
    tall_spec = pl.BlockSpec((shards, rows, width), lambda r: (0, r, 0))
    return pl.pallas_call(
        widen_back_kernel,
        out_shape=jax.ShapeDtypeStruct((tokens, depth), BF16),
        grid=(tokens // rows,),
        in_specs=[
            tall_spec,
            tall_spec,
            pl.BlockSpec(weights.shape, lambda r: (0, 0, 0, 0), pipeline_mode=pl.Buffered(1)),
        ],
        out_specs=pl.BlockSpec((rows, depth), lambda r: (r, 0)),
        cost_estimate=BRIEF,
        compiler_params=params(1),
    )(d_gate, d_up, weights)


def stage_step(stage):
    return jnp.where(stage == 0, 3, jnp.where(stage == 3, 0, stage))


class Square:
    def __init__(self, acc, mine, away, twin, moved, corner, landed, tsend, trecv, msend, mrecv, csend, crecv):
        self.acc, self.mine, self.away, self.twin = acc, mine, away, twin
        self.moved, self.corner, self.landed = moved, corner, landed
        self.tsend, self.trecv, self.msend, self.mrecv = tsend, trecv, msend, mrecv
        self.csend, self.crecv = csend, crecv
        self.chip, self.core = place()
        self.rows = mine.shape[1]
        self.half = self.rows // 2

    def greet(self):
        peers = [(flip(self.chip, s, 4), self.core) for s in (1, 2)]
        greet(peers + [(self.chip, 1 - self.core)])

    def twin_copy(self, stage):
        return remote(
            self.away.at[stage], self.twin.at[stage], self.tsend.at[stage], self.trecv.at[stage],
            self.chip, 1 - self.core,
        )

    def offer(self, stage):
        own, other = self.core * self.rows, (1 - self.core) * self.rows
        self.mine[stage] = self.acc[pl.ds(pl.multiple_of(own, self.rows), self.rows)].astype(BF16)
        self.away[stage] = self.acc[pl.ds(pl.multiple_of(other, self.rows), self.rows)].astype(BF16)
        self.twin_copy(stage).start()

    def at(self, h):
        return pl.ds(h * self.half, self.half)

    def both(self, stage, h):
        return self.mine[stage, self.at(h)].astype(F32) + self.twin[stage, self.at(h)].astype(F32)

    def corner_copy(self, h):
        return remote(
            self.moved.at[0, self.at(h)], self.corner.at[h], self.csend.at[h], self.crecv.at[h],
            flip(self.chip, h + 1, 4), self.core,
        )

    def copy(self, stage, h):
        return remote(
            self.moved.at[stage, self.at(h)], self.landed.at[stage - 1, self.at(h)],
            self.msend.at[stage - 1, h], self.mrecv.at[stage - 1, h],
            flip(self.chip, stage, 4), self.core,
        )

    def corners(self):
        self.twin_copy(0).wait_recv()
        for h in range(2):
            self.moved[0, self.at(h)] = self.both(0, h).astype(BF16)
            self.corner_copy(h).start()

    def plain(self, stage):
        self.twin_copy(stage).wait_recv()
        h = stage - 1
        self.moved[stage, self.at(h)] = self.both(stage, h).astype(BF16)
        self.copy(stage, h).start()

    def joined(self, stage):
        h = 2 - stage
        self.corner_copy(h).wait_recv()
        total = self.both(stage, h) + self.corner[h].astype(F32)
        self.moved[stage, self.at(h)] = total.astype(BF16)
        self.copy(stage, h).start()

    def finish(self, o_ref):
        self.twin_copy(3).wait_recv()
        for h in range(2):
            o_ref[self.at(h)] = self.both(3, h)
        for stage, h in ((1, 0), (2, 1), (2, 0), (1, 1)):
            self.copy(stage, h).wait_recv()
            o_ref[self.at(h)] += self.landed[stage - 1, self.at(h)].astype(F32)
        for stage in (1, 2):
            for h in range(2):
                self.copy(stage, h).wait_send()
        for h in range(2):
            self.corner_copy(h).wait_send()
        for stage in range(4):
            self.twin_copy(stage).wait_send()


def square_kernel(compute, count, *refs):
    operands, o_ref, scratch = refs[:count], refs[count], refs[count + 1 :]
    run = Square(*scratch)
    stage = pl.program_id(0)

    @pl.when(stage == 0)
    def _():
        run.greet()

    @pl.when(stage == 3)
    def _():
        run.plain(2)
        run.joined(2)
        run.joined(1)

    target = jnp.bitwise_xor(run.chip, stage_step(stage))
    width = 2 * run.rows
    run.acc[...] = compute(operands, pl.ds(pl.multiple_of(target * width, width), width))
    run.offer(stage)

    @pl.when(stage == 1)
    def _():
        run.corners()

    @pl.when(stage == 2)
    def _():
        run.plain(1)

    @pl.when(stage == 3)
    def _():
        run.finish(o_ref)


def square_reduce(compute, operands, rows, call_id):
    block = (rows, D)

    def held(shape):
        return pl.BlockSpec(shape, lambda s: (0,) * len(shape), pipeline_mode=pl.Buffered(1))

    return pl.pallas_call(
        functools.partial(square_kernel, compute, len(operands)),
        out_shape=jax.ShapeDtypeStruct(block, F32),
        grid=(4,),
        in_specs=[held(x.shape) for x in operands],
        out_specs=held(block),
        scratch_shapes=[
            pltpu.VMEM((2 * rows, D), F32),
            pltpu.VMEM((4,) + block, BF16),
            pltpu.VMEM((4,) + block, BF16),
            pltpu.VMEM((4,) + block, BF16),
            pltpu.VMEM((3,) + block, BF16),
            pltpu.VMEM((2, rows // 2, D), BF16),
            pltpu.VMEM((2,) + block, BF16),
            pltpu.SemaphoreType.DMA((4,)),
            pltpu.SemaphoreType.DMA((4,)),
            pltpu.SemaphoreType.DMA((2, 2)),
            pltpu.SemaphoreType.DMA((2, 2)),
            pltpu.SemaphoreType.DMA((2,)),
            pltpu.SemaphoreType.DMA((2,)),
        ],
        cost_estimate=BRIEF,
        compiler_params=pltpu.CompilerParams(
            collective_id=call_id, has_side_effects=True, vmem_limit_bytes=60 << 20
        ),
    )(*operands)


def widen_back_rows(refs, rows):
    dg_ref, du_ref, w_ref = refs
    total = None
    for i in range(w_ref.shape[0]):
        part = dot_nt(dg_ref[i, rows], w_ref[i, 0]) + dot_nt(du_ref[i, rows], w_ref[i, 1])
        total = part if total is None else total + part
    return total


def project_back_rows(refs, rows):
    d_ref, w_ref = refs
    return dot_nt(d_ref[rows], w_ref[...])


def mix_rows(refs, rows):
    h_ref, w_ref = refs
    total = None
    for i in range(w_ref.shape[0]):
        part = matmul(h_ref[i, rows], w_ref[i])
        total = part if total is None else total + part
    return total


def twin_kernel(compute, count, *refs):
    operands, (o_ref, corner_ref, x_ref, y_ref) = refs[:count], refs[count : count + 4]
    acc, mine, away, twin, tsend, trecv = refs[count + 4 :]
    chip, core = place()
    stage = pl.program_id(0)
    rows = o_ref.shape[0]

    def copy(s):
        return remote(away.at[s], twin.at[s], tsend.at[s], trecv.at[s], chip, 1 - core)

    def both(s):
        copy(s).wait_recv()
        return mine[s].astype(F32) + twin[s].astype(F32)

    @pl.when(stage == 0)
    def _():
        greet([(chip, 1 - core)])

    target = jnp.bitwise_xor(chip, stage_step(stage)) * 2 * rows
    acc[...] = compute(operands, pl.ds(pl.multiple_of(target, 2 * rows), 2 * rows))
    mine[stage] = acc[pl.ds(pl.multiple_of(core * rows, rows), rows)].astype(BF16)
    away[stage] = acc[pl.ds(pl.multiple_of((1 - core) * rows, rows), rows)].astype(BF16)
    copy(stage).start()

    for s, part_ref in enumerate((corner_ref, x_ref, y_ref)):

        @pl.when(stage == s + 1)
        def _(s=s, part_ref=part_ref):
            part_ref[...] = both(s).astype(BF16)

    @pl.when(stage == 3)
    def _():
        o_ref[...] = both(3)
        for s in range(4):
            copy(s).wait_send()


def twin_reduce(compute, operands, rows, call_id):
    block = (rows, D)

    def held(shape):
        return pl.BlockSpec(shape, lambda s: (0,) * len(shape), pipeline_mode=pl.Buffered(1))

    return pl.pallas_call(
        functools.partial(twin_kernel, compute, len(operands)),
        out_shape=(jax.ShapeDtypeStruct(block, F32),) + (jax.ShapeDtypeStruct(block, BF16),) * 3,
        grid=(4,),
        in_specs=[held(x.shape) for x in operands],
        out_specs=(held(block),) * 4,
        scratch_shapes=[
            pltpu.VMEM((2 * rows, D), F32),
            pltpu.VMEM((4,) + block, BF16),
            pltpu.VMEM((4,) + block, BF16),
            pltpu.VMEM((4,) + block, BF16),
            pltpu.SemaphoreType.DMA((4,)),
            pltpu.SemaphoreType.DMA((4,)),
        ],
        cost_estimate=BRIEF,
        compiler_params=pltpu.CompilerParams(
            collective_id=call_id, has_side_effects=True, vmem_limit_bytes=60 << 20
        ),
    )(*operands)


def swap_others(parts):
    return tuple(swap_chips(part, step) for step, part in zip((3, 1, 2), parts))


def join(own, came):
    for part in came:
        own = own + part.astype(F32)
    return own


def entry_kernel(
    grps, chips, tok_ref, cot_ref, pack_ref, all_tok, all_cot, all_pack,
    tsend, trecv, tlocal, csend, crecv, clocal, psend, precv, plocal, zsend, zrecv, usend, dsend,
):
    grp = lax.axis_index("grp")
    chip, core = place()
    me = chip * 2 + core
    above, below = lax.rem(grp + 1, grps), lax.rem(grp + grps - 1, grps)
    near = [(flip(chip, s, chips), c) for s in range(1, chips) for c in (core, 1 - core)]
    near = near + [(chip, 1 - core)]
    barrier = pltpu.get_barrier_semaphore()
    for g in (above, below):
        pl.semaphore_signal(barrier, inc=1, device_id={"grp": g}, device_id_type=MESH)
    for to, c in near:
        pl.semaphore_signal(
            barrier, inc=1, device_id={"chip": to, "core": c}, device_id_type=MESH
        )
    pl.semaphore_wait(barrier, len(near) + 2)

    tok = Gather(chips, False, tok_ref, all_tok, tsend, trecv, tlocal)
    cot = Gather(chips, False, cot_ref, all_cot, csend, crecv, clocal)
    packs = []
    for i, (to, c) in enumerate(near):
        copy = remote(
            pack_ref.at[to * 2 + c], all_pack.at[grp, me], psend.at[i], precv.at[me], to, c
        )
        copy.start()
        packs.append(copy)
    mine = pltpu.make_async_copy(pack_ref.at[me], all_pack.at[grp, me], plocal)
    mine.start()
    tok.start()
    cot.start()
    for to, c in near:
        slot = to * 2 + c
        remote(
            pack_ref.at[me], all_pack.at[grp, slot], psend.at[0], precv.at[slot], to, c
        ).wait_recv()
    mine.wait()

    def z_copy(block, sem, to):
        return pltpu.make_async_remote_copy(
            src_ref=all_pack.at[block],
            dst_ref=all_pack.at[block],
            send_sem=sem,
            recv_sem=zrecv.at[block],
            device_id={"grp": to},
            device_id_type=MESH,
        )

    has_above, has_below = grp + 1 < grps, grp > 0

    def send(step, block, up):
        @pl.when(has_above if up else has_below)
        def _():
            z_copy(block, (usend if up else dsend).at[step], above if up else below).start()

    def relay(step):
        low, high = grp - step, grp + step

        @pl.when(low >= 0)
        def _():
            z_copy(low, zsend, below).wait_recv()
            send(step, low, True)

        @pl.when(high < grps)
        def _():
            z_copy(high, zsend, above).wait_recv()
            send(step, high, False)

    send(0, grp, True)
    send(0, grp, False)
    tok.relay(0, 4)
    relay(1)
    tok.relay(4, None)
    for step in range(2, grps - 1):
        relay(step)
    cot.relay(0, 4)
    if grps > 2:
        relay(grps - 1)
    cot.relay(4, None)
    tok.finish()
    cot.finish()
    for copy in packs:
        copy.wait_send()
    for step in range(grps):
        for up in (True, False):
            held = grp - step >= 0 if up else grp + step < grps

            @pl.when(held & (has_above if up else has_below))
            def _(step=step, up=up):
                block = grp - step if up else grp + step
                z_copy(block, (usend if up else dsend).at[step], above if up else below).wait_send()


def entry(tokens, cotangent, packed, grps, chips, call_id):
    devs = 2 * chips
    return pl.pallas_call(
        functools.partial(entry_kernel, grps, chips),
        out_shape=(
            jax.ShapeDtypeStruct((devs,) + tokens.shape, BF16),
            jax.ShapeDtypeStruct((devs,) + cotangent.shape, BF16),
            jax.ShapeDtypeStruct((grps,) + packed.shape, BF16),
        ),
        in_specs=[ANY] * 3,
        out_specs=(ANY,) * 3,
        scratch_shapes=gather_sems(chips)
        + gather_sems(chips)
        + [
            pltpu.SemaphoreType.DMA((devs,)),
            pltpu.SemaphoreType.DMA((devs,)),
            pltpu.SemaphoreType.DMA,
            pltpu.SemaphoreType.DMA,
            pltpu.SemaphoreType.DMA((grps,)),
            pltpu.SemaphoreType.DMA((grps,)),
            pltpu.SemaphoreType.DMA((grps,)),
        ],
        cost_estimate=BRIEF,
        compiler_params=pltpu.CompilerParams(collective_id=call_id, has_side_effects=True),
    )(tokens, cotangent, packed)


def project_kernel(used, x_ref, w_ref, n_ref, qkv_ref, gain_ref):
    @pl.when(pl.program_id(0) == 0)
    def _():
        gain_ref[...] = w_ref[:, used:].astype(F32).T[:8]

    values = x_ref[...].astype(F32)
    factor = lax.rsqrt(jnp.mean(values * values, axis=-1, keepdims=True) + EPSILON)
    normed = (values * factor * gain_ref[0:1]).astype(BF16)
    n_ref[...] = normed
    qkv_ref[...] = matmul(normed, w_ref[:, :used]).astype(BF16)


def project(tokens, packed, used):
    count, depth = tokens.shape
    rows = tile_rows(count, 256)
    return pl.pallas_call(
        functools.partial(project_kernel, used),
        out_shape=(
            jax.ShapeDtypeStruct((count, depth), BF16),
            jax.ShapeDtypeStruct((count, used), BF16),
            jax.ShapeDtypeStruct((8, depth), F32),
        ),
        grid=(count // rows,),
        in_specs=[
            pl.BlockSpec((rows, depth), lambda r: (r, 0)),
            pl.BlockSpec(packed.shape, lambda r: (0, 0)),
        ],
        out_specs=(
            pl.BlockSpec((rows, depth), lambda r: (r, 0)),
            pl.BlockSpec((rows, used), lambda r: (r, 0)),
            pl.BlockSpec((8, depth), lambda r: (0, 0)),
        ),
        cost_estimate=BRIEF,
        compiler_params=params(1),
    )(tokens, packed)


def turn_kernel(
    count, res_ref, dn_ref, cot_ref, gain_ref, branch_ref, own_ref, *refs
):
    came, (att_ref, w_ref, lay_ref, dres_ref, tot_ref, datt_ref, grad_ref, dba) = refs[:count], refs[count:]

    @pl.when(pl.program_id(0) == 0)
    def _():
        residual = res_ref[...]
        mlp = own_ref[...]
        for part_ref in came:
            mlp = mlp + part_ref[...].astype(F32)
        mlp = RESID_MULT * mlp
        layer_out = residual + mlp
        lay_ref[...] = layer_out.astype(BF16)
        attn = RESID_MULT * branch_ref[...]
        grad = dn_ref[...]
        scaled = gain_ref[1:2] * grad
        factor = lax.rsqrt(jnp.mean(residual * residual, axis=-1, keepdims=True) + EPSILON)
        inner = jnp.mean(residual * scaled, axis=-1, keepdims=True)
        d_residual = cot_ref[...].astype(F32) + factor * scaled
        d_residual = d_residual - residual * (factor * factor * factor * inner)
        dres_ref[...] = d_residual
        dba[...] = (RESID_MULT * d_residual).astype(BF16)
        d_gain = jnp.sum(grad * residual * factor, axis=0, keepdims=True)
        width = tot_ref.shape[1]
        tot_ref[...] = jnp.zeros_like(tot_ref)
        for r in range(pl.cdiv(D, width)):
            last = min(width, D - r * width)
            tot_ref[r : r + 1, :last] = d_gain[:, r * width : r * width + last]
        lane = lax.broadcasted_iota(jnp.int32, (1, 128), 1)
        row = jnp.zeros((1, 128), F32)
        for i, part in enumerate((layer_out, attn, mlp)):
            square = jnp.sum(jnp.sum(part * part, axis=0, keepdims=True), axis=1, keepdims=True)
            row = jnp.where(lane == i, square, row)
        tot_ref[7:8, :128] = row

    datt_ref[...] = dot_nt(dba[...], w_ref[...]).astype(BF16)
    grad_ref[...] = matmul(att_ref[...].T, dba[...]).astype(BF16)


def turn(residual, d_normed, cotangent, gains, branch, own, came, attended, weights):
    rows = residual.shape[0]
    cols = 256
    flat = jax.ShapeDtypeStruct((rows, D), F32)

    def held(shape):
        return pl.BlockSpec(shape, lambda j: (0,) * len(shape), pipeline_mode=pl.Buffered(1))

    return pl.pallas_call(
        functools.partial(turn_kernel, len(came)),
        out_shape=(
            jax.ShapeDtypeStruct((rows, D), BF16),
            flat,
            jax.ShapeDtypeStruct((8, 3 * D // 16), F32),
            jax.ShapeDtypeStruct((rows, D), BF16),
            jax.ShapeDtypeStruct((D, D), BF16),
        ),
        grid=(D // cols,),
        in_specs=[held((rows, D))] * 3
        + [held((8, D))]
        + [held((rows, D))] * (2 + len(came))
        + [
            pl.BlockSpec((rows, cols), lambda j: (0, j)),
            pl.BlockSpec((cols, D), lambda j: (j, 0)),
        ],
        out_specs=(
            held((rows, D)),
            held((rows, D)),
            held((8, 3 * D // 16)),
            pl.BlockSpec((rows, cols), lambda j: (0, j)),
            pl.BlockSpec((cols, D), lambda j: (j, 0)),
        ),
        scratch_shapes=[pltpu.VMEM((rows, D), BF16)],
        cost_estimate=BRIEF,
        compiler_params=params(1),
    )(residual, d_normed, cotangent, gains, branch, own, *came, attended, weights)


def norm_parts(values):
    factor = lax.rsqrt(jnp.mean(values * values, axis=-1, keepdims=True) + EPSILON)
    return factor


def norm_back(values, factor, gain, grad):
    scaled = gain * grad
    inner = jnp.mean(values * scaled, axis=-1, keepdims=True)
    return factor * scaled - values * (factor * factor * factor * inner), jnp.sum(
        grad * values * factor, axis=0
    )


def on_device(
    tokens,
    block_group,
    block_slot,
    attn_gain,
    w_query,
    w_key,
    w_value,
    w_out,
    mlp_gain,
    w_gate,
    w_up,
    w_down,
    cotangent,
):
    grps = lax.axis_size("grp")
    devs = lax.axis_size(PLANE)
    chips = devs // 2
    rows = tokens.shape[0]
    w_rows = w_query.shape[0]
    q_heads = HEADS // devs
    kv_heads = 1
    assert devs % KV_HEADS == 0
    kv_copies = max(1, devs // KV_HEADS)
    q_cols, kv_cols = q_heads * HEAD_DIM, kv_heads * HEAD_DIM
    row_blocks = rows // BLOCK * devs
    row_groups = row_blocks // GROUP_BLOCKS

    row_first = lax.axis_index("grp") * row_blocks
    keys = lax.dynamic_slice_in_dim(block_group, row_first, row_blocks) * GROUP_BLOCKS
    keys = keys + lax.dynamic_slice_in_dim(block_slot, row_first, row_blocks)
    rank = jnp.sum((keys[None, :] < keys[:, None]).astype(jnp.int32), axis=1)
    ids = jnp.arange(row_blocks, dtype=jnp.int32)
    order = jnp.sum(jnp.where(rank[None, :] == ids[:, None], ids[None, :], 0), axis=1)

    def kv_split(w):
        w = w.reshape(w_rows, devs // kv_copies, kv_cols)
        return jnp.repeat(w, kv_copies, axis=1) if kv_copies > 1 else w

    gains = jnp.stack([attn_gain, mlp_gain], axis=1)
    cols = D // 4
    room = cols - q_cols - 2 * kv_cols
    gains = jnp.pad(gains, ((0, 0), (0, room - 2)))
    gains = jnp.broadcast_to(gains[:, None, :], (w_rows, devs, room))
    packed = jnp.concatenate(
        [w_query.reshape(w_rows, devs, q_cols), kv_split(w_key), kv_split(w_value), gains], axis=2
    )
    packed = jnp.swapaxes(packed, 0, 1)
    used = q_cols + 2 * kv_cols
    out_full = gather(w_out[None], "grp")
    upstream = cotangent.astype(F32)
    d_branch_mlp = (RESID_MULT * upstream).astype(BF16)
    all_tokens, d_branch_mlp, packed = entry(tokens, d_branch_mlp, packed, grps, chips, 2)
    packed = packed.reshape(D, cols)
    normed_one, qkv, gains = project(all_tokens.reshape(devs * rows, D), packed, used)
    gain_one, gain_two, w_qkv = gains[0], gains[1], packed[:, :used]
    d_branch_mlp = d_branch_mlp.reshape(devs * rows, D)
    attended = attend(qkv, order, q_heads)
    attended = plane_exchange(
        attended, (rows, D), by_rows(rows), by_cols(q_cols), chips, 3
    )

    out_full = plane_gather(out_full, chips, 4, inner=True).reshape(D, D)
    layer_in = tokens.astype(F32)
    branch_attn = matmul(attended, out_full)
    residual = layer_in + RESID_MULT * branch_attn
    factor_two = norm_parts(residual)
    normed_two = (residual * factor_two * gain_two).astype(BF16)
    normed_two = plane_gather(normed_two, chips, 1).reshape(devs * rows, D)
    wide_w = gather(jnp.stack([w_gate, w_up])[None], "grp")
    down_w = gather(w_down[None], "grp")
    hidden, hidden_t, silu, slope, normed_t = widen(normed_two, wide_w)
    part_down = down_part(hidden_t, d_branch_mlp)
    part_down, hidden, silu = lax.optimization_barrier((part_down, hidden, silu))
    grad_down = scatter(part_down, "grp")
    if chips == 4:
        branch_mlp, *shares = twin_reduce(mix_rows, (hidden, down_w), rows, 11)
        shares, silu = lax.optimization_barrier((shares, silu))
        shares = swap_others(shares)
    d_gate, d_up = narrow_back(silu, slope, d_branch_mlp, down_w)
    if chips == 4:
        part_wide = widen_part(normed_t, d_gate, d_up)
        part_wide, shares, d_gate, d_up = lax.optimization_barrier(
            (part_wide, shares, d_gate, d_up)
        )
        grad_wide = scatter(part_wide, "grp")
        d_normed_two = square_reduce(widen_back_rows, (d_gate, d_up, wide_w), rows, 10)
    else:
        part_wide = widen_part(normed_t, d_gate, d_up)
        part_wide, d_gate, d_up = lax.optimization_barrier((part_wide, d_gate, d_up))
        grad_wide = scatter(part_wide, "grp")
        d_normed_two = widen_back(d_gate, d_up, wide_w)
        d_normed_two = plane_reduce(d_normed_two.reshape(devs, rows, D), chips, 5)
        branch_mlp = mix(hidden, down_w)
        branch_mlp = plane_reduce(branch_mlp.reshape(devs, rows, D), chips, 5)

    layer_out, d_residual, totals, d_attended, grad_out = turn(
        residual,
        d_normed_two,
        cotangent,
        gains,
        branch_attn,
        branch_mlp,
        shares if chips == 4 else (),
        attended,
        out_full,
    )
    if chips == 4:
        drift_out = Drift(grad_out.reshape(grps, 4, 2, w_rows, D), 1)
    d_attended, totals = exchange_total(
        d_attended, totals, (devs * rows, q_cols), rows, q_cols, grps, chips, 7
    )
    if chips == 4:
        sent_out, d_attended = lax.optimization_barrier((drift_out.parts(), d_attended))
        sent_out = swap_others((sent_out[2], sent_out[0], sent_out[1]))
    d_attended, grad_down = lax.optimization_barrier((d_attended, grad_down))
    d_qkv = attend_back(qkv, d_attended, order, q_heads)
    if chips == 4:
        sent_out, d_qkv = lax.optimization_barrier((sent_out, d_qkv))
    sent = over_rows(normed_one, d_qkv).astype(BF16)
    sent, d_qkv, grad_wide = lax.optimization_barrier((sent, d_qkv, grad_wide))
    sent = scatter(sent, "grp")
    d_normed_one = over_cols(d_qkv, w_qkv).astype(BF16).reshape(devs, rows, D)
    if chips == 4:
        sent_out, d_normed_one = lax.optimization_barrier((sent_out, d_normed_one))
        grad_out = drift_out.finish(sent_out).astype(BF16)
    else:
        grad_out = plane_reduce(
            grad_out.reshape(grps, devs, w_rows, D), chips, 6, dtype=BF16, inner=True
        )
    grad_out, d_normed_one = lax.optimization_barrier((grad_out, d_normed_one))
    grad_out = scatter(grad_out, "grp")
    d_normed_one = plane_reduce(d_normed_one, chips, 5)
    d_normed_one, sent = lax.optimization_barrier((d_normed_one, sent))
    d_input_norm, _ = norm_back(layer_in, norm_parts(layer_in), gain_one, d_normed_one)
    tokens_grad = (d_residual + d_input_norm).astype(BF16)
    sent = sent.reshape(devs, w_rows, q_cols + 2 * kv_cols)
    sent = plane_exchange(sent, sent.shape, by_slot, by_slot, chips, 9)
    sent, grad_out = lax.optimization_barrier((sent, grad_out))
    sent, grad_out = sent.astype(F32), grad_out.reshape(w_rows, D).astype(F32)

    def kv_join(g):
        g = g.reshape(devs // kv_copies, kv_copies, w_rows, kv_cols)
        g = jnp.sum(g, axis=1) if kv_copies > 1 else g[:, 0]
        return jnp.swapaxes(g, 0, 1).reshape(w_rows, KV_HEADS * HEAD_DIM)

    grad_query = jnp.swapaxes(sent[:, :, :q_cols], 0, 1).reshape(w_rows, D)
    grad_key = kv_join(sent[:, :, q_cols : q_cols + kv_cols])
    grad_value = kv_join(sent[:, :, q_cols + kv_cols : q_cols + 2 * kv_cols])

    gain_one_grad = sum(
        jnp.sum(weight.astype(F32) * grad, axis=1)
        for weight, grad in ((w_query, grad_query), (w_key, grad_key), (w_value, grad_value))
    ) / attn_gain.astype(F32)
    rms_stats = jnp.sqrt(totals[7, :3] / (rows * grps * devs * D))
    gain_first = (lax.axis_index("grp") * devs + lax.axis_index(PLANE)) * w_rows
    gain_two_grad = lax.dynamic_slice(totals.reshape(-1), (gain_first,), (w_rows,))
    return (
        layer_out,
        tokens_grad,
        gain_one_grad,
        grad_query,
        grad_key,
        grad_value,
        grad_out,
        gain_two_grad,
        grad_wide[0, 0].astype(F32),
        grad_wide[0, 1].astype(F32),
        grad_down[0].astype(F32),
        rms_stats,
    )


def solution(mesh):
    shape = (mesh.shape["grp"], mesh.shape["blk"] // 2, 2)
    mesh = Mesh(mesh.devices.reshape(shape), EVERY)
    row, col, vec = P(EVERY, None), P(None, EVERY), P(EVERY)
    return jax.shard_map(
        on_device,
        mesh=mesh,
        in_specs=(row, P(), P(), vec, row, row, row, row, vec, col, col, row, row),
        out_specs=(row, row, vec, row, row, row, row, vec, col, col, row, P()),
        check_vma=False,
    )
```

```python
import functools

import jax
import jax.numpy as jnp
from jax import lax
from jax.experimental import pallas as pl
from jax.experimental.pallas import tpu as pltpu
from jax.sharding import Mesh
from jax.sharding import PartitionSpec as P

D = 2048
HEADS = 32
KV_HEADS = 8
HEAD_DIM = 64
BLOCK = 128
PROMPT_BLOCKS = 8
GROUP_BLOCKS = 16
PER_GROUP = HEADS // KV_HEADS

ATTN_MULT = 0.015625
RESID_MULT = 0.22
EPSILON = 1e-05
MASKED = -1e30

PLANE = ("chip", "core")
EVERY = ("grp", "chip", "core")
BF16 = jnp.bfloat16
F32 = jnp.float32


MESH = pl.DeviceIdType.MESH
BRIEF = pl.CostEstimate(flops=1000, bytes_accessed=1000, transcendentals=0)
ANY = pl.BlockSpec(memory_space=pl.ANY)
VMEM = pl.BlockSpec(memory_space=pltpu.VMEM)


def place():
    return lax.axis_index("chip"), lax.axis_index("core")


def flip(chip, step, chips):
    return jnp.bitwise_xor(chip, step) if chips == 4 else lax.rem(chip + step, chips)


def unflip(chip, step, chips):
    return jnp.bitwise_xor(chip, step) if chips == 4 else lax.rem(chip + chips - step, chips)


def greet(peers):
    barrier = pltpu.get_barrier_semaphore()
    for chip, core in peers:
        pl.semaphore_signal(
            barrier, inc=1, device_id={"chip": chip, "core": core}, device_id_type=MESH
        )
    pl.semaphore_wait(barrier, len(peers))


def remote(src, dst, send, recv, chip, core):
    return pltpu.make_async_remote_copy(
        src_ref=src,
        dst_ref=dst,
        send_sem=send,
        recv_sem=recv,
        device_id={"chip": chip, "core": core},
        device_id_type=MESH,
    )


class Gather:
    def __init__(self, chips, inner, x_ref, o_ref, send, recv, local):
        self.chips, self.inner, self.x, self.o = chips, inner, x_ref, o_ref
        self.send, self.recv, self.local = send, recv, local
        self.chip, self.core = place()
        self.half = x_ref.shape[0] // 2
        self.started = []

    def greet(self):
        steps = (1, 2) if self.chips == 4 else range(1, self.chips)
        peers = [(flip(self.chip, s, self.chips), self.core) for s in steps]
        greet(peers + [(self.chip, 1 - self.core)])

    def piece(self, slot, h):
        at = pl.ds(h * self.half, self.half)
        return self.o.at[at, slot] if self.inner else self.o.at[slot, at]

    def own(self, h):
        return self.x.at[pl.ds(h * self.half, self.half)]

    def slot(self, chip, core):
        return chip * 2 + core

    def push(self, src, slot, h, chip, core):
        i = len(self.started)
        copy = remote(src, self.piece(slot, h), self.send.at[i], self.recv.at[slot, h], chip, core)
        copy.start()
        self.started.append(copy)

    def wait_for(self, slot, h):
        remote(
            self.own(h), self.piece(slot, h), self.send.at[0], self.recv.at[slot, h],
            self.chip, 1 - self.core,
        ).wait_recv()

    def start(self):
        me = self.slot(self.chip, self.core)
        if self.chips == 4:
            for h, s in ((0, 1), (1, 2), (1, 1), (0, 2)):
                self.push(self.own(h), me, h, flip(self.chip, s, 4), self.core)
        else:
            for s in range(1, self.chips):
                for h in range(2):
                    self.push(self.own(h), me, h, flip(self.chip, s, self.chips), self.core)
        for h in range(2):
            self.push(self.own(h), me, h, self.chip, 1 - self.core)
        whole = self.o.at[:, me] if self.inner else self.o.at[me]
        self.mine = pltpu.make_async_copy(self.x, whole, self.local)
        self.mine.start()

    def relay(self, first=0, last=None):
        if self.chips == 4:
            plan = ((1, 0, 2), (2, 1, 1), (1, 1, 0), (2, 0, 0), (3, 0, 0), (3, 1, 0))
        else:
            plan = tuple((s, h, 0) for s in range(1, self.chips) for h in range(2))
        for s, h, onward in plan[first:last]:
            slot = self.slot(unflip(self.chip, s, self.chips), self.core)
            self.wait_for(slot, h)
            if onward:
                self.push(self.piece(slot, h), slot, h, flip(self.chip, onward, 4), self.core)
            self.push(self.piece(slot, h), slot, h, self.chip, 1 - self.core)

    def finish(self):
        for s in range(self.chips):
            slot = self.slot(unflip(self.chip, s, self.chips), 1 - self.core)
            for h in range(2):
                self.wait_for(slot, h)
        for copy in self.started:
            copy.wait_send()
        self.mine.wait()


def gather_sems(chips):
    return [
        pltpu.SemaphoreType.DMA((4 * chips + 4,)),
        pltpu.SemaphoreType.DMA((2 * chips, 2)),
        pltpu.SemaphoreType.DMA,
    ]


def gather_kernel(chips, inner, x_ref, o_ref, *sems):
    run = Gather(chips, inner, x_ref, o_ref, *sems)
    run.greet()
    run.start()
    run.relay()
    run.finish()


def plane_gather(x, chips, call_id, inner=False):
    devs = 2 * chips
    shape = (x.shape[0], devs) + x.shape[1:] if inner else (devs,) + x.shape
    return pl.pallas_call(
        functools.partial(gather_kernel, chips, inner),
        out_shape=jax.ShapeDtypeStruct(shape, x.dtype),
        in_specs=[ANY],
        out_specs=ANY,
        scratch_shapes=gather_sems(chips),
        cost_estimate=BRIEF,
        compiler_params=pltpu.CompilerParams(collective_id=call_id, has_side_effects=True),
    )(x)


def reduce_kernel(chips, inner, p_ref, o_ref, total, mine, twin, moved, corner, landed, lsem, tsend, trecv, msend, mrecv, csend, crecv):
    chip, core = place()
    sib = 1 - core
    half = (p_ref.shape[0] if inner else p_ref.shape[1]) // 2
    block = (lambda slot: p_ref.at[:, slot]) if inner else (lambda slot: p_ref.at[slot])
    steps = (1, 2) if chips == 4 else tuple(range(1, chips))
    peers = [(flip(chip, s, chips), core) for s in steps]
    greet(peers + [(chip, sib)])
    order = (3, 1, 2, 0) if chips == 4 else tuple(range(1, chips)) + (0,)
    loads, twins = {}, {}
    for s in order:
        to = flip(chip, s, chips) * 2
        twins[s] = remote(block(to + sib), twin.at[s], tsend.at[s], trecv.at[s], chip, sib)
        twins[s].start()
        loads[s] = pltpu.make_async_copy(block(to + core), mine.at[s], lsem.at[s])
        loads[s].start()

    def part(s, h):
        at = pl.ds(h * half, half)
        return mine[s, at].astype(F32) + twin[s, at].astype(F32)

    def ready(s):
        loads[s].wait()
        twins[s].wait_recv()

    sent = []
    if chips == 4:
        corners = []
        ready(3)
        for h, s in ((0, 1), (1, 2)):
            moved[3, pl.ds(h * half, half)] = part(3, h).astype(BF16)
            copy = remote(moved.at[3, pl.ds(h * half, half)], corner.at[h], csend.at[h], crecv.at[h], flip(chip, s, 4), core)
            copy.start()
            corners.append(copy)

        def send(s, h):
            at = pl.ds(h * half, half)
            copy = remote(moved.at[s, at], landed.at[s - 1, at], msend.at[s - 1, h], mrecv.at[s - 1, h], flip(chip, s, 4), core)
            copy.start()
            sent.append(copy)

        for s, h in ((1, 0), (2, 1)):
            ready(s)
            moved[s, pl.ds(h * half, half)] = part(s, h).astype(BF16)
            send(s, h)
        for s, h in ((2, 0), (1, 1)):
            corners[h].wait_recv()
            moved[s, pl.ds(h * half, half)] = (part(s, h) + corner[h].astype(F32)).astype(BF16)
            send(s, h)
        for copy in corners:
            copy.wait_send()
    else:
        for s in steps:
            ready(s)
            for h in range(2):
                at = pl.ds(h * half, half)
                moved[s, at] = part(s, h).astype(BF16)
                copy = remote(moved.at[s, at], landed.at[s - 1, at], msend.at[s - 1, h], mrecv.at[s - 1, h], flip(chip, s, chips), core)
                copy.start()
                sent.append(copy)
    ready(0)
    for h in range(2):
        total[pl.ds(h * half, half)] = part(0, h)
    for copy in sent:
        copy.wait()
    for s in steps[:-1]:
        total[...] += landed[s - 1].astype(F32)
    o_ref[...] = (total[...] + landed[steps[-1] - 1].astype(F32)).astype(o_ref.dtype)
    for s in order:
        twins[s].wait_send()


def plane_reduce(p, chips, call_id, dtype=F32, inner=False):
    block = (p.shape[0],) + p.shape[2:] if inner else p.shape[1:]
    steps = 2 if chips == 4 else chips - 1
    return pl.pallas_call(
        functools.partial(reduce_kernel, chips, inner),
        out_shape=jax.ShapeDtypeStruct(block, dtype),
        in_specs=[ANY],
        out_specs=VMEM,
        scratch_shapes=[
            pltpu.VMEM(block, F32),
            pltpu.VMEM((chips,) + block, BF16),
            pltpu.VMEM((chips,) + block, BF16),
            pltpu.VMEM((chips,) + block, BF16),
            pltpu.VMEM((2, block[0] // 2) + block[1:], BF16),
            pltpu.VMEM((steps,) + block, BF16),
            pltpu.SemaphoreType.DMA((chips,)),
            pltpu.SemaphoreType.DMA((chips,)),
            pltpu.SemaphoreType.DMA((chips,)),
            pltpu.SemaphoreType.DMA((steps, 2)),
            pltpu.SemaphoreType.DMA((steps, 2)),
            pltpu.SemaphoreType.DMA((2,)),
            pltpu.SemaphoreType.DMA((2,)),
        ],
        cost_estimate=BRIEF,
        compiler_params=pltpu.CompilerParams(
            collective_id=call_id, has_side_effects=True, vmem_limit_bytes=56 << 20
        ),
    )(p)


def swap_chips(values, step):
    return lax.ppermute(values, "chip", [(c, c ^ step) for c in range(4)])


class Drift:
    def __init__(self, mine, away, axis):
        self.axis = axis
        self.chip, self.core = place()
        self.mine = mine
        self.twin = lax.ppermute(away, "core", [(0, 1), (1, 0)])

    def part(self, step):
        at = jnp.bitwise_xor(self.chip, step)
        mine = lax.dynamic_index_in_dim(self.mine, at, self.axis, keepdims=False)
        twin = lax.dynamic_index_in_dim(self.twin, at, self.axis, keepdims=False)
        return mine.astype(F32) + twin.astype(F32)

    def parts(self):
        return tuple(self.part(step).astype(BF16) for step in (1, 2, 3))

    def finish(self, came):
        total = self.part(0)
        for part in came:
            total = total + part.astype(F32)
        return total


def exchange_kernel(chips, cut, paste, x_ref, o_ref, send, recv, local):
    chip, core = place()
    me = chip * 2 + core
    peers = [(flip(chip, s, chips), c) for s in range(1, chips) for c in (core, 1 - core)]
    peers = peers + [(chip, 1 - core)]
    greet(peers)
    far = [p for p in ([3, 1, 2] if chips == 4 else range(1, chips))]
    order = [(flip(chip, s, chips), c) for s in far for c in (core, 1 - core)] + [(chip, 1 - core)]
    copies = []
    for i, (to, c) in enumerate(order):
        copy = remote(cut(x_ref, to * 2 + c), paste(o_ref, me), send.at[i], recv.at[me], to, c)
        copy.start()
        copies.append(copy)
    mine = pltpu.make_async_copy(cut(x_ref, me), paste(o_ref, me), local)
    mine.start()
    for s in far:
        for c in (core, 1 - core):
            slot = unflip(chip, s, chips) * 2 + c
            remote(cut(x_ref, me), paste(o_ref, slot), send.at[0], recv.at[slot], chip, 1 - core).wait_recv()
    slot = chip * 2 + 1 - core
    remote(cut(x_ref, me), paste(o_ref, slot), send.at[0], recv.at[slot], chip, 1 - core).wait_recv()
    for copy in copies:
        copy.wait_send()
    mine.wait()


def plane_exchange(x, shape, cut, paste, chips, call_id):
    return pl.pallas_call(
        functools.partial(exchange_kernel, chips, cut, paste),
        out_shape=jax.ShapeDtypeStruct(shape, x.dtype),
        in_specs=[ANY],
        out_specs=ANY,
        scratch_shapes=[
            pltpu.SemaphoreType.DMA((2 * chips,)),
            pltpu.SemaphoreType.DMA((2 * chips,)),
            pltpu.SemaphoreType.DMA,
        ],
        cost_estimate=BRIEF,
        compiler_params=pltpu.CompilerParams(collective_id=call_id, has_side_effects=True),
    )(x)


def by_slot(ref, dev):
    return ref.at[dev]


def by_rows(rows):
    return lambda ref, dev: ref.at[pl.ds(pl.multiple_of(dev * rows, rows), rows)]


def by_cols(cols):
    return lambda ref, dev: ref.at[:, pl.ds(pl.multiple_of(dev * cols, cols), cols)]


def matmul(left, right):
    return jnp.dot(left, right, preferred_element_type=F32)


def over_rows(left, right):
    return lax.dot_general(left, right, (((0,), (0,)), ((), ())), preferred_element_type=F32)


def over_cols(left, right):
    return lax.dot_general(left, right, (((1,), (1,)), ((), ())), preferred_element_type=F32)


def gather(values, axes, axis=0):
    return lax.all_gather(values, axes, axis=axis, tiled=True)


def scatter(values, axes, axis=0):
    return lax.psum_scatter(values, axes, scatter_dimension=axis, tiled=True)


def dot_nt(left, right):
    return lax.dot_general(left, right, (((1,), (1,)), ((), ())), preferred_element_type=F32)


def head_stack(values, heads):
    col_head = lax.broadcasted_iota(jnp.int32, values.shape, 1) // HEAD_DIM
    return jnp.concatenate(
        [jnp.where(col_head == h, values, jnp.zeros_like(values)) for h in range(heads)], axis=0
    )


def head_pick(stacked, heads):
    rows = stacked.shape[0] // heads
    col_head = lax.broadcasted_iota(jnp.int32, (rows, stacked.shape[1]), 1) // HEAD_DIM
    total = jnp.zeros((rows, stacked.shape[1]), F32)
    for h in range(heads):
        total = jnp.where(col_head == h, stacked[h * rows : (h + 1) * rows], total)
    return total


def head_fold(values, heads):
    total = values[:, :HEAD_DIM]
    for h in range(1, heads):
        total = total + values[:, h * HEAD_DIM : (h + 1) * HEAD_DIM]
    return total


def repeat_heads(values, heads):
    return jnp.concatenate([values] * heads, axis=1)


def own_rows(order_ref, slot):
    return pl.ds(pl.multiple_of(order_ref[slot] * BLOCK, BLOCK), BLOCK)


def load_prompt(heads, order_ref, qkv_ref, k_ref, v_ref, first):
    q_cols = heads * HEAD_DIM
    for s in range(PROMPT_BLOCKS):
        pair = qkv_ref[own_rows(order_ref, first + s), q_cols:]
        at = pl.ds(s * BLOCK, BLOCK)
        k_ref[at] = repeat_heads(pair[:, :HEAD_DIM], heads)
        v_ref[at] = repeat_heads(pair[:, HEAD_DIM:], heads)


def by_keys(slot, body):
    prompt = PROMPT_BLOCKS * BLOCK
    quarter = prompt // 4
    seen = jnp.minimum(slot, PROMPT_BLOCKS) * BLOCK
    for n in range(1, 5):
        low = (n - 1) * quarter if n > 1 else -1

        @pl.when((seen > low) & (seen <= n * quarter))
        def _(n=n):
            body(n * quarter)


def soft_parts(heads, slot, q_stack, k_far, k_own):
    far = dot_nt(k_far, q_stack)
    own = dot_nt(k_own, q_stack)
    limit = jnp.minimum(slot, PROMPT_BLOCKS) * BLOCK
    far = jnp.where(lax.broadcasted_iota(jnp.int32, far.shape, 0) < limit, far, MASKED)
    key = lax.broadcasted_iota(jnp.int32, own.shape, 0)
    row = lax.broadcasted_iota(jnp.int32, own.shape, 1) % BLOCK
    own = jnp.where(key <= row, own, MASKED)
    peak = jnp.maximum(jnp.max(far, axis=0, keepdims=True), jnp.max(own, axis=0, keepdims=True))
    far, own = jnp.exp(far - peak), jnp.exp(own - peak)
    scale = 1.0 / (jnp.sum(far, axis=0, keepdims=True) + jnp.sum(own, axis=0, keepdims=True))
    return far * scale, own * scale


def scaled_stack(q, heads):
    return head_stack((q.astype(F32) * ATTN_MULT).astype(BF16), heads)


def attend_kernel(heads, order_ref, qkv_ref, o_ref, k_ref, v_ref, vt_ref):
    first, slot = pl.program_id(0) * GROUP_BLOCKS, pl.program_id(1)
    q_cols = heads * HEAD_DIM

    @pl.when(slot == 0)
    def _():
        load_prompt(heads, order_ref, qkv_ref, k_ref, v_ref, first)
        vt_ref[...] = v_ref[...].astype(F32).T.astype(BF16)

    rows = own_rows(order_ref, first + slot)
    mine = qkv_ref[rows, :]
    k_own = repeat_heads(mine[:, q_cols : q_cols + HEAD_DIM], heads)
    v_own = repeat_heads(mine[:, q_cols + HEAD_DIM :], heads)
    q_stack = scaled_stack(mine[:, :q_cols], heads)

    def body(count):
        far, own = soft_parts(heads, slot, q_stack, k_ref[:count], k_own)
        mixed = matmul(vt_ref[:, :count], far.astype(BF16))
        mixed += matmul(v_own.astype(F32).T.astype(BF16), own.astype(BF16))
        o_ref[rows, :] = head_pick(mixed.T, heads).astype(BF16)

    by_keys(slot, body)


def attend_back_kernel(
    heads, order_ref, qkv_ref, d_ref, o_ref, k_ref, v_ref, kt_ref, dk_ref, dv_ref
):
    first, slot = pl.program_id(0) * GROUP_BLOCKS, pl.program_id(1)
    q_cols = heads * HEAD_DIM

    @pl.when(slot == 0)
    def _():
        load_prompt(heads, order_ref, qkv_ref, k_ref, v_ref, first)
        kt_ref[...] = k_ref[...].astype(F32).T.astype(BF16)
        dk_ref[...] = jnp.zeros_like(dk_ref)
        dv_ref[...] = jnp.zeros_like(dv_ref)

    rows = own_rows(order_ref, first + slot)
    mine = qkv_ref[rows, :]
    k_own = repeat_heads(mine[:, q_cols : q_cols + HEAD_DIM], heads)
    v_own = repeat_heads(mine[:, q_cols + HEAD_DIM :], heads)
    q_stack = scaled_stack(mine[:, :q_cols], heads)
    d_stack = head_stack(d_ref[rows, :], heads)

    def fold(d_k, d_v):
        return jnp.concatenate([head_fold(d_k, heads), head_fold(d_v, heads)], axis=1).astype(BF16)

    def body(count):
        far, own = soft_parts(heads, slot, q_stack, k_ref[:count], k_own)
        d_far, d_own = dot_nt(v_ref[:count], d_stack), dot_nt(v_own, d_stack)
        mean = jnp.sum(far * d_far, axis=0, keepdims=True)
        mean += jnp.sum(own * d_own, axis=0, keepdims=True)
        d_far = (far * (d_far - mean)).astype(BF16)
        d_own = (own * (d_own - mean)).astype(BF16)
        dv_ref[:count] += matmul(far.astype(BF16), d_stack)
        dk_ref[:count] += matmul(d_far, q_stack)
        dv_own = matmul(own.astype(BF16), d_stack)
        dk_own = matmul(d_own, q_stack)
        d_q = matmul(kt_ref[:, :count], d_far) + matmul(k_own.astype(F32).T.astype(BF16), d_own)
        o_ref[rows, :q_cols] = (head_pick(d_q.T, heads) * ATTN_MULT).astype(BF16)

        @pl.when(slot < PROMPT_BLOCKS)
        def _():
            at = pl.ds(pl.multiple_of(slot * BLOCK, BLOCK), BLOCK)
            dk_ref[at] += dk_own
            dv_ref[at] += dv_own

        @pl.when(slot >= PROMPT_BLOCKS)
        def _():
            o_ref[rows, q_cols:] = fold(dk_own, dv_own)

    by_keys(slot, body)

    @pl.when(slot == GROUP_BLOCKS - 1)
    def _():
        for s in range(PROMPT_BLOCKS):
            at = pl.ds(s * BLOCK, BLOCK)
            o_ref[own_rows(order_ref, first + s), q_cols:] = fold(dk_ref[at], dv_ref[at])


def whole(shape):
    return pl.BlockSpec(shape, lambda g, s, order: (0,) * len(shape))


def attend(qkv, order, heads):
    tokens, cols = qkv.shape
    prompt, q_cols = PROMPT_BLOCKS * BLOCK, heads * HEAD_DIM
    return pl.pallas_call(
        functools.partial(attend_kernel, heads),
        out_shape=jax.ShapeDtypeStruct((tokens, q_cols), BF16),
        grid_spec=pltpu.PrefetchScalarGridSpec(
            num_scalar_prefetch=1,
            grid=(tokens // (GROUP_BLOCKS * BLOCK), GROUP_BLOCKS),
            in_specs=[whole((tokens, cols))],
            out_specs=whole((tokens, q_cols)),
            scratch_shapes=[
                pltpu.VMEM((prompt, q_cols), BF16),
                pltpu.VMEM((prompt, q_cols), BF16),
                pltpu.VMEM((q_cols, prompt), BF16),
            ],
        ),
        cost_estimate=BRIEF,
        compiler_params=pltpu.CompilerParams(vmem_limit_bytes=40 << 20),
    )(order, qkv)


def attend_back(qkv, d_attended, order, heads):
    tokens, cols = qkv.shape
    prompt, q_cols = PROMPT_BLOCKS * BLOCK, heads * HEAD_DIM
    return pl.pallas_call(
        functools.partial(attend_back_kernel, heads),
        out_shape=jax.ShapeDtypeStruct((tokens, cols), BF16),
        grid_spec=pltpu.PrefetchScalarGridSpec(
            num_scalar_prefetch=1,
            grid=(tokens // (GROUP_BLOCKS * BLOCK), GROUP_BLOCKS),
            in_specs=[whole((tokens, cols)), whole((tokens, q_cols))],
            out_specs=whole((tokens, cols)),
            scratch_shapes=[
                pltpu.VMEM((prompt, q_cols), BF16),
                pltpu.VMEM((prompt, q_cols), BF16),
                pltpu.VMEM((q_cols, prompt), BF16),
                pltpu.VMEM((prompt, q_cols), F32),
                pltpu.VMEM((prompt, q_cols), F32),
            ],
        ),
        cost_estimate=BRIEF,
        compiler_params=pltpu.CompilerParams(vmem_limit_bytes=40 << 20),
    )(order, qkv, d_attended)


def exchange_total_kernel(
    grps, chips, cut, paste, x_ref, t_ref, o_ref, sum_ref,
    over_z, over_plane, send, recv, local, zsend, zrecv, psend, precv,
):
    grp = lax.axis_index("grp")
    chip, core = place()
    me = chip * 2 + core
    far = [lax.rem(grp + s, grps) for s in range(1, grps)]
    steps = (3, 1, 2) if chips == 4 else tuple(range(1, chips))
    near = [(flip(chip, s, chips), c) for s in steps for c in (core, 1 - core)]
    near = near + [(chip, 1 - core)]
    barrier = pltpu.get_barrier_semaphore()
    for g in far:
        pl.semaphore_signal(barrier, inc=1, device_id={"grp": g}, device_id_type=MESH)
    for to, c in near:
        pl.semaphore_signal(
            barrier, inc=1, device_id={"chip": to, "core": c}, device_id_type=MESH
        )
    pl.semaphore_wait(barrier, len(far) + len(near))

    def z_copy(slot, sem, to):
        return pltpu.make_async_remote_copy(
            src_ref=t_ref,
            dst_ref=over_z.at[slot],
            send_sem=sem,
            recv_sem=zrecv.at[slot],
            device_id={"grp": to},
            device_id_type=MESH,
        )

    copies = []
    for i, g in enumerate(far):
        copy = z_copy(grp, zsend.at[i], g)
        copy.start()
        copies.append(copy)
    for i, (to, c) in enumerate(near):
        copy = remote(cut(x_ref, to * 2 + c), paste(o_ref, me), send.at[i], recv.at[me], to, c)
        copy.start()
        copies.append(copy)
    mine = pltpu.make_async_copy(cut(x_ref, me), paste(o_ref, me), local)
    mine.start()
    over_z[grp] = t_ref[...]
    for g in far:
        z_copy(g, zsend.at[0], g).wait_recv()
    over_plane[me] = jnp.sum(over_z[...], axis=0)
    for i, (to, c) in enumerate(near):
        copy = remote(over_plane.at[me], over_plane.at[me], psend.at[i], precv.at[me], to, c)
        copy.start()
        copies.append(copy)
    for to, c in near:
        slot = to * 2 + c
        remote(cut(x_ref, me), paste(o_ref, slot), send.at[0], recv.at[slot], to, c).wait_recv()
        remote(over_plane.at[me], over_plane.at[slot], psend.at[0], precv.at[slot], to, c).wait_recv()
    for copy in copies:
        copy.wait_send()
    mine.wait()
    sum_ref[...] = jnp.sum(over_plane[...], axis=0)


def exchange_total(x, t, shape, rows, cols, grps, chips, call_id):
    devs = 2 * chips
    return pl.pallas_call(
        functools.partial(exchange_total_kernel, grps, chips, by_cols(cols), by_rows(rows)),
        out_shape=(
            jax.ShapeDtypeStruct(shape, x.dtype),
            jax.ShapeDtypeStruct(t.shape, F32),
        ),
        in_specs=[ANY, VMEM],
        out_specs=(ANY, VMEM),
        scratch_shapes=[
            pltpu.VMEM((grps,) + t.shape, F32),
            pltpu.VMEM((devs,) + t.shape, F32),
            pltpu.SemaphoreType.DMA((devs,)),
            pltpu.SemaphoreType.DMA((devs,)),
            pltpu.SemaphoreType.DMA,
            pltpu.SemaphoreType.DMA((grps,)),
            pltpu.SemaphoreType.DMA((grps,)),
            pltpu.SemaphoreType.DMA((devs,)),
            pltpu.SemaphoreType.DMA((devs,)),
        ],
        cost_estimate=BRIEF,
        compiler_params=pltpu.CompilerParams(collective_id=call_id, has_side_effects=True),
    )(x, t)


def params(axes, mib=56):
    return pltpu.CompilerParams(
        dimension_semantics=("arbitrary",) * axes, vmem_limit_bytes=mib << 20
    )


def tile_rows(count, limit):
    while count % limit:
        limit //= 2
    return limit


def widen_kernel(n_ref, w_ref, h_ref, ht_ref, s_ref, t_ref, nt_ref):
    values = n_ref[...]
    gate, up = matmul(values, w_ref[0, 0]), matmul(values, w_ref[0, 1])
    sig = 1.0 / (1.0 + jnp.exp(-gate))
    silu = gate * sig
    hidden = (silu * up).astype(BF16)
    h_ref[0] = hidden
    ht_ref[0] = hidden.T
    s_ref[0] = silu.astype(BF16)
    t_ref[0] = (up * (sig * (1.0 + gate * (1.0 - sig)))).astype(BF16)

    @pl.when(pl.program_id(1) == 0)
    def _():
        nt_ref[...] = values.T


def widen(normed, weights):
    tokens, depth = normed.shape
    shards, _, _, width = weights.shape
    rows = tile_rows(tokens, 1024)
    tall = jax.ShapeDtypeStruct((shards, tokens, width), BF16)
    tall_spec = pl.BlockSpec((1, rows, width), lambda r, s: (s, r, 0))
    return pl.pallas_call(
        widen_kernel,
        out_shape=(
            tall,
            jax.ShapeDtypeStruct((shards, width, tokens), BF16),
            tall,
            tall,
            jax.ShapeDtypeStruct((depth, tokens), BF16),
        ),
        grid=(tokens // rows, shards),
        in_specs=[
            pl.BlockSpec((rows, depth), lambda r, s: (r, 0)),
            pl.BlockSpec((1, 2, depth, width), lambda r, s: (s, 0, 0, 0)),
        ],
        out_specs=(
            tall_spec,
            pl.BlockSpec((1, width, rows), lambda r, s: (s, 0, r)),
            tall_spec,
            tall_spec,
            pl.BlockSpec((depth, rows), lambda r, s: (0, r)),
        ),
        cost_estimate=BRIEF,
        compiler_params=params(2),
    )(normed, weights)


def down_part_kernel(ht_ref, d_ref, o_ref):
    o_ref[0] = matmul(ht_ref[0], d_ref[...]).astype(BF16)


def down_part(hidden_t, upstream):
    shards, width, tokens = hidden_t.shape
    depth = upstream.shape[1]
    cols = tile_rows(depth, 1024)
    return pl.pallas_call(
        down_part_kernel,
        out_shape=jax.ShapeDtypeStruct((shards, width, depth), BF16),
        grid=(depth // cols, shards),
        in_specs=[
            pl.BlockSpec((1, width, tokens), lambda c, s: (s, 0, 0)),
            pl.BlockSpec((tokens, cols), lambda c, s: (0, c)),
        ],
        out_specs=pl.BlockSpec((1, width, cols), lambda c, s: (s, 0, c)),
        cost_estimate=BRIEF,
        compiler_params=params(2),
    )(hidden_t, upstream)


def mix_kernel(h_ref, w_ref, m_ref):
    mixed = None
    for i in range(w_ref.shape[0]):
        part = matmul(h_ref[i], w_ref[i])
        mixed = part if mixed is None else mixed + part
    m_ref[...] = mixed.astype(BF16)


def narrow_specs(hidden, weights):
    shards, tokens, width = hidden.shape
    depth = weights.shape[2]
    rows = tile_rows(tokens, 512)
    return (
        tokens // rows,
        pl.BlockSpec((shards, rows, width), lambda r: (0, r, 0)),
        pl.BlockSpec((rows, depth), lambda r: (r, 0)),
        pl.BlockSpec(weights.shape, lambda r: (0, 0, 0), pipeline_mode=pl.Buffered(1)),
    )


def mix(hidden, weights):
    steps, tall_spec, flat_spec, weight_spec = narrow_specs(hidden, weights)
    return pl.pallas_call(
        mix_kernel,
        out_shape=jax.ShapeDtypeStruct((hidden.shape[1], weights.shape[2]), BF16),
        grid=(steps,),
        in_specs=[tall_spec, weight_spec],
        out_specs=flat_spec,
        cost_estimate=BRIEF,
        compiler_params=params(1),
    )(hidden, weights)


def narrow_back_kernel(s_ref, t_ref, d_ref, w_ref, dg_ref, du_ref):
    upstream = d_ref[...]
    for i in range(w_ref.shape[0]):
        d_hidden = dot_nt(upstream, w_ref[i])
        dg_ref[i] = (d_hidden * t_ref[i].astype(F32)).astype(BF16)
        du_ref[i] = (d_hidden * s_ref[i].astype(F32)).astype(BF16)


def narrow_back(silu, slope, upstream, weights):
    steps, tall_spec, flat_spec, weight_spec = narrow_specs(silu, weights)
    tall = jax.ShapeDtypeStruct(silu.shape, BF16)
    return pl.pallas_call(
        narrow_back_kernel,
        out_shape=(tall, tall),
        grid=(steps,),
        in_specs=[tall_spec, tall_spec, flat_spec, weight_spec],
        out_specs=(tall_spec, tall_spec),
        cost_estimate=BRIEF,
        compiler_params=params(1),
    )(silu, slope, upstream, weights)


def widen_part_kernel(nt_ref, dg_ref, du_ref, o_ref):
    values = nt_ref[...]
    o_ref[0, 0] = matmul(values, dg_ref[0]).astype(BF16)
    o_ref[0, 1] = matmul(values, du_ref[0]).astype(BF16)


def widen_part(normed_t, d_gate, d_up):
    depth, tokens = normed_t.shape
    shards, _, width = d_gate.shape
    rows = tile_rows(depth, 1024)
    tall_spec = pl.BlockSpec((1, tokens, width), lambda r, s: (s, 0, 0))
    return pl.pallas_call(
        widen_part_kernel,
        out_shape=jax.ShapeDtypeStruct((shards, 2, depth, width), BF16),
        grid=(depth // rows, shards),
        in_specs=[pl.BlockSpec((rows, tokens), lambda r, s: (r, 0)), tall_spec, tall_spec],
        out_specs=pl.BlockSpec((1, 2, rows, width), lambda r, s: (s, 0, r, 0)),
        cost_estimate=BRIEF,
        compiler_params=params(2),
    )(normed_t, d_gate, d_up)


def widen_back_kernel(dg_ref, du_ref, w_ref, o_ref):
    total = None
    for i in range(w_ref.shape[0]):
        part = dot_nt(dg_ref[i], w_ref[i, 0]) + dot_nt(du_ref[i], w_ref[i, 1])
        total = part if total is None else total + part
    o_ref[...] = total.astype(BF16)


def widen_back(d_gate, d_up, weights):
    shards, tokens, width = d_gate.shape
    depth = weights.shape[2]
    rows = tile_rows(tokens, 512)
    tall_spec = pl.BlockSpec((shards, rows, width), lambda r: (0, r, 0))
    return pl.pallas_call(
        widen_back_kernel,
        out_shape=jax.ShapeDtypeStruct((tokens, depth), BF16),
        grid=(tokens // rows,),
        in_specs=[
            tall_spec,
            tall_spec,
            pl.BlockSpec(weights.shape, lambda r: (0, 0, 0, 0), pipeline_mode=pl.Buffered(1)),
        ],
        out_specs=pl.BlockSpec((rows, depth), lambda r: (r, 0)),
        cost_estimate=BRIEF,
        compiler_params=params(1),
    )(d_gate, d_up, weights)


def stage_step(stage):
    return jnp.where(stage == 0, 3, jnp.where(stage == 3, 0, stage))


class Square:
    def __init__(self, acc, mine, away, twin, moved, corner, landed, tsend, trecv, msend, mrecv, csend, crecv):
        self.acc, self.mine, self.away, self.twin = acc, mine, away, twin
        self.moved, self.corner, self.landed = moved, corner, landed
        self.tsend, self.trecv, self.msend, self.mrecv = tsend, trecv, msend, mrecv
        self.csend, self.crecv = csend, crecv
        self.chip, self.core = place()
        self.rows = mine.shape[1]
        self.half = self.rows // 2

    def greet(self):
        peers = [(flip(self.chip, s, 4), self.core) for s in (1, 2)]
        greet(peers + [(self.chip, 1 - self.core)])

    def twin_copy(self, stage):
        return remote(
            self.away.at[stage], self.twin.at[stage], self.tsend.at[stage], self.trecv.at[stage],
            self.chip, 1 - self.core,
        )

    def offer(self, stage):
        own, other = self.core * self.rows, (1 - self.core) * self.rows
        self.mine[stage] = self.acc[pl.ds(pl.multiple_of(own, self.rows), self.rows)].astype(BF16)
        self.away[stage] = self.acc[pl.ds(pl.multiple_of(other, self.rows), self.rows)].astype(BF16)
        self.twin_copy(stage).start()

    def at(self, h):
        return pl.ds(h * self.half, self.half)

    def both(self, stage, h):
        return self.mine[stage, self.at(h)].astype(F32) + self.twin[stage, self.at(h)].astype(F32)

    def corner_copy(self, h):
        return remote(
            self.moved.at[0, self.at(h)], self.corner.at[h], self.csend.at[h], self.crecv.at[h],
            flip(self.chip, h + 1, 4), self.core,
        )

    def copy(self, stage, h):
        return remote(
            self.moved.at[stage, self.at(h)], self.landed.at[stage - 1, self.at(h)],
            self.msend.at[stage - 1, h], self.mrecv.at[stage - 1, h],
            flip(self.chip, stage, 4), self.core,
        )

    def corners(self):
        self.twin_copy(0).wait_recv()
        for h in range(2):
            self.moved[0, self.at(h)] = self.both(0, h).astype(BF16)
            self.corner_copy(h).start()

    def plain(self, stage):
        self.twin_copy(stage).wait_recv()
        h = stage - 1
        self.moved[stage, self.at(h)] = self.both(stage, h).astype(BF16)
        self.copy(stage, h).start()

    def joined(self, stage):
        h = 2 - stage
        self.corner_copy(h).wait_recv()
        total = self.both(stage, h) + self.corner[h].astype(F32)
        self.moved[stage, self.at(h)] = total.astype(BF16)
        self.copy(stage, h).start()

    def finish(self, o_ref):
        self.twin_copy(3).wait_recv()
        for h in range(2):
            o_ref[self.at(h)] = self.both(3, h)
        for stage, h in ((1, 0), (2, 1), (2, 0), (1, 1)):
            self.copy(stage, h).wait_recv()
            o_ref[self.at(h)] += self.landed[stage - 1, self.at(h)].astype(F32)
        for stage in (1, 2):
            for h in range(2):
                self.copy(stage, h).wait_send()
        for h in range(2):
            self.corner_copy(h).wait_send()
        for stage in range(4):
            self.twin_copy(stage).wait_send()


def square_kernel(compute, count, *refs):
    operands, o_ref, scratch = refs[:count], refs[count], refs[count + 1 :]
    run = Square(*scratch)
    stage = pl.program_id(0)

    @pl.when(stage == 0)
    def _():
        run.greet()

    @pl.when(stage == 3)
    def _():
        run.plain(2)
        run.joined(2)
        run.joined(1)

    target = jnp.bitwise_xor(run.chip, stage_step(stage))
    width = 2 * run.rows
    run.acc[...] = compute(operands, pl.ds(pl.multiple_of(target * width, width), width))
    run.offer(stage)

    @pl.when(stage == 1)
    def _():
        run.corners()

    @pl.when(stage == 2)
    def _():
        run.plain(1)

    @pl.when(stage == 3)
    def _():
        run.finish(o_ref)


def square_reduce(compute, operands, rows, call_id):
    block = (rows, D)

    def held(shape):
        return pl.BlockSpec(shape, lambda s: (0,) * len(shape), pipeline_mode=pl.Buffered(1))

    return pl.pallas_call(
        functools.partial(square_kernel, compute, len(operands)),
        out_shape=jax.ShapeDtypeStruct(block, F32),
        grid=(4,),
        in_specs=[held(x.shape) for x in operands],
        out_specs=held(block),
        scratch_shapes=[
            pltpu.VMEM((2 * rows, D), F32),
            pltpu.VMEM((4,) + block, BF16),
            pltpu.VMEM((4,) + block, BF16),
            pltpu.VMEM((4,) + block, BF16),
            pltpu.VMEM((3,) + block, BF16),
            pltpu.VMEM((2, rows // 2, D), BF16),
            pltpu.VMEM((2,) + block, BF16),
            pltpu.SemaphoreType.DMA((4,)),
            pltpu.SemaphoreType.DMA((4,)),
            pltpu.SemaphoreType.DMA((2, 2)),
            pltpu.SemaphoreType.DMA((2, 2)),
            pltpu.SemaphoreType.DMA((2,)),
            pltpu.SemaphoreType.DMA((2,)),
        ],
        cost_estimate=BRIEF,
        compiler_params=pltpu.CompilerParams(
            collective_id=call_id, has_side_effects=True, vmem_limit_bytes=60 << 20
        ),
    )(*operands)


def widen_back_rows(refs, rows):
    dg_ref, du_ref, w_ref = refs
    total = None
    for i in range(w_ref.shape[0]):
        part = dot_nt(dg_ref[i, rows], w_ref[i, 0]) + dot_nt(du_ref[i, rows], w_ref[i, 1])
        total = part if total is None else total + part
    return total


def project_back_rows(refs, rows):
    d_ref, w_ref = refs
    return dot_nt(d_ref[rows], w_ref[...])


def mix_rows(refs, rows):
    h_ref, w_ref = refs
    total = None
    for i in range(w_ref.shape[0]):
        part = matmul(h_ref[i, rows], w_ref[i])
        total = part if total is None else total + part
    return total


def twin_kernel(compute, count, *refs):
    operands, (o_ref, corner_ref, x_ref, y_ref) = refs[:count], refs[count : count + 4]
    acc, mine, away, twin, tsend, trecv = refs[count + 4 :]
    chip, core = place()
    stage = pl.program_id(0)
    rows = o_ref.shape[0]

    def copy(s):
        return remote(away.at[s], twin.at[s], tsend.at[s], trecv.at[s], chip, 1 - core)

    def both(s):
        copy(s).wait_recv()
        return mine[s].astype(F32) + twin[s].astype(F32)

    @pl.when(stage == 0)
    def _():
        greet([(chip, 1 - core)])

    target = jnp.bitwise_xor(chip, stage_step(stage)) * 2 * rows
    acc[...] = compute(operands, pl.ds(pl.multiple_of(target, 2 * rows), 2 * rows))
    mine[stage] = acc[pl.ds(pl.multiple_of(core * rows, rows), rows)].astype(BF16)
    away[stage] = acc[pl.ds(pl.multiple_of((1 - core) * rows, rows), rows)].astype(BF16)
    copy(stage).start()

    for s, part_ref in enumerate((corner_ref, x_ref, y_ref)):

        @pl.when(stage == s + 1)
        def _(s=s, part_ref=part_ref):
            part_ref[...] = both(s).astype(BF16)

    @pl.when(stage == 3)
    def _():
        o_ref[...] = both(3)
        for s in range(4):
            copy(s).wait_send()


def twin_reduce(compute, operands, rows, call_id):
    block = (rows, D)

    def held(shape):
        return pl.BlockSpec(shape, lambda s: (0,) * len(shape), pipeline_mode=pl.Buffered(1))

    return pl.pallas_call(
        functools.partial(twin_kernel, compute, len(operands)),
        out_shape=(jax.ShapeDtypeStruct(block, F32),) + (jax.ShapeDtypeStruct(block, BF16),) * 3,
        grid=(4,),
        in_specs=[held(x.shape) for x in operands],
        out_specs=(held(block),) * 4,
        scratch_shapes=[
            pltpu.VMEM((2 * rows, D), F32),
            pltpu.VMEM((4,) + block, BF16),
            pltpu.VMEM((4,) + block, BF16),
            pltpu.VMEM((4,) + block, BF16),
            pltpu.SemaphoreType.DMA((4,)),
            pltpu.SemaphoreType.DMA((4,)),
        ],
        cost_estimate=BRIEF,
        compiler_params=pltpu.CompilerParams(
            collective_id=call_id, has_side_effects=True, vmem_limit_bytes=60 << 20
        ),
    )(*operands)


def swap_others(parts):
    return tuple(swap_chips(part, step) for step, part in zip((3, 1, 2), parts))


def join(own, came):
    for part in came:
        own = own + part.astype(F32)
    return own


def entry_kernel(
    grps, chips, tok_ref, cot_ref, pack_ref, tile_ref, all_tok, all_cot, all_pack, all_tile,
    tsend, trecv, tlocal, csend, crecv, clocal, psend, precv, plocal, zrecv, usend, dsend,
):
    grp = lax.axis_index("grp")
    chip, core = place()
    me = chip * 2 + core
    above, below = lax.rem(grp + 1, grps), lax.rem(grp + grps - 1, grps)
    near = [(flip(chip, s, chips), c) for s in range(1, chips) for c in (core, 1 - core)]
    near = near + [(chip, 1 - core)]
    barrier = pltpu.get_barrier_semaphore()
    for g in (above, below):
        pl.semaphore_signal(barrier, inc=1, device_id={"grp": g}, device_id_type=MESH)
    for to, c in near:
        pl.semaphore_signal(
            barrier, inc=1, device_id={"chip": to, "core": c}, device_id_type=MESH
        )
    pl.semaphore_wait(barrier, len(near) + 2)

    tok = Gather(chips, False, tok_ref, all_tok, tsend, trecv, tlocal)
    cot = Gather(chips, False, cot_ref, all_cot, csend, crecv, clocal)
    packs, mine = [], []
    for i, (to, c) in enumerate(near):
        copy = remote(
            pack_ref.at[to * 2 + c], all_pack.at[grp, me], psend.at[0, i], precv.at[0, me], to, c
        )
        copy.start()
        packs.append(copy)
        copy = remote(tile_ref, all_tile.at[grp, me], psend.at[1, i], precv.at[1, me], to, c)
        copy.start()
        packs.append(copy)
    for k, (src, dst) in enumerate(((pack_ref.at[me], all_pack), (tile_ref, all_tile))):
        mine.append(pltpu.make_async_copy(src, dst.at[grp, me], plocal.at[k]))
        mine[k].start()
    tok.start()
    for to, c in near:
        slot = to * 2 + c
        for k, (src, dst) in enumerate(((pack_ref.at[me], all_pack), (tile_ref, all_tile))):
            remote(src, dst.at[grp, slot], psend.at[k, 0], precv.at[k, slot], to, c).wait_recv()
    for copy in mine:
        copy.wait()

    def z_copies(block, sems, step, to):
        return [
            pltpu.make_async_remote_copy(
                src_ref=whole.at[block],
                dst_ref=whole.at[block],
                send_sem=sems.at[k, step],
                recv_sem=zrecv.at[k, block],
                device_id={"grp": to},
                device_id_type=MESH,
            )
            for k, whole in enumerate((all_pack, all_tile))
        ]

    has_above, has_below = grp + 1 < grps, grp > 0

    def send(step, block, up):
        @pl.when(has_above if up else has_below)
        def _():
            for copy in z_copies(block, usend if up else dsend, step, above if up else below):
                copy.start()

    def relay(step):
        low, high = grp - step, grp + step

        @pl.when(low >= 0)
        def _():
            for copy in z_copies(low, usend, 0, below):
                copy.wait_recv()
            send(step, low, True)

        @pl.when(high < grps)
        def _():
            for copy in z_copies(high, dsend, 0, above):
                copy.wait_recv()
            send(step, high, False)

    send(0, grp, True)
    send(0, grp, False)
    tok.relay(0, 4)
    relay(1)
    cot.start()
    tok.relay(4, None)
    for step in range(2, grps - 1):
        relay(step)
    cot.relay(0, 4)
    if grps > 2:
        relay(grps - 1)
    cot.relay(4, None)
    tok.finish()
    cot.finish()
    for copy in packs:
        copy.wait_send()
    for step in range(grps):
        for up in (True, False):
            held = grp - step >= 0 if up else grp + step < grps

            @pl.when(held & (has_above if up else has_below))
            def _(step=step, up=up):
                block = grp - step if up else grp + step
                sems, to = (usend, above) if up else (dsend, below)
                for copy in z_copies(block, sems, step, to):
                    copy.wait_send()


def entry(tokens, cotangent, packed, tile, grps, chips, call_id):
    devs = 2 * chips
    return pl.pallas_call(
        functools.partial(entry_kernel, grps, chips),
        out_shape=(
            jax.ShapeDtypeStruct((devs,) + tokens.shape, BF16),
            jax.ShapeDtypeStruct((devs,) + cotangent.shape, BF16),
            jax.ShapeDtypeStruct((grps,) + packed.shape, BF16),
            jax.ShapeDtypeStruct((grps, devs) + tile.shape, BF16),
        ),
        in_specs=[ANY] * 4,
        out_specs=(ANY,) * 4,
        scratch_shapes=gather_sems(chips)
        + gather_sems(chips)
        + [
            pltpu.SemaphoreType.DMA((2, devs)),
            pltpu.SemaphoreType.DMA((2, devs)),
            pltpu.SemaphoreType.DMA((2,)),
            pltpu.SemaphoreType.DMA((2, grps)),
            pltpu.SemaphoreType.DMA((2, grps)),
            pltpu.SemaphoreType.DMA((2, grps)),
        ],
        cost_estimate=BRIEF,
        compiler_params=pltpu.CompilerParams(collective_id=call_id, has_side_effects=True),
    )(tokens, cotangent, packed, tile)


def project_kernel(width, x_ref, w_ref, tile_ref, n_ref, qkv_ref, gain_ref):
    @pl.when(pl.program_id(0) == 0)
    def _():
        gain_ref[...] = jnp.zeros_like(gain_ref)
        for f in range(tile_ref.shape[0]):
            gain_ref[0:2, f * width : (f + 1) * width] = tile_ref[f, 0:2, :width].astype(F32)

    values = x_ref[...].astype(F32)
    factor = lax.rsqrt(jnp.mean(values * values, axis=-1, keepdims=True) + EPSILON)
    normed = (values * factor * gain_ref[0:1]).astype(BF16)
    n_ref[...] = normed
    qkv_ref[...] = matmul(normed, w_ref[...]).astype(BF16)


def project(tokens, weights, tiles):
    count, depth = tokens.shape
    used = weights.shape[1]
    rows = tile_rows(count, 256)
    return pl.pallas_call(
        functools.partial(project_kernel, depth // tiles.shape[0]),
        out_shape=(
            jax.ShapeDtypeStruct((count, depth), BF16),
            jax.ShapeDtypeStruct((count, used), BF16),
            jax.ShapeDtypeStruct((8, depth), F32),
        ),
        grid=(count // rows,),
        in_specs=[
            pl.BlockSpec((rows, depth), lambda r: (r, 0)),
            pl.BlockSpec(weights.shape, lambda r: (0, 0)),
            pl.BlockSpec(tiles.shape, lambda r: (0, 0, 0)),
        ],
        out_specs=(
            pl.BlockSpec((rows, depth), lambda r: (r, 0)),
            pl.BlockSpec((rows, used), lambda r: (r, 0)),
            pl.BlockSpec((8, depth), lambda r: (0, 0)),
        ),
        cost_estimate=BRIEF,
        compiler_params=params(1),
    )(tokens, weights, tiles)


def turn_kernel(
    count, res_ref, dn_ref, cot_ref, gain_ref, branch_ref, own_ref, *refs
):
    came, (att_ref, w_ref, lay_ref, dres_ref, tot_ref, datt_ref, *grad_refs, dba) = refs[:count], refs[count:]

    @pl.when(pl.program_id(0) == 0)
    def _():
        residual = res_ref[...]
        mlp = own_ref[...]
        for part_ref in came:
            mlp = mlp + part_ref[...].astype(F32)
        mlp = RESID_MULT * mlp
        layer_out = residual + mlp
        lay_ref[...] = layer_out.astype(BF16)
        attn = RESID_MULT * branch_ref[...]
        grad = dn_ref[...]
        scaled = gain_ref[1:2] * grad
        factor = lax.rsqrt(jnp.mean(residual * residual, axis=-1, keepdims=True) + EPSILON)
        inner = jnp.mean(residual * scaled, axis=-1, keepdims=True)
        d_residual = cot_ref[...].astype(F32) + factor * scaled
        d_residual = d_residual - residual * (factor * factor * factor * inner)
        dres_ref[...] = d_residual
        dba[...] = (RESID_MULT * d_residual).astype(BF16)
        d_gain = jnp.sum(grad * residual * factor, axis=0, keepdims=True)
        width = tot_ref.shape[1]
        tot_ref[...] = jnp.zeros_like(tot_ref)
        for r in range(pl.cdiv(D, width)):
            last = min(width, D - r * width)
            tot_ref[r : r + 1, :last] = d_gain[:, r * width : r * width + last]
        lane = lax.broadcasted_iota(jnp.int32, (1, 128), 1)
        row = jnp.zeros((1, 128), F32)
        for i, part in enumerate((layer_out, attn, mlp)):
            square = jnp.sum(jnp.sum(part * part, axis=0, keepdims=True), axis=1, keepdims=True)
            row = jnp.where(lane == i, square, row)
        tot_ref[7:8, :128] = row

    datt_ref[...] = dot_nt(dba[...], w_ref[...]).astype(BF16)
    grad = matmul(att_ref[...].T, dba[...])
    if len(grad_refs) == 1:
        grad_refs[0][...] = grad.astype(BF16)
        return
    mine_ref, away_ref, acc = grad_refs
    acc[...] = grad
    core = lax.axis_index("core")
    width = mine_ref.shape[2]
    for i in range(mine_ref.shape[1]):
        for ref, c in ((mine_ref, core), (away_ref, 1 - core)):
            at = pl.multiple_of((2 * i + c) * width, width)
            ref[0, i] = acc[pl.ds(at, width)].astype(BF16)


def turn(residual, d_normed, cotangent, gains, branch, own, came, attended, weights, width):
    rows = residual.shape[0]
    cols = 4 * width if came else 256
    scratch = [pltpu.VMEM((rows, D), BF16)]
    grads = (jax.ShapeDtypeStruct((D, D), BF16),)
    grad_specs = (pl.BlockSpec((cols, D), lambda j: (j, 0)),)
    if came:
        half = (D // (8 * width), 4, width, D)
        grads = (jax.ShapeDtypeStruct(half, BF16),) * 2
        grad_specs = (pl.BlockSpec((1, 2, width, D), lambda j: (j // 2, j % 2, 0, 0)),) * 2
        scratch = [pltpu.VMEM((cols, D), F32)] + scratch
    flat = jax.ShapeDtypeStruct((rows, D), F32)

    def held(shape):
        return pl.BlockSpec(shape, lambda j: (0,) * len(shape), pipeline_mode=pl.Buffered(1))

    return pl.pallas_call(
        functools.partial(turn_kernel, len(came)),
        out_shape=(
            jax.ShapeDtypeStruct((rows, D), BF16),
            flat,
            jax.ShapeDtypeStruct((8, 3 * D // 16), F32),
            jax.ShapeDtypeStruct((rows, D), BF16),
        )
        + grads,
        grid=(D // cols,),
        in_specs=[held((rows, D))] * 3
        + [held((8, D))]
        + [held((rows, D))] * (2 + len(came))
        + [
            pl.BlockSpec((rows, cols), lambda j: (0, j)),
            pl.BlockSpec((cols, D), lambda j: (j, 0)),
        ],
        out_specs=(
            held((rows, D)),
            held((rows, D)),
            held((8, 3 * D // 16)),
            pl.BlockSpec((rows, cols), lambda j: (0, j)),
        )
        + grad_specs,
        scratch_shapes=scratch,
        cost_estimate=BRIEF,
        compiler_params=params(1),
    )(residual, d_normed, cotangent, gains, branch, own, *came, attended, weights)


def norm_parts(values):
    factor = lax.rsqrt(jnp.mean(values * values, axis=-1, keepdims=True) + EPSILON)
    return factor


def norm_back(values, factor, gain, grad):
    scaled = gain * grad
    inner = jnp.mean(values * scaled, axis=-1, keepdims=True)
    return factor * scaled - values * (factor * factor * factor * inner), jnp.sum(
        grad * values * factor, axis=0
    )


def on_device(
    tokens,
    block_group,
    block_slot,
    attn_gain,
    w_query,
    w_key,
    w_value,
    w_out,
    mlp_gain,
    w_gate,
    w_up,
    w_down,
    cotangent,
):
    grps = lax.axis_size("grp")
    devs = lax.axis_size(PLANE)
    chips = devs // 2
    rows = tokens.shape[0]
    w_rows = w_query.shape[0]
    q_heads = HEADS // devs
    kv_heads = 1
    assert devs % KV_HEADS == 0
    kv_copies = max(1, devs // KV_HEADS)
    q_cols, kv_cols = q_heads * HEAD_DIM, kv_heads * HEAD_DIM
    row_blocks = rows // BLOCK * devs
    row_groups = row_blocks // GROUP_BLOCKS

    row_first = lax.axis_index("grp") * row_blocks
    keys = lax.dynamic_slice_in_dim(block_group, row_first, row_blocks) * GROUP_BLOCKS
    keys = keys + lax.dynamic_slice_in_dim(block_slot, row_first, row_blocks)
    rank = jnp.sum((keys[None, :] < keys[:, None]).astype(jnp.int32), axis=1)
    ids = jnp.arange(row_blocks, dtype=jnp.int32)
    order = jnp.sum(jnp.where(rank[None, :] == ids[:, None], ids[None, :], 0), axis=1)

    def kv_split(w):
        w = w.reshape(w_rows, devs // kv_copies, kv_cols)
        return jnp.repeat(w, kv_copies, axis=1) if kv_copies > 1 else w

    packed = jnp.concatenate(
        [w_query.reshape(w_rows, devs, q_cols), kv_split(w_key), kv_split(w_value)], axis=2
    )
    packed = jnp.swapaxes(packed, 0, 1)
    used = q_cols + 2 * kv_cols
    tile = jnp.pad(jnp.stack([attn_gain, mlp_gain]), ((0, 14), (0, 128 - w_rows)))
    out_full = gather(w_out[None], "grp")
    upstream = cotangent.astype(F32)
    d_branch_mlp = (RESID_MULT * upstream).astype(BF16)
    all_tokens, d_branch_mlp, w_qkv, tiles = entry(
        tokens, d_branch_mlp, packed, tile, grps, chips, 2
    )
    w_qkv, tiles = w_qkv.reshape(D, used), tiles.reshape(-1, 16, 128)
    normed_one, qkv, gains = project(all_tokens.reshape(devs * rows, D), w_qkv, tiles)
    gain_one, gain_two = gains[0], gains[1]
    d_branch_mlp = d_branch_mlp.reshape(devs * rows, D)
    attended = attend(qkv, order, q_heads)
    attended = plane_exchange(
        attended, (rows, D), by_rows(rows), by_cols(q_cols), chips, 3
    )

    out_full = plane_gather(out_full, chips, 4, inner=True).reshape(D, D)
    layer_in = tokens.astype(F32)
    branch_attn = matmul(attended, out_full)
    residual = layer_in + RESID_MULT * branch_attn
    factor_two = norm_parts(residual)
    normed_two = (residual * factor_two * gain_two).astype(BF16)
    normed_two = plane_gather(normed_two, chips, 1).reshape(devs * rows, D)
    wide_w = gather(jnp.stack([w_gate, w_up])[None], "grp")
    down_w = gather(w_down[None], "grp")
    hidden, hidden_t, silu, slope, normed_t = widen(normed_two, wide_w)
    part_down = down_part(hidden_t, d_branch_mlp)
    part_down, hidden, silu = lax.optimization_barrier((part_down, hidden, silu))
    grad_down = scatter(part_down, "grp")
    if chips == 4:
        branch_mlp, *shares = twin_reduce(mix_rows, (hidden, down_w), rows, 11)
        shares, silu = lax.optimization_barrier((shares, silu))
        shares = swap_others(shares)
    d_gate, d_up = narrow_back(silu, slope, d_branch_mlp, down_w)
    if chips == 4:
        part_wide = widen_part(normed_t, d_gate, d_up)
        part_wide, shares, d_gate, d_up = lax.optimization_barrier(
            (part_wide, shares, d_gate, d_up)
        )
        grad_wide = scatter(part_wide, "grp")
        d_normed_two = square_reduce(widen_back_rows, (d_gate, d_up, wide_w), rows, 10)
    else:
        part_wide = widen_part(normed_t, d_gate, d_up)
        part_wide, d_gate, d_up = lax.optimization_barrier((part_wide, d_gate, d_up))
        grad_wide = scatter(part_wide, "grp")
        d_normed_two = widen_back(d_gate, d_up, wide_w)
        d_normed_two = plane_reduce(d_normed_two.reshape(devs, rows, D), chips, 5)
        branch_mlp = mix(hidden, down_w)
        branch_mlp = plane_reduce(branch_mlp.reshape(devs, rows, D), chips, 5)

    layer_out, d_residual, totals, d_attended, grad_out, *away = turn(
        residual,
        d_normed_two,
        cotangent,
        gains,
        branch_attn,
        branch_mlp,
        shares if chips == 4 else (),
        attended,
        out_full,
        w_rows,
    )
    if chips == 4:
        drift_out = Drift(grad_out, *away, 1)
    d_attended, totals = exchange_total(
        d_attended, totals, (devs * rows, q_cols), rows, q_cols, grps, chips, 7
    )
    if chips == 4:
        sent_out, d_attended = lax.optimization_barrier((drift_out.parts(), d_attended))
        sent_out = swap_others((sent_out[2], sent_out[0], sent_out[1]))
    d_attended, grad_down = lax.optimization_barrier((d_attended, grad_down))
    d_qkv = attend_back(qkv, d_attended, order, q_heads)
    if chips == 4:
        sent_out, d_qkv = lax.optimization_barrier((sent_out, d_qkv))
    sent = over_rows(normed_one, d_qkv).astype(BF16)
    sent, d_qkv, grad_wide = lax.optimization_barrier((sent, d_qkv, grad_wide))
    sent = scatter(sent, "grp")
    d_normed_one = over_cols(d_qkv, w_qkv).astype(BF16).reshape(devs, rows, D)
    if chips == 4:
        sent_out, d_normed_one = lax.optimization_barrier((sent_out, d_normed_one))
        grad_out = drift_out.finish(sent_out).astype(BF16)
    else:
        grad_out = plane_reduce(
            grad_out.reshape(grps, devs, w_rows, D), chips, 6, dtype=BF16, inner=True
        )
    grad_out, d_normed_one = lax.optimization_barrier((grad_out, d_normed_one))
    grad_out = scatter(grad_out, "grp")
    d_normed_one = plane_reduce(d_normed_one, chips, 5)
    d_normed_one, sent = lax.optimization_barrier((d_normed_one, sent))
    d_input_norm, _ = norm_back(layer_in, norm_parts(layer_in), gain_one, d_normed_one)
    tokens_grad = (d_residual + d_input_norm).astype(BF16)
    sent = sent.reshape(devs, w_rows, q_cols + 2 * kv_cols)
    sent = plane_exchange(sent, sent.shape, by_slot, by_slot, chips, 9)
    sent, grad_out = lax.optimization_barrier((sent, grad_out))
    sent, grad_out = sent.astype(F32), grad_out.reshape(w_rows, D).astype(F32)

    def kv_join(g):
        g = g.reshape(devs // kv_copies, kv_copies, w_rows, kv_cols)
        g = jnp.sum(g, axis=1) if kv_copies > 1 else g[:, 0]
        return jnp.swapaxes(g, 0, 1).reshape(w_rows, KV_HEADS * HEAD_DIM)

    grad_query = jnp.swapaxes(sent[:, :, :q_cols], 0, 1).reshape(w_rows, D)
    grad_key = kv_join(sent[:, :, q_cols : q_cols + kv_cols])
    grad_value = kv_join(sent[:, :, q_cols + kv_cols : q_cols + 2 * kv_cols])

    gain_one_grad = sum(
        jnp.sum(weight.astype(F32) * grad, axis=1)
        for weight, grad in ((w_query, grad_query), (w_key, grad_key), (w_value, grad_value))
    ) / attn_gain.astype(F32)
    rms_stats = jnp.sqrt(totals[7, :3] / (rows * grps * devs * D))
    gain_first = (lax.axis_index("grp") * devs + lax.axis_index(PLANE)) * w_rows
    gain_two_grad = lax.dynamic_slice(totals.reshape(-1), (gain_first,), (w_rows,))
    return (
        layer_out,
        tokens_grad,
        gain_one_grad,
        grad_query,
        grad_key,
        grad_value,
        grad_out,
        gain_two_grad,
        grad_wide[0, 0].astype(F32),
        grad_wide[0, 1].astype(F32),
        grad_down[0].astype(F32),
        rms_stats,
    )


def solution(mesh):
    shape = (mesh.shape["grp"], mesh.shape["blk"] // 2, 2)
    mesh = Mesh(mesh.devices.reshape(shape), EVERY)
    row, col, vec = P(EVERY, None), P(None, EVERY), P(EVERY)
    return jax.shard_map(
        on_device,
        mesh=mesh,
        in_specs=(row, P(), P(), vec, row, row, row, row, vec, col, col, row, row),
        out_specs=(row, row, vec, row, row, row, row, vec, col, col, row, P()),
        check_vma=False,
    )
```

```python
import functools

import jax
import jax.numpy as jnp
from jax import lax
from jax.experimental import pallas as pl
from jax.experimental.pallas import tpu as pltpu
from jax.sharding import Mesh
from jax.sharding import PartitionSpec as P

D = 2048
HEADS = 32
KV_HEADS = 8
HEAD_DIM = 64
BLOCK = 128
PROMPT_BLOCKS = 8
GROUP_BLOCKS = 16
PER_GROUP = HEADS // KV_HEADS

ATTN_MULT = 0.015625
RESID_MULT = 0.22
EPSILON = 1e-05
MASKED = -1e30

PLANE = ("chip", "core")
EVERY = ("grp", "chip", "core")
BF16 = jnp.bfloat16
F32 = jnp.float32


MESH = pl.DeviceIdType.MESH
BRIEF = pl.CostEstimate(flops=1000, bytes_accessed=1000, transcendentals=0)
ANY = pl.BlockSpec(memory_space=pl.ANY)
VMEM = pl.BlockSpec(memory_space=pltpu.VMEM)


def place():
    return lax.axis_index("chip"), lax.axis_index("core")


def flip(chip, step, chips):
    return jnp.bitwise_xor(chip, step) if chips == 4 else lax.rem(chip + step, chips)


def unflip(chip, step, chips):
    return jnp.bitwise_xor(chip, step) if chips == 4 else lax.rem(chip + chips - step, chips)


def greet(peers):
    barrier = pltpu.get_barrier_semaphore()
    for chip, core in peers:
        pl.semaphore_signal(
            barrier, inc=1, device_id={"chip": chip, "core": core}, device_id_type=MESH
        )
    pl.semaphore_wait(barrier, len(peers))


def remote(src, dst, send, recv, chip, core):
    return pltpu.make_async_remote_copy(
        src_ref=src,
        dst_ref=dst,
        send_sem=send,
        recv_sem=recv,
        device_id={"chip": chip, "core": core},
        device_id_type=MESH,
    )


class Gather:
    def __init__(self, chips, inner, x_ref, o_ref, send, recv, local):
        self.chips, self.inner, self.x, self.o = chips, inner, x_ref, o_ref
        self.send, self.recv, self.local = send, recv, local
        self.chip, self.core = place()
        self.half = x_ref.shape[0] // 2
        self.started = []

    def greet(self):
        steps = (1, 2) if self.chips == 4 else range(1, self.chips)
        peers = [(flip(self.chip, s, self.chips), self.core) for s in steps]
        greet(peers + [(self.chip, 1 - self.core)])

    def piece(self, slot, h):
        at = pl.ds(h * self.half, self.half)
        return self.o.at[at, slot] if self.inner else self.o.at[slot, at]

    def own(self, h):
        return self.x.at[pl.ds(h * self.half, self.half)]

    def slot(self, chip, core):
        return chip * 2 + core

    def push(self, src, slot, h, chip, core):
        i = len(self.started)
        copy = remote(src, self.piece(slot, h), self.send.at[i], self.recv.at[slot, h], chip, core)
        copy.start()
        self.started.append(copy)

    def wait_for(self, slot, h):
        remote(
            self.own(h), self.piece(slot, h), self.send.at[0], self.recv.at[slot, h],
            self.chip, 1 - self.core,
        ).wait_recv()

    def start(self):
        me = self.slot(self.chip, self.core)
        if self.chips == 4:
            for h, s in ((0, 1), (1, 2), (1, 1), (0, 2)):
                self.push(self.own(h), me, h, flip(self.chip, s, 4), self.core)
        else:
            for s in range(1, self.chips):
                for h in range(2):
                    self.push(self.own(h), me, h, flip(self.chip, s, self.chips), self.core)
        for h in range(2):
            self.push(self.own(h), me, h, self.chip, 1 - self.core)
        whole = self.o.at[:, me] if self.inner else self.o.at[me]
        self.mine = pltpu.make_async_copy(self.x, whole, self.local)
        self.mine.start()

    def relay(self, first=0, last=None):
        if self.chips == 4:
            plan = ((1, 0, 2), (2, 1, 1), (1, 1, 0), (2, 0, 0), (3, 0, 0), (3, 1, 0))
        else:
            plan = tuple((s, h, 0) for s in range(1, self.chips) for h in range(2))
        for s, h, onward in plan[first:last]:
            slot = self.slot(unflip(self.chip, s, self.chips), self.core)
            self.wait_for(slot, h)
            if onward:
                self.push(self.piece(slot, h), slot, h, flip(self.chip, onward, 4), self.core)
            self.push(self.piece(slot, h), slot, h, self.chip, 1 - self.core)

    def finish(self):
        for s in range(self.chips):
            slot = self.slot(unflip(self.chip, s, self.chips), 1 - self.core)
            for h in range(2):
                self.wait_for(slot, h)
        for copy in self.started:
            copy.wait_send()
        self.mine.wait()


def gather_sems(chips):
    return [
        pltpu.SemaphoreType.DMA((4 * chips + 4,)),
        pltpu.SemaphoreType.DMA((2 * chips, 2)),
        pltpu.SemaphoreType.DMA,
    ]


def gather_kernel(chips, inner, x_ref, o_ref, *sems):
    run = Gather(chips, inner, x_ref, o_ref, *sems)
    run.greet()
    run.start()
    run.relay()
    run.finish()


def plane_gather(x, chips, call_id, inner=False):
    devs = 2 * chips
    shape = (x.shape[0], devs) + x.shape[1:] if inner else (devs,) + x.shape
    return pl.pallas_call(
        functools.partial(gather_kernel, chips, inner),
        out_shape=jax.ShapeDtypeStruct(shape, x.dtype),
        in_specs=[ANY],
        out_specs=ANY,
        scratch_shapes=gather_sems(chips),
        cost_estimate=BRIEF,
        compiler_params=pltpu.CompilerParams(collective_id=call_id, has_side_effects=True),
    )(x)


def reduce_kernel(chips, inner, p_ref, o_ref, total, mine, twin, moved, corner, landed, lsem, tsend, trecv, msend, mrecv, csend, crecv):
    chip, core = place()
    sib = 1 - core
    half = (p_ref.shape[0] if inner else p_ref.shape[1]) // 2
    block = (lambda slot: p_ref.at[:, slot]) if inner else (lambda slot: p_ref.at[slot])
    steps = (1, 2) if chips == 4 else tuple(range(1, chips))
    peers = [(flip(chip, s, chips), core) for s in steps]
    greet(peers + [(chip, sib)])
    order = (3, 1, 2, 0) if chips == 4 else tuple(range(1, chips)) + (0,)
    loads, twins = {}, {}
    for s in order:
        to = flip(chip, s, chips) * 2
        twins[s] = remote(block(to + sib), twin.at[s], tsend.at[s], trecv.at[s], chip, sib)
        twins[s].start()
        loads[s] = pltpu.make_async_copy(block(to + core), mine.at[s], lsem.at[s])
        loads[s].start()

    def part(s, h):
        at = pl.ds(h * half, half)
        return mine[s, at].astype(F32) + twin[s, at].astype(F32)

    def ready(s):
        loads[s].wait()
        twins[s].wait_recv()

    sent = []
    if chips == 4:
        corners = []
        ready(3)
        for h, s in ((0, 1), (1, 2)):
            moved[3, pl.ds(h * half, half)] = part(3, h).astype(BF16)
            copy = remote(moved.at[3, pl.ds(h * half, half)], corner.at[h], csend.at[h], crecv.at[h], flip(chip, s, 4), core)
            copy.start()
            corners.append(copy)

        def send(s, h):
            at = pl.ds(h * half, half)
            copy = remote(moved.at[s, at], landed.at[s - 1, at], msend.at[s - 1, h], mrecv.at[s - 1, h], flip(chip, s, 4), core)
            copy.start()
            sent.append(copy)

        for s, h in ((1, 0), (2, 1)):
            ready(s)
            moved[s, pl.ds(h * half, half)] = part(s, h).astype(BF16)
            send(s, h)
        for s, h in ((2, 0), (1, 1)):
            corners[h].wait_recv()
            moved[s, pl.ds(h * half, half)] = (part(s, h) + corner[h].astype(F32)).astype(BF16)
            send(s, h)
        for copy in corners:
            copy.wait_send()
    else:
        for s in steps:
            ready(s)
            for h in range(2):
                at = pl.ds(h * half, half)
                moved[s, at] = part(s, h).astype(BF16)
                copy = remote(moved.at[s, at], landed.at[s - 1, at], msend.at[s - 1, h], mrecv.at[s - 1, h], flip(chip, s, chips), core)
                copy.start()
                sent.append(copy)
    ready(0)
    for h in range(2):
        total[pl.ds(h * half, half)] = part(0, h)
    for copy in sent:
        copy.wait()
    for s in steps[:-1]:
        total[...] += landed[s - 1].astype(F32)
    o_ref[...] = (total[...] + landed[steps[-1] - 1].astype(F32)).astype(o_ref.dtype)
    for s in order:
        twins[s].wait_send()


def plane_reduce(p, chips, call_id, dtype=F32, inner=False):
    block = (p.shape[0],) + p.shape[2:] if inner else p.shape[1:]
    steps = 2 if chips == 4 else chips - 1
    return pl.pallas_call(
        functools.partial(reduce_kernel, chips, inner),
        out_shape=jax.ShapeDtypeStruct(block, dtype),
        in_specs=[ANY],
        out_specs=VMEM,
        scratch_shapes=[
            pltpu.VMEM(block, F32),
            pltpu.VMEM((chips,) + block, BF16),
            pltpu.VMEM((chips,) + block, BF16),
            pltpu.VMEM((chips,) + block, BF16),
            pltpu.VMEM((2, block[0] // 2) + block[1:], BF16),
            pltpu.VMEM((steps,) + block, BF16),
            pltpu.SemaphoreType.DMA((chips,)),
            pltpu.SemaphoreType.DMA((chips,)),
            pltpu.SemaphoreType.DMA((chips,)),
            pltpu.SemaphoreType.DMA((steps, 2)),
            pltpu.SemaphoreType.DMA((steps, 2)),
            pltpu.SemaphoreType.DMA((2,)),
            pltpu.SemaphoreType.DMA((2,)),
        ],
        cost_estimate=BRIEF,
        compiler_params=pltpu.CompilerParams(
            collective_id=call_id, has_side_effects=True, vmem_limit_bytes=56 << 20
        ),
    )(p)


def swap_chips(values, step):
    return lax.ppermute(values, "chip", [(c, c ^ step) for c in range(4)])


class Drift:
    def __init__(self, mine, away, axis):
        self.axis = axis
        self.chip, self.core = place()
        self.mine = mine
        self.twin = lax.ppermute(away, "core", [(0, 1), (1, 0)])

    def part(self, step):
        at = jnp.bitwise_xor(self.chip, step)
        mine = lax.dynamic_index_in_dim(self.mine, at, self.axis, keepdims=False)
        twin = lax.dynamic_index_in_dim(self.twin, at, self.axis, keepdims=False)
        return mine.astype(F32) + twin.astype(F32)

    def parts(self):
        return tuple(self.part(step).astype(BF16) for step in (1, 2, 3))

    def finish(self, came):
        total = self.part(0)
        for part in came:
            total = total + part.astype(F32)
        return total


def exchange_kernel(chips, cut, paste, x_ref, o_ref, send, recv, local):
    chip, core = place()
    me = chip * 2 + core
    peers = [(flip(chip, s, chips), c) for s in range(1, chips) for c in (core, 1 - core)]
    peers = peers + [(chip, 1 - core)]
    greet(peers)
    far = [p for p in ([3, 1, 2] if chips == 4 else range(1, chips))]
    order = [(flip(chip, s, chips), c) for s in far for c in (core, 1 - core)] + [(chip, 1 - core)]
    copies = []
    for i, (to, c) in enumerate(order):
        copy = remote(cut(x_ref, to * 2 + c), paste(o_ref, me), send.at[i], recv.at[me], to, c)
        copy.start()
        copies.append(copy)
    mine = pltpu.make_async_copy(cut(x_ref, me), paste(o_ref, me), local)
    mine.start()
    for s in far:
        for c in (core, 1 - core):
            slot = unflip(chip, s, chips) * 2 + c
            remote(cut(x_ref, me), paste(o_ref, slot), send.at[0], recv.at[slot], chip, 1 - core).wait_recv()
    slot = chip * 2 + 1 - core
    remote(cut(x_ref, me), paste(o_ref, slot), send.at[0], recv.at[slot], chip, 1 - core).wait_recv()
    for copy in copies:
        copy.wait_send()
    mine.wait()


def plane_exchange(x, shape, cut, paste, chips, call_id):
    return pl.pallas_call(
        functools.partial(exchange_kernel, chips, cut, paste),
        out_shape=jax.ShapeDtypeStruct(shape, x.dtype),
        in_specs=[ANY],
        out_specs=ANY,
        scratch_shapes=[
            pltpu.SemaphoreType.DMA((2 * chips,)),
            pltpu.SemaphoreType.DMA((2 * chips,)),
            pltpu.SemaphoreType.DMA,
        ],
        cost_estimate=BRIEF,
        compiler_params=pltpu.CompilerParams(collective_id=call_id, has_side_effects=True),
    )(x)


def by_slot(ref, dev):
    return ref.at[dev]


def by_rows(rows):
    return lambda ref, dev: ref.at[pl.ds(pl.multiple_of(dev * rows, rows), rows)]


def by_cols(cols):
    return lambda ref, dev: ref.at[:, pl.ds(pl.multiple_of(dev * cols, cols), cols)]


def matmul(left, right):
    return jnp.dot(left, right, preferred_element_type=F32)


def over_rows(left, right):
    return lax.dot_general(left, right, (((0,), (0,)), ((), ())), preferred_element_type=F32)


def over_cols(left, right):
    return lax.dot_general(left, right, (((1,), (1,)), ((), ())), preferred_element_type=F32)


def gather(values, axes, axis=0):
    return lax.all_gather(values, axes, axis=axis, tiled=True)


def scatter(values, axes, axis=0):
    return lax.psum_scatter(values, axes, scatter_dimension=axis, tiled=True)


def dot_nt(left, right):
    return lax.dot_general(left, right, (((1,), (1,)), ((), ())), preferred_element_type=F32)


def head_stack(values, heads):
    col_head = lax.broadcasted_iota(jnp.int32, values.shape, 1) // HEAD_DIM
    return jnp.concatenate(
        [jnp.where(col_head == h, values, jnp.zeros_like(values)) for h in range(heads)], axis=0
    )


def head_pick(stacked, heads):
    rows = stacked.shape[0] // heads
    col_head = lax.broadcasted_iota(jnp.int32, (rows, stacked.shape[1]), 1) // HEAD_DIM
    total = jnp.zeros((rows, stacked.shape[1]), F32)
    for h in range(heads):
        total = jnp.where(col_head == h, stacked[h * rows : (h + 1) * rows], total)
    return total


def head_fold(values, heads):
    total = values[:, :HEAD_DIM]
    for h in range(1, heads):
        total = total + values[:, h * HEAD_DIM : (h + 1) * HEAD_DIM]
    return total


def repeat_heads(values, heads):
    return jnp.concatenate([values] * heads, axis=1)


def own_rows(order_ref, slot):
    return pl.ds(pl.multiple_of(order_ref[slot] * BLOCK, BLOCK), BLOCK)


def load_prompt(heads, order_ref, qkv_ref, k_ref, v_ref, first):
    q_cols = heads * HEAD_DIM
    for s in range(PROMPT_BLOCKS):
        pair = qkv_ref[own_rows(order_ref, first + s), q_cols:]
        at = pl.ds(s * BLOCK, BLOCK)
        k_ref[at] = repeat_heads(pair[:, :HEAD_DIM], heads)
        v_ref[at] = repeat_heads(pair[:, HEAD_DIM:], heads)


def by_keys(slot, body):
    prompt = PROMPT_BLOCKS * BLOCK
    quarter = prompt // 4
    seen = jnp.minimum(slot, PROMPT_BLOCKS) * BLOCK
    for n in range(1, 5):
        low = (n - 1) * quarter if n > 1 else -1

        @pl.when((seen > low) & (seen <= n * quarter))
        def _(n=n):
            body(n * quarter)


def soft_parts(heads, slot, q_stack, k_far, k_own):
    far = dot_nt(k_far, q_stack)
    own = dot_nt(k_own, q_stack)
    limit = jnp.minimum(slot, PROMPT_BLOCKS) * BLOCK
    far = jnp.where(lax.broadcasted_iota(jnp.int32, far.shape, 0) < limit, far, MASKED)
    key = lax.broadcasted_iota(jnp.int32, own.shape, 0)
    row = lax.broadcasted_iota(jnp.int32, own.shape, 1) % BLOCK
    own = jnp.where(key <= row, own, MASKED)
    peak = jnp.maximum(jnp.max(far, axis=0, keepdims=True), jnp.max(own, axis=0, keepdims=True))
    far, own = jnp.exp(far - peak), jnp.exp(own - peak)
    scale = 1.0 / (jnp.sum(far, axis=0, keepdims=True) + jnp.sum(own, axis=0, keepdims=True))
    return far * scale, own * scale


def scaled_stack(q, heads):
    return head_stack((q.astype(F32) * ATTN_MULT).astype(BF16), heads)


def attend_kernel(heads, order_ref, qkv_ref, o_ref, k_ref, v_ref, vt_ref):
    first, slot = pl.program_id(0) * GROUP_BLOCKS, pl.program_id(1)
    q_cols = heads * HEAD_DIM

    @pl.when(slot == 0)
    def _():
        load_prompt(heads, order_ref, qkv_ref, k_ref, v_ref, first)
        vt_ref[...] = v_ref[...].astype(F32).T.astype(BF16)

    rows = own_rows(order_ref, first + slot)
    mine = qkv_ref[rows, :]
    k_own = repeat_heads(mine[:, q_cols : q_cols + HEAD_DIM], heads)
    v_own = repeat_heads(mine[:, q_cols + HEAD_DIM :], heads)
    q_stack = scaled_stack(mine[:, :q_cols], heads)

    def body(count):
        far, own = soft_parts(heads, slot, q_stack, k_ref[:count], k_own)
        mixed = matmul(vt_ref[:, :count], far.astype(BF16))
        mixed += matmul(v_own.astype(F32).T.astype(BF16), own.astype(BF16))
        o_ref[rows, :] = head_pick(mixed.T, heads).astype(BF16)

    by_keys(slot, body)


def attend_back_kernel(
    heads, order_ref, qkv_ref, d_ref, o_ref, k_ref, v_ref, kt_ref, dk_ref, dv_ref
):
    first, slot = pl.program_id(0) * GROUP_BLOCKS, pl.program_id(1)
    q_cols = heads * HEAD_DIM

    @pl.when(slot == 0)
    def _():
        load_prompt(heads, order_ref, qkv_ref, k_ref, v_ref, first)
        kt_ref[...] = k_ref[...].astype(F32).T.astype(BF16)
        dk_ref[...] = jnp.zeros_like(dk_ref)
        dv_ref[...] = jnp.zeros_like(dv_ref)

    rows = own_rows(order_ref, first + slot)
    mine = qkv_ref[rows, :]
    k_own = repeat_heads(mine[:, q_cols : q_cols + HEAD_DIM], heads)
    v_own = repeat_heads(mine[:, q_cols + HEAD_DIM :], heads)
    q_stack = scaled_stack(mine[:, :q_cols], heads)
    d_stack = head_stack(d_ref[rows, :], heads)

    def fold(d_k, d_v):
        return jnp.concatenate([head_fold(d_k, heads), head_fold(d_v, heads)], axis=1).astype(BF16)

    def body(count):
        far, own = soft_parts(heads, slot, q_stack, k_ref[:count], k_own)
        d_far, d_own = dot_nt(v_ref[:count], d_stack), dot_nt(v_own, d_stack)
        mean = jnp.sum(far * d_far, axis=0, keepdims=True)
        mean += jnp.sum(own * d_own, axis=0, keepdims=True)
        d_far = (far * (d_far - mean)).astype(BF16)
        d_own = (own * (d_own - mean)).astype(BF16)
        dv_ref[:count] += matmul(far.astype(BF16), d_stack)
        dk_ref[:count] += matmul(d_far, q_stack)
        dv_own = matmul(own.astype(BF16), d_stack)
        dk_own = matmul(d_own, q_stack)
        d_q = matmul(kt_ref[:, :count], d_far) + matmul(k_own.astype(F32).T.astype(BF16), d_own)
        o_ref[rows, :q_cols] = (head_pick(d_q.T, heads) * ATTN_MULT).astype(BF16)

        @pl.when(slot < PROMPT_BLOCKS)
        def _():
            at = pl.ds(pl.multiple_of(slot * BLOCK, BLOCK), BLOCK)
            dk_ref[at] += dk_own
            dv_ref[at] += dv_own

        @pl.when(slot >= PROMPT_BLOCKS)
        def _():
            o_ref[rows, q_cols:] = fold(dk_own, dv_own)

    by_keys(slot, body)

    @pl.when(slot == GROUP_BLOCKS - 1)
    def _():
        for s in range(PROMPT_BLOCKS):
            at = pl.ds(s * BLOCK, BLOCK)
            o_ref[own_rows(order_ref, first + s), q_cols:] = fold(dk_ref[at], dv_ref[at])


def whole(shape):
    return pl.BlockSpec(shape, lambda g, s, order: (0,) * len(shape))


def attend(qkv, order, heads):
    tokens, cols = qkv.shape
    prompt, q_cols = PROMPT_BLOCKS * BLOCK, heads * HEAD_DIM
    return pl.pallas_call(
        functools.partial(attend_kernel, heads),
        out_shape=jax.ShapeDtypeStruct((tokens, q_cols), BF16),
        grid_spec=pltpu.PrefetchScalarGridSpec(
            num_scalar_prefetch=1,
            grid=(tokens // (GROUP_BLOCKS * BLOCK), GROUP_BLOCKS),
            in_specs=[whole((tokens, cols))],
            out_specs=whole((tokens, q_cols)),
            scratch_shapes=[
                pltpu.VMEM((prompt, q_cols), BF16),
                pltpu.VMEM((prompt, q_cols), BF16),
                pltpu.VMEM((q_cols, prompt), BF16),
            ],
        ),
        cost_estimate=BRIEF,
        compiler_params=pltpu.CompilerParams(vmem_limit_bytes=40 << 20),
    )(order, qkv)


def attend_back(qkv, d_attended, order, heads):
    tokens, cols = qkv.shape
    prompt, q_cols = PROMPT_BLOCKS * BLOCK, heads * HEAD_DIM
    return pl.pallas_call(
        functools.partial(attend_back_kernel, heads),
        out_shape=jax.ShapeDtypeStruct((tokens, cols), BF16),
        grid_spec=pltpu.PrefetchScalarGridSpec(
            num_scalar_prefetch=1,
            grid=(tokens // (GROUP_BLOCKS * BLOCK), GROUP_BLOCKS),
            in_specs=[whole((tokens, cols)), whole((tokens, q_cols))],
            out_specs=whole((tokens, cols)),
            scratch_shapes=[
                pltpu.VMEM((prompt, q_cols), BF16),
                pltpu.VMEM((prompt, q_cols), BF16),
                pltpu.VMEM((q_cols, prompt), BF16),
                pltpu.VMEM((prompt, q_cols), F32),
                pltpu.VMEM((prompt, q_cols), F32),
            ],
        ),
        cost_estimate=BRIEF,
        compiler_params=pltpu.CompilerParams(vmem_limit_bytes=40 << 20),
    )(order, qkv, d_attended)


def exchange_total_kernel(
    grps, chips, cut, paste, x_ref, t_ref, o_ref, sum_ref,
    over_z, over_plane, send, recv, local, zsend, zrecv, psend, precv,
):
    grp = lax.axis_index("grp")
    chip, core = place()
    me = chip * 2 + core
    far = [lax.rem(grp + s, grps) for s in range(1, grps)]
    steps = (3, 1, 2) if chips == 4 else tuple(range(1, chips))
    near = [(flip(chip, s, chips), c) for s in steps for c in (core, 1 - core)]
    near = near + [(chip, 1 - core)]
    barrier = pltpu.get_barrier_semaphore()
    for g in far:
        pl.semaphore_signal(barrier, inc=1, device_id={"grp": g}, device_id_type=MESH)
    for to, c in near:
        pl.semaphore_signal(
            barrier, inc=1, device_id={"chip": to, "core": c}, device_id_type=MESH
        )
    pl.semaphore_wait(barrier, len(far) + len(near))

    def z_copy(slot, sem, to):
        return pltpu.make_async_remote_copy(
            src_ref=t_ref,
            dst_ref=over_z.at[slot],
            send_sem=sem,
            recv_sem=zrecv.at[slot],
            device_id={"grp": to},
            device_id_type=MESH,
        )

    copies = []
    for i, g in enumerate(far):
        copy = z_copy(grp, zsend.at[i], g)
        copy.start()
        copies.append(copy)
    for i, (to, c) in enumerate(near):
        copy = remote(cut(x_ref, to * 2 + c), paste(o_ref, me), send.at[i], recv.at[me], to, c)
        copy.start()
        copies.append(copy)
    mine = pltpu.make_async_copy(cut(x_ref, me), paste(o_ref, me), local)
    mine.start()
    over_z[grp] = t_ref[...]
    for g in far:
        z_copy(g, zsend.at[0], g).wait_recv()
    over_plane[me] = jnp.sum(over_z[...], axis=0)
    for i, (to, c) in enumerate(near):
        copy = remote(over_plane.at[me], over_plane.at[me], psend.at[i], precv.at[me], to, c)
        copy.start()
        copies.append(copy)
    for to, c in near:
        slot = to * 2 + c
        remote(cut(x_ref, me), paste(o_ref, slot), send.at[0], recv.at[slot], to, c).wait_recv()
        remote(over_plane.at[me], over_plane.at[slot], psend.at[0], precv.at[slot], to, c).wait_recv()
    for copy in copies:
        copy.wait_send()
    mine.wait()
    sum_ref[...] = jnp.sum(over_plane[...], axis=0)


def exchange_total(x, t, shape, rows, cols, grps, chips, call_id):
    devs = 2 * chips
    return pl.pallas_call(
        functools.partial(exchange_total_kernel, grps, chips, by_cols(cols), by_rows(rows)),
        out_shape=(
            jax.ShapeDtypeStruct(shape, x.dtype),
            jax.ShapeDtypeStruct(t.shape, F32),
        ),
        in_specs=[ANY, VMEM],
        out_specs=(ANY, VMEM),
        scratch_shapes=[
            pltpu.VMEM((grps,) + t.shape, F32),
            pltpu.VMEM((devs,) + t.shape, F32),
            pltpu.SemaphoreType.DMA((devs,)),
            pltpu.SemaphoreType.DMA((devs,)),
            pltpu.SemaphoreType.DMA,
            pltpu.SemaphoreType.DMA((grps,)),
            pltpu.SemaphoreType.DMA((grps,)),
            pltpu.SemaphoreType.DMA((devs,)),
            pltpu.SemaphoreType.DMA((devs,)),
        ],
        cost_estimate=BRIEF,
        compiler_params=pltpu.CompilerParams(collective_id=call_id, has_side_effects=True),
    )(x, t)


def params(axes, mib=56):
    return pltpu.CompilerParams(
        dimension_semantics=("arbitrary",) * axes, vmem_limit_bytes=mib << 20
    )


def tile_rows(count, limit):
    while count % limit:
        limit //= 2
    return limit


def widen_kernel(n_ref, w_ref, h_ref, ht_ref, s_ref, t_ref, nt_ref):
    values = n_ref[...]
    gate, up = matmul(values, w_ref[0, 0]), matmul(values, w_ref[0, 1])
    sig = 1.0 / (1.0 + jnp.exp(-gate))
    silu = gate * sig
    hidden = (silu * up).astype(BF16)
    h_ref[0] = hidden
    ht_ref[0] = hidden.T
    s_ref[0] = silu.astype(BF16)
    t_ref[0] = (up * (sig * (1.0 + gate * (1.0 - sig)))).astype(BF16)

    @pl.when(pl.program_id(1) == 0)
    def _():
        nt_ref[...] = values.T


def widen(normed, weights):
    tokens, depth = normed.shape
    shards, _, _, width = weights.shape
    rows = tile_rows(tokens, 1024)
    tall = jax.ShapeDtypeStruct((shards, tokens, width), BF16)
    tall_spec = pl.BlockSpec((1, rows, width), lambda r, s: (s, r, 0))
    return pl.pallas_call(
        widen_kernel,
        out_shape=(
            tall,
            jax.ShapeDtypeStruct((shards, width, tokens), BF16),
            tall,
            tall,
            jax.ShapeDtypeStruct((depth, tokens), BF16),
        ),
        grid=(tokens // rows, shards),
        in_specs=[
            pl.BlockSpec((rows, depth), lambda r, s: (r, 0)),
            pl.BlockSpec((1, 2, depth, width), lambda r, s: (s, 0, 0, 0)),
        ],
        out_specs=(
            tall_spec,
            pl.BlockSpec((1, width, rows), lambda r, s: (s, 0, r)),
            tall_spec,
            tall_spec,
            pl.BlockSpec((depth, rows), lambda r, s: (0, r)),
        ),
        cost_estimate=BRIEF,
        compiler_params=params(2),
    )(normed, weights)


def down_part_kernel(ht_ref, d_ref, o_ref):
    o_ref[0] = matmul(ht_ref[0], d_ref[...]).astype(BF16)


def down_part(hidden_t, upstream):
    shards, width, tokens = hidden_t.shape
    depth = upstream.shape[1]
    cols = tile_rows(depth, 1024)
    return pl.pallas_call(
        down_part_kernel,
        out_shape=jax.ShapeDtypeStruct((shards, width, depth), BF16),
        grid=(depth // cols, shards),
        in_specs=[
            pl.BlockSpec((1, width, tokens), lambda c, s: (s, 0, 0)),
            pl.BlockSpec((tokens, cols), lambda c, s: (0, c)),
        ],
        out_specs=pl.BlockSpec((1, width, cols), lambda c, s: (s, 0, c)),
        cost_estimate=BRIEF,
        compiler_params=params(2),
    )(hidden_t, upstream)


def mix_kernel(h_ref, w_ref, m_ref):
    mixed = None
    for i in range(w_ref.shape[0]):
        part = matmul(h_ref[i], w_ref[i])
        mixed = part if mixed is None else mixed + part
    m_ref[...] = mixed.astype(BF16)


def narrow_specs(hidden, weights):
    shards, tokens, width = hidden.shape
    depth = weights.shape[2]
    rows = tile_rows(tokens, 512)
    return (
        tokens // rows,
        pl.BlockSpec((shards, rows, width), lambda r: (0, r, 0)),
        pl.BlockSpec((rows, depth), lambda r: (r, 0)),
        pl.BlockSpec(weights.shape, lambda r: (0, 0, 0), pipeline_mode=pl.Buffered(1)),
    )


def mix(hidden, weights):
    steps, tall_spec, flat_spec, weight_spec = narrow_specs(hidden, weights)
    return pl.pallas_call(
        mix_kernel,
        out_shape=jax.ShapeDtypeStruct((hidden.shape[1], weights.shape[2]), BF16),
        grid=(steps,),
        in_specs=[tall_spec, weight_spec],
        out_specs=flat_spec,
        cost_estimate=BRIEF,
        compiler_params=params(1),
    )(hidden, weights)


def narrow_back_kernel(s_ref, t_ref, d_ref, w_ref, dg_ref, du_ref):
    upstream = d_ref[...]
    for i in range(w_ref.shape[0]):
        d_hidden = dot_nt(upstream, w_ref[i])
        dg_ref[i] = (d_hidden * t_ref[i].astype(F32)).astype(BF16)
        du_ref[i] = (d_hidden * s_ref[i].astype(F32)).astype(BF16)


def narrow_back(silu, slope, upstream, weights):
    steps, tall_spec, flat_spec, weight_spec = narrow_specs(silu, weights)
    tall = jax.ShapeDtypeStruct(silu.shape, BF16)
    return pl.pallas_call(
        narrow_back_kernel,
        out_shape=(tall, tall),
        grid=(steps,),
        in_specs=[tall_spec, tall_spec, flat_spec, weight_spec],
        out_specs=(tall_spec, tall_spec),
        cost_estimate=BRIEF,
        compiler_params=params(1),
    )(silu, slope, upstream, weights)


def widen_part_kernel(nt_ref, dg_ref, du_ref, o_ref):
    values = nt_ref[...]
    o_ref[0, 0] = matmul(values, dg_ref[0]).astype(BF16)
    o_ref[0, 1] = matmul(values, du_ref[0]).astype(BF16)


def widen_part(normed_t, d_gate, d_up):
    depth, tokens = normed_t.shape
    shards, _, width = d_gate.shape
    rows = tile_rows(depth, 1024)
    tall_spec = pl.BlockSpec((1, tokens, width), lambda r, s: (s, 0, 0))
    return pl.pallas_call(
        widen_part_kernel,
        out_shape=jax.ShapeDtypeStruct((shards, 2, depth, width), BF16),
        grid=(depth // rows, shards),
        in_specs=[pl.BlockSpec((rows, tokens), lambda r, s: (r, 0)), tall_spec, tall_spec],
        out_specs=pl.BlockSpec((1, 2, rows, width), lambda r, s: (s, 0, r, 0)),
        cost_estimate=BRIEF,
        compiler_params=params(2),
    )(normed_t, d_gate, d_up)


def widen_back_kernel(dg_ref, du_ref, w_ref, o_ref):
    total = None
    for i in range(w_ref.shape[0]):
        part = dot_nt(dg_ref[i], w_ref[i, 0]) + dot_nt(du_ref[i], w_ref[i, 1])
        total = part if total is None else total + part
    o_ref[...] = total.astype(BF16)


def widen_back(d_gate, d_up, weights):
    shards, tokens, width = d_gate.shape
    depth = weights.shape[2]
    rows = tile_rows(tokens, 512)
    tall_spec = pl.BlockSpec((shards, rows, width), lambda r: (0, r, 0))
    return pl.pallas_call(
        widen_back_kernel,
        out_shape=jax.ShapeDtypeStruct((tokens, depth), BF16),
        grid=(tokens // rows,),
        in_specs=[
            tall_spec,
            tall_spec,
            pl.BlockSpec(weights.shape, lambda r: (0, 0, 0, 0), pipeline_mode=pl.Buffered(1)),
        ],
        out_specs=pl.BlockSpec((rows, depth), lambda r: (r, 0)),
        cost_estimate=BRIEF,
        compiler_params=params(1),
    )(d_gate, d_up, weights)


def stage_step(stage):
    return jnp.where(stage == 0, 3, jnp.where(stage == 3, 0, stage))


class Square:
    def __init__(self, acc, mine, away, twin, moved, corner, landed, tsend, trecv, msend, mrecv, csend, crecv):
        self.acc, self.mine, self.away, self.twin = acc, mine, away, twin
        self.moved, self.corner, self.landed = moved, corner, landed
        self.tsend, self.trecv, self.msend, self.mrecv = tsend, trecv, msend, mrecv
        self.csend, self.crecv = csend, crecv
        self.chip, self.core = place()
        self.rows = mine.shape[1]
        self.half = self.rows // 2

    def greet(self):
        peers = [(flip(self.chip, s, 4), self.core) for s in (1, 2)]
        greet(peers + [(self.chip, 1 - self.core)])

    def twin_copy(self, stage):
        return remote(
            self.away.at[stage], self.twin.at[stage], self.tsend.at[stage], self.trecv.at[stage],
            self.chip, 1 - self.core,
        )

    def offer(self, stage):
        own, other = self.core * self.rows, (1 - self.core) * self.rows
        self.mine[stage] = self.acc[pl.ds(pl.multiple_of(own, self.rows), self.rows)].astype(BF16)
        self.away[stage] = self.acc[pl.ds(pl.multiple_of(other, self.rows), self.rows)].astype(BF16)
        self.twin_copy(stage).start()

    def at(self, h):
        return pl.ds(h * self.half, self.half)

    def both(self, stage, h):
        return self.mine[stage, self.at(h)].astype(F32) + self.twin[stage, self.at(h)].astype(F32)

    def corner_copy(self, h):
        return remote(
            self.moved.at[0, self.at(h)], self.corner.at[h], self.csend.at[h], self.crecv.at[h],
            flip(self.chip, h + 1, 4), self.core,
        )

    def copy(self, stage, h):
        return remote(
            self.moved.at[stage, self.at(h)], self.landed.at[stage - 1, self.at(h)],
            self.msend.at[stage - 1, h], self.mrecv.at[stage - 1, h],
            flip(self.chip, stage, 4), self.core,
        )

    def corners(self):
        self.twin_copy(0).wait_recv()
        for h in range(2):
            self.moved[0, self.at(h)] = self.both(0, h).astype(BF16)
            self.corner_copy(h).start()

    def plain(self, stage):
        self.twin_copy(stage).wait_recv()
        h = stage - 1
        self.moved[stage, self.at(h)] = self.both(stage, h).astype(BF16)
        self.copy(stage, h).start()

    def joined(self, stage):
        h = 2 - stage
        self.corner_copy(h).wait_recv()
        total = self.both(stage, h) + self.corner[h].astype(F32)
        self.moved[stage, self.at(h)] = total.astype(BF16)
        self.copy(stage, h).start()

    def finish(self, o_ref):
        self.twin_copy(3).wait_recv()
        for h in range(2):
            o_ref[self.at(h)] = self.both(3, h)
        for stage, h in ((1, 0), (2, 1), (2, 0), (1, 1)):
            self.copy(stage, h).wait_recv()
            o_ref[self.at(h)] += self.landed[stage - 1, self.at(h)].astype(F32)
        for stage in (1, 2):
            for h in range(2):
                self.copy(stage, h).wait_send()
        for h in range(2):
            self.corner_copy(h).wait_send()
        for stage in range(4):
            self.twin_copy(stage).wait_send()


def square_kernel(compute, count, *refs):
    operands, o_ref, scratch = refs[:count], refs[count], refs[count + 1 :]
    run = Square(*scratch)
    stage = pl.program_id(0)

    @pl.when(stage == 0)
    def _():
        run.greet()

    @pl.when(stage == 3)
    def _():
        run.plain(2)
        run.joined(2)
        run.joined(1)

    target = jnp.bitwise_xor(run.chip, stage_step(stage))
    width = 2 * run.rows
    run.acc[...] = compute(operands, pl.ds(pl.multiple_of(target * width, width), width))
    run.offer(stage)

    @pl.when(stage == 1)
    def _():
        run.corners()

    @pl.when(stage == 2)
    def _():
        run.plain(1)

    @pl.when(stage == 3)
    def _():
        run.finish(o_ref)


def square_reduce(compute, operands, rows, call_id):
    block = (rows, D)

    def held(shape):
        return pl.BlockSpec(shape, lambda s: (0,) * len(shape), pipeline_mode=pl.Buffered(1))

    return pl.pallas_call(
        functools.partial(square_kernel, compute, len(operands)),
        out_shape=jax.ShapeDtypeStruct(block, F32),
        grid=(4,),
        in_specs=[held(x.shape) for x in operands],
        out_specs=held(block),
        scratch_shapes=[
            pltpu.VMEM((2 * rows, D), F32),
            pltpu.VMEM((4,) + block, BF16),
            pltpu.VMEM((4,) + block, BF16),
            pltpu.VMEM((4,) + block, BF16),
            pltpu.VMEM((3,) + block, BF16),
            pltpu.VMEM((2, rows // 2, D), BF16),
            pltpu.VMEM((2,) + block, BF16),
            pltpu.SemaphoreType.DMA((4,)),
            pltpu.SemaphoreType.DMA((4,)),
            pltpu.SemaphoreType.DMA((2, 2)),
            pltpu.SemaphoreType.DMA((2, 2)),
            pltpu.SemaphoreType.DMA((2,)),
            pltpu.SemaphoreType.DMA((2,)),
        ],
        cost_estimate=BRIEF,
        compiler_params=pltpu.CompilerParams(
            collective_id=call_id, has_side_effects=True, vmem_limit_bytes=60 << 20
        ),
    )(*operands)


def widen_back_rows(refs, rows):
    dg_ref, du_ref, w_ref = refs
    total = None
    for i in range(w_ref.shape[0]):
        part = dot_nt(dg_ref[i, rows], w_ref[i, 0]) + dot_nt(du_ref[i, rows], w_ref[i, 1])
        total = part if total is None else total + part
    return total


def project_back_rows(refs, rows):
    d_ref, w_ref = refs
    return dot_nt(d_ref[rows], w_ref[...])


def mix_rows(refs, rows):
    h_ref, w_ref = refs
    total = None
    for i in range(w_ref.shape[0]):
        part = matmul(h_ref[i, rows], w_ref[i])
        total = part if total is None else total + part
    return total


def twin_kernel(compute, count, *refs):
    operands, (o_ref, corner_ref, x_ref, y_ref) = refs[:count], refs[count : count + 4]
    acc, mine, away, twin, tsend, trecv = refs[count + 4 :]
    chip, core = place()
    stage = pl.program_id(0)
    rows = o_ref.shape[0]

    def copy(s):
        return remote(away.at[s], twin.at[s], tsend.at[s], trecv.at[s], chip, 1 - core)

    def both(s):
        copy(s).wait_recv()
        return mine[s].astype(F32) + twin[s].astype(F32)

    @pl.when(stage == 0)
    def _():
        greet([(chip, 1 - core)])

    target = jnp.bitwise_xor(chip, stage_step(stage)) * 2 * rows
    acc[...] = compute(operands, pl.ds(pl.multiple_of(target, 2 * rows), 2 * rows))
    mine[stage] = acc[pl.ds(pl.multiple_of(core * rows, rows), rows)].astype(BF16)
    away[stage] = acc[pl.ds(pl.multiple_of((1 - core) * rows, rows), rows)].astype(BF16)
    copy(stage).start()

    for s, part_ref in enumerate((corner_ref, x_ref, y_ref)):

        @pl.when(stage == s + 1)
        def _(s=s, part_ref=part_ref):
            part_ref[...] = both(s).astype(BF16)

    @pl.when(stage == 3)
    def _():
        o_ref[...] = both(3)
        for s in range(4):
            copy(s).wait_send()


def twin_reduce(compute, operands, rows, call_id):
    block = (rows, D)

    def held(shape):
        return pl.BlockSpec(shape, lambda s: (0,) * len(shape), pipeline_mode=pl.Buffered(1))

    return pl.pallas_call(
        functools.partial(twin_kernel, compute, len(operands)),
        out_shape=(jax.ShapeDtypeStruct(block, F32),) + (jax.ShapeDtypeStruct(block, BF16),) * 3,
        grid=(4,),
        in_specs=[held(x.shape) for x in operands],
        out_specs=(held(block),) * 4,
        scratch_shapes=[
            pltpu.VMEM((2 * rows, D), F32),
            pltpu.VMEM((4,) + block, BF16),
            pltpu.VMEM((4,) + block, BF16),
            pltpu.VMEM((4,) + block, BF16),
            pltpu.SemaphoreType.DMA((4,)),
            pltpu.SemaphoreType.DMA((4,)),
        ],
        cost_estimate=BRIEF,
        compiler_params=pltpu.CompilerParams(
            collective_id=call_id, has_side_effects=True, vmem_limit_bytes=60 << 20
        ),
    )(*operands)


def swap_others(parts):
    return tuple(swap_chips(part, step) for step, part in zip((3, 1, 2), parts))


def join(own, came):
    for part in came:
        own = own + part.astype(F32)
    return own


def entry_kernel(
    grps, chips, tok_ref, cot_ref, pack_ref, tile_ref, all_tok, all_cot, all_pack, all_tile,
    tsend, trecv, tlocal, csend, crecv, clocal, psend, precv, plocal, zrecv, usend, dsend,
):
    grp = lax.axis_index("grp")
    chip, core = place()
    me = chip * 2 + core
    above, below = lax.rem(grp + 1, grps), lax.rem(grp + grps - 1, grps)
    near = [(flip(chip, s, chips), c) for s in range(1, chips) for c in (core, 1 - core)]
    near = near + [(chip, 1 - core)]
    barrier = pltpu.get_barrier_semaphore()
    for g in (above, below):
        pl.semaphore_signal(barrier, inc=1, device_id={"grp": g}, device_id_type=MESH)
    for to, c in near:
        pl.semaphore_signal(
            barrier, inc=1, device_id={"chip": to, "core": c}, device_id_type=MESH
        )
    pl.semaphore_wait(barrier, len(near) + 2)

    tok = Gather(chips, False, tok_ref, all_tok, tsend, trecv, tlocal)
    cot = Gather(chips, False, cot_ref, all_cot, csend, crecv, clocal)
    packs, mine = [], []
    for i, (to, c) in enumerate(near):
        copy = remote(
            pack_ref.at[to * 2 + c], all_pack.at[grp, me], psend.at[0, i], precv.at[0, me], to, c
        )
        copy.start()
        packs.append(copy)
        copy = remote(tile_ref, all_tile.at[grp, me], psend.at[1, i], precv.at[1, me], to, c)
        copy.start()
        packs.append(copy)
    for k, (src, dst) in enumerate(((pack_ref.at[me], all_pack), (tile_ref, all_tile))):
        mine.append(pltpu.make_async_copy(src, dst.at[grp, me], plocal.at[k]))
        mine[k].start()
    tok.start()
    for to, c in near:
        slot = to * 2 + c
        for k, (src, dst) in enumerate(((pack_ref.at[me], all_pack), (tile_ref, all_tile))):
            remote(src, dst.at[grp, slot], psend.at[k, 0], precv.at[k, slot], to, c).wait_recv()
    for copy in mine:
        copy.wait()

    def z_copies(block, sems, step, to):
        return [
            pltpu.make_async_remote_copy(
                src_ref=whole.at[block],
                dst_ref=whole.at[block],
                send_sem=sems.at[k, step],
                recv_sem=zrecv.at[k, block],
                device_id={"grp": to},
                device_id_type=MESH,
            )
            for k, whole in enumerate((all_pack, all_tile))
        ]

    has_above, has_below = grp + 1 < grps, grp > 0

    def send(step, block, up):
        @pl.when(has_above if up else has_below)
        def _():
            for copy in z_copies(block, usend if up else dsend, step, above if up else below):
                copy.start()

    def relay(step):
        low, high = grp - step, grp + step

        @pl.when(low >= 0)
        def _():
            for copy in z_copies(low, usend, 0, below):
                copy.wait_recv()
            send(step, low, True)

        @pl.when(high < grps)
        def _():
            for copy in z_copies(high, dsend, 0, above):
                copy.wait_recv()
            send(step, high, False)

    send(0, grp, True)
    send(0, grp, False)
    tok.relay(0, 4)
    relay(1)
    cot.start()
    tok.relay(4, None)
    for step in range(2, grps - 1):
        relay(step)
    cot.relay(0, 4)
    if grps > 2:
        relay(grps - 1)
    cot.relay(4, None)
    tok.finish()
    cot.finish()
    for copy in packs:
        copy.wait_send()
    for step in range(grps):
        for up in (True, False):
            held = grp - step >= 0 if up else grp + step < grps

            @pl.when(held & (has_above if up else has_below))
            def _(step=step, up=up):
                block = grp - step if up else grp + step
                sems, to = (usend, above) if up else (dsend, below)
                for copy in z_copies(block, sems, step, to):
                    copy.wait_send()


def entry(tokens, cotangent, packed, tile, grps, chips, call_id):
    devs = 2 * chips
    return pl.pallas_call(
        functools.partial(entry_kernel, grps, chips),
        out_shape=(
            jax.ShapeDtypeStruct((devs,) + tokens.shape, BF16),
            jax.ShapeDtypeStruct((devs,) + cotangent.shape, BF16),
            jax.ShapeDtypeStruct((grps,) + packed.shape, BF16),
            jax.ShapeDtypeStruct((grps, devs) + tile.shape, BF16),
        ),
        in_specs=[ANY] * 4,
        out_specs=(ANY,) * 4,
        scratch_shapes=gather_sems(chips)
        + gather_sems(chips)
        + [
            pltpu.SemaphoreType.DMA((2, devs)),
            pltpu.SemaphoreType.DMA((2, devs)),
            pltpu.SemaphoreType.DMA((2,)),
            pltpu.SemaphoreType.DMA((2, grps)),
            pltpu.SemaphoreType.DMA((2, grps)),
            pltpu.SemaphoreType.DMA((2, grps)),
        ],
        cost_estimate=BRIEF,
        compiler_params=pltpu.CompilerParams(collective_id=call_id, has_side_effects=True),
    )(tokens, cotangent, packed, tile)


def project_kernel(width, x_ref, w_ref, tile_ref, n_ref, qkv_ref, gain_ref):
    @pl.when(pl.program_id(0) == 0)
    def _():
        gain_ref[...] = jnp.zeros_like(gain_ref)
        for f in range(tile_ref.shape[0]):
            gain_ref[0:2, f * width : (f + 1) * width] = tile_ref[f, 0:2, :width].astype(F32)

    values = x_ref[...].astype(F32)
    factor = lax.rsqrt(jnp.mean(values * values, axis=-1, keepdims=True) + EPSILON)
    normed = (values * factor * gain_ref[0:1]).astype(BF16)
    n_ref[...] = normed
    qkv_ref[...] = matmul(normed, w_ref[...]).astype(BF16)


def project(tokens, weights, tiles):
    count, depth = tokens.shape
    used = weights.shape[1]
    rows = tile_rows(count, 256)
    return pl.pallas_call(
        functools.partial(project_kernel, depth // tiles.shape[0]),
        out_shape=(
            jax.ShapeDtypeStruct((count, depth), BF16),
            jax.ShapeDtypeStruct((count, used), BF16),
            jax.ShapeDtypeStruct((8, depth), F32),
        ),
        grid=(count // rows,),
        in_specs=[
            pl.BlockSpec((rows, depth), lambda r: (r, 0)),
            pl.BlockSpec(weights.shape, lambda r: (0, 0)),
            pl.BlockSpec(tiles.shape, lambda r: (0, 0, 0)),
        ],
        out_specs=(
            pl.BlockSpec((rows, depth), lambda r: (r, 0)),
            pl.BlockSpec((rows, used), lambda r: (r, 0)),
            pl.BlockSpec((8, depth), lambda r: (0, 0)),
        ),
        cost_estimate=BRIEF,
        compiler_params=params(1),
    )(tokens, weights, tiles)


def turn_kernel(
    count, res_ref, dn_ref, cot_ref, gain_ref, branch_ref, own_ref, *refs
):
    came, (att_ref, w_ref, lay_ref, dres_ref, tot_ref, datt_ref, *grad_refs, dba) = refs[:count], refs[count:]

    @pl.when(pl.program_id(0) == 0)
    def _():
        residual = res_ref[...]
        mlp = own_ref[...]
        for part_ref in came:
            mlp = mlp + part_ref[...].astype(F32)
        mlp = RESID_MULT * mlp
        layer_out = residual + mlp
        lay_ref[...] = layer_out.astype(BF16)
        attn = RESID_MULT * branch_ref[...]
        grad = dn_ref[...]
        scaled = gain_ref[1:2] * grad
        factor = lax.rsqrt(jnp.mean(residual * residual, axis=-1, keepdims=True) + EPSILON)
        inner = jnp.mean(residual * scaled, axis=-1, keepdims=True)
        d_residual = cot_ref[...].astype(F32) + factor * scaled
        d_residual = d_residual - residual * (factor * factor * factor * inner)
        dres_ref[...] = d_residual
        dba[...] = (RESID_MULT * d_residual).astype(BF16)
        d_gain = jnp.sum(grad * residual * factor, axis=0, keepdims=True)
        width = tot_ref.shape[1]
        tot_ref[...] = jnp.zeros_like(tot_ref)
        for r in range(pl.cdiv(D, width)):
            last = min(width, D - r * width)
            tot_ref[r : r + 1, :last] = d_gain[:, r * width : r * width + last]
        lane = lax.broadcasted_iota(jnp.int32, (1, 128), 1)
        row = jnp.zeros((1, 128), F32)
        for i, part in enumerate((layer_out, attn, mlp)):
            square = jnp.sum(jnp.sum(part * part, axis=0, keepdims=True), axis=1, keepdims=True)
            row = jnp.where(lane == i, square, row)
        tot_ref[7:8, :128] = row

    datt_ref[...] = dot_nt(dba[...], w_ref[...]).astype(BF16)
    grad = matmul(att_ref[...].T, dba[...])
    if len(grad_refs) == 1:
        grad_refs[0][...] = grad.astype(BF16)
        return
    mine_ref, away_ref = grad_refs
    first = lax.axis_index("core") == 0
    width = mine_ref.shape[2]
    for i in range(mine_ref.shape[1]):
        even = grad[2 * i * width : (2 * i + 1) * width]
        odd = grad[(2 * i + 1) * width : (2 * i + 2) * width]
        mine_ref[0, i] = jnp.where(first, even, odd).astype(BF16)
        away_ref[0, i] = jnp.where(first, odd, even).astype(BF16)


def turn(residual, d_normed, cotangent, gains, branch, own, came, attended, weights, width):
    rows = residual.shape[0]
    cols = 4 * width if came else 256
    scratch = [pltpu.VMEM((rows, D), BF16)]
    grads = (jax.ShapeDtypeStruct((D, D), BF16),)
    grad_specs = (pl.BlockSpec((cols, D), lambda j: (j, 0)),)
    if came:
        half = (D // (8 * width), 4, width, D)
        grads = (jax.ShapeDtypeStruct(half, BF16),) * 2
        grad_specs = (pl.BlockSpec((1, 2, width, D), lambda j: (j // 2, j % 2, 0, 0)),) * 2
    flat = jax.ShapeDtypeStruct((rows, D), F32)

    def held(shape):
        return pl.BlockSpec(shape, lambda j: (0,) * len(shape), pipeline_mode=pl.Buffered(1))

    return pl.pallas_call(
        functools.partial(turn_kernel, len(came)),
        out_shape=(
            jax.ShapeDtypeStruct((rows, D), BF16),
            flat,
            jax.ShapeDtypeStruct((8, 3 * D // 16), F32),
            jax.ShapeDtypeStruct((rows, D), BF16),
        )
        + grads,
        grid=(D // cols,),
        in_specs=[held((rows, D))] * 3
        + [held((8, D))]
        + [held((rows, D))] * (2 + len(came))
        + [
            pl.BlockSpec((rows, cols), lambda j: (0, j)),
            pl.BlockSpec((cols, D), lambda j: (j, 0)),
        ],
        out_specs=(
            held((rows, D)),
            held((rows, D)),
            held((8, 3 * D // 16)),
            pl.BlockSpec((rows, cols), lambda j: (0, j)),
        )
        + grad_specs,
        scratch_shapes=scratch,
        cost_estimate=BRIEF,
        compiler_params=params(1),
    )(residual, d_normed, cotangent, gains, branch, own, *came, attended, weights)


def split_kernel(copies, q_cols, kv_cols, x_ref, wq_ref, wk_ref, wv_ref, q_ref, k_ref, v_ref, sum_ref):
    total = jnp.zeros(sum_ref.shape, F32)
    for s in range(x_ref.shape[0]):
        block = x_ref[s].astype(F32)
        at = slice(s * q_cols, (s + 1) * q_cols)
        q_ref[:, at] = block[:, :q_cols]
        weight = wq_ref[:, at].astype(F32)
        total += jnp.sum(block[:, :q_cols] * weight, axis=1, keepdims=True)
    for h in range(x_ref.shape[0] // copies):
        at = slice(h * kv_cols, (h + 1) * kv_cols)
        pair = x_ref[h * copies, :, q_cols:].astype(F32)
        for c in range(1, copies):
            pair += x_ref[h * copies + c, :, q_cols:].astype(F32)
        for ref, w_ref, part in (
            (k_ref, wk_ref, pair[:, :kv_cols]),
            (v_ref, wv_ref, pair[:, kv_cols:]),
        ):
            ref[:, at] = part
            total += jnp.sum(part * w_ref[:, at].astype(F32), axis=1, keepdims=True)
    sum_ref[...] = total


def split(sent, w_query, w_key, w_value, copies, q_cols, kv_cols):
    rows = w_query.shape[0]
    return pl.pallas_call(
        functools.partial(split_kernel, copies, q_cols, kv_cols),
        out_shape=tuple(
            jax.ShapeDtypeStruct(shape, F32)
            for shape in (w_query.shape, w_key.shape, w_value.shape, (rows, 1))
        ),
        in_specs=[VMEM] * 4,
        out_specs=(VMEM,) * 4,
        cost_estimate=BRIEF,
    )(sent, w_query, w_key, w_value)


def norm_parts(values):
    factor = lax.rsqrt(jnp.mean(values * values, axis=-1, keepdims=True) + EPSILON)
    return factor


def norm_back(values, factor, gain, grad):
    scaled = gain * grad
    inner = jnp.mean(values * scaled, axis=-1, keepdims=True)
    return factor * scaled - values * (factor * factor * factor * inner), jnp.sum(
        grad * values * factor, axis=0
    )


def on_device(
    tokens,
    block_group,
    block_slot,
    attn_gain,
    w_query,
    w_key,
    w_value,
    w_out,
    mlp_gain,
    w_gate,
    w_up,
    w_down,
    cotangent,
):
    grps = lax.axis_size("grp")
    devs = lax.axis_size(PLANE)
    chips = devs // 2
    rows = tokens.shape[0]
    w_rows = w_query.shape[0]
    q_heads = HEADS // devs
    kv_heads = 1
    assert devs % KV_HEADS == 0
    kv_copies = max(1, devs // KV_HEADS)
    q_cols, kv_cols = q_heads * HEAD_DIM, kv_heads * HEAD_DIM
    row_blocks = rows // BLOCK * devs
    row_groups = row_blocks // GROUP_BLOCKS

    row_first = lax.axis_index("grp") * row_blocks
    keys = lax.dynamic_slice_in_dim(block_group, row_first, row_blocks) * GROUP_BLOCKS
    keys = keys + lax.dynamic_slice_in_dim(block_slot, row_first, row_blocks)
    rank = jnp.sum((keys[None, :] < keys[:, None]).astype(jnp.int32), axis=1)
    ids = jnp.arange(row_blocks, dtype=jnp.int32)
    order = jnp.sum(jnp.where(rank[None, :] == ids[:, None], ids[None, :], 0), axis=1)

    def kv_split(w):
        w = w.reshape(w_rows, devs // kv_copies, kv_cols)
        return jnp.repeat(w, kv_copies, axis=1) if kv_copies > 1 else w

    packed = jnp.concatenate(
        [w_query.reshape(w_rows, devs, q_cols), kv_split(w_key), kv_split(w_value)], axis=2
    )
    packed = jnp.swapaxes(packed, 0, 1)
    used = q_cols + 2 * kv_cols
    tile = jnp.pad(jnp.stack([attn_gain, mlp_gain]), ((0, 14), (0, 128 - w_rows)))
    out_full = gather(w_out[None], "grp")
    upstream = cotangent.astype(F32)
    d_branch_mlp = (RESID_MULT * upstream).astype(BF16)
    all_tokens, d_branch_mlp, w_qkv, tiles = entry(
        tokens, d_branch_mlp, packed, tile, grps, chips, 2
    )
    w_qkv, tiles = w_qkv.reshape(D, used), tiles.reshape(-1, 16, 128)
    normed_one, qkv, gains = project(all_tokens.reshape(devs * rows, D), w_qkv, tiles)
    gain_one, gain_two = gains[0], gains[1]
    d_branch_mlp = d_branch_mlp.reshape(devs * rows, D)
    attended = attend(qkv, order, q_heads)
    attended = plane_exchange(
        attended, (rows, D), by_rows(rows), by_cols(q_cols), chips, 3
    )

    out_full = plane_gather(out_full, chips, 4, inner=True).reshape(D, D)
    layer_in = tokens.astype(F32)
    branch_attn = matmul(attended, out_full)
    residual = layer_in + RESID_MULT * branch_attn
    factor_two = norm_parts(residual)
    normed_two = (residual * factor_two * gain_two).astype(BF16)
    normed_two = plane_gather(normed_two, chips, 1).reshape(devs * rows, D)
    wide_w = gather(jnp.stack([w_gate, w_up])[None], "grp")
    down_w = gather(w_down[None], "grp")
    hidden, hidden_t, silu, slope, normed_t = widen(normed_two, wide_w)
    part_down = down_part(hidden_t, d_branch_mlp)
    part_down, hidden, silu = lax.optimization_barrier((part_down, hidden, silu))
    grad_down = scatter(part_down, "grp")
    if chips == 4:
        branch_mlp, *shares = twin_reduce(mix_rows, (hidden, down_w), rows, 11)
        shares, silu = lax.optimization_barrier((shares, silu))
        shares = swap_others(shares)
    d_gate, d_up = narrow_back(silu, slope, d_branch_mlp, down_w)
    if chips == 4:
        part_wide = widen_part(normed_t, d_gate, d_up)
        part_wide, shares, d_gate, d_up = lax.optimization_barrier(
            (part_wide, shares, d_gate, d_up)
        )
        grad_wide = scatter(part_wide, "grp")
        d_normed_two = square_reduce(widen_back_rows, (d_gate, d_up, wide_w), rows, 10)
    else:
        part_wide = widen_part(normed_t, d_gate, d_up)
        part_wide, d_gate, d_up = lax.optimization_barrier((part_wide, d_gate, d_up))
        grad_wide = scatter(part_wide, "grp")
        d_normed_two = widen_back(d_gate, d_up, wide_w)
        d_normed_two = plane_reduce(d_normed_two.reshape(devs, rows, D), chips, 5)
        branch_mlp = mix(hidden, down_w)
        branch_mlp = plane_reduce(branch_mlp.reshape(devs, rows, D), chips, 5)

    layer_out, d_residual, totals, d_attended, grad_out, *away = turn(
        residual,
        d_normed_two,
        cotangent,
        gains,
        branch_attn,
        branch_mlp,
        shares if chips == 4 else (),
        attended,
        out_full,
        w_rows,
    )
    if chips == 4:
        drift_out = Drift(grad_out, *away, 1)
    d_attended, totals = exchange_total(
        d_attended, totals, (devs * rows, q_cols), rows, q_cols, grps, chips, 7
    )
    if chips == 4:
        sent_out, d_attended = lax.optimization_barrier((drift_out.parts(), d_attended))
        sent_out = swap_others((sent_out[2], sent_out[0], sent_out[1]))
    d_attended, grad_down = lax.optimization_barrier((d_attended, grad_down))
    d_qkv = attend_back(qkv, d_attended, order, q_heads)
    if chips == 4:
        sent_out, d_qkv = lax.optimization_barrier((sent_out, d_qkv))
    sent = over_rows(normed_one, d_qkv).astype(BF16)
    sent, d_qkv, grad_wide = lax.optimization_barrier((sent, d_qkv, grad_wide))
    sent = scatter(sent, "grp")
    d_normed_one = over_cols(d_qkv, w_qkv).astype(BF16).reshape(devs, rows, D)
    if chips == 4:
        sent_out, d_normed_one = lax.optimization_barrier((sent_out, d_normed_one))
        grad_out = drift_out.finish(sent_out).astype(BF16)
    else:
        grad_out = plane_reduce(
            grad_out.reshape(grps, devs, w_rows, D), chips, 6, dtype=BF16, inner=True
        )
    grad_out, d_normed_one = lax.optimization_barrier((grad_out, d_normed_one))
    grad_out = scatter(grad_out, "grp")
    d_normed_one = plane_reduce(d_normed_one, chips, 5)
    d_normed_one, sent = lax.optimization_barrier((d_normed_one, sent))
    d_input_norm, _ = norm_back(layer_in, norm_parts(layer_in), gain_one, d_normed_one)
    tokens_grad = (d_residual + d_input_norm).astype(BF16)
    sent = sent.reshape(devs, w_rows, q_cols + 2 * kv_cols)
    sent = plane_exchange(sent, sent.shape, by_slot, by_slot, chips, 9)
    sent, grad_out = lax.optimization_barrier((sent, grad_out))
    grad_out = grad_out.reshape(w_rows, D).astype(F32)

    grad_query, grad_key, grad_value, gain_sum = split(
        sent, w_query, w_key, w_value, kv_copies, q_cols, kv_cols
    )
    gain_one_grad = gain_sum[:, 0] / attn_gain.astype(F32)
    rms_stats = jnp.sqrt(totals[7, :3] / (rows * grps * devs * D))
    gain_first = (lax.axis_index("grp") * devs + lax.axis_index(PLANE)) * w_rows
    gain_two_grad = lax.dynamic_slice(totals.reshape(-1), (gain_first,), (w_rows,))
    return (
        layer_out,
        tokens_grad,
        gain_one_grad,
        grad_query,
        grad_key,
        grad_value,
        grad_out,
        gain_two_grad,
        grad_wide[0, 0].astype(F32),
        grad_wide[0, 1].astype(F32),
        grad_down[0].astype(F32),
        rms_stats,
    )


def solution(mesh):
    shape = (mesh.shape["grp"], mesh.shape["blk"] // 2, 2)
    mesh = Mesh(mesh.devices.reshape(shape), EVERY)
    row, col, vec = P(EVERY, None), P(None, EVERY), P(EVERY)
    return jax.shard_map(
        on_device,
        mesh=mesh,
        in_specs=(row, P(), P(), vec, row, row, row, row, vec, col, col, row, row),
        out_specs=(row, row, vec, row, row, row, row, vec, col, col, row, P()),
        check_vma=False,
    )
```

```python
import functools

import jax
import jax.numpy as jnp
from jax import lax
from jax.experimental import pallas as pl
from jax.experimental.pallas import tpu as pltpu
from jax.sharding import Mesh
from jax.sharding import PartitionSpec as P

D = 2048
HEADS = 32
KV_HEADS = 8
HEAD_DIM = 64
BLOCK = 128
PROMPT_BLOCKS = 8
GROUP_BLOCKS = 16
PER_GROUP = HEADS // KV_HEADS

ATTN_MULT = 0.015625
RESID_MULT = 0.22
EPSILON = 1e-05
MASKED = -1e30

PLANE = ("chip", "core")
EVERY = ("grp", "chip", "core")
BF16 = jnp.bfloat16
F32 = jnp.float32


MESH = pl.DeviceIdType.MESH
BRIEF = pl.CostEstimate(flops=1000, bytes_accessed=1000, transcendentals=0)
ANY = pl.BlockSpec(memory_space=pl.ANY)
VMEM = pl.BlockSpec(memory_space=pltpu.VMEM)


def place():
    return lax.axis_index("chip"), lax.axis_index("core")


def flip(chip, step, chips):
    return jnp.bitwise_xor(chip, step) if chips == 4 else lax.rem(chip + step, chips)


def unflip(chip, step, chips):
    return jnp.bitwise_xor(chip, step) if chips == 4 else lax.rem(chip + chips - step, chips)


def greet(peers):
    barrier = pltpu.get_barrier_semaphore()
    for chip, core in peers:
        pl.semaphore_signal(
            barrier, inc=1, device_id={"chip": chip, "core": core}, device_id_type=MESH
        )
    pl.semaphore_wait(barrier, len(peers))


def remote(src, dst, send, recv, chip, core):
    return pltpu.make_async_remote_copy(
        src_ref=src,
        dst_ref=dst,
        send_sem=send,
        recv_sem=recv,
        device_id={"chip": chip, "core": core},
        device_id_type=MESH,
    )


class Gather:
    def __init__(self, chips, inner, x_ref, o_ref, send, recv, local):
        self.chips, self.inner, self.x, self.o = chips, inner, x_ref, o_ref
        self.send, self.recv, self.local = send, recv, local
        self.chip, self.core = place()
        self.half = x_ref.shape[0] // 2
        self.started = []

    def greet(self):
        steps = (1, 2) if self.chips == 4 else range(1, self.chips)
        peers = [(flip(self.chip, s, self.chips), self.core) for s in steps]
        greet(peers + [(self.chip, 1 - self.core)])

    def piece(self, slot, h):
        at = pl.ds(h * self.half, self.half)
        return self.o.at[at, slot] if self.inner else self.o.at[slot, at]

    def own(self, h):
        return self.x.at[pl.ds(h * self.half, self.half)]

    def slot(self, chip, core):
        return chip * 2 + core

    def push(self, src, slot, h, chip, core):
        i = len(self.started)
        copy = remote(src, self.piece(slot, h), self.send.at[i], self.recv.at[slot, h], chip, core)
        copy.start()
        self.started.append(copy)

    def wait_for(self, slot, h):
        remote(
            self.own(h), self.piece(slot, h), self.send.at[0], self.recv.at[slot, h],
            self.chip, 1 - self.core,
        ).wait_recv()

    def start(self):
        me = self.slot(self.chip, self.core)
        if self.chips == 4:
            for h, s in ((0, 1), (1, 2), (1, 1), (0, 2)):
                self.push(self.own(h), me, h, flip(self.chip, s, 4), self.core)
        else:
            for s in range(1, self.chips):
                for h in range(2):
                    self.push(self.own(h), me, h, flip(self.chip, s, self.chips), self.core)
        for h in range(2):
            self.push(self.own(h), me, h, self.chip, 1 - self.core)
        whole = self.o.at[:, me] if self.inner else self.o.at[me]
        self.mine = pltpu.make_async_copy(self.x, whole, self.local)
        self.mine.start()

    def relay(self, first=0, last=None):
        if self.chips == 4:
            plan = ((1, 0, 2), (2, 1, 1), (1, 1, 0), (2, 0, 0), (3, 0, 0), (3, 1, 0))
        else:
            plan = tuple((s, h, 0) for s in range(1, self.chips) for h in range(2))
        for s, h, onward in plan[first:last]:
            slot = self.slot(unflip(self.chip, s, self.chips), self.core)
            self.wait_for(slot, h)
            if onward:
                self.push(self.piece(slot, h), slot, h, flip(self.chip, onward, 4), self.core)
            self.push(self.piece(slot, h), slot, h, self.chip, 1 - self.core)

    def finish(self):
        for s in range(self.chips):
            slot = self.slot(unflip(self.chip, s, self.chips), 1 - self.core)
            for h in range(2):
                self.wait_for(slot, h)
        for copy in self.started:
            copy.wait_send()
        self.mine.wait()


def gather_sems(chips):
    return [
        pltpu.SemaphoreType.DMA((4 * chips + 4,)),
        pltpu.SemaphoreType.DMA((2 * chips, 2)),
        pltpu.SemaphoreType.DMA,
    ]


def gather_kernel(chips, inner, x_ref, o_ref, *sems):
    run = Gather(chips, inner, x_ref, o_ref, *sems)
    run.greet()
    run.start()
    run.relay()
    run.finish()


def plane_gather(x, chips, call_id, inner=False):
    devs = 2 * chips
    shape = (x.shape[0], devs) + x.shape[1:] if inner else (devs,) + x.shape
    return pl.pallas_call(
        functools.partial(gather_kernel, chips, inner),
        out_shape=jax.ShapeDtypeStruct(shape, x.dtype),
        in_specs=[ANY],
        out_specs=ANY,
        scratch_shapes=gather_sems(chips),
        cost_estimate=BRIEF,
        compiler_params=pltpu.CompilerParams(collective_id=call_id, has_side_effects=True),
    )(x)


def reduce_kernel(chips, inner, p_ref, o_ref, total, mine, twin, moved, corner, landed, lsem, tsend, trecv, msend, mrecv, csend, crecv):
    chip, core = place()
    sib = 1 - core
    half = (p_ref.shape[0] if inner else p_ref.shape[1]) // 2
    block = (lambda slot: p_ref.at[:, slot]) if inner else (lambda slot: p_ref.at[slot])
    steps = (1, 2) if chips == 4 else tuple(range(1, chips))
    peers = [(flip(chip, s, chips), core) for s in steps]
    greet(peers + [(chip, sib)])
    order = (3, 1, 2, 0) if chips == 4 else tuple(range(1, chips)) + (0,)
    loads, twins = {}, {}
    for s in order:
        to = flip(chip, s, chips) * 2
        twins[s] = remote(block(to + sib), twin.at[s], tsend.at[s], trecv.at[s], chip, sib)
        twins[s].start()
        loads[s] = pltpu.make_async_copy(block(to + core), mine.at[s], lsem.at[s])
        loads[s].start()

    def part(s, h):
        at = pl.ds(h * half, half)
        return mine[s, at].astype(F32) + twin[s, at].astype(F32)

    def ready(s):
        loads[s].wait()
        twins[s].wait_recv()

    sent = []
    if chips == 4:
        corners = []
        ready(3)
        for h, s in ((0, 1), (1, 2)):
            moved[3, pl.ds(h * half, half)] = part(3, h).astype(BF16)
            copy = remote(moved.at[3, pl.ds(h * half, half)], corner.at[h], csend.at[h], crecv.at[h], flip(chip, s, 4), core)
            copy.start()
            corners.append(copy)

        def send(s, h):
            at = pl.ds(h * half, half)
            copy = remote(moved.at[s, at], landed.at[s - 1, at], msend.at[s - 1, h], mrecv.at[s - 1, h], flip(chip, s, 4), core)
            copy.start()
            sent.append(copy)

        for s, h in ((1, 0), (2, 1)):
            ready(s)
            moved[s, pl.ds(h * half, half)] = part(s, h).astype(BF16)
            send(s, h)
        for s, h in ((2, 0), (1, 1)):
            corners[h].wait_recv()
            moved[s, pl.ds(h * half, half)] = (part(s, h) + corner[h].astype(F32)).astype(BF16)
            send(s, h)
        for copy in corners:
            copy.wait_send()
    else:
        for s in steps:
            ready(s)
            for h in range(2):
                at = pl.ds(h * half, half)
                moved[s, at] = part(s, h).astype(BF16)
                copy = remote(moved.at[s, at], landed.at[s - 1, at], msend.at[s - 1, h], mrecv.at[s - 1, h], flip(chip, s, chips), core)
                copy.start()
                sent.append(copy)
    ready(0)
    for h in range(2):
        total[pl.ds(h * half, half)] = part(0, h)
    for copy in sent:
        copy.wait()
    for s in steps[:-1]:
        total[...] += landed[s - 1].astype(F32)
    o_ref[...] = (total[...] + landed[steps[-1] - 1].astype(F32)).astype(o_ref.dtype)
    for s in order:
        twins[s].wait_send()


def plane_reduce(p, chips, call_id, dtype=F32, inner=False):
    block = (p.shape[0],) + p.shape[2:] if inner else p.shape[1:]
    steps = 2 if chips == 4 else chips - 1
    return pl.pallas_call(
        functools.partial(reduce_kernel, chips, inner),
        out_shape=jax.ShapeDtypeStruct(block, dtype),
        in_specs=[ANY],
        out_specs=VMEM,
        scratch_shapes=[
            pltpu.VMEM(block, F32),
            pltpu.VMEM((chips,) + block, BF16),
            pltpu.VMEM((chips,) + block, BF16),
            pltpu.VMEM((chips,) + block, BF16),
            pltpu.VMEM((2, block[0] // 2) + block[1:], BF16),
            pltpu.VMEM((steps,) + block, BF16),
            pltpu.SemaphoreType.DMA((chips,)),
            pltpu.SemaphoreType.DMA((chips,)),
            pltpu.SemaphoreType.DMA((chips,)),
            pltpu.SemaphoreType.DMA((steps, 2)),
            pltpu.SemaphoreType.DMA((steps, 2)),
            pltpu.SemaphoreType.DMA((2,)),
            pltpu.SemaphoreType.DMA((2,)),
        ],
        cost_estimate=BRIEF,
        compiler_params=pltpu.CompilerParams(
            collective_id=call_id, has_side_effects=True, vmem_limit_bytes=56 << 20
        ),
    )(p)


def swap_chips(values, step):
    return lax.ppermute(values, "chip", [(c, c ^ step) for c in range(4)])


class Drift:
    def __init__(self, mine, away):
        self.mine = mine
        self.twin = lax.ppermute(away, "core", [(0, 1), (1, 0)])

    def parts(self):
        self.own, *others = twin_add(self.mine, self.twin)
        return others


def twin_add_kernel(mine_ref, twin_ref, *refs):
    chip = lax.axis_index("chip")
    for step, ref in zip((0, 3, 1, 2), refs):
        at = jnp.bitwise_xor(chip, step)
        ref[0] = (mine_ref[0, at].astype(F32) + twin_ref[0, at].astype(F32)).astype(ref.dtype)


def twin_add(mine, twin):
    grps, _, rows, cols = mine.shape
    spec = pl.BlockSpec((1, 4, rows, cols), lambda g: (g, 0, 0, 0))
    part_spec = pl.BlockSpec((1, rows, cols), lambda g: (g, 0, 0))
    part = (grps, rows, cols)
    return pl.pallas_call(
        twin_add_kernel,
        out_shape=(jax.ShapeDtypeStruct(part, F32),) + (jax.ShapeDtypeStruct(part, BF16),) * 3,
        grid=(grps,),
        in_specs=[spec, spec],
        out_specs=(part_spec,) * 4,
        cost_estimate=BRIEF,
    )(mine, twin)


def exchange_kernel(chips, cut, paste, x_ref, o_ref, send, recv, local):
    chip, core = place()
    me = chip * 2 + core
    peers = [(flip(chip, s, chips), c) for s in range(1, chips) for c in (core, 1 - core)]
    peers = peers + [(chip, 1 - core)]
    greet(peers)
    far = [p for p in ([3, 1, 2] if chips == 4 else range(1, chips))]
    order = [(flip(chip, s, chips), c) for s in far for c in (core, 1 - core)] + [(chip, 1 - core)]
    copies = []
    for i, (to, c) in enumerate(order):
        copy = remote(cut(x_ref, to * 2 + c), paste(o_ref, me), send.at[i], recv.at[me], to, c)
        copy.start()
        copies.append(copy)
    mine = pltpu.make_async_copy(cut(x_ref, me), paste(o_ref, me), local)
    mine.start()
    for s in far:
        for c in (core, 1 - core):
            slot = unflip(chip, s, chips) * 2 + c
            remote(cut(x_ref, me), paste(o_ref, slot), send.at[0], recv.at[slot], chip, 1 - core).wait_recv()
    slot = chip * 2 + 1 - core
    remote(cut(x_ref, me), paste(o_ref, slot), send.at[0], recv.at[slot], chip, 1 - core).wait_recv()
    for copy in copies:
        copy.wait_send()
    mine.wait()


def plane_exchange(x, shape, cut, paste, chips, call_id):
    return pl.pallas_call(
        functools.partial(exchange_kernel, chips, cut, paste),
        out_shape=jax.ShapeDtypeStruct(shape, x.dtype),
        in_specs=[ANY],
        out_specs=ANY,
        scratch_shapes=[
            pltpu.SemaphoreType.DMA((2 * chips,)),
            pltpu.SemaphoreType.DMA((2 * chips,)),
            pltpu.SemaphoreType.DMA,
        ],
        cost_estimate=BRIEF,
        compiler_params=pltpu.CompilerParams(collective_id=call_id, has_side_effects=True),
    )(x)


def by_slot(ref, dev):
    return ref.at[dev]


def by_rows(rows):
    return lambda ref, dev: ref.at[pl.ds(pl.multiple_of(dev * rows, rows), rows)]


def by_cols(cols):
    return lambda ref, dev: ref.at[:, pl.ds(pl.multiple_of(dev * cols, cols), cols)]


def matmul(left, right):
    return jnp.dot(left, right, preferred_element_type=F32)


def over_rows(left, right):
    return lax.dot_general(left, right, (((0,), (0,)), ((), ())), preferred_element_type=F32)


def over_cols(left, right):
    return lax.dot_general(left, right, (((1,), (1,)), ((), ())), preferred_element_type=F32)


def gather(values, axes, axis=0):
    return lax.all_gather(values, axes, axis=axis, tiled=True)


def scatter(values, axes, axis=0):
    return lax.psum_scatter(values, axes, scatter_dimension=axis, tiled=True)


def dot_nt(left, right):
    return lax.dot_general(left, right, (((1,), (1,)), ((), ())), preferred_element_type=F32)


def head_stack(values, heads):
    col_head = lax.broadcasted_iota(jnp.int32, values.shape, 1) // HEAD_DIM
    return jnp.concatenate(
        [jnp.where(col_head == h, values, jnp.zeros_like(values)) for h in range(heads)], axis=0
    )


def head_pick(stacked, heads):
    rows = stacked.shape[0] // heads
    col_head = lax.broadcasted_iota(jnp.int32, (rows, stacked.shape[1]), 1) // HEAD_DIM
    total = jnp.zeros((rows, stacked.shape[1]), F32)
    for h in range(heads):
        total = jnp.where(col_head == h, stacked[h * rows : (h + 1) * rows], total)
    return total


def head_fold(values, heads):
    total = values[:, :HEAD_DIM]
    for h in range(1, heads):
        total = total + values[:, h * HEAD_DIM : (h + 1) * HEAD_DIM]
    return total


def repeat_heads(values, heads):
    return jnp.concatenate([values] * heads, axis=1)


def own_rows(order_ref, slot):
    return pl.ds(pl.multiple_of(order_ref[slot] * BLOCK, BLOCK), BLOCK)


def load_prompt(heads, order_ref, qkv_ref, k_ref, v_ref, first):
    q_cols = heads * HEAD_DIM
    for s in range(PROMPT_BLOCKS):
        pair = qkv_ref[own_rows(order_ref, first + s), q_cols:]
        at = pl.ds(s * BLOCK, BLOCK)
        k_ref[at] = repeat_heads(pair[:, :HEAD_DIM], heads)
        v_ref[at] = repeat_heads(pair[:, HEAD_DIM:], heads)


def by_keys(slot, body):
    prompt = PROMPT_BLOCKS * BLOCK
    quarter = prompt // 4
    seen = jnp.minimum(slot, PROMPT_BLOCKS) * BLOCK
    for n in range(1, 5):
        low = (n - 1) * quarter if n > 1 else -1

        @pl.when((seen > low) & (seen <= n * quarter))
        def _(n=n):
            body(n * quarter)


def soft_parts(heads, slot, q_stack, k_far, k_own):
    far = dot_nt(k_far, q_stack)
    own = dot_nt(k_own, q_stack)
    limit = jnp.minimum(slot, PROMPT_BLOCKS) * BLOCK
    far = jnp.where(lax.broadcasted_iota(jnp.int32, far.shape, 0) < limit, far, MASKED)
    key = lax.broadcasted_iota(jnp.int32, own.shape, 0)
    row = lax.broadcasted_iota(jnp.int32, own.shape, 1) % BLOCK
    own = jnp.where(key <= row, own, MASKED)
    peak = jnp.maximum(jnp.max(far, axis=0, keepdims=True), jnp.max(own, axis=0, keepdims=True))
    far, own = jnp.exp(far - peak), jnp.exp(own - peak)
    scale = 1.0 / (jnp.sum(far, axis=0, keepdims=True) + jnp.sum(own, axis=0, keepdims=True))
    return far * scale, own * scale


def scaled_stack(q, heads):
    return head_stack((q.astype(F32) * ATTN_MULT).astype(BF16), heads)


def attend_kernel(heads, order_ref, qkv_ref, o_ref, k_ref, v_ref, vt_ref):
    first, slot = pl.program_id(0) * GROUP_BLOCKS, pl.program_id(1)
    q_cols = heads * HEAD_DIM

    @pl.when(slot == 0)
    def _():
        load_prompt(heads, order_ref, qkv_ref, k_ref, v_ref, first)
        vt_ref[...] = v_ref[...].astype(F32).T.astype(BF16)

    rows = own_rows(order_ref, first + slot)
    mine = qkv_ref[rows, :]
    k_own = repeat_heads(mine[:, q_cols : q_cols + HEAD_DIM], heads)
    v_own = repeat_heads(mine[:, q_cols + HEAD_DIM :], heads)
    q_stack = scaled_stack(mine[:, :q_cols], heads)

    def body(count):
        far, own = soft_parts(heads, slot, q_stack, k_ref[:count], k_own)
        mixed = matmul(vt_ref[:, :count], far.astype(BF16))
        mixed += matmul(v_own.astype(F32).T.astype(BF16), own.astype(BF16))
        o_ref[rows, :] = head_pick(mixed.T, heads).astype(BF16)

    by_keys(slot, body)


def attend_back_kernel(
    heads, order_ref, qkv_ref, d_ref, o_ref, k_ref, v_ref, kt_ref, dk_ref, dv_ref
):
    first, slot = pl.program_id(0) * GROUP_BLOCKS, pl.program_id(1)
    q_cols = heads * HEAD_DIM

    @pl.when(slot == 0)
    def _():
        load_prompt(heads, order_ref, qkv_ref, k_ref, v_ref, first)
        kt_ref[...] = k_ref[...].astype(F32).T.astype(BF16)
        dk_ref[...] = jnp.zeros_like(dk_ref)
        dv_ref[...] = jnp.zeros_like(dv_ref)

    rows = own_rows(order_ref, first + slot)
    mine = qkv_ref[rows, :]
    k_own = repeat_heads(mine[:, q_cols : q_cols + HEAD_DIM], heads)
    v_own = repeat_heads(mine[:, q_cols + HEAD_DIM :], heads)
    q_stack = scaled_stack(mine[:, :q_cols], heads)
    d_stack = head_stack(d_ref[rows, :], heads)

    def fold(d_k, d_v):
        return jnp.concatenate([head_fold(d_k, heads), head_fold(d_v, heads)], axis=1).astype(BF16)

    def body(count):
        far, own = soft_parts(heads, slot, q_stack, k_ref[:count], k_own)
        d_far, d_own = dot_nt(v_ref[:count], d_stack), dot_nt(v_own, d_stack)
        mean = jnp.sum(far * d_far, axis=0, keepdims=True)
        mean += jnp.sum(own * d_own, axis=0, keepdims=True)
        d_far = (far * (d_far - mean)).astype(BF16)
        d_own = (own * (d_own - mean)).astype(BF16)
        dv_ref[:count] += matmul(far.astype(BF16), d_stack)
        dk_ref[:count] += matmul(d_far, q_stack)
        dv_own = matmul(own.astype(BF16), d_stack)
        dk_own = matmul(d_own, q_stack)
        d_q = matmul(kt_ref[:, :count], d_far) + matmul(k_own.astype(F32).T.astype(BF16), d_own)
        o_ref[rows, :q_cols] = (head_pick(d_q.T, heads) * ATTN_MULT).astype(BF16)

        @pl.when(slot < PROMPT_BLOCKS)
        def _():
            at = pl.ds(pl.multiple_of(slot * BLOCK, BLOCK), BLOCK)
            dk_ref[at] += dk_own
            dv_ref[at] += dv_own

        @pl.when(slot >= PROMPT_BLOCKS)
        def _():
            o_ref[rows, q_cols:] = fold(dk_own, dv_own)

    by_keys(slot, body)

    @pl.when(slot == GROUP_BLOCKS - 1)
    def _():
        for s in range(PROMPT_BLOCKS):
            at = pl.ds(s * BLOCK, BLOCK)
            o_ref[own_rows(order_ref, first + s), q_cols:] = fold(dk_ref[at], dv_ref[at])


def whole(shape):
    return pl.BlockSpec(shape, lambda g, s, order: (0,) * len(shape))


def attend(qkv, order, heads):
    tokens, cols = qkv.shape
    prompt, q_cols = PROMPT_BLOCKS * BLOCK, heads * HEAD_DIM
    return pl.pallas_call(
        functools.partial(attend_kernel, heads),
        out_shape=jax.ShapeDtypeStruct((tokens, q_cols), BF16),
        grid_spec=pltpu.PrefetchScalarGridSpec(
            num_scalar_prefetch=1,
            grid=(tokens // (GROUP_BLOCKS * BLOCK), GROUP_BLOCKS),
            in_specs=[whole((tokens, cols))],
            out_specs=whole((tokens, q_cols)),
            scratch_shapes=[
                pltpu.VMEM((prompt, q_cols), BF16),
                pltpu.VMEM((prompt, q_cols), BF16),
                pltpu.VMEM((q_cols, prompt), BF16),
            ],
        ),
        cost_estimate=BRIEF,
        compiler_params=pltpu.CompilerParams(vmem_limit_bytes=40 << 20),
    )(order, qkv)


def attend_back(qkv, d_attended, order, heads):
    tokens, cols = qkv.shape
    prompt, q_cols = PROMPT_BLOCKS * BLOCK, heads * HEAD_DIM
    return pl.pallas_call(
        functools.partial(attend_back_kernel, heads),
        out_shape=jax.ShapeDtypeStruct((tokens, cols), BF16),
        grid_spec=pltpu.PrefetchScalarGridSpec(
            num_scalar_prefetch=1,
            grid=(tokens // (GROUP_BLOCKS * BLOCK), GROUP_BLOCKS),
            in_specs=[whole((tokens, cols)), whole((tokens, q_cols))],
            out_specs=whole((tokens, cols)),
            scratch_shapes=[
                pltpu.VMEM((prompt, q_cols), BF16),
                pltpu.VMEM((prompt, q_cols), BF16),
                pltpu.VMEM((q_cols, prompt), BF16),
                pltpu.VMEM((prompt, q_cols), F32),
                pltpu.VMEM((prompt, q_cols), F32),
            ],
        ),
        cost_estimate=BRIEF,
        compiler_params=pltpu.CompilerParams(vmem_limit_bytes=40 << 20),
    )(order, qkv, d_attended)


def exchange_total_kernel(
    grps, chips, cut, paste, x_ref, t_ref, o_ref, sum_ref,
    over_z, over_plane, send, recv, local, zsend, zrecv, psend, precv,
):
    grp = lax.axis_index("grp")
    chip, core = place()
    me = chip * 2 + core
    far = [lax.rem(grp + s, grps) for s in range(1, grps)]
    steps = (3, 1, 2) if chips == 4 else tuple(range(1, chips))
    near = [(flip(chip, s, chips), c) for s in steps for c in (core, 1 - core)]
    near = near + [(chip, 1 - core)]
    barrier = pltpu.get_barrier_semaphore()
    for g in far:
        pl.semaphore_signal(barrier, inc=1, device_id={"grp": g}, device_id_type=MESH)
    for to, c in near:
        pl.semaphore_signal(
            barrier, inc=1, device_id={"chip": to, "core": c}, device_id_type=MESH
        )
    pl.semaphore_wait(barrier, len(far) + len(near))

    def z_copy(slot, sem, to):
        return pltpu.make_async_remote_copy(
            src_ref=t_ref,
            dst_ref=over_z.at[slot],
            send_sem=sem,
            recv_sem=zrecv.at[slot],
            device_id={"grp": to},
            device_id_type=MESH,
        )

    copies = []
    for i, g in enumerate(far):
        copy = z_copy(grp, zsend.at[i], g)
        copy.start()
        copies.append(copy)
    for i, (to, c) in enumerate(near):
        copy = remote(cut(x_ref, to * 2 + c), paste(o_ref, me), send.at[i], recv.at[me], to, c)
        copy.start()
        copies.append(copy)
    mine = pltpu.make_async_copy(cut(x_ref, me), paste(o_ref, me), local)
    mine.start()
    over_z[grp] = t_ref[...]
    for g in far:
        z_copy(g, zsend.at[0], g).wait_recv()
    over_plane[me] = jnp.sum(over_z[...], axis=0)
    for i, (to, c) in enumerate(near):
        copy = remote(over_plane.at[me], over_plane.at[me], psend.at[i], precv.at[me], to, c)
        copy.start()
        copies.append(copy)
    for to, c in near:
        slot = to * 2 + c
        remote(cut(x_ref, me), paste(o_ref, slot), send.at[0], recv.at[slot], to, c).wait_recv()
        remote(over_plane.at[me], over_plane.at[slot], psend.at[0], precv.at[slot], to, c).wait_recv()
    for copy in copies:
        copy.wait_send()
    mine.wait()
    sum_ref[...] = jnp.sum(over_plane[...], axis=0)


def exchange_total(x, t, shape, rows, cols, grps, chips, call_id):
    devs = 2 * chips
    return pl.pallas_call(
        functools.partial(exchange_total_kernel, grps, chips, by_cols(cols), by_rows(rows)),
        out_shape=(
            jax.ShapeDtypeStruct(shape, x.dtype),
            jax.ShapeDtypeStruct(t.shape, F32),
        ),
        in_specs=[ANY, VMEM],
        out_specs=(ANY, VMEM),
        scratch_shapes=[
            pltpu.VMEM((grps,) + t.shape, F32),
            pltpu.VMEM((devs,) + t.shape, F32),
            pltpu.SemaphoreType.DMA((devs,)),
            pltpu.SemaphoreType.DMA((devs,)),
            pltpu.SemaphoreType.DMA,
            pltpu.SemaphoreType.DMA((grps,)),
            pltpu.SemaphoreType.DMA((grps,)),
            pltpu.SemaphoreType.DMA((devs,)),
            pltpu.SemaphoreType.DMA((devs,)),
        ],
        cost_estimate=BRIEF,
        compiler_params=pltpu.CompilerParams(collective_id=call_id, has_side_effects=True),
    )(x, t)


def params(axes, mib=56):
    return pltpu.CompilerParams(
        dimension_semantics=("arbitrary",) * axes, vmem_limit_bytes=mib << 20
    )


def tile_rows(count, limit):
    while count % limit:
        limit //= 2
    return limit


def widen_kernel(n_ref, w_ref, h_ref, ht_ref, s_ref, t_ref, nt_ref):
    values = n_ref[...]
    gate, up = matmul(values, w_ref[0, 0]), matmul(values, w_ref[0, 1])
    sig = 1.0 / (1.0 + jnp.exp(-gate))
    silu = gate * sig
    hidden = (silu * up).astype(BF16)
    h_ref[0] = hidden
    ht_ref[0] = hidden.T
    s_ref[0] = silu.astype(BF16)
    t_ref[0] = (up * (sig * (1.0 + gate * (1.0 - sig)))).astype(BF16)

    @pl.when(pl.program_id(1) == 0)
    def _():
        nt_ref[...] = values.T


def widen(normed, weights):
    tokens, depth = normed.shape
    shards, _, _, width = weights.shape
    rows = tile_rows(tokens, 1024)
    tall = jax.ShapeDtypeStruct((shards, tokens, width), BF16)
    tall_spec = pl.BlockSpec((1, rows, width), lambda r, s: (s, r, 0))
    return pl.pallas_call(
        widen_kernel,
        out_shape=(
            tall,
            jax.ShapeDtypeStruct((shards, width, tokens), BF16),
            tall,
            tall,
            jax.ShapeDtypeStruct((depth, tokens), BF16),
        ),
        grid=(tokens // rows, shards),
        in_specs=[
            pl.BlockSpec((rows, depth), lambda r, s: (r, 0)),
            pl.BlockSpec((1, 2, depth, width), lambda r, s: (s, 0, 0, 0)),
        ],
        out_specs=(
            tall_spec,
            pl.BlockSpec((1, width, rows), lambda r, s: (s, 0, r)),
            tall_spec,
            tall_spec,
            pl.BlockSpec((depth, rows), lambda r, s: (0, r)),
        ),
        cost_estimate=BRIEF,
        compiler_params=params(2),
    )(normed, weights)


def down_part_kernel(ht_ref, d_ref, o_ref):
    o_ref[0] = matmul(ht_ref[0], d_ref[...]).astype(BF16)


def down_part(hidden_t, upstream):
    shards, width, tokens = hidden_t.shape
    depth = upstream.shape[1]
    cols = tile_rows(depth, 1024)
    return pl.pallas_call(
        down_part_kernel,
        out_shape=jax.ShapeDtypeStruct((shards, width, depth), BF16),
        grid=(depth // cols, shards),
        in_specs=[
            pl.BlockSpec((1, width, tokens), lambda c, s: (s, 0, 0)),
            pl.BlockSpec((tokens, cols), lambda c, s: (0, c)),
        ],
        out_specs=pl.BlockSpec((1, width, cols), lambda c, s: (s, 0, c)),
        cost_estimate=BRIEF,
        compiler_params=params(2),
    )(hidden_t, upstream)


def mix_kernel(h_ref, w_ref, m_ref):
    mixed = None
    for i in range(w_ref.shape[0]):
        part = matmul(h_ref[i], w_ref[i])
        mixed = part if mixed is None else mixed + part
    m_ref[...] = mixed.astype(BF16)


def narrow_specs(hidden, weights):
    shards, tokens, width = hidden.shape
    depth = weights.shape[2]
    rows = tile_rows(tokens, 512)
    return (
        tokens // rows,
        pl.BlockSpec((shards, rows, width), lambda r: (0, r, 0)),
        pl.BlockSpec((rows, depth), lambda r: (r, 0)),
        pl.BlockSpec(weights.shape, lambda r: (0, 0, 0), pipeline_mode=pl.Buffered(1)),
    )


def mix(hidden, weights):
    steps, tall_spec, flat_spec, weight_spec = narrow_specs(hidden, weights)
    return pl.pallas_call(
        mix_kernel,
        out_shape=jax.ShapeDtypeStruct((hidden.shape[1], weights.shape[2]), BF16),
        grid=(steps,),
        in_specs=[tall_spec, weight_spec],
        out_specs=flat_spec,
        cost_estimate=BRIEF,
        compiler_params=params(1),
    )(hidden, weights)


def narrow_back_kernel(s_ref, t_ref, d_ref, w_ref, dg_ref, du_ref):
    upstream = d_ref[...]
    for i in range(w_ref.shape[0]):
        d_hidden = dot_nt(upstream, w_ref[i])
        dg_ref[i] = (d_hidden * t_ref[i].astype(F32)).astype(BF16)
        du_ref[i] = (d_hidden * s_ref[i].astype(F32)).astype(BF16)


def narrow_back(silu, slope, upstream, weights):
    steps, tall_spec, flat_spec, weight_spec = narrow_specs(silu, weights)
    tall = jax.ShapeDtypeStruct(silu.shape, BF16)
    return pl.pallas_call(
        narrow_back_kernel,
        out_shape=(tall, tall),
        grid=(steps,),
        in_specs=[tall_spec, tall_spec, flat_spec, weight_spec],
        out_specs=(tall_spec, tall_spec),
        cost_estimate=BRIEF,
        compiler_params=params(1),
    )(silu, slope, upstream, weights)


def widen_part_kernel(nt_ref, dg_ref, du_ref, o_ref):
    values = nt_ref[...]
    o_ref[0, 0] = matmul(values, dg_ref[0]).astype(BF16)
    o_ref[0, 1] = matmul(values, du_ref[0]).astype(BF16)


def widen_part(normed_t, d_gate, d_up):
    depth, tokens = normed_t.shape
    shards, _, width = d_gate.shape
    rows = tile_rows(depth, 1024)
    tall_spec = pl.BlockSpec((1, tokens, width), lambda r, s: (s, 0, 0))
    return pl.pallas_call(
        widen_part_kernel,
        out_shape=jax.ShapeDtypeStruct((shards, 2, depth, width), BF16),
        grid=(depth // rows, shards),
        in_specs=[pl.BlockSpec((rows, tokens), lambda r, s: (r, 0)), tall_spec, tall_spec],
        out_specs=pl.BlockSpec((1, 2, rows, width), lambda r, s: (s, 0, r, 0)),
        cost_estimate=BRIEF,
        compiler_params=params(2),
    )(normed_t, d_gate, d_up)


def widen_back_kernel(dg_ref, du_ref, w_ref, o_ref):
    total = None
    for i in range(w_ref.shape[0]):
        part = dot_nt(dg_ref[i], w_ref[i, 0]) + dot_nt(du_ref[i], w_ref[i, 1])
        total = part if total is None else total + part
    o_ref[...] = total.astype(BF16)


def widen_back(d_gate, d_up, weights):
    shards, tokens, width = d_gate.shape
    depth = weights.shape[2]
    rows = tile_rows(tokens, 512)
    tall_spec = pl.BlockSpec((shards, rows, width), lambda r: (0, r, 0))
    return pl.pallas_call(
        widen_back_kernel,
        out_shape=jax.ShapeDtypeStruct((tokens, depth), BF16),
        grid=(tokens // rows,),
        in_specs=[
            tall_spec,
            tall_spec,
            pl.BlockSpec(weights.shape, lambda r: (0, 0, 0, 0), pipeline_mode=pl.Buffered(1)),
        ],
        out_specs=pl.BlockSpec((rows, depth), lambda r: (r, 0)),
        cost_estimate=BRIEF,
        compiler_params=params(1),
    )(d_gate, d_up, weights)


def stage_step(stage):
    return jnp.where(stage == 0, 3, jnp.where(stage == 3, 0, stage))


class Square:
    def __init__(self, acc, mine, away, twin, moved, corner, landed, tsend, trecv, msend, mrecv, csend, crecv):
        self.acc, self.mine, self.away, self.twin = acc, mine, away, twin
        self.moved, self.corner, self.landed = moved, corner, landed
        self.tsend, self.trecv, self.msend, self.mrecv = tsend, trecv, msend, mrecv
        self.csend, self.crecv = csend, crecv
        self.chip, self.core = place()
        self.rows = mine.shape[1]
        self.half = self.rows // 2

    def greet(self):
        peers = [(flip(self.chip, s, 4), self.core) for s in (1, 2)]
        greet(peers + [(self.chip, 1 - self.core)])

    def twin_copy(self, stage):
        return remote(
            self.away.at[stage], self.twin.at[stage], self.tsend.at[stage], self.trecv.at[stage],
            self.chip, 1 - self.core,
        )

    def offer(self, stage):
        own, other = self.core * self.rows, (1 - self.core) * self.rows
        self.mine[stage] = self.acc[pl.ds(pl.multiple_of(own, self.rows), self.rows)].astype(BF16)
        self.away[stage] = self.acc[pl.ds(pl.multiple_of(other, self.rows), self.rows)].astype(BF16)
        self.twin_copy(stage).start()

    def at(self, h):
        return pl.ds(h * self.half, self.half)

    def both(self, stage, h):
        return self.mine[stage, self.at(h)].astype(F32) + self.twin[stage, self.at(h)].astype(F32)

    def corner_copy(self, h):
        return remote(
            self.moved.at[0, self.at(h)], self.corner.at[h], self.csend.at[h], self.crecv.at[h],
            flip(self.chip, h + 1, 4), self.core,
        )

    def copy(self, stage, h):
        return remote(
            self.moved.at[stage, self.at(h)], self.landed.at[stage - 1, self.at(h)],
            self.msend.at[stage - 1, h], self.mrecv.at[stage - 1, h],
            flip(self.chip, stage, 4), self.core,
        )

    def corners(self):
        self.twin_copy(0).wait_recv()
        for h in range(2):
            self.moved[0, self.at(h)] = self.both(0, h).astype(BF16)
            self.corner_copy(h).start()

    def plain(self, stage):
        self.twin_copy(stage).wait_recv()
        h = stage - 1
        self.moved[stage, self.at(h)] = self.both(stage, h).astype(BF16)
        self.copy(stage, h).start()

    def joined(self, stage):
        h = 2 - stage
        self.corner_copy(h).wait_recv()
        total = self.both(stage, h) + self.corner[h].astype(F32)
        self.moved[stage, self.at(h)] = total.astype(BF16)
        self.copy(stage, h).start()

    def finish(self, o_ref):
        self.twin_copy(3).wait_recv()
        for h in range(2):
            o_ref[self.at(h)] = self.both(3, h)
        for stage, h in ((1, 0), (2, 1), (2, 0), (1, 1)):
            self.copy(stage, h).wait_recv()
            o_ref[self.at(h)] += self.landed[stage - 1, self.at(h)].astype(F32)
        for stage in (1, 2):
            for h in range(2):
                self.copy(stage, h).wait_send()
        for h in range(2):
            self.corner_copy(h).wait_send()
        for stage in range(4):
            self.twin_copy(stage).wait_send()


def square_kernel(compute, count, *refs):
    operands, o_ref, scratch = refs[:count], refs[count], refs[count + 1 :]
    run = Square(*scratch)
    stage = pl.program_id(0)

    @pl.when(stage == 0)
    def _():
        run.greet()

    @pl.when(stage == 3)
    def _():
        run.plain(2)
        run.joined(2)
        run.joined(1)

    target = jnp.bitwise_xor(run.chip, stage_step(stage))
    width = 2 * run.rows
    run.acc[...] = compute(operands, pl.ds(pl.multiple_of(target * width, width), width))
    run.offer(stage)

    @pl.when(stage == 1)
    def _():
        run.corners()

    @pl.when(stage == 2)
    def _():
        run.plain(1)

    @pl.when(stage == 3)
    def _():
        run.finish(o_ref)


def square_reduce(compute, operands, rows, call_id):
    block = (rows, D)

    def held(shape):
        return pl.BlockSpec(shape, lambda s: (0,) * len(shape), pipeline_mode=pl.Buffered(1))

    return pl.pallas_call(
        functools.partial(square_kernel, compute, len(operands)),
        out_shape=jax.ShapeDtypeStruct(block, F32),
        grid=(4,),
        in_specs=[held(x.shape) for x in operands],
        out_specs=held(block),
        scratch_shapes=[
            pltpu.VMEM((2 * rows, D), F32),
            pltpu.VMEM((4,) + block, BF16),
            pltpu.VMEM((4,) + block, BF16),
            pltpu.VMEM((4,) + block, BF16),
            pltpu.VMEM((3,) + block, BF16),
            pltpu.VMEM((2, rows // 2, D), BF16),
            pltpu.VMEM((2,) + block, BF16),
            pltpu.SemaphoreType.DMA((4,)),
            pltpu.SemaphoreType.DMA((4,)),
            pltpu.SemaphoreType.DMA((2, 2)),
            pltpu.SemaphoreType.DMA((2, 2)),
            pltpu.SemaphoreType.DMA((2,)),
            pltpu.SemaphoreType.DMA((2,)),
        ],
        cost_estimate=BRIEF,
        compiler_params=pltpu.CompilerParams(
            collective_id=call_id, has_side_effects=True, vmem_limit_bytes=60 << 20
        ),
    )(*operands)


def widen_back_rows(refs, rows):
    dg_ref, du_ref, w_ref = refs
    total = None
    for i in range(w_ref.shape[0]):
        part = dot_nt(dg_ref[i, rows], w_ref[i, 0]) + dot_nt(du_ref[i, rows], w_ref[i, 1])
        total = part if total is None else total + part
    return total


def project_back_rows(refs, rows):
    d_ref, w_ref = refs
    return dot_nt(d_ref[rows], w_ref[...])


def mix_rows(refs, rows):
    h_ref, w_ref = refs
    total = None
    for i in range(w_ref.shape[0]):
        part = matmul(h_ref[i, rows], w_ref[i])
        total = part if total is None else total + part
    return total


def twin_kernel(compute, count, *refs):
    operands, (o_ref, corner_ref, x_ref, y_ref) = refs[:count], refs[count : count + 4]
    acc, mine, away, twin, tsend, trecv = refs[count + 4 :]
    chip, core = place()
    stage = pl.program_id(0)
    rows = o_ref.shape[0]

    def copy(s):
        return remote(away.at[s], twin.at[s], tsend.at[s], trecv.at[s], chip, 1 - core)

    def both(s):
        copy(s).wait_recv()
        return mine[s].astype(F32) + twin[s].astype(F32)

    @pl.when(stage == 0)
    def _():
        greet([(chip, 1 - core)])

    target = jnp.bitwise_xor(chip, stage_step(stage)) * 2 * rows
    acc[...] = compute(operands, pl.ds(pl.multiple_of(target, 2 * rows), 2 * rows))
    mine[stage] = acc[pl.ds(pl.multiple_of(core * rows, rows), rows)].astype(BF16)
    away[stage] = acc[pl.ds(pl.multiple_of((1 - core) * rows, rows), rows)].astype(BF16)
    copy(stage).start()

    for s, part_ref in enumerate((corner_ref, x_ref, y_ref)):

        @pl.when(stage == s + 1)
        def _(s=s, part_ref=part_ref):
            part_ref[...] = both(s).astype(BF16)

    @pl.when(stage == 3)
    def _():
        o_ref[...] = both(3)
        for s in range(4):
            copy(s).wait_send()


def twin_reduce(compute, operands, rows, call_id):
    block = (rows, D)

    def held(shape):
        return pl.BlockSpec(shape, lambda s: (0,) * len(shape), pipeline_mode=pl.Buffered(1))

    return pl.pallas_call(
        functools.partial(twin_kernel, compute, len(operands)),
        out_shape=(jax.ShapeDtypeStruct(block, F32),) + (jax.ShapeDtypeStruct(block, BF16),) * 3,
        grid=(4,),
        in_specs=[held(x.shape) for x in operands],
        out_specs=(held(block),) * 4,
        scratch_shapes=[
            pltpu.VMEM((2 * rows, D), F32),
            pltpu.VMEM((4,) + block, BF16),
            pltpu.VMEM((4,) + block, BF16),
            pltpu.VMEM((4,) + block, BF16),
            pltpu.SemaphoreType.DMA((4,)),
            pltpu.SemaphoreType.DMA((4,)),
        ],
        cost_estimate=BRIEF,
        compiler_params=pltpu.CompilerParams(
            collective_id=call_id, has_side_effects=True, vmem_limit_bytes=60 << 20
        ),
    )(*operands)


def swap_others(parts):
    return tuple(swap_chips(part, step) for step, part in zip((3, 1, 2), parts))


def join(own, came):
    for part in came:
        own = own + part.astype(F32)
    return own


def entry_kernel(
    grps, chips, tok_ref, cot_ref, pack_ref, tile_ref, all_tok, all_cot, all_pack, all_tile,
    tsend, trecv, tlocal, csend, crecv, clocal, psend, precv, plocal, zrecv, usend, dsend,
):
    grp = lax.axis_index("grp")
    chip, core = place()
    me = chip * 2 + core
    above, below = lax.rem(grp + 1, grps), lax.rem(grp + grps - 1, grps)
    near = [(flip(chip, s, chips), c) for s in range(1, chips) for c in (core, 1 - core)]
    near = near + [(chip, 1 - core)]
    barrier = pltpu.get_barrier_semaphore()
    for g in (above, below):
        pl.semaphore_signal(barrier, inc=1, device_id={"grp": g}, device_id_type=MESH)
    for to, c in near:
        pl.semaphore_signal(
            barrier, inc=1, device_id={"chip": to, "core": c}, device_id_type=MESH
        )
    pl.semaphore_wait(barrier, len(near) + 2)

    tok = Gather(chips, False, tok_ref, all_tok, tsend, trecv, tlocal)
    cot = Gather(chips, False, cot_ref, all_cot, csend, crecv, clocal)
    packs, mine = [], []
    for i, (to, c) in enumerate(near):
        copy = remote(
            pack_ref.at[to * 2 + c], all_pack.at[grp, me], psend.at[0, i], precv.at[0, me], to, c
        )
        copy.start()
        packs.append(copy)
        copy = remote(tile_ref, all_tile.at[grp, me], psend.at[1, i], precv.at[1, me], to, c)
        copy.start()
        packs.append(copy)
    for k, (src, dst) in enumerate(((pack_ref.at[me], all_pack), (tile_ref, all_tile))):
        mine.append(pltpu.make_async_copy(src, dst.at[grp, me], plocal.at[k]))
        mine[k].start()
    tok.start()
    for to, c in near:
        slot = to * 2 + c
        for k, (src, dst) in enumerate(((pack_ref.at[me], all_pack), (tile_ref, all_tile))):
            remote(src, dst.at[grp, slot], psend.at[k, 0], precv.at[k, slot], to, c).wait_recv()
    for copy in mine:
        copy.wait()

    def z_copies(block, sems, step, to):
        return [
            pltpu.make_async_remote_copy(
                src_ref=whole.at[block],
                dst_ref=whole.at[block],
                send_sem=sems.at[k, step],
                recv_sem=zrecv.at[k, block],
                device_id={"grp": to},
                device_id_type=MESH,
            )
            for k, whole in enumerate((all_pack, all_tile))
        ]

    has_above, has_below = grp + 1 < grps, grp > 0

    def send(step, block, up):
        @pl.when(has_above if up else has_below)
        def _():
            for copy in z_copies(block, usend if up else dsend, step, above if up else below):
                copy.start()

    def relay(step):
        low, high = grp - step, grp + step

        @pl.when(low >= 0)
        def _():
            for copy in z_copies(low, usend, 0, below):
                copy.wait_recv()
            send(step, low, True)

        @pl.when(high < grps)
        def _():
            for copy in z_copies(high, dsend, 0, above):
                copy.wait_recv()
            send(step, high, False)

    send(0, grp, True)
    send(0, grp, False)
    tok.relay(0, 4)
    relay(1)
    cot.start()
    tok.relay(4, None)
    for step in range(2, grps - 1):
        relay(step)
    cot.relay(0, 4)
    if grps > 2:
        relay(grps - 1)
    cot.relay(4, None)
    tok.finish()
    cot.finish()
    for copy in packs:
        copy.wait_send()
    for step in range(grps):
        for up in (True, False):
            held = grp - step >= 0 if up else grp + step < grps

            @pl.when(held & (has_above if up else has_below))
            def _(step=step, up=up):
                block = grp - step if up else grp + step
                sems, to = (usend, above) if up else (dsend, below)
                for copy in z_copies(block, sems, step, to):
                    copy.wait_send()


def entry(tokens, cotangent, packed, tile, grps, chips, call_id):
    devs = 2 * chips
    return pl.pallas_call(
        functools.partial(entry_kernel, grps, chips),
        out_shape=(
            jax.ShapeDtypeStruct((devs,) + tokens.shape, BF16),
            jax.ShapeDtypeStruct((devs,) + cotangent.shape, BF16),
            jax.ShapeDtypeStruct((grps,) + packed.shape, BF16),
            jax.ShapeDtypeStruct((grps, devs) + tile.shape, BF16),
        ),
        in_specs=[ANY] * 4,
        out_specs=(ANY,) * 4,
        scratch_shapes=gather_sems(chips)
        + gather_sems(chips)
        + [
            pltpu.SemaphoreType.DMA((2, devs)),
            pltpu.SemaphoreType.DMA((2, devs)),
            pltpu.SemaphoreType.DMA((2,)),
            pltpu.SemaphoreType.DMA((2, grps)),
            pltpu.SemaphoreType.DMA((2, grps)),
            pltpu.SemaphoreType.DMA((2, grps)),
        ],
        cost_estimate=BRIEF,
        compiler_params=pltpu.CompilerParams(collective_id=call_id, has_side_effects=True),
    )(tokens, cotangent, packed, tile)


def project_kernel(width, x_ref, w_ref, tile_ref, n_ref, qkv_ref, gain_ref):
    @pl.when(pl.program_id(0) == 0)
    def _():
        gain_ref[...] = jnp.zeros_like(gain_ref)
        for f in range(tile_ref.shape[0]):
            gain_ref[0:2, f * width : (f + 1) * width] = tile_ref[f, 0:2, :width].astype(F32)

    values = x_ref[...].astype(F32)
    factor = lax.rsqrt(jnp.mean(values * values, axis=-1, keepdims=True) + EPSILON)
    normed = (values * factor * gain_ref[0:1]).astype(BF16)
    n_ref[...] = normed
    qkv_ref[...] = matmul(normed, w_ref[...]).astype(BF16)


def project(tokens, weights, tiles):
    count, depth = tokens.shape
    used = weights.shape[1]
    rows = tile_rows(count, 256)
    return pl.pallas_call(
        functools.partial(project_kernel, depth // tiles.shape[0]),
        out_shape=(
            jax.ShapeDtypeStruct((count, depth), BF16),
            jax.ShapeDtypeStruct((count, used), BF16),
            jax.ShapeDtypeStruct((8, depth), F32),
        ),
        grid=(count // rows,),
        in_specs=[
            pl.BlockSpec((rows, depth), lambda r: (r, 0)),
            pl.BlockSpec(weights.shape, lambda r: (0, 0)),
            pl.BlockSpec(tiles.shape, lambda r: (0, 0, 0)),
        ],
        out_specs=(
            pl.BlockSpec((rows, depth), lambda r: (r, 0)),
            pl.BlockSpec((rows, used), lambda r: (r, 0)),
            pl.BlockSpec((8, depth), lambda r: (0, 0)),
        ),
        cost_estimate=BRIEF,
        compiler_params=params(1),
    )(tokens, weights, tiles)


def turn_kernel(
    count, res_ref, dn_ref, cot_ref, gain_ref, branch_ref, own_ref, *refs
):
    came, (att_ref, w_ref, lay_ref, dres_ref, tot_ref, datt_ref, *grad_refs, dba) = refs[:count], refs[count:]

    @pl.when(pl.program_id(0) == 0)
    def _():
        residual = res_ref[...]
        mlp = own_ref[...]
        for part_ref in came:
            mlp = mlp + part_ref[...].astype(F32)
        mlp = RESID_MULT * mlp
        layer_out = residual + mlp
        lay_ref[...] = layer_out.astype(BF16)
        attn = RESID_MULT * branch_ref[...]
        grad = dn_ref[...]
        scaled = gain_ref[1:2] * grad
        factor = lax.rsqrt(jnp.mean(residual * residual, axis=-1, keepdims=True) + EPSILON)
        inner = jnp.mean(residual * scaled, axis=-1, keepdims=True)
        d_residual = cot_ref[...].astype(F32) + factor * scaled
        d_residual = d_residual - residual * (factor * factor * factor * inner)
        dres_ref[...] = d_residual
        dba[...] = (RESID_MULT * d_residual).astype(BF16)
        d_gain = jnp.sum(grad * residual * factor, axis=0, keepdims=True)
        width = tot_ref.shape[1]
        tot_ref[...] = jnp.zeros_like(tot_ref)
        for r in range(pl.cdiv(D, width)):
            last = min(width, D - r * width)
            tot_ref[r : r + 1, :last] = d_gain[:, r * width : r * width + last]
        lane = lax.broadcasted_iota(jnp.int32, (1, 128), 1)
        row = jnp.zeros((1, 128), F32)
        for i, part in enumerate((layer_out, attn, mlp)):
            square = jnp.sum(jnp.sum(part * part, axis=0, keepdims=True), axis=1, keepdims=True)
            row = jnp.where(lane == i, square, row)
        tot_ref[7:8, :128] = row

    datt_ref[...] = dot_nt(dba[...], w_ref[...]).astype(BF16)
    grad = matmul(att_ref[...].T, dba[...])
    if len(grad_refs) == 1:
        grad_refs[0][...] = grad.astype(BF16)
        return
    mine_ref, away_ref = grad_refs
    first = lax.axis_index("core") == 0
    width = mine_ref.shape[2]
    for i in range(mine_ref.shape[1]):
        even = grad[2 * i * width : (2 * i + 1) * width]
        odd = grad[(2 * i + 1) * width : (2 * i + 2) * width]
        mine_ref[0, i] = jnp.where(first, even, odd).astype(BF16)
        away_ref[0, i] = jnp.where(first, odd, even).astype(BF16)


def turn(residual, d_normed, cotangent, gains, branch, own, came, attended, weights, width):
    rows = residual.shape[0]
    cols = 4 * width if came else 256
    scratch = [pltpu.VMEM((rows, D), BF16)]
    grads = (jax.ShapeDtypeStruct((D, D), BF16),)
    grad_specs = (pl.BlockSpec((cols, D), lambda j: (j, 0)),)
    if came:
        half = (D // (8 * width), 4, width, D)
        grads = (jax.ShapeDtypeStruct(half, BF16),) * 2
        grad_specs = (pl.BlockSpec((1, 2, width, D), lambda j: (j // 2, j % 2, 0, 0)),) * 2
    flat = jax.ShapeDtypeStruct((rows, D), F32)

    def held(shape):
        return pl.BlockSpec(shape, lambda j: (0,) * len(shape), pipeline_mode=pl.Buffered(1))

    return pl.pallas_call(
        functools.partial(turn_kernel, len(came)),
        out_shape=(
            jax.ShapeDtypeStruct((rows, D), BF16),
            flat,
            jax.ShapeDtypeStruct((8, 3 * D // 16), F32),
            jax.ShapeDtypeStruct((rows, D), BF16),
        )
        + grads,
        grid=(D // cols,),
        in_specs=[held((rows, D))] * 3
        + [held((8, D))]
        + [held((rows, D))] * (2 + len(came))
        + [
            pl.BlockSpec((rows, cols), lambda j: (0, j)),
            pl.BlockSpec((cols, D), lambda j: (j, 0)),
        ],
        out_specs=(
            held((rows, D)),
            held((rows, D)),
            held((8, 3 * D // 16)),
            pl.BlockSpec((rows, cols), lambda j: (0, j)),
        )
        + grad_specs,
        scratch_shapes=scratch,
        cost_estimate=BRIEF,
        compiler_params=params(1),
    )(residual, d_normed, cotangent, gains, branch, own, *came, attended, weights)


def split_kernel(copies, q_cols, kv_cols, x_ref, wq_ref, wk_ref, wv_ref, q_ref, k_ref, v_ref, sum_ref):
    total = jnp.zeros(sum_ref.shape, F32)
    for s in range(x_ref.shape[0]):
        block = x_ref[s].astype(F32)
        at = slice(s * q_cols, (s + 1) * q_cols)
        q_ref[:, at] = block[:, :q_cols]
        weight = wq_ref[:, at].astype(F32)
        total += jnp.sum(block[:, :q_cols] * weight, axis=1, keepdims=True)
    for h in range(x_ref.shape[0] // copies):
        at = slice(h * kv_cols, (h + 1) * kv_cols)
        pair = x_ref[h * copies, :, q_cols:].astype(F32)
        for c in range(1, copies):
            pair += x_ref[h * copies + c, :, q_cols:].astype(F32)
        for ref, w_ref, part in (
            (k_ref, wk_ref, pair[:, :kv_cols]),
            (v_ref, wv_ref, pair[:, kv_cols:]),
        ):
            ref[:, at] = part
            total += jnp.sum(part * w_ref[:, at].astype(F32), axis=1, keepdims=True)
    sum_ref[...] = total


def split(sent, w_query, w_key, w_value, copies, q_cols, kv_cols):
    rows = w_query.shape[0]
    return pl.pallas_call(
        functools.partial(split_kernel, copies, q_cols, kv_cols),
        out_shape=tuple(
            jax.ShapeDtypeStruct(shape, F32)
            for shape in (w_query.shape, w_key.shape, w_value.shape, (rows, 1))
        ),
        in_specs=[VMEM] * 4,
        out_specs=(VMEM,) * 4,
        cost_estimate=BRIEF,
    )(sent, w_query, w_key, w_value)


def norm_parts(values):
    factor = lax.rsqrt(jnp.mean(values * values, axis=-1, keepdims=True) + EPSILON)
    return factor


def norm_back(values, factor, gain, grad):
    scaled = gain * grad
    inner = jnp.mean(values * scaled, axis=-1, keepdims=True)
    return factor * scaled - values * (factor * factor * factor * inner), jnp.sum(
        grad * values * factor, axis=0
    )


def on_device(
    tokens,
    block_group,
    block_slot,
    attn_gain,
    w_query,
    w_key,
    w_value,
    w_out,
    mlp_gain,
    w_gate,
    w_up,
    w_down,
    cotangent,
):
    grps = lax.axis_size("grp")
    devs = lax.axis_size(PLANE)
    chips = devs // 2
    rows = tokens.shape[0]
    w_rows = w_query.shape[0]
    q_heads = HEADS // devs
    kv_heads = 1
    assert devs % KV_HEADS == 0
    kv_copies = max(1, devs // KV_HEADS)
    q_cols, kv_cols = q_heads * HEAD_DIM, kv_heads * HEAD_DIM
    row_blocks = rows // BLOCK * devs
    row_groups = row_blocks // GROUP_BLOCKS

    row_first = lax.axis_index("grp") * row_blocks
    keys = lax.dynamic_slice_in_dim(block_group, row_first, row_blocks) * GROUP_BLOCKS
    keys = keys + lax.dynamic_slice_in_dim(block_slot, row_first, row_blocks)
    rank = jnp.sum((keys[None, :] < keys[:, None]).astype(jnp.int32), axis=1)
    ids = jnp.arange(row_blocks, dtype=jnp.int32)
    order = jnp.sum(jnp.where(rank[None, :] == ids[:, None], ids[None, :], 0), axis=1)

    def kv_split(w):
        w = w.reshape(w_rows, devs // kv_copies, kv_cols)
        return jnp.repeat(w, kv_copies, axis=1) if kv_copies > 1 else w

    packed = jnp.concatenate(
        [w_query.reshape(w_rows, devs, q_cols), kv_split(w_key), kv_split(w_value)], axis=2
    )
    packed = jnp.swapaxes(packed, 0, 1)
    used = q_cols + 2 * kv_cols
    tile = jnp.pad(jnp.stack([attn_gain, mlp_gain]), ((0, 14), (0, 128 - w_rows)))
    out_full = gather(w_out[None], "grp")
    upstream = cotangent.astype(F32)
    d_branch_mlp = (RESID_MULT * upstream).astype(BF16)
    all_tokens, d_branch_mlp, w_qkv, tiles = entry(
        tokens, d_branch_mlp, packed, tile, grps, chips, 2
    )
    w_qkv, tiles = w_qkv.reshape(D, used), tiles.reshape(-1, 16, 128)
    normed_one, qkv, gains = project(all_tokens.reshape(devs * rows, D), w_qkv, tiles)
    gain_one, gain_two = gains[0], gains[1]
    d_branch_mlp = d_branch_mlp.reshape(devs * rows, D)
    attended = attend(qkv, order, q_heads)
    attended = plane_exchange(
        attended, (rows, D), by_rows(rows), by_cols(q_cols), chips, 3
    )

    out_full = plane_gather(out_full, chips, 4, inner=True).reshape(D, D)
    layer_in = tokens.astype(F32)
    branch_attn = matmul(attended, out_full)
    residual = layer_in + RESID_MULT * branch_attn
    factor_two = norm_parts(residual)
    normed_two = (residual * factor_two * gain_two).astype(BF16)
    normed_two = plane_gather(normed_two, chips, 1).reshape(devs * rows, D)
    wide_w = gather(jnp.stack([w_gate, w_up])[None], "grp")
    down_w = gather(w_down[None], "grp")
    hidden, hidden_t, silu, slope, normed_t = widen(normed_two, wide_w)
    part_down = down_part(hidden_t, d_branch_mlp)
    part_down, hidden, silu = lax.optimization_barrier((part_down, hidden, silu))
    grad_down = scatter(part_down, "grp")
    if chips == 4:
        branch_mlp, *shares = twin_reduce(mix_rows, (hidden, down_w), rows, 11)
        shares, silu = lax.optimization_barrier((shares, silu))
        shares = swap_others(shares)
    d_gate, d_up = narrow_back(silu, slope, d_branch_mlp, down_w)
    if chips == 4:
        part_wide = widen_part(normed_t, d_gate, d_up)
        part_wide, shares, d_gate, d_up = lax.optimization_barrier(
            (part_wide, shares, d_gate, d_up)
        )
        grad_wide = scatter(part_wide, "grp")
        d_normed_two = square_reduce(widen_back_rows, (d_gate, d_up, wide_w), rows, 10)
    else:
        part_wide = widen_part(normed_t, d_gate, d_up)
        part_wide, d_gate, d_up = lax.optimization_barrier((part_wide, d_gate, d_up))
        grad_wide = scatter(part_wide, "grp")
        d_normed_two = widen_back(d_gate, d_up, wide_w)
        d_normed_two = plane_reduce(d_normed_two.reshape(devs, rows, D), chips, 5)
        branch_mlp = mix(hidden, down_w)
        branch_mlp = plane_reduce(branch_mlp.reshape(devs, rows, D), chips, 5)

    layer_out, d_residual, totals, d_attended, grad_out, *away = turn(
        residual,
        d_normed_two,
        cotangent,
        gains,
        branch_attn,
        branch_mlp,
        shares if chips == 4 else (),
        attended,
        out_full,
        w_rows,
    )
    if chips == 4:
        drift_out = Drift(grad_out, *away)
    d_attended, totals = exchange_total(
        d_attended, totals, (devs * rows, q_cols), rows, q_cols, grps, chips, 7
    )
    if chips == 4:
        sent_out, d_attended = lax.optimization_barrier((drift_out.parts(), d_attended))
        sent_out = swap_others(sent_out)
    d_attended, grad_down = lax.optimization_barrier((d_attended, grad_down))
    d_qkv = attend_back(qkv, d_attended, order, q_heads)
    if chips == 4:
        sent_out, d_qkv = lax.optimization_barrier((sent_out, d_qkv))
    sent = over_rows(normed_one, d_qkv).astype(BF16)
    sent, d_qkv, grad_wide = lax.optimization_barrier((sent, d_qkv, grad_wide))
    sent = scatter(sent, "grp")
    d_normed_one = over_cols(d_qkv, w_qkv).astype(BF16).reshape(devs, rows, D)
    if chips == 4:
        sent_out, d_normed_one = lax.optimization_barrier((sent_out, d_normed_one))
        grad_out = join(drift_out.own, sent_out).astype(BF16)
    else:
        grad_out = plane_reduce(
            grad_out.reshape(grps, devs, w_rows, D), chips, 6, dtype=BF16, inner=True
        )
    grad_out, d_normed_one = lax.optimization_barrier((grad_out, d_normed_one))
    grad_out = scatter(grad_out, "grp")
    d_normed_one = plane_reduce(d_normed_one, chips, 5)
    d_normed_one, sent = lax.optimization_barrier((d_normed_one, sent))
    d_input_norm, _ = norm_back(layer_in, norm_parts(layer_in), gain_one, d_normed_one)
    tokens_grad = (d_residual + d_input_norm).astype(BF16)
    sent = sent.reshape(devs, w_rows, q_cols + 2 * kv_cols)
    sent = plane_exchange(sent, sent.shape, by_slot, by_slot, chips, 9)
    sent, grad_out = lax.optimization_barrier((sent, grad_out))
    grad_out = grad_out.reshape(w_rows, D).astype(F32)

    grad_query, grad_key, grad_value, gain_sum = split(
        sent, w_query, w_key, w_value, kv_copies, q_cols, kv_cols
    )
    gain_one_grad = gain_sum[:, 0] / attn_gain.astype(F32)
    rms_stats = jnp.sqrt(totals[7, :3] / (rows * grps * devs * D))
    gain_first = (lax.axis_index("grp") * devs + lax.axis_index(PLANE)) * w_rows
    gain_two_grad = lax.dynamic_slice(totals.reshape(-1), (gain_first,), (w_rows,))
    return (
        layer_out,
        tokens_grad,
        gain_one_grad,
        grad_query,
        grad_key,
        grad_value,
        grad_out,
        gain_two_grad,
        grad_wide[0, 0].astype(F32),
        grad_wide[0, 1].astype(F32),
        grad_down[0].astype(F32),
        rms_stats,
    )


def solution(mesh):
    shape = (mesh.shape["grp"], mesh.shape["blk"] // 2, 2)
    mesh = Mesh(mesh.devices.reshape(shape), EVERY)
    row, col, vec = P(EVERY, None), P(None, EVERY), P(EVERY)
    return jax.shard_map(
        on_device,
        mesh=mesh,
        in_specs=(row, P(), P(), vec, row, row, row, row, vec, col, col, row, row),
        out_specs=(row, row, vec, row, row, row, row, vec, col, col, row, P()),
        check_vma=False,
    )
```

```python
import functools

import jax
import jax.numpy as jnp
from jax import lax
from jax.experimental import pallas as pl
from jax.experimental.pallas import tpu as pltpu
from jax.sharding import Mesh
from jax.sharding import PartitionSpec as P

D = 2048
HEADS = 32
KV_HEADS = 8
HEAD_DIM = 64
BLOCK = 128
PROMPT_BLOCKS = 8
GROUP_BLOCKS = 16
PER_GROUP = HEADS // KV_HEADS

ATTN_MULT = 0.015625
RESID_MULT = 0.22
EPSILON = 1e-05
MASKED = -1e30

PLANE = ("chip", "core")
EVERY = ("grp", "chip", "core")
BF16 = jnp.bfloat16
F32 = jnp.float32


MESH = pl.DeviceIdType.MESH
BRIEF = pl.CostEstimate(flops=1000, bytes_accessed=1000, transcendentals=0)
ANY = pl.BlockSpec(memory_space=pl.ANY)
VMEM = pl.BlockSpec(memory_space=pltpu.VMEM)


def place():
    return lax.axis_index("chip"), lax.axis_index("core")


def flip(chip, step, chips):
    return jnp.bitwise_xor(chip, step) if chips == 4 else lax.rem(chip + step, chips)


def unflip(chip, step, chips):
    return jnp.bitwise_xor(chip, step) if chips == 4 else lax.rem(chip + chips - step, chips)


def greet(peers):
    barrier = pltpu.get_barrier_semaphore()
    for chip, core in peers:
        pl.semaphore_signal(
            barrier, inc=1, device_id={"chip": chip, "core": core}, device_id_type=MESH
        )
    pl.semaphore_wait(barrier, len(peers))


def remote(src, dst, send, recv, chip, core):
    return pltpu.make_async_remote_copy(
        src_ref=src,
        dst_ref=dst,
        send_sem=send,
        recv_sem=recv,
        device_id={"chip": chip, "core": core},
        device_id_type=MESH,
    )


class Gather:
    def __init__(self, chips, inner, x_ref, o_ref, send, recv, local):
        self.chips, self.inner, self.x, self.o = chips, inner, x_ref, o_ref
        self.send, self.recv, self.local = send, recv, local
        self.chip, self.core = place()
        self.half = x_ref.shape[0] // 2
        self.started = []

    def greet(self):
        steps = (1, 2) if self.chips == 4 else range(1, self.chips)
        peers = [(flip(self.chip, s, self.chips), self.core) for s in steps]
        greet(peers + [(self.chip, 1 - self.core)])

    def piece(self, slot, h):
        at = pl.ds(h * self.half, self.half)
        return self.o.at[at, slot] if self.inner else self.o.at[slot, at]

    def own(self, h):
        return self.x.at[pl.ds(h * self.half, self.half)]

    def slot(self, chip, core):
        return chip * 2 + core

    def push(self, src, slot, h, chip, core):
        i = len(self.started)
        copy = remote(src, self.piece(slot, h), self.send.at[i], self.recv.at[slot, h], chip, core)
        copy.start()
        self.started.append(copy)

    def wait_for(self, slot, h):
        remote(
            self.own(h), self.piece(slot, h), self.send.at[0], self.recv.at[slot, h],
            self.chip, 1 - self.core,
        ).wait_recv()

    def start(self):
        me = self.slot(self.chip, self.core)
        if self.chips == 4:
            for h, s in ((0, 1), (1, 2), (1, 1), (0, 2)):
                self.push(self.own(h), me, h, flip(self.chip, s, 4), self.core)
        else:
            for s in range(1, self.chips):
                for h in range(2):
                    self.push(self.own(h), me, h, flip(self.chip, s, self.chips), self.core)
        for h in range(2):
            self.push(self.own(h), me, h, self.chip, 1 - self.core)
        whole = self.o.at[:, me] if self.inner else self.o.at[me]
        self.mine = pltpu.make_async_copy(self.x, whole, self.local)
        self.mine.start()

    def relay(self, first=0, last=None):
        if self.chips == 4:
            plan = ((1, 0, 2), (2, 1, 1), (1, 1, 0), (2, 0, 0), (3, 0, 0), (3, 1, 0))
        else:
            plan = tuple((s, h, 0) for s in range(1, self.chips) for h in range(2))
        for s, h, onward in plan[first:last]:
            slot = self.slot(unflip(self.chip, s, self.chips), self.core)
            self.wait_for(slot, h)
            if onward:
                self.push(self.piece(slot, h), slot, h, flip(self.chip, onward, 4), self.core)
            self.push(self.piece(slot, h), slot, h, self.chip, 1 - self.core)

    def finish(self):
        for s in range(self.chips):
            slot = self.slot(unflip(self.chip, s, self.chips), 1 - self.core)
            for h in range(2):
                self.wait_for(slot, h)
        for copy in self.started:
            copy.wait_send()
        self.mine.wait()


def gather_sems(chips):
    return [
        pltpu.SemaphoreType.DMA((4 * chips + 4,)),
        pltpu.SemaphoreType.DMA((2 * chips, 2)),
        pltpu.SemaphoreType.DMA,
    ]


def gather_kernel(chips, inner, x_ref, o_ref, *sems):
    run = Gather(chips, inner, x_ref, o_ref, *sems)
    run.greet()
    run.start()
    run.relay()
    run.finish()


def plane_gather(x, chips, call_id, inner=False):
    devs = 2 * chips
    shape = (x.shape[0], devs) + x.shape[1:] if inner else (devs,) + x.shape
    return pl.pallas_call(
        functools.partial(gather_kernel, chips, inner),
        out_shape=jax.ShapeDtypeStruct(shape, x.dtype),
        in_specs=[ANY],
        out_specs=ANY,
        scratch_shapes=gather_sems(chips),
        cost_estimate=BRIEF,
        compiler_params=pltpu.CompilerParams(collective_id=call_id, has_side_effects=True),
    )(x)


def reduce_kernel(chips, inner, p_ref, o_ref, total, mine, twin, moved, corner, landed, lsem, tsend, trecv, msend, mrecv, csend, crecv):
    chip, core = place()
    sib = 1 - core
    half = (p_ref.shape[0] if inner else p_ref.shape[1]) // 2
    block = (lambda slot: p_ref.at[:, slot]) if inner else (lambda slot: p_ref.at[slot])
    steps = (1, 2) if chips == 4 else tuple(range(1, chips))
    peers = [(flip(chip, s, chips), core) for s in steps]
    greet(peers + [(chip, sib)])
    order = (3, 1, 2, 0) if chips == 4 else tuple(range(1, chips)) + (0,)
    loads, twins = {}, {}
    for s in order:
        to = flip(chip, s, chips) * 2
        twins[s] = remote(block(to + sib), twin.at[s], tsend.at[s], trecv.at[s], chip, sib)
        twins[s].start()
        loads[s] = pltpu.make_async_copy(block(to + core), mine.at[s], lsem.at[s])
        loads[s].start()

    def part(s, h):
        at = pl.ds(h * half, half)
        return mine[s, at].astype(F32) + twin[s, at].astype(F32)

    def ready(s):
        loads[s].wait()
        twins[s].wait_recv()

    sent = []
    if chips == 4:
        corners = []
        ready(3)
        for h, s in ((0, 1), (1, 2)):
            moved[3, pl.ds(h * half, half)] = part(3, h).astype(BF16)
            copy = remote(moved.at[3, pl.ds(h * half, half)], corner.at[h], csend.at[h], crecv.at[h], flip(chip, s, 4), core)
            copy.start()
            corners.append(copy)

        def send(s, h):
            at = pl.ds(h * half, half)
            copy = remote(moved.at[s, at], landed.at[s - 1, at], msend.at[s - 1, h], mrecv.at[s - 1, h], flip(chip, s, 4), core)
            copy.start()
            sent.append(copy)

        for s, h in ((1, 0), (2, 1)):
            ready(s)
            moved[s, pl.ds(h * half, half)] = part(s, h).astype(BF16)
            send(s, h)
        for s, h in ((2, 0), (1, 1)):
            corners[h].wait_recv()
            moved[s, pl.ds(h * half, half)] = (part(s, h) + corner[h].astype(F32)).astype(BF16)
            send(s, h)
        for copy in corners:
            copy.wait_send()
    else:
        for s in steps:
            ready(s)
            for h in range(2):
                at = pl.ds(h * half, half)
                moved[s, at] = part(s, h).astype(BF16)
                copy = remote(moved.at[s, at], landed.at[s - 1, at], msend.at[s - 1, h], mrecv.at[s - 1, h], flip(chip, s, chips), core)
                copy.start()
                sent.append(copy)
    ready(0)
    for h in range(2):
        total[pl.ds(h * half, half)] = part(0, h)
    for copy in sent:
        copy.wait()
    for s in steps[:-1]:
        total[...] += landed[s - 1].astype(F32)
    o_ref[...] = (total[...] + landed[steps[-1] - 1].astype(F32)).astype(o_ref.dtype)
    for s in order:
        twins[s].wait_send()


def plane_reduce(p, chips, call_id, dtype=F32, inner=False):
    block = (p.shape[0],) + p.shape[2:] if inner else p.shape[1:]
    steps = 2 if chips == 4 else chips - 1
    return pl.pallas_call(
        functools.partial(reduce_kernel, chips, inner),
        out_shape=jax.ShapeDtypeStruct(block, dtype),
        in_specs=[ANY],
        out_specs=VMEM,
        scratch_shapes=[
            pltpu.VMEM(block, F32),
            pltpu.VMEM((chips,) + block, BF16),
            pltpu.VMEM((chips,) + block, BF16),
            pltpu.VMEM((chips,) + block, BF16),
            pltpu.VMEM((2, block[0] // 2) + block[1:], BF16),
            pltpu.VMEM((steps,) + block, BF16),
            pltpu.SemaphoreType.DMA((chips,)),
            pltpu.SemaphoreType.DMA((chips,)),
            pltpu.SemaphoreType.DMA((chips,)),
            pltpu.SemaphoreType.DMA((steps, 2)),
            pltpu.SemaphoreType.DMA((steps, 2)),
            pltpu.SemaphoreType.DMA((2,)),
            pltpu.SemaphoreType.DMA((2,)),
        ],
        cost_estimate=BRIEF,
        compiler_params=pltpu.CompilerParams(
            collective_id=call_id, has_side_effects=True, vmem_limit_bytes=56 << 20
        ),
    )(p)


def swap_chips(values, step):
    return lax.ppermute(values, "chip", [(c, c ^ step) for c in range(4)])


class Drift:
    def __init__(self, mine, away):
        self.mine = mine
        self.twin = lax.ppermute(away, "core", [(0, 1), (1, 0)])

    def parts(self):
        self.own, *others = twin_add(self.mine, self.twin)
        return others


def twin_add_kernel(mine_ref, twin_ref, *refs):
    chip = lax.axis_index("chip")
    for step, ref in zip((0, 3, 1, 2), refs):
        at = jnp.bitwise_xor(chip, step)
        ref[0] = (mine_ref[0, at].astype(F32) + twin_ref[0, at].astype(F32)).astype(ref.dtype)


def twin_add(mine, twin):
    grps, _, rows, cols = mine.shape
    spec = pl.BlockSpec((1, 4, rows, cols), lambda g: (g, 0, 0, 0))
    part_spec = pl.BlockSpec((1, rows, cols), lambda g: (g, 0, 0))
    part = (grps, rows, cols)
    return pl.pallas_call(
        twin_add_kernel,
        out_shape=(jax.ShapeDtypeStruct(part, F32),) + (jax.ShapeDtypeStruct(part, BF16),) * 3,
        grid=(grps,),
        in_specs=[spec, spec],
        out_specs=(part_spec,) * 4,
        cost_estimate=BRIEF,
    )(mine, twin)


def exchange_kernel(chips, cut, paste, x_ref, o_ref, send, recv, local):
    chip, core = place()
    me = chip * 2 + core
    peers = [(flip(chip, s, chips), c) for s in range(1, chips) for c in (core, 1 - core)]
    peers = peers + [(chip, 1 - core)]
    greet(peers)
    far = [p for p in ([3, 1, 2] if chips == 4 else range(1, chips))]
    order = [(flip(chip, s, chips), c) for s in far for c in (core, 1 - core)] + [(chip, 1 - core)]
    copies = []
    for i, (to, c) in enumerate(order):
        copy = remote(cut(x_ref, to * 2 + c), paste(o_ref, me), send.at[i], recv.at[me], to, c)
        copy.start()
        copies.append(copy)
    mine = pltpu.make_async_copy(cut(x_ref, me), paste(o_ref, me), local)
    mine.start()
    for s in far:
        for c in (core, 1 - core):
            slot = unflip(chip, s, chips) * 2 + c
            remote(cut(x_ref, me), paste(o_ref, slot), send.at[0], recv.at[slot], chip, 1 - core).wait_recv()
    slot = chip * 2 + 1 - core
    remote(cut(x_ref, me), paste(o_ref, slot), send.at[0], recv.at[slot], chip, 1 - core).wait_recv()
    for copy in copies:
        copy.wait_send()
    mine.wait()


def plane_exchange(x, shape, cut, paste, chips, call_id):
    return pl.pallas_call(
        functools.partial(exchange_kernel, chips, cut, paste),
        out_shape=jax.ShapeDtypeStruct(shape, x.dtype),
        in_specs=[ANY],
        out_specs=ANY,
        scratch_shapes=[
            pltpu.SemaphoreType.DMA((2 * chips,)),
            pltpu.SemaphoreType.DMA((2 * chips,)),
            pltpu.SemaphoreType.DMA,
        ],
        cost_estimate=BRIEF,
        compiler_params=pltpu.CompilerParams(collective_id=call_id, has_side_effects=True),
    )(x)


def by_slot(ref, dev):
    return ref.at[dev]


def by_rows(rows):
    return lambda ref, dev: ref.at[pl.ds(pl.multiple_of(dev * rows, rows), rows)]


def by_cols(cols):
    return lambda ref, dev: ref.at[:, pl.ds(pl.multiple_of(dev * cols, cols), cols)]


def matmul(left, right):
    return jnp.dot(left, right, preferred_element_type=F32)


def over_rows(left, right):
    return lax.dot_general(left, right, (((0,), (0,)), ((), ())), preferred_element_type=F32)


def over_cols(left, right):
    return lax.dot_general(left, right, (((1,), (1,)), ((), ())), preferred_element_type=F32)


def gather(values, axes, axis=0):
    return lax.all_gather(values, axes, axis=axis, tiled=True)


def scatter(values, axes, axis=0):
    return lax.psum_scatter(values, axes, scatter_dimension=axis, tiled=True)


def dot_nt(left, right):
    return lax.dot_general(left, right, (((1,), (1,)), ((), ())), preferred_element_type=F32)


def head_stack(values, heads):
    col_head = lax.broadcasted_iota(jnp.int32, values.shape, 1) // HEAD_DIM
    return jnp.concatenate(
        [jnp.where(col_head == h, values, jnp.zeros_like(values)) for h in range(heads)], axis=0
    )


def head_pick(stacked, heads):
    rows = stacked.shape[0] // heads
    col_head = lax.broadcasted_iota(jnp.int32, (rows, stacked.shape[1]), 1) // HEAD_DIM
    total = jnp.zeros((rows, stacked.shape[1]), F32)
    for h in range(heads):
        total = jnp.where(col_head == h, stacked[h * rows : (h + 1) * rows], total)
    return total


def head_fold(values, heads):
    total = values[:, :HEAD_DIM]
    for h in range(1, heads):
        total = total + values[:, h * HEAD_DIM : (h + 1) * HEAD_DIM]
    return total


def repeat_heads(values, heads):
    return jnp.concatenate([values] * heads, axis=1)


def own_rows(order_ref, slot):
    return pl.ds(pl.multiple_of(order_ref[slot] * BLOCK, BLOCK), BLOCK)


def load_prompt(heads, order_ref, qkv_ref, k_ref, v_ref, first):
    q_cols = heads * HEAD_DIM
    for s in range(PROMPT_BLOCKS):
        pair = qkv_ref[own_rows(order_ref, first + s), q_cols:]
        at = pl.ds(s * BLOCK, BLOCK)
        k_ref[at] = repeat_heads(pair[:, :HEAD_DIM], heads)
        v_ref[at] = repeat_heads(pair[:, HEAD_DIM:], heads)


def by_keys(slot, body):
    prompt = PROMPT_BLOCKS * BLOCK
    quarter = prompt // 4
    seen = jnp.minimum(slot, PROMPT_BLOCKS) * BLOCK
    for n in range(1, 5):
        low = (n - 1) * quarter if n > 1 else -1

        @pl.when((seen > low) & (seen <= n * quarter))
        def _(n=n):
            body(n * quarter)


def soft_parts(heads, slot, q_stack, k_far, k_own):
    far = dot_nt(k_far, q_stack)
    own = dot_nt(k_own, q_stack)
    limit = jnp.minimum(slot, PROMPT_BLOCKS) * BLOCK
    far = jnp.where(lax.broadcasted_iota(jnp.int32, far.shape, 0) < limit, far, MASKED)
    key = lax.broadcasted_iota(jnp.int32, own.shape, 0)
    row = lax.broadcasted_iota(jnp.int32, own.shape, 1) % BLOCK
    own = jnp.where(key <= row, own, MASKED)
    peak = jnp.maximum(jnp.max(far, axis=0, keepdims=True), jnp.max(own, axis=0, keepdims=True))
    far, own = jnp.exp(far - peak), jnp.exp(own - peak)
    scale = 1.0 / (jnp.sum(far, axis=0, keepdims=True) + jnp.sum(own, axis=0, keepdims=True))
    return far * scale, own * scale


def scaled_stack(q, heads):
    return head_stack((q.astype(F32) * ATTN_MULT).astype(BF16), heads)


def attend_kernel(heads, order_ref, qkv_ref, o_ref, k_ref, v_ref, vt_ref):
    first, slot = pl.program_id(0) * GROUP_BLOCKS, pl.program_id(1)
    q_cols = heads * HEAD_DIM

    @pl.when(slot == 0)
    def _():
        load_prompt(heads, order_ref, qkv_ref, k_ref, v_ref, first)
        vt_ref[...] = v_ref[...].astype(F32).T.astype(BF16)

    rows = own_rows(order_ref, first + slot)
    mine = qkv_ref[rows, :]
    k_own = repeat_heads(mine[:, q_cols : q_cols + HEAD_DIM], heads)
    v_own = repeat_heads(mine[:, q_cols + HEAD_DIM :], heads)
    q_stack = scaled_stack(mine[:, :q_cols], heads)

    def body(count):
        far, own = soft_parts(heads, slot, q_stack, k_ref[:count], k_own)
        mixed = matmul(vt_ref[:, :count], far.astype(BF16))
        mixed += matmul(v_own.astype(F32).T.astype(BF16), own.astype(BF16))
        o_ref[rows, :] = head_pick(mixed.T, heads).astype(BF16)

    by_keys(slot, body)


def attend_back_kernel(
    heads, order_ref, qkv_ref, d_ref, o_ref, k_ref, v_ref, kt_ref, dk_ref, dv_ref
):
    first, slot = pl.program_id(0) * GROUP_BLOCKS, pl.program_id(1)
    q_cols = heads * HEAD_DIM

    @pl.when(slot == 0)
    def _():
        load_prompt(heads, order_ref, qkv_ref, k_ref, v_ref, first)
        kt_ref[...] = k_ref[...].astype(F32).T.astype(BF16)
        dk_ref[...] = jnp.zeros_like(dk_ref)
        dv_ref[...] = jnp.zeros_like(dv_ref)

    rows = own_rows(order_ref, first + slot)
    mine = qkv_ref[rows, :]
    k_own = repeat_heads(mine[:, q_cols : q_cols + HEAD_DIM], heads)
    v_own = repeat_heads(mine[:, q_cols + HEAD_DIM :], heads)
    q_stack = scaled_stack(mine[:, :q_cols], heads)
    d_stack = head_stack(d_ref[rows, :], heads)

    def fold(d_k, d_v):
        return jnp.concatenate([head_fold(d_k, heads), head_fold(d_v, heads)], axis=1).astype(BF16)

    def body(count):
        far, own = soft_parts(heads, slot, q_stack, k_ref[:count], k_own)
        d_far, d_own = dot_nt(v_ref[:count], d_stack), dot_nt(v_own, d_stack)
        mean = jnp.sum(far * d_far, axis=0, keepdims=True)
        mean += jnp.sum(own * d_own, axis=0, keepdims=True)
        d_far = (far * (d_far - mean)).astype(BF16)
        d_own = (own * (d_own - mean)).astype(BF16)
        dv_ref[:count] += matmul(far.astype(BF16), d_stack)
        dk_ref[:count] += matmul(d_far, q_stack)
        dv_own = matmul(own.astype(BF16), d_stack)
        dk_own = matmul(d_own, q_stack)
        d_q = matmul(kt_ref[:, :count], d_far) + matmul(k_own.astype(F32).T.astype(BF16), d_own)
        o_ref[rows, :q_cols] = (head_pick(d_q.T, heads) * ATTN_MULT).astype(BF16)

        @pl.when(slot < PROMPT_BLOCKS)
        def _():
            at = pl.ds(pl.multiple_of(slot * BLOCK, BLOCK), BLOCK)
            dk_ref[at] += dk_own
            dv_ref[at] += dv_own

        @pl.when(slot >= PROMPT_BLOCKS)
        def _():
            o_ref[rows, q_cols:] = fold(dk_own, dv_own)

    by_keys(slot, body)

    @pl.when(slot == GROUP_BLOCKS - 1)
    def _():
        for s in range(PROMPT_BLOCKS):
            at = pl.ds(s * BLOCK, BLOCK)
            o_ref[own_rows(order_ref, first + s), q_cols:] = fold(dk_ref[at], dv_ref[at])


def whole(shape):
    return pl.BlockSpec(shape, lambda g, s, order: (0,) * len(shape))


def attend(qkv, order, heads):
    tokens, cols = qkv.shape
    prompt, q_cols = PROMPT_BLOCKS * BLOCK, heads * HEAD_DIM
    return pl.pallas_call(
        functools.partial(attend_kernel, heads),
        out_shape=jax.ShapeDtypeStruct((tokens, q_cols), BF16),
        grid_spec=pltpu.PrefetchScalarGridSpec(
            num_scalar_prefetch=1,
            grid=(tokens // (GROUP_BLOCKS * BLOCK), GROUP_BLOCKS),
            in_specs=[whole((tokens, cols))],
            out_specs=whole((tokens, q_cols)),
            scratch_shapes=[
                pltpu.VMEM((prompt, q_cols), BF16),
                pltpu.VMEM((prompt, q_cols), BF16),
                pltpu.VMEM((q_cols, prompt), BF16),
            ],
        ),
        cost_estimate=BRIEF,
        compiler_params=pltpu.CompilerParams(vmem_limit_bytes=40 << 20),
    )(order, qkv)


def attend_back(qkv, d_attended, order, heads):
    tokens, cols = qkv.shape
    prompt, q_cols = PROMPT_BLOCKS * BLOCK, heads * HEAD_DIM
    return pl.pallas_call(
        functools.partial(attend_back_kernel, heads),
        out_shape=jax.ShapeDtypeStruct((tokens, cols), BF16),
        grid_spec=pltpu.PrefetchScalarGridSpec(
            num_scalar_prefetch=1,
            grid=(tokens // (GROUP_BLOCKS * BLOCK), GROUP_BLOCKS),
            in_specs=[whole((tokens, cols)), whole((tokens, q_cols))],
            out_specs=whole((tokens, cols)),
            scratch_shapes=[
                pltpu.VMEM((prompt, q_cols), BF16),
                pltpu.VMEM((prompt, q_cols), BF16),
                pltpu.VMEM((q_cols, prompt), BF16),
                pltpu.VMEM((prompt, q_cols), F32),
                pltpu.VMEM((prompt, q_cols), F32),
            ],
        ),
        cost_estimate=BRIEF,
        compiler_params=pltpu.CompilerParams(vmem_limit_bytes=40 << 20),
    )(order, qkv, d_attended)


def exchange_total_kernel(
    grps, chips, cut, paste, x_ref, t_ref, o_ref, sum_ref,
    over_z, over_plane, send, recv, local, zsend, zrecv, psend, precv,
):
    grp = lax.axis_index("grp")
    chip, core = place()
    me = chip * 2 + core
    far = [lax.rem(grp + s, grps) for s in range(1, grps)]
    steps = (3, 1, 2) if chips == 4 else tuple(range(1, chips))
    near = [(flip(chip, s, chips), c) for s in steps for c in (core, 1 - core)]
    near = near + [(chip, 1 - core)]
    barrier = pltpu.get_barrier_semaphore()
    for g in far:
        pl.semaphore_signal(barrier, inc=1, device_id={"grp": g}, device_id_type=MESH)
    for to, c in near:
        pl.semaphore_signal(
            barrier, inc=1, device_id={"chip": to, "core": c}, device_id_type=MESH
        )
    pl.semaphore_wait(barrier, len(far) + len(near))

    def z_copy(slot, sem, to):
        return pltpu.make_async_remote_copy(
            src_ref=t_ref,
            dst_ref=over_z.at[slot],
            send_sem=sem,
            recv_sem=zrecv.at[slot],
            device_id={"grp": to},
            device_id_type=MESH,
        )

    copies = []
    for i, g in enumerate(far):
        copy = z_copy(grp, zsend.at[i], g)
        copy.start()
        copies.append(copy)
    for i, (to, c) in enumerate(near):
        copy = remote(cut(x_ref, to * 2 + c), paste(o_ref, me), send.at[i], recv.at[me], to, c)
        copy.start()
        copies.append(copy)
    mine = pltpu.make_async_copy(cut(x_ref, me), paste(o_ref, me), local)
    mine.start()
    over_z[grp] = t_ref[...]
    for g in far:
        z_copy(g, zsend.at[0], g).wait_recv()
    over_plane[me] = jnp.sum(over_z[...], axis=0)
    for i, (to, c) in enumerate(near):
        copy = remote(over_plane.at[me], over_plane.at[me], psend.at[i], precv.at[me], to, c)
        copy.start()
        copies.append(copy)
    for to, c in near:
        slot = to * 2 + c
        remote(cut(x_ref, me), paste(o_ref, slot), send.at[0], recv.at[slot], to, c).wait_recv()
        remote(over_plane.at[me], over_plane.at[slot], psend.at[0], precv.at[slot], to, c).wait_recv()
    for copy in copies:
        copy.wait_send()
    mine.wait()
    sum_ref[...] = jnp.sum(over_plane[...], axis=0)


def exchange_total(x, t, shape, rows, cols, grps, chips, call_id):
    devs = 2 * chips
    return pl.pallas_call(
        functools.partial(exchange_total_kernel, grps, chips, by_cols(cols), by_rows(rows)),
        out_shape=(
            jax.ShapeDtypeStruct(shape, x.dtype),
            jax.ShapeDtypeStruct(t.shape, F32),
        ),
        in_specs=[ANY, VMEM],
        out_specs=(ANY, VMEM),
        scratch_shapes=[
            pltpu.VMEM((grps,) + t.shape, F32),
            pltpu.VMEM((devs,) + t.shape, F32),
            pltpu.SemaphoreType.DMA((devs,)),
            pltpu.SemaphoreType.DMA((devs,)),
            pltpu.SemaphoreType.DMA,
            pltpu.SemaphoreType.DMA((grps,)),
            pltpu.SemaphoreType.DMA((grps,)),
            pltpu.SemaphoreType.DMA((devs,)),
            pltpu.SemaphoreType.DMA((devs,)),
        ],
        cost_estimate=BRIEF,
        compiler_params=pltpu.CompilerParams(collective_id=call_id, has_side_effects=True),
    )(x, t)


def params(axes, mib=56):
    return pltpu.CompilerParams(
        dimension_semantics=("arbitrary",) * axes, vmem_limit_bytes=mib << 20
    )


def tile_rows(count, limit):
    while count % limit:
        limit //= 2
    return limit


def widen_kernel(n_ref, w_ref, h_ref, ht_ref, s_ref, t_ref, nt_ref):
    values = n_ref[...]
    gate, up = matmul(values, w_ref[0, 0]), matmul(values, w_ref[0, 1])
    sig = 1.0 / (1.0 + jnp.exp(-gate))
    silu = gate * sig
    hidden = (silu * up).astype(BF16)
    h_ref[0] = hidden
    ht_ref[0] = hidden.T
    s_ref[0] = silu.astype(BF16)
    t_ref[0] = (up * (sig * (1.0 + gate * (1.0 - sig)))).astype(BF16)

    @pl.when(pl.program_id(1) == 0)
    def _():
        nt_ref[...] = values.T


def widen(normed, weights):
    tokens, depth = normed.shape
    shards, _, _, width = weights.shape
    rows = tile_rows(tokens, 1024)
    tall = jax.ShapeDtypeStruct((shards, tokens, width), BF16)
    tall_spec = pl.BlockSpec((1, rows, width), lambda r, s: (s, r, 0))
    return pl.pallas_call(
        widen_kernel,
        out_shape=(
            tall,
            jax.ShapeDtypeStruct((shards, width, tokens), BF16),
            tall,
            tall,
            jax.ShapeDtypeStruct((depth, tokens), BF16),
        ),
        grid=(tokens // rows, shards),
        in_specs=[
            pl.BlockSpec((rows, depth), lambda r, s: (r, 0)),
            pl.BlockSpec((1, 2, depth, width), lambda r, s: (s, 0, 0, 0)),
        ],
        out_specs=(
            tall_spec,
            pl.BlockSpec((1, width, rows), lambda r, s: (s, 0, r)),
            tall_spec,
            tall_spec,
            pl.BlockSpec((depth, rows), lambda r, s: (0, r)),
        ),
        cost_estimate=BRIEF,
        compiler_params=params(2),
    )(normed, weights)


def down_part_kernel(ht_ref, d_ref, o_ref):
    o_ref[0] = matmul(ht_ref[0], d_ref[...]).astype(BF16)


def down_part(hidden_t, upstream):
    shards, width, tokens = hidden_t.shape
    depth = upstream.shape[1]
    cols = tile_rows(depth, 1024)
    return pl.pallas_call(
        down_part_kernel,
        out_shape=jax.ShapeDtypeStruct((shards, width, depth), BF16),
        grid=(depth // cols, shards),
        in_specs=[
            pl.BlockSpec((1, width, tokens), lambda c, s: (s, 0, 0)),
            pl.BlockSpec((tokens, cols), lambda c, s: (0, c)),
        ],
        out_specs=pl.BlockSpec((1, width, cols), lambda c, s: (s, 0, c)),
        cost_estimate=BRIEF,
        compiler_params=params(2),
    )(hidden_t, upstream)


def mix_kernel(h_ref, w_ref, m_ref):
    mixed = None
    for i in range(w_ref.shape[0]):
        part = matmul(h_ref[i], w_ref[i])
        mixed = part if mixed is None else mixed + part
    m_ref[...] = mixed.astype(BF16)


def narrow_specs(hidden, weights):
    shards, tokens, width = hidden.shape
    depth = weights.shape[2]
    rows = tile_rows(tokens, 512)
    return (
        tokens // rows,
        pl.BlockSpec((shards, rows, width), lambda r: (0, r, 0)),
        pl.BlockSpec((rows, depth), lambda r: (r, 0)),
        pl.BlockSpec(weights.shape, lambda r: (0, 0, 0), pipeline_mode=pl.Buffered(1)),
    )


def mix(hidden, weights):
    steps, tall_spec, flat_spec, weight_spec = narrow_specs(hidden, weights)
    return pl.pallas_call(
        mix_kernel,
        out_shape=jax.ShapeDtypeStruct((hidden.shape[1], weights.shape[2]), BF16),
        grid=(steps,),
        in_specs=[tall_spec, weight_spec],
        out_specs=flat_spec,
        cost_estimate=BRIEF,
        compiler_params=params(1),
    )(hidden, weights)


def narrow_back_kernel(s_ref, t_ref, d_ref, w_ref, dg_ref, du_ref):
    upstream = d_ref[...]
    for i in range(w_ref.shape[0]):
        d_hidden = dot_nt(upstream, w_ref[i])
        dg_ref[i] = (d_hidden * t_ref[i].astype(F32)).astype(BF16)
        du_ref[i] = (d_hidden * s_ref[i].astype(F32)).astype(BF16)


def narrow_back(silu, slope, upstream, weights):
    steps, tall_spec, flat_spec, weight_spec = narrow_specs(silu, weights)
    tall = jax.ShapeDtypeStruct(silu.shape, BF16)
    return pl.pallas_call(
        narrow_back_kernel,
        out_shape=(tall, tall),
        grid=(steps,),
        in_specs=[tall_spec, tall_spec, flat_spec, weight_spec],
        out_specs=(tall_spec, tall_spec),
        cost_estimate=BRIEF,
        compiler_params=params(1),
    )(silu, slope, upstream, weights)


def widen_part_kernel(nt_ref, dg_ref, du_ref, o_ref):
    values = nt_ref[...]
    o_ref[0, 0] = matmul(values, dg_ref[0]).astype(BF16)
    o_ref[0, 1] = matmul(values, du_ref[0]).astype(BF16)


def widen_part(normed_t, d_gate, d_up):
    depth, tokens = normed_t.shape
    shards, _, width = d_gate.shape
    rows = tile_rows(depth, 1024)
    tall_spec = pl.BlockSpec((1, tokens, width), lambda r, s: (s, 0, 0))
    return pl.pallas_call(
        widen_part_kernel,
        out_shape=jax.ShapeDtypeStruct((shards, 2, depth, width), BF16),
        grid=(depth // rows, shards),
        in_specs=[pl.BlockSpec((rows, tokens), lambda r, s: (r, 0)), tall_spec, tall_spec],
        out_specs=pl.BlockSpec((1, 2, rows, width), lambda r, s: (s, 0, r, 0)),
        cost_estimate=BRIEF,
        compiler_params=params(2),
    )(normed_t, d_gate, d_up)


def widen_back_kernel(dg_ref, du_ref, w_ref, o_ref):
    total = None
    for i in range(w_ref.shape[0]):
        part = dot_nt(dg_ref[i], w_ref[i, 0]) + dot_nt(du_ref[i], w_ref[i, 1])
        total = part if total is None else total + part
    o_ref[...] = total.astype(BF16)


def widen_back(d_gate, d_up, weights):
    shards, tokens, width = d_gate.shape
    depth = weights.shape[2]
    rows = tile_rows(tokens, 512)
    tall_spec = pl.BlockSpec((shards, rows, width), lambda r: (0, r, 0))
    return pl.pallas_call(
        widen_back_kernel,
        out_shape=jax.ShapeDtypeStruct((tokens, depth), BF16),
        grid=(tokens // rows,),
        in_specs=[
            tall_spec,
            tall_spec,
            pl.BlockSpec(weights.shape, lambda r: (0, 0, 0, 0), pipeline_mode=pl.Buffered(1)),
        ],
        out_specs=pl.BlockSpec((rows, depth), lambda r: (r, 0)),
        cost_estimate=BRIEF,
        compiler_params=params(1),
    )(d_gate, d_up, weights)


def stage_step(stage):
    return jnp.where(stage == 0, 3, jnp.where(stage == 3, 0, stage))


class Square:
    def __init__(self, acc, mine, away, twin, moved, corner, landed, tsend, trecv, msend, mrecv, csend, crecv):
        self.acc, self.mine, self.away, self.twin = acc, mine, away, twin
        self.moved, self.corner, self.landed = moved, corner, landed
        self.tsend, self.trecv, self.msend, self.mrecv = tsend, trecv, msend, mrecv
        self.csend, self.crecv = csend, crecv
        self.chip, self.core = place()
        self.rows = mine.shape[1]
        self.half = self.rows // 2

    def greet(self):
        peers = [(flip(self.chip, s, 4), self.core) for s in (1, 2)]
        greet(peers + [(self.chip, 1 - self.core)])

    def twin_copy(self, stage):
        return remote(
            self.away.at[stage], self.twin.at[stage], self.tsend.at[stage], self.trecv.at[stage],
            self.chip, 1 - self.core,
        )

    def offer(self, stage):
        own, other = self.core * self.rows, (1 - self.core) * self.rows
        self.mine[stage] = self.acc[pl.ds(pl.multiple_of(own, self.rows), self.rows)].astype(BF16)
        self.away[stage] = self.acc[pl.ds(pl.multiple_of(other, self.rows), self.rows)].astype(BF16)
        self.twin_copy(stage).start()

    def at(self, h):
        return pl.ds(h * self.half, self.half)

    def both(self, stage, h):
        return self.mine[stage, self.at(h)].astype(F32) + self.twin[stage, self.at(h)].astype(F32)

    def corner_copy(self, h):
        return remote(
            self.moved.at[0, self.at(h)], self.corner.at[h], self.csend.at[h], self.crecv.at[h],
            flip(self.chip, h + 1, 4), self.core,
        )

    def copy(self, stage, h):
        return remote(
            self.moved.at[stage, self.at(h)], self.landed.at[stage - 1, self.at(h)],
            self.msend.at[stage - 1, h], self.mrecv.at[stage - 1, h],
            flip(self.chip, stage, 4), self.core,
        )

    def corners(self):
        self.twin_copy(0).wait_recv()
        for h in range(2):
            self.moved[0, self.at(h)] = self.both(0, h).astype(BF16)
            self.corner_copy(h).start()

    def plain(self, stage):
        self.twin_copy(stage).wait_recv()
        h = stage - 1
        self.moved[stage, self.at(h)] = self.both(stage, h).astype(BF16)
        self.copy(stage, h).start()

    def joined(self, stage):
        h = 2 - stage
        self.corner_copy(h).wait_recv()
        total = self.both(stage, h) + self.corner[h].astype(F32)
        self.moved[stage, self.at(h)] = total.astype(BF16)
        self.copy(stage, h).start()

    def finish(self, o_ref):
        self.twin_copy(3).wait_recv()
        for h in range(2):
            o_ref[self.at(h)] = self.both(3, h)
        for stage, h in ((1, 0), (2, 1), (2, 0), (1, 1)):
            self.copy(stage, h).wait_recv()
            o_ref[self.at(h)] += self.landed[stage - 1, self.at(h)].astype(F32)
        for stage in (1, 2):
            for h in range(2):
                self.copy(stage, h).wait_send()
        for h in range(2):
            self.corner_copy(h).wait_send()
        for stage in range(4):
            self.twin_copy(stage).wait_send()


def square_kernel(compute, count, *refs):
    operands, o_ref, scratch = refs[:count], refs[count], refs[count + 1 :]
    run = Square(*scratch)
    stage = pl.program_id(0)

    @pl.when(stage == 0)
    def _():
        run.greet()

    @pl.when(stage == 3)
    def _():
        run.plain(2)
        run.joined(2)
        run.joined(1)

    target = jnp.bitwise_xor(run.chip, stage_step(stage))
    width = 2 * run.rows
    run.acc[...] = compute(operands, pl.ds(pl.multiple_of(target * width, width), width))
    run.offer(stage)

    @pl.when(stage == 1)
    def _():
        run.corners()

    @pl.when(stage == 2)
    def _():
        run.plain(1)

    @pl.when(stage == 3)
    def _():
        run.finish(o_ref)


def square_reduce(compute, operands, rows, call_id):
    block = (rows, D)

    def held(shape):
        return pl.BlockSpec(shape, lambda s: (0,) * len(shape), pipeline_mode=pl.Buffered(1))

    return pl.pallas_call(
        functools.partial(square_kernel, compute, len(operands)),
        out_shape=jax.ShapeDtypeStruct(block, F32),
        grid=(4,),
        in_specs=[held(x.shape) for x in operands],
        out_specs=held(block),
        scratch_shapes=[
            pltpu.VMEM((2 * rows, D), F32),
            pltpu.VMEM((4,) + block, BF16),
            pltpu.VMEM((4,) + block, BF16),
            pltpu.VMEM((4,) + block, BF16),
            pltpu.VMEM((3,) + block, BF16),
            pltpu.VMEM((2, rows // 2, D), BF16),
            pltpu.VMEM((2,) + block, BF16),
            pltpu.SemaphoreType.DMA((4,)),
            pltpu.SemaphoreType.DMA((4,)),
            pltpu.SemaphoreType.DMA((2, 2)),
            pltpu.SemaphoreType.DMA((2, 2)),
            pltpu.SemaphoreType.DMA((2,)),
            pltpu.SemaphoreType.DMA((2,)),
        ],
        cost_estimate=BRIEF,
        compiler_params=pltpu.CompilerParams(
            collective_id=call_id, has_side_effects=True, vmem_limit_bytes=60 << 20
        ),
    )(*operands)


def widen_back_rows(refs, rows):
    dg_ref, du_ref, w_ref = refs
    total = None
    for i in range(w_ref.shape[0]):
        part = dot_nt(dg_ref[i, rows], w_ref[i, 0]) + dot_nt(du_ref[i, rows], w_ref[i, 1])
        total = part if total is None else total + part
    return total


def project_back_rows(refs, rows):
    d_ref, w_ref = refs
    return dot_nt(d_ref[rows], w_ref[...])


def mix_rows(refs, rows):
    h_ref, w_ref = refs
    total = None
    for i in range(w_ref.shape[0]):
        part = matmul(h_ref[i, rows], w_ref[i])
        total = part if total is None else total + part
    return total


def twin_kernel(compute, count, *refs):
    operands, (o_ref, corner_ref, x_ref, y_ref) = refs[:count], refs[count : count + 4]
    acc, mine, away, twin, tsend, trecv = refs[count + 4 :]
    chip, core = place()
    stage = pl.program_id(0)
    rows = o_ref.shape[0]

    def copy(s):
        return remote(away.at[s], twin.at[s], tsend.at[s], trecv.at[s], chip, 1 - core)

    def both(s):
        copy(s).wait_recv()
        return mine[s].astype(F32) + twin[s].astype(F32)

    @pl.when(stage == 0)
    def _():
        greet([(chip, 1 - core)])

    target = jnp.bitwise_xor(chip, stage_step(stage)) * 2 * rows
    acc[...] = compute(operands, pl.ds(pl.multiple_of(target, 2 * rows), 2 * rows))
    mine[stage] = acc[pl.ds(pl.multiple_of(core * rows, rows), rows)].astype(BF16)
    away[stage] = acc[pl.ds(pl.multiple_of((1 - core) * rows, rows), rows)].astype(BF16)
    copy(stage).start()

    for s, part_ref in enumerate((corner_ref, x_ref, y_ref)):

        @pl.when(stage == s + 1)
        def _(s=s, part_ref=part_ref):
            part_ref[...] = both(s).astype(BF16)

    @pl.when(stage == 3)
    def _():
        o_ref[...] = both(3)
        for s in range(4):
            copy(s).wait_send()


def twin_reduce(compute, operands, rows, call_id):
    block = (rows, D)

    def held(shape):
        return pl.BlockSpec(shape, lambda s: (0,) * len(shape), pipeline_mode=pl.Buffered(1))

    return pl.pallas_call(
        functools.partial(twin_kernel, compute, len(operands)),
        out_shape=(jax.ShapeDtypeStruct(block, F32),) + (jax.ShapeDtypeStruct(block, BF16),) * 3,
        grid=(4,),
        in_specs=[held(x.shape) for x in operands],
        out_specs=(held(block),) * 4,
        scratch_shapes=[
            pltpu.VMEM((2 * rows, D), F32),
            pltpu.VMEM((4,) + block, BF16),
            pltpu.VMEM((4,) + block, BF16),
            pltpu.VMEM((4,) + block, BF16),
            pltpu.SemaphoreType.DMA((4,)),
            pltpu.SemaphoreType.DMA((4,)),
        ],
        cost_estimate=BRIEF,
        compiler_params=pltpu.CompilerParams(
            collective_id=call_id, has_side_effects=True, vmem_limit_bytes=60 << 20
        ),
    )(*operands)


def swap_others(parts):
    return tuple(swap_chips(part, step) for step, part in zip((3, 1, 2), parts))


def join(own, came):
    for part in came:
        own = own + part.astype(F32)
    return own


def entry_kernel(
    grps, chips, tok_ref, cot_ref, pack_ref, tile_ref, all_tok, all_cot, all_pack, all_tile,
    tsend, trecv, tlocal, csend, crecv, clocal, psend, precv, plocal, zrecv, usend, dsend,
):
    grp = lax.axis_index("grp")
    chip, core = place()
    me = chip * 2 + core
    above, below = lax.rem(grp + 1, grps), lax.rem(grp + grps - 1, grps)
    near = [(flip(chip, s, chips), c) for s in range(1, chips) for c in (core, 1 - core)]
    near = near + [(chip, 1 - core)]
    barrier = pltpu.get_barrier_semaphore()
    for g in (above, below):
        pl.semaphore_signal(barrier, inc=1, device_id={"grp": g}, device_id_type=MESH)
    for to, c in near:
        pl.semaphore_signal(
            barrier, inc=1, device_id={"chip": to, "core": c}, device_id_type=MESH
        )
    pl.semaphore_wait(barrier, len(near) + 2)

    tok = Gather(chips, False, tok_ref, all_tok, tsend, trecv, tlocal)
    cot = Gather(chips, False, cot_ref, all_cot, csend, crecv, clocal)
    packs, mine = [], []
    for i, (to, c) in enumerate(near):
        copy = remote(
            pack_ref.at[to * 2 + c], all_pack.at[grp, me], psend.at[0, i], precv.at[0, me], to, c
        )
        copy.start()
        packs.append(copy)
        copy = remote(tile_ref, all_tile.at[grp, me], psend.at[1, i], precv.at[1, me], to, c)
        copy.start()
        packs.append(copy)
    for k, (src, dst) in enumerate(((pack_ref.at[me], all_pack), (tile_ref, all_tile))):
        mine.append(pltpu.make_async_copy(src, dst.at[grp, me], plocal.at[k]))
        mine[k].start()
    for to, c in near:
        slot = to * 2 + c
        for k, (src, dst) in enumerate(((pack_ref.at[me], all_pack), (tile_ref, all_tile))):
            remote(src, dst.at[grp, slot], psend.at[k, 0], precv.at[k, slot], to, c).wait_recv()
    for copy in mine:
        copy.wait()

    def z_copies(block, sems, step, to):
        return [
            pltpu.make_async_remote_copy(
                src_ref=whole.at[block],
                dst_ref=whole.at[block],
                send_sem=sems.at[k, step],
                recv_sem=zrecv.at[k, block],
                device_id={"grp": to},
                device_id_type=MESH,
            )
            for k, whole in enumerate((all_pack, all_tile))
        ]

    has_above, has_below = grp + 1 < grps, grp > 0

    def send(step, block, up):
        @pl.when(has_above if up else has_below)
        def _():
            for copy in z_copies(block, usend if up else dsend, step, above if up else below):
                copy.start()

    def relay(step):
        low, high = grp - step, grp + step

        @pl.when(low >= 0)
        def _():
            for copy in z_copies(low, usend, 0, below):
                copy.wait_recv()
            send(step, low, True)

        @pl.when(high < grps)
        def _():
            for copy in z_copies(high, dsend, 0, above):
                copy.wait_recv()
            send(step, high, False)

    send(0, grp, True)
    send(0, grp, False)
    tok.start()
    tok.relay(0, 4)
    relay(1)
    cot.start()
    tok.relay(4, None)
    for step in range(2, grps - 1):
        relay(step)
    cot.relay(0, 4)
    if grps > 2:
        relay(grps - 1)
    cot.relay(4, None)
    tok.finish()
    cot.finish()
    for copy in packs:
        copy.wait_send()
    for step in range(grps):
        for up in (True, False):
            held = grp - step >= 0 if up else grp + step < grps

            @pl.when(held & (has_above if up else has_below))
            def _(step=step, up=up):
                block = grp - step if up else grp + step
                sems, to = (usend, above) if up else (dsend, below)
                for copy in z_copies(block, sems, step, to):
                    copy.wait_send()


def entry(tokens, cotangent, packed, tile, grps, chips, call_id):
    devs = 2 * chips
    return pl.pallas_call(
        functools.partial(entry_kernel, grps, chips),
        out_shape=(
            jax.ShapeDtypeStruct((devs,) + tokens.shape, BF16),
            jax.ShapeDtypeStruct((devs,) + cotangent.shape, BF16),
            jax.ShapeDtypeStruct((grps,) + packed.shape, BF16),
            jax.ShapeDtypeStruct((grps, devs) + tile.shape, BF16),
        ),
        in_specs=[ANY] * 4,
        out_specs=(ANY,) * 4,
        scratch_shapes=gather_sems(chips)
        + gather_sems(chips)
        + [
            pltpu.SemaphoreType.DMA((2, devs)),
            pltpu.SemaphoreType.DMA((2, devs)),
            pltpu.SemaphoreType.DMA((2,)),
            pltpu.SemaphoreType.DMA((2, grps)),
            pltpu.SemaphoreType.DMA((2, grps)),
            pltpu.SemaphoreType.DMA((2, grps)),
        ],
        cost_estimate=BRIEF,
        compiler_params=pltpu.CompilerParams(collective_id=call_id, has_side_effects=True),
    )(tokens, cotangent, packed, tile)


def project_kernel(width, x_ref, w_ref, tile_ref, n_ref, qkv_ref, gain_ref):
    @pl.when(pl.program_id(0) == 0)
    def _():
        gain_ref[...] = jnp.zeros_like(gain_ref)
        for f in range(tile_ref.shape[0]):
            gain_ref[0:2, f * width : (f + 1) * width] = tile_ref[f, 0:2, :width].astype(F32)

    values = x_ref[...].astype(F32)
    factor = lax.rsqrt(jnp.mean(values * values, axis=-1, keepdims=True) + EPSILON)
    normed = (values * factor * gain_ref[0:1]).astype(BF16)
    n_ref[...] = normed
    qkv_ref[...] = matmul(normed, w_ref[...]).astype(BF16)


def project(tokens, weights, tiles):
    count, depth = tokens.shape
    used = weights.shape[1]
    rows = tile_rows(count, 256)
    return pl.pallas_call(
        functools.partial(project_kernel, depth // tiles.shape[0]),
        out_shape=(
            jax.ShapeDtypeStruct((count, depth), BF16),
            jax.ShapeDtypeStruct((count, used), BF16),
            jax.ShapeDtypeStruct((8, depth), F32),
        ),
        grid=(count // rows,),
        in_specs=[
            pl.BlockSpec((rows, depth), lambda r: (r, 0)),
            pl.BlockSpec(weights.shape, lambda r: (0, 0)),
            pl.BlockSpec(tiles.shape, lambda r: (0, 0, 0)),
        ],
        out_specs=(
            pl.BlockSpec((rows, depth), lambda r: (r, 0)),
            pl.BlockSpec((rows, used), lambda r: (r, 0)),
            pl.BlockSpec((8, depth), lambda r: (0, 0)),
        ),
        cost_estimate=BRIEF,
        compiler_params=params(1),
    )(tokens, weights, tiles)


def turn_kernel(
    count, res_ref, dn_ref, cot_ref, gain_ref, branch_ref, own_ref, *refs
):
    came, (att_ref, w_ref, lay_ref, dres_ref, tot_ref, datt_ref, *grad_refs, dba) = refs[:count], refs[count:]

    @pl.when(pl.program_id(0) == 0)
    def _():
        residual = res_ref[...]
        mlp = own_ref[...]
        for part_ref in came:
            mlp = mlp + part_ref[...].astype(F32)
        mlp = RESID_MULT * mlp
        layer_out = residual + mlp
        lay_ref[...] = layer_out.astype(BF16)
        attn = RESID_MULT * branch_ref[...]
        grad = dn_ref[...]
        scaled = gain_ref[1:2] * grad
        factor = lax.rsqrt(jnp.mean(residual * residual, axis=-1, keepdims=True) + EPSILON)
        inner = jnp.mean(residual * scaled, axis=-1, keepdims=True)
        d_residual = cot_ref[...].astype(F32) + factor * scaled
        d_residual = d_residual - residual * (factor * factor * factor * inner)
        dres_ref[...] = d_residual
        dba[...] = (RESID_MULT * d_residual).astype(BF16)
        d_gain = jnp.sum(grad * residual * factor, axis=0, keepdims=True)
        width = tot_ref.shape[1]
        tot_ref[...] = jnp.zeros_like(tot_ref)
        for r in range(pl.cdiv(D, width)):
            last = min(width, D - r * width)
            tot_ref[r : r + 1, :last] = d_gain[:, r * width : r * width + last]
        lane = lax.broadcasted_iota(jnp.int32, (1, 128), 1)
        row = jnp.zeros((1, 128), F32)
        for i, part in enumerate((layer_out, attn, mlp)):
            square = jnp.sum(jnp.sum(part * part, axis=0, keepdims=True), axis=1, keepdims=True)
            row = jnp.where(lane == i, square, row)
        tot_ref[7:8, :128] = row

    datt_ref[...] = dot_nt(dba[...], w_ref[...]).astype(BF16)
    grad = matmul(att_ref[...].T, dba[...])
    if len(grad_refs) == 1:
        grad_refs[0][...] = grad.astype(BF16)
        return
    mine_ref, away_ref = grad_refs
    first = lax.axis_index("core") == 0
    width = mine_ref.shape[2]
    for i in range(mine_ref.shape[1]):
        even = grad[2 * i * width : (2 * i + 1) * width]
        odd = grad[(2 * i + 1) * width : (2 * i + 2) * width]
        mine_ref[0, i] = jnp.where(first, even, odd).astype(BF16)
        away_ref[0, i] = jnp.where(first, odd, even).astype(BF16)


def turn(residual, d_normed, cotangent, gains, branch, own, came, attended, weights, width):
    rows = residual.shape[0]
    cols = 4 * width if came else 256
    scratch = [pltpu.VMEM((rows, D), BF16)]
    grads = (jax.ShapeDtypeStruct((D, D), BF16),)
    grad_specs = (pl.BlockSpec((cols, D), lambda j: (j, 0)),)
    if came:
        half = (D // (8 * width), 4, width, D)
        grads = (jax.ShapeDtypeStruct(half, BF16),) * 2
        grad_specs = (pl.BlockSpec((1, 2, width, D), lambda j: (j // 2, j % 2, 0, 0)),) * 2
    flat = jax.ShapeDtypeStruct((rows, D), F32)

    def held(shape):
        return pl.BlockSpec(shape, lambda j: (0,) * len(shape), pipeline_mode=pl.Buffered(1))

    return pl.pallas_call(
        functools.partial(turn_kernel, len(came)),
        out_shape=(
            jax.ShapeDtypeStruct((rows, D), BF16),
            flat,
            jax.ShapeDtypeStruct((8, 3 * D // 16), F32),
            jax.ShapeDtypeStruct((rows, D), BF16),
        )
        + grads,
        grid=(D // cols,),
        in_specs=[held((rows, D))] * 3
        + [held((8, D))]
        + [held((rows, D))] * (2 + len(came))
        + [
            pl.BlockSpec((rows, cols), lambda j: (0, j)),
            pl.BlockSpec((cols, D), lambda j: (j, 0)),
        ],
        out_specs=(
            held((rows, D)),
            held((rows, D)),
            held((8, 3 * D // 16)),
            pl.BlockSpec((rows, cols), lambda j: (0, j)),
        )
        + grad_specs,
        scratch_shapes=scratch,
        cost_estimate=BRIEF,
        compiler_params=params(1),
    )(residual, d_normed, cotangent, gains, branch, own, *came, attended, weights)


def split_kernel(copies, q_cols, kv_cols, x_ref, wq_ref, wk_ref, wv_ref, q_ref, k_ref, v_ref, sum_ref):
    total = jnp.zeros(sum_ref.shape, F32)
    for s in range(x_ref.shape[0]):
        block = x_ref[s].astype(F32)
        at = slice(s * q_cols, (s + 1) * q_cols)
        q_ref[:, at] = block[:, :q_cols]
        weight = wq_ref[:, at].astype(F32)
        total += jnp.sum(block[:, :q_cols] * weight, axis=1, keepdims=True)
    for h in range(x_ref.shape[0] // copies):
        at = slice(h * kv_cols, (h + 1) * kv_cols)
        pair = x_ref[h * copies, :, q_cols:].astype(F32)
        for c in range(1, copies):
            pair += x_ref[h * copies + c, :, q_cols:].astype(F32)
        for ref, w_ref, part in (
            (k_ref, wk_ref, pair[:, :kv_cols]),
            (v_ref, wv_ref, pair[:, kv_cols:]),
        ):
            ref[:, at] = part
            total += jnp.sum(part * w_ref[:, at].astype(F32), axis=1, keepdims=True)
    sum_ref[...] = total


def split(sent, w_query, w_key, w_value, copies, q_cols, kv_cols):
    rows = w_query.shape[0]
    return pl.pallas_call(
        functools.partial(split_kernel, copies, q_cols, kv_cols),
        out_shape=tuple(
            jax.ShapeDtypeStruct(shape, F32)
            for shape in (w_query.shape, w_key.shape, w_value.shape, (rows, 1))
        ),
        in_specs=[VMEM] * 4,
        out_specs=(VMEM,) * 4,
        cost_estimate=BRIEF,
    )(sent, w_query, w_key, w_value)


def norm_parts(values):
    factor = lax.rsqrt(jnp.mean(values * values, axis=-1, keepdims=True) + EPSILON)
    return factor


def norm_back(values, factor, gain, grad):
    scaled = gain * grad
    inner = jnp.mean(values * scaled, axis=-1, keepdims=True)
    return factor * scaled - values * (factor * factor * factor * inner), jnp.sum(
        grad * values * factor, axis=0
    )


def on_device(
    tokens,
    block_group,
    block_slot,
    attn_gain,
    w_query,
    w_key,
    w_value,
    w_out,
    mlp_gain,
    w_gate,
    w_up,
    w_down,
    cotangent,
):
    grps = lax.axis_size("grp")
    devs = lax.axis_size(PLANE)
    chips = devs // 2
    rows = tokens.shape[0]
    w_rows = w_query.shape[0]
    q_heads = HEADS // devs
    kv_heads = 1
    assert devs % KV_HEADS == 0
    kv_copies = max(1, devs // KV_HEADS)
    q_cols, kv_cols = q_heads * HEAD_DIM, kv_heads * HEAD_DIM
    row_blocks = rows // BLOCK * devs
    row_groups = row_blocks // GROUP_BLOCKS

    row_first = lax.axis_index("grp") * row_blocks
    keys = lax.dynamic_slice_in_dim(block_group, row_first, row_blocks) * GROUP_BLOCKS
    keys = keys + lax.dynamic_slice_in_dim(block_slot, row_first, row_blocks)
    rank = jnp.sum((keys[None, :] < keys[:, None]).astype(jnp.int32), axis=1)
    ids = jnp.arange(row_blocks, dtype=jnp.int32)
    order = jnp.sum(jnp.where(rank[None, :] == ids[:, None], ids[None, :], 0), axis=1)

    def kv_split(w):
        w = w.reshape(w_rows, devs // kv_copies, kv_cols)
        return jnp.repeat(w, kv_copies, axis=1) if kv_copies > 1 else w

    packed = jnp.concatenate(
        [w_query.reshape(w_rows, devs, q_cols), kv_split(w_key), kv_split(w_value)], axis=2
    )
    packed = jnp.swapaxes(packed, 0, 1)
    used = q_cols + 2 * kv_cols
    tile = jnp.pad(jnp.stack([attn_gain, mlp_gain]), ((0, 14), (0, 128 - w_rows)))
    out_full = gather(w_out[None], "grp")
    upstream = cotangent.astype(F32)
    d_branch_mlp = (RESID_MULT * upstream).astype(BF16)
    all_tokens, d_branch_mlp, w_qkv, tiles = entry(
        tokens, d_branch_mlp, packed, tile, grps, chips, 2
    )
    w_qkv, tiles = w_qkv.reshape(D, used), tiles.reshape(-1, 16, 128)
    normed_one, qkv, gains = project(all_tokens.reshape(devs * rows, D), w_qkv, tiles)
    gain_one, gain_two = gains[0], gains[1]
    d_branch_mlp = d_branch_mlp.reshape(devs * rows, D)
    attended = attend(qkv, order, q_heads)
    attended = plane_exchange(
        attended, (rows, D), by_rows(rows), by_cols(q_cols), chips, 3
    )

    out_full = plane_gather(out_full, chips, 4, inner=True).reshape(D, D)
    layer_in = tokens.astype(F32)
    branch_attn = matmul(attended, out_full)
    residual = layer_in + RESID_MULT * branch_attn
    factor_two = norm_parts(residual)
    normed_two = (residual * factor_two * gain_two).astype(BF16)
    normed_two = plane_gather(normed_two, chips, 1).reshape(devs * rows, D)
    wide_w = gather(jnp.stack([w_gate, w_up])[None], "grp")
    down_w = gather(w_down[None], "grp")
    hidden, hidden_t, silu, slope, normed_t = widen(normed_two, wide_w)
    part_down = down_part(hidden_t, d_branch_mlp)
    part_down, hidden, silu = lax.optimization_barrier((part_down, hidden, silu))
    grad_down = scatter(part_down, "grp")
    if chips == 4:
        branch_mlp, *shares = twin_reduce(mix_rows, (hidden, down_w), rows, 11)
        shares, silu = lax.optimization_barrier((shares, silu))
        shares = swap_others(shares)
    d_gate, d_up = narrow_back(silu, slope, d_branch_mlp, down_w)
    if chips == 4:
        part_wide = widen_part(normed_t, d_gate, d_up)
        part_wide, shares, d_gate, d_up = lax.optimization_barrier(
            (part_wide, shares, d_gate, d_up)
        )
        grad_wide = scatter(part_wide, "grp")
        d_normed_two = square_reduce(widen_back_rows, (d_gate, d_up, wide_w), rows, 10)
    else:
        part_wide = widen_part(normed_t, d_gate, d_up)
        part_wide, d_gate, d_up = lax.optimization_barrier((part_wide, d_gate, d_up))
        grad_wide = scatter(part_wide, "grp")
        d_normed_two = widen_back(d_gate, d_up, wide_w)
        d_normed_two = plane_reduce(d_normed_two.reshape(devs, rows, D), chips, 5)
        branch_mlp = mix(hidden, down_w)
        branch_mlp = plane_reduce(branch_mlp.reshape(devs, rows, D), chips, 5)

    layer_out, d_residual, totals, d_attended, grad_out, *away = turn(
        residual,
        d_normed_two,
        cotangent,
        gains,
        branch_attn,
        branch_mlp,
        shares if chips == 4 else (),
        attended,
        out_full,
        w_rows,
    )
    if chips == 4:
        drift_out = Drift(grad_out, *away)
    d_attended, totals = exchange_total(
        d_attended, totals, (devs * rows, q_cols), rows, q_cols, grps, chips, 7
    )
    if chips == 4:
        sent_out, d_attended = lax.optimization_barrier((drift_out.parts(), d_attended))
        sent_out = swap_others(sent_out)
    d_attended, grad_down = lax.optimization_barrier((d_attended, grad_down))
    d_qkv = attend_back(qkv, d_attended, order, q_heads)
    if chips == 4:
        sent_out, d_qkv = lax.optimization_barrier((sent_out, d_qkv))
    sent = over_rows(normed_one, d_qkv).astype(BF16)
    sent, d_qkv, grad_wide = lax.optimization_barrier((sent, d_qkv, grad_wide))
    sent = scatter(sent, "grp")
    d_normed_one = over_cols(d_qkv, w_qkv).astype(BF16).reshape(devs, rows, D)
    if chips == 4:
        sent_out, d_normed_one = lax.optimization_barrier((sent_out, d_normed_one))
        grad_out = join(drift_out.own, sent_out).astype(BF16)
    else:
        grad_out = plane_reduce(
            grad_out.reshape(grps, devs, w_rows, D), chips, 6, dtype=BF16, inner=True
        )
    grad_out, d_normed_one = lax.optimization_barrier((grad_out, d_normed_one))
    grad_out = scatter(grad_out, "grp")
    d_normed_one = plane_reduce(d_normed_one, chips, 5)
    d_normed_one, sent = lax.optimization_barrier((d_normed_one, sent))
    d_input_norm, _ = norm_back(layer_in, norm_parts(layer_in), gain_one, d_normed_one)
    tokens_grad = (d_residual + d_input_norm).astype(BF16)
    sent = sent.reshape(devs, w_rows, q_cols + 2 * kv_cols)
    sent = plane_exchange(sent, sent.shape, by_slot, by_slot, chips, 9)
    sent, grad_out = lax.optimization_barrier((sent, grad_out))
    grad_out = grad_out.reshape(w_rows, D).astype(F32)

    grad_query, grad_key, grad_value, gain_sum = split(
        sent, w_query, w_key, w_value, kv_copies, q_cols, kv_cols
    )
    gain_one_grad = gain_sum[:, 0] / attn_gain.astype(F32)
    rms_stats = jnp.sqrt(totals[7, :3] / (rows * grps * devs * D))
    gain_first = (lax.axis_index("grp") * devs + lax.axis_index(PLANE)) * w_rows
    gain_two_grad = lax.dynamic_slice(totals.reshape(-1), (gain_first,), (w_rows,))
    return (
        layer_out,
        tokens_grad,
        gain_one_grad,
        grad_query,
        grad_key,
        grad_value,
        grad_out,
        gain_two_grad,
        grad_wide[0, 0].astype(F32),
        grad_wide[0, 1].astype(F32),
        grad_down[0].astype(F32),
        rms_stats,
    )


def solution(mesh):
    shape = (mesh.shape["grp"], mesh.shape["blk"] // 2, 2)
    mesh = Mesh(mesh.devices.reshape(shape), EVERY)
    row, col, vec = P(EVERY, None), P(None, EVERY), P(EVERY)
    return jax.shard_map(
        on_device,
        mesh=mesh,
        in_specs=(row, P(), P(), vec, row, row, row, row, vec, col, col, row, row),
        out_specs=(row, row, vec, row, row, row, row, vec, col, col, row, P()),
        check_vma=False,
    )
```
